32 devices in a mesh: seq: 4 (over y, x), tok: 8 (over z, core).
Axes of the slice: x: 2, y: 2, z: 4, core: 2. Of those that a mesh axis runs over, the one named last changes fastest.
Arguments:
- inputs: bfloat16 [8, 1024, 768], P('seq', 'tok'), may hold values from -7.5 to 7.5
- lengths: int32 [8], P('seq'), may hold values from 256 to 1024, as said below
- bounds: int32 [8, 65], P('seq'), may hold values from 0 to 1024, as said below
- w_query: float32 [768, 768], P(('seq', 'tok')), may hold values from -0.3125 to 0.3125
- w_key: float32 [768, 768], P(('seq', 'tok')), may hold values from -0.3125 to 0.3125
- w_value: float32 [768, 768], P(('seq', 'tok')), may hold values from -0.21875 to 0.21875
- w_out: float32 [768, 768], P(('seq', 'tok')), may hold values from -0.4375 to 0.4375
- w_conv: float32 [12, 33], replicated, may hold values from -1.2 to 1.2
- w_in: float32 [768, 3072], P(('seq', 'tok')), may hold values from -0.21875 to 0.21875
- w_back: float32 [3072, 768], P(('seq', 'tok')), may hold values from -0.109375 to 0.109375
- b_in: float32 [3072], P(('seq', 'tok')), may hold values from -1.5 to 1.5
- gains: float32 [2, 768], P(None, ('seq', 'tok')), may hold values from 0.5 to 1.5
- shifts: float32 [6, 768], P(None, ('seq', 'tok')), may hold values from -1.5 to 1.5
- cotangent: bfloat16 [8, 1024, 768], P('seq', 'tok'), may hold values from -6 to 6
Outputs:
- result: float32 [8, 1024, 768], P('seq', 'tok')
- grad_inputs: float32 [8, 1024, 768], P('seq', 'tok')
- grad_w_query: float32 [768, 768], P(('seq', 'tok'))
- grad_w_key: float32 [768, 768], P(('seq', 'tok'))
- grad_w_value: float32 [768, 768], P(('seq', 'tok'))
- grad_w_out: float32 [768, 768], P(('seq', 'tok'))
- grad_w_conv: float32 [12, 33], replicated
- grad_w_in: float32 [768, 3072], P(('seq', 'tok'))
- grad_w_back: float32 [3072, 768], P(('seq', 'tok'))
- grad_b_in: float32 [3072], P(('seq', 'tok'))
- grad_gains: float32 [2, 768], P(None, ('seq', 'tok'))
- grad_shifts: float32 [6, 768], P(None, ('seq', 'tok'))
The draws below stay inside these ranges and needn't reach their ends.
Inputs may be any that keep to these rules, and one draw needn't show every extreme that they name: `lengths`: some sequence has length exactly 1024. bounds[b, j] = (j * lengths[b]) // 64, integer division.
All inputs are finite; a program needn't handle non-finite values.
Results may differ from the reference program's by a relative error of at most 0.015.
The reference program's roundings to bfloat16 on the way count: a program that leaves them out, or rounds other values in their place, can miss the bound.
Values may be sent and summed in bfloat16 or wider, within the bound.
A program may use at most 192 MiB of HBM per device.

```python
import jax
import jax.numpy as jnp
from jax import lax

D = 768
HEADS = 12
FF = 3072
LANDMARKS = 64
ITERS = 6
CONV = 33
LENGTH = 1024
SEQS = 8


def length_draw(key):
    drawn = jax.random.randint(jax.random.fold_in(key, 11), (SEQS,), LENGTH // 4, LENGTH + 1)
    order = jax.random.permutation(jax.random.fold_in(key, 12), SEQS)
    drawn = drawn.at[order[SEQS - 1]].set(LENGTH // 4)
    drawn = drawn.at[order[0]].set(LENGTH)
    return drawn.astype(jnp.int32)


def draw_lengths(key, part):
    return length_draw(key)


def draw_bounds(key, part):
    drawn = length_draw(key)
    steps_list = jnp.arange(LANDMARKS + 1, dtype=jnp.int32)
    return (steps_list[None, :] * drawn[:, None] // LANDMARKS).astype(jnp.int32)


def draw_inputs(key, part):
    block_len = LENGTH // (2 * LANDMARKS)
    noise_key = jax.random.fold_in(key, 21)
    common_key = jax.random.fold_in(key, 22)
    noise = jnp.clip(0.7 * jax.random.normal(noise_key, (SEQS, LENGTH, D), jnp.float32), -3.5, 3.5)
    common = jnp.clip(jax.random.normal(common_key, (SEQS, 2 * LANDMARKS, D), jnp.float32), -4.0, 4.0)
    return (noise + jnp.repeat(common, block_len, axis=1)).astype(jnp.bfloat16)


def raised(result, own_key, source, target, parts, factor):
    def block_of(axis_at):
        return (jnp.arange(result.shape[axis_at]) // (result.shape[axis_at] // parts)).reshape((-1,) + (1,) * (result.ndim - 1 - axis_at))

    near = jax.random.permutation(own_key, parts)[block_of(target)]
    far = (block_of(target) + parts // 2) % parts
    return jnp.where((block_of(source) == near) | (block_of(source) == far), factor * result, result)


def block_scale(own_key, extent, shards, low, top_value):
    loudness = 1.0
    for axis_at, blocks in shards:
        steps = jax.random.uniform(jax.random.fold_in(jax.random.fold_in(own_key, 6), axis_at), (blocks,), jnp.float32, low / len(shards), top_value / len(shards))
        loudness = loudness * jnp.repeat(jnp.exp(steps), extent[axis_at] // blocks).reshape((-1,) + (1,) * (len(extent) - 1 - axis_at))
    return loudness


def scatter_about(key, dims, scale, most, pieces=(), kind=jnp.bfloat16):
    array = jax.random.normal(key, dims, jnp.float32) * scale
    if len(pieces) > 0:
        array = block_scale(key, dims, pieces, -0.22, 0.18) * array
    return jnp.clip(array, min=-most, max=most).astype(kind)


def gaussian_with(own_key, dims, scale, limit, cuts, heavy, kind=jnp.bfloat16):
    entries = scale * jax.random.normal(own_key, dims, jnp.float32)
    if cuts:
        entries = entries * block_scale(own_key, dims, cuts, -0.22, 0.18)
    return jnp.clip(raised(entries, jax.random.fold_in(own_key, 3), *heavy), -limit, limit).astype(kind)


def setup_inputs(seed: int = 0) -> dict:
    keys = jax.random.split(jax.random.key(seed), 15)
    inputs = draw_inputs(jax.random.fold_in(keys[14], 71), 0)
    lengths = draw_lengths(jax.random.fold_in(keys[14], 71), 0)
    bounds = draw_bounds(jax.random.fold_in(keys[14], 71), 0)
    w_query = scatter_about(keys[3], (D, D), (D // 2) ** -0.5, 0.3125, ((0, 32),), jnp.float32)
    w_key = scatter_about(keys[4], (D, D), (D // 2) ** -0.5, 0.3125, ((0, 32),), jnp.float32)
    w_value = scatter_about(keys[5], (D, D), D ** -0.5, 0.21875, ((0, 32),), jnp.float32)
    w_out = scatter_about(keys[6], (D, D), (D // 4) ** -0.5, 0.4375, ((0, 32),), jnp.float32)
    w_conv = scatter_about(keys[7], (HEADS, CONV), 0.2, 1.2, (), jnp.float32)
    w_in = scatter_about(keys[8], (D, FF), D ** -0.5, 0.21875, ((0, 32),), jnp.float32)
    w_back = scatter_about(keys[9], (FF, D), FF ** -0.5, 0.109375, ((0, 32),), jnp.float32)
    b_in = scatter_about(keys[10], (FF,), 0.3, 1.5, ((0, 32),), jnp.float32)
    gains = jnp.clip(1.0 + 0.1 * jax.random.normal(keys[11], (2, D), jnp.float32), 0.5, 1.5)
    shifts = scatter_about(keys[12], (6, D), 0.3, 1.5, ((1, 32),), jnp.float32)
    cotangent = gaussian_with(keys[13], (SEQS, LENGTH, D), 1.0, 6.0, ((0, 4), (1, 8)), (1, 2, 8, 2.0))
    return dict(inputs=inputs, lengths=lengths, bounds=bounds, w_query=w_query, w_key=w_key, w_value=w_value, w_out=w_out, w_conv=w_conv, w_in=w_in, w_back=w_back, b_in=b_in, gains=gains, shifts=shifts, cotangent=cotangent)


EPSILON = 1e-05
EXACT_PRECISION = lax.Precision.HIGHEST

@jax.custom_vjp
def lower_precision(v):
    return lax.optimization_barrier(v.astype(jnp.bfloat16)).astype(jnp.float32)

@jax.custom_vjp
def lower_precision_backward(v):
    return v

def low_keep(v):
    return (lower_precision(v), None)

def low_pass(kept, grad):
    return (grad,)

def back_keep(v):
    return (v, None)

def back_low(kept, grad):
    return (lower_precision(grad),)
lower_precision.defvjp(low_keep, low_pass)
lower_precision_backward.defvjp(back_keep, back_low)

def layer_norm(hidden, gain_row, shift_row):
    center = hidden - lax.optimization_barrier(jnp.mean(hidden, axis=-1, keepdims=True))
    spread = lax.optimization_barrier(jnp.mean(center * center, axis=-1, keepdims=True))
    return center * lax.rsqrt(spread + EPSILON) * gain_row + shift_row

def newton_inverse(kernel):
    column_sum = lax.optimization_barrier(jnp.sum(kernel, axis=-2))
    factor = 1.0 / lax.optimization_barrier(jnp.max(column_sum, axis=-1))
    approx = jnp.swapaxes(kernel, -1, -2) * factor[..., None, None]
    identity = jnp.eye(kernel.shape[-1], dtype=jnp.float32)
    for sweep_index in range(ITERS):
        product = jnp.matmul(kernel, approx, precision=EXACT_PRECISION)
        inner_term = 7.0 * identity - product
        inner_term = 15.0 * identity - jnp.matmul(product, inner_term, precision=EXACT_PRECISION)
        inner_term = 13.0 * identity - jnp.matmul(product, inner_term, precision=EXACT_PRECISION)
        approx = 0.25 * jnp.matmul(approx, inner_term, precision=EXACT_PRECISION)
    return approx

def mixer_core(query_marks, key_marks, numerator, denom):
    score_scale_factor = query_marks.shape[-1] ** (-0.5)
    scores = jnp.einsum('bihd,bjhd->bhij', query_marks, key_marks, precision=EXACT_PRECISION) * score_scale_factor
    middle = jax.nn.softmax(scores, axis=-1)
    pseudo = newton_inverse(middle)
    summary = numerator / denom[..., None]
    return jnp.einsum('bhij,bhjd->bhid', pseudo, summary, precision=EXACT_PRECISION)

def one_sequence(weights, seq_rows, length, edge_list):
    w_query, w_key, w_value, w_out, w_conv, w_in, w_back, b_in, gains, shifts = weights
    slot_count, model_width = seq_rows.shape
    head_count, tap_count = w_conv.shape
    head_dim = model_width // head_count
    rim_width = tap_count // 2
    score_scale_factor = head_dim ** (-0.5)
    position = jnp.arange(slot_count, dtype=jnp.int32)
    valid_mask = (position < length).astype(jnp.float32)
    member = ((position[None, :] >= edge_list[:-1, None]) & (position[None, :] < edge_list[1:, None])).astype(jnp.float32)
    part_count = (edge_list[1:] - edge_list[:-1]).astype(jnp.float32)
    query_rows = lower_precision_backward(jnp.dot(seq_rows, w_query, precision=EXACT_PRECISION)) + shifts[0]
    key_rows = lower_precision_backward(jnp.dot(seq_rows, w_key, precision=EXACT_PRECISION))
    value_rows = lower_precision_backward(jnp.dot(seq_rows, w_value, precision=EXACT_PRECISION)) + shifts[1]
    mark_query = lower_precision(jnp.dot(member, query_rows, precision=EXACT_PRECISION) / part_count[:, None])
    mark_key = lower_precision(jnp.dot(member, key_rows, precision=EXACT_PRECISION) / part_count[:, None])
    query_head_rows = lower_precision(query_rows).reshape(slot_count, head_count, head_dim)
    key_head_rows = lower_precision(key_rows).reshape(slot_count, head_count, head_dim)
    value_head_rows = lower_precision(value_rows * valid_mask[:, None]).reshape(slot_count, head_count, head_dim)
    landmark_query_heads = mark_query.reshape(-1, head_count, head_dim)
    landmark_key_heads = mark_key.reshape(-1, head_count, head_dim)
    first_score_matrix = lower_precision_backward(jnp.einsum('cqr,wqr->cqw', query_head_rows, landmark_key_heads, precision=EXACT_PRECISION)) * score_scale_factor
    first_score_kernel = lower_precision(jax.nn.softmax(first_score_matrix, axis=-1))
    third_score_matrix = lower_precision_backward(jnp.einsum('bxk,axk->xba', landmark_query_heads, key_head_rows, precision=EXACT_PRECISION)) * score_scale_factor
    third_score_matrix = jnp.where(valid_mask[None, None, :] > 0, third_score_matrix, -1e+30)
    third_exponential = jnp.exp(third_score_matrix - lax.optimization_barrier(jnp.max(third_score_matrix, axis=-1, keepdims=True)))
    denom = lax.optimization_barrier(jnp.sum(third_exponential, axis=-1))
    numerator = lower_precision_backward(jnp.einsum('brn,nbt->brt', lower_precision(third_exponential), value_head_rows, precision=EXACT_PRECISION))
    mixed_output = lower_precision(mixer_core(landmark_query_heads[None], landmark_key_heads[None], numerator[None], denom[None])[0])
    attention_forward = jnp.einsum('zer,ern->zen', first_score_kernel, mixed_output, precision=EXACT_PRECISION)
    padded = jnp.pad(value_head_rows, ((rim_width, rim_width), (0, 0), (0, 0)))
    conv_out = jnp.zeros_like(attention_forward)
    for offset in range(tap_count):
        conv_out = conv_out + w_conv[:, offset][None, :, None] * padded[offset:offset + slot_count]
    mix_total = lower_precision_backward((attention_forward + conv_out).reshape(slot_count, model_width))
    first_sum = seq_rows + lower_precision_backward(jnp.dot(lower_precision(mix_total), w_out, precision=EXACT_PRECISION)) + shifts[2]
    normed = layer_norm(first_sum, gains[0], shifts[3])
    pre_act = lower_precision_backward(jnp.dot(lower_precision(normed), w_in, precision=EXACT_PRECISION)) + b_in
    active = jax.nn.gelu(pre_act, approximate=False)
    second_sum = normed + lower_precision_backward(jnp.dot(lower_precision(active), w_back, precision=EXACT_PRECISION)) + shifts[4]
    return layer_norm(second_sum, gains[1], shifts[5]) * valid_mask[:, None]

def reference(inputs, lengths, bounds, w_query, w_key, w_value, w_out, w_conv, w_in, w_back, b_in, gains, shifts, cotangent):
    params = (w_query, w_key, w_value, w_out, w_conv, w_in, w_back, b_in, gains, shifts)

    def forward(params, source):
        rounded = tuple((lower_precision(element) for element in params[:4])) + (params[4],) + tuple((lower_precision(element) for element in params[5:]))

        def scan_step(state_carry, packed):
            seq_rows, length, edge_list = packed
            return (state_carry, jax.checkpoint(one_sequence)(rounded, seq_rows, length, edge_list))
        unused, outputs = lax.scan(scan_step, jnp.zeros((), jnp.float32), (source, lengths, bounds))
        return outputs
    source = inputs.astype(jnp.float32)
    outputs, pullback = jax.vjp(forward, params, source)
    grad_params, grad_source = pullback(cotangent.astype(jnp.float32))
    return (outputs, grad_source, grad_params[0], grad_params[1], grad_params[2], grad_params[3], grad_params[4], grad_params[5], grad_params[6], grad_params[7], grad_params[8], grad_params[9])
```

```python
import functools

import jax
import jax.numpy as jnp
from jax import lax
from jax.experimental import pallas as pl
from jax.experimental.pallas import tpu as pltpu
from jax.sharding import PartitionSpec as P

ITERS = 6


EPSILON = 1e-05
EXACT_PRECISION = lax.Precision.HIGHEST


def padded_2(cells, sides, width):
    for axis, dim in sides:
        count = lax.axis_size(axis)
        ends = count - 1
        head = lax.slice_in_dim(cells, 0, width, axis=dim)
        tail = lax.slice_in_dim(cells, cells.shape[dim] - width, cells.shape[dim], axis=dim)
        cells = jnp.concatenate(
            [
                lax.ppermute(tail, axis, [(i, (i + 1) % count) for i in range(ends)]),
                cells,
                lax.ppermute(head, axis, [((i + 1) % count, i) for i in range(ends)]),
            ],
            axis=dim,
        )
    return cells


def layer_norm(hidden, gain_row, shift_row):
    center = hidden - jnp.mean(hidden, axis=-1, keepdims=True)
    spread = jnp.mean(center * center, axis=-1, keepdims=True)
    return center * lax.rsqrt(spread + EPSILON) * gain_row + shift_row


def newton_inverse(kernel):
    column_sum = jnp.sum(kernel, axis=-2)
    factor = 1.0 / jnp.max(column_sum, axis=-1)
    approx = jnp.swapaxes(kernel, -1, -2) * factor[..., None, None]
    identity = jnp.eye(kernel.shape[-1], dtype=jnp.float32)
    for sweep_index in range(ITERS):
        product = jnp.matmul(kernel, approx, precision=EXACT_PRECISION)
        inner_term = 7.0 * identity - product
        inner_term = 15.0 * identity - jnp.matmul(product, inner_term, precision=EXACT_PRECISION)
        inner_term = 13.0 * identity - jnp.matmul(product, inner_term, precision=EXACT_PRECISION)
        approx = 0.25 * jnp.matmul(approx, inner_term, precision=EXACT_PRECISION)
    return approx


def mixer_core(query_marks, key_marks, numerator, denom):
    score_scale_factor = query_marks.shape[-1] ** (-0.5)
    scores = (
        jnp.einsum("bihd,bjhd->bhij", query_marks, key_marks, precision=EXACT_PRECISION)
        * score_scale_factor
    )
    middle = jax.nn.softmax(scores, axis=-1)
    pseudo = newton_inverse(middle)
    summary = numerator / denom[..., None]
    return jnp.einsum("bhij,bhjd->bhid", pseudo, summary, precision=EXACT_PRECISION)


def gelu_exact(pre_act):
    return jax.nn.gelu(pre_act, approximate=False)


def product_low(pattern, left, right):
    return jnp.einsum(pattern, left, right, preferred_element_type=jnp.float32)


def shards(
    inputs,
    lengths,
    bounds,
    w_query,
    w_key,
    w_value,
    w_out,
    w_conv,
    w_in,
    w_back,
    b_in,
    gains,
    shifts,
    cotangent,
):
    seq_count, slot_count, model_width = inputs.shape
    head_count, tap_count = w_conv.shape
    head_dim = model_width // head_count
    rim_width = tap_count // 2
    mark_count = bounds.shape[1] - 1
    row_count = seq_count * slot_count
    score_scale_factor = head_dim ** (-0.5)
    first_slot = lax.axis_index("tok") * slot_count
    position = first_slot + jnp.arange(slot_count, dtype=jnp.int32)
    valid_mask = (position[None, :] < lengths[:, None]).astype(jnp.float32)
    member = (
        (position[None, None, :] >= bounds[:, :-1, None])
        & (position[None, None, :] < bounds[:, 1:, None])
    ).astype(jnp.float32)
    part_count = (bounds[:, 1:] - bounds[:, :-1]).astype(jnp.float32)
    gathered = (
        lax.all_gather(w_query.astype(jnp.bfloat16), ("seq", "tok"), axis=0, tiled=True),
        lax.all_gather(w_key.astype(jnp.bfloat16), ("seq", "tok"), axis=0, tiled=True),
        lax.all_gather(w_value.astype(jnp.bfloat16), ("seq", "tok"), axis=0, tiled=True),
        lax.all_gather(w_out.astype(jnp.bfloat16), ("seq", "tok"), axis=0, tiled=True),
        lax.all_gather(w_in.astype(jnp.bfloat16), ("seq", "tok"), axis=0, tiled=True),
        lax.all_gather(w_back.astype(jnp.bfloat16), ("seq", "tok"), axis=0, tiled=True),
        lax.all_gather(b_in.astype(jnp.bfloat16), ("seq", "tok"), axis=0, tiled=True),
        lax.all_gather(gains.astype(jnp.bfloat16), ("seq", "tok"), axis=1, tiled=True),
        lax.all_gather(shifts.astype(jnp.bfloat16), ("seq", "tok"), axis=1, tiled=True),
    )
    query_mat, key_mat, value_mat, out_mat, in_mat, back_mat, bias_vec, gain_vec, shift_vec = (
        gathered
    )
    bias_rows = bias_vec.astype(jnp.float32)
    gain_rows = gain_vec.astype(jnp.float32)
    shift_rows = shift_vec.astype(jnp.float32)
    flat_rows = inputs.reshape(row_count, model_width)
    query_rows = jnp.dot(flat_rows, query_mat, preferred_element_type=jnp.float32) + shift_rows[0]
    key_rows = jnp.dot(flat_rows, key_mat, preferred_element_type=jnp.float32)
    value_rows = jnp.dot(flat_rows, value_mat, preferred_element_type=jnp.float32) + shift_rows[1]
    part_query = jnp.einsum(
        "bms,bsd->bmd",
        member,
        query_rows.reshape(seq_count, slot_count, model_width),
        precision=EXACT_PRECISION,
    )
    part_key = jnp.einsum(
        "bms,bsd->bmd",
        member,
        key_rows.reshape(seq_count, slot_count, model_width),
        precision=EXACT_PRECISION,
    )
    sum_query, sum_key = lax.psum((part_query, part_key), "tok")
    mark_query = (
        (sum_query / part_count[..., None])
        .astype(jnp.bfloat16)
        .reshape(seq_count, mark_count, head_count, head_dim)
    )
    mark_key = (
        (sum_key / part_count[..., None])
        .astype(jnp.bfloat16)
        .reshape(seq_count, mark_count, head_count, head_dim)
    )
    query_head_rows = query_rows.astype(jnp.bfloat16).reshape(
        seq_count, slot_count, head_count, head_dim
    )
    key_head_rows = key_rows.astype(jnp.bfloat16).reshape(
        seq_count, slot_count, head_count, head_dim
    )
    v_low = (value_rows.reshape(seq_count, slot_count, model_width) * valid_mask[..., None]).astype(
        jnp.bfloat16
    )
    value_head_rows = v_low.reshape(seq_count, slot_count, head_count, head_dim)
    first_score_matrix = (
        product_low("bshd,bmhd->bshm", query_head_rows, mark_key) * score_scale_factor
    )
    first_score_kernel = jax.nn.softmax(first_score_matrix, axis=-1)
    first_low = first_score_kernel.astype(jnp.bfloat16)
    third_score_matrix = (
        product_low("bmhd,bshd->bhms", mark_query, key_head_rows) * score_scale_factor
    )
    third_score_matrix = jnp.where(valid_mask[:, None, None, :] > 0, third_score_matrix, -1e30)
    score_top = lax.pmax(jnp.max(third_score_matrix, axis=-1), "tok")
    third_exponential = jnp.exp(third_score_matrix - score_top[..., None])
    third_low = third_exponential.astype(jnp.bfloat16)
    numerator, denom = lax.psum(
        (
            product_low("bhms,bshd->bhmd", third_low, value_head_rows),
            jnp.sum(third_exponential, axis=-1),
        ),
        "tok",
    )
    mixed_output, core_back = jax.vjp(
        mixer_core, mark_query.astype(jnp.float32), mark_key.astype(jnp.float32), numerator, denom
    )
    mixed_low = mixed_output.astype(jnp.bfloat16)
    attention_forward = product_low("bshm,bhmd->bshd", first_low, mixed_low)
    padded = padded_2(v_low, (("tok", 1),), rim_width)
    padded_heads = padded.astype(jnp.float32).reshape(
        seq_count, slot_count + 2 * rim_width, head_count, head_dim
    )
    conv_out = jnp.zeros_like(attention_forward)
    for offset in range(tap_count):
        conv_out = (
            conv_out
            + w_conv[:, offset][None, None, :, None] * padded_heads[:, offset : offset + slot_count]
        )
    mix_low = (attention_forward + conv_out).reshape(row_count, model_width).astype(jnp.bfloat16)
    first_sum = (
        flat_rows.astype(jnp.float32)
        + jnp.dot(mix_low, out_mat, preferred_element_type=jnp.float32)
        + shift_rows[2]
    )
    normed, norm_one_back = jax.vjp(layer_norm, first_sum, gain_rows[0], shift_rows[3])
    normed_low = normed.astype(jnp.bfloat16)
    pre_act = jnp.dot(normed_low, in_mat, preferred_element_type=jnp.float32) + bias_rows
    active, gelu_back = jax.vjp(gelu_exact, pre_act)
    active_low = active.astype(jnp.bfloat16)
    second_sum = (
        normed + jnp.dot(active_low, back_mat, preferred_element_type=jnp.float32) + shift_rows[4]
    )
    final_raw, norm_two_back = jax.vjp(layer_norm, second_sum, gain_rows[1], shift_rows[5])
    valid_rows = valid_mask.reshape(row_count, 1)
    result = final_raw * valid_rows
    back_weights = (
        lax.all_gather(w_query.astype(jnp.bfloat16), ("seq", "tok"), axis=0, tiled=True),
        lax.all_gather(w_key.astype(jnp.bfloat16), ("seq", "tok"), axis=0, tiled=True),
        lax.all_gather(w_value.astype(jnp.bfloat16), ("seq", "tok"), axis=0, tiled=True),
        lax.all_gather(w_out.astype(jnp.bfloat16), ("seq", "tok"), axis=0, tiled=True),
        lax.all_gather(w_in.astype(jnp.bfloat16), ("seq", "tok"), axis=0, tiled=True),
        lax.all_gather(w_back.astype(jnp.bfloat16), ("seq", "tok"), axis=0, tiled=True),
    )
    query_back, key_back, value_back, out_back, in_back, back_back = back_weights
    grad_out = cotangent.reshape(row_count, model_width).astype(jnp.float32) * valid_rows
    grad_second, grad_gain_two, grad_shift_five = norm_two_back(grad_out)
    grad_second_low = grad_second.astype(jnp.bfloat16)
    grad_shift_four = jnp.sum(grad_second, axis=0)
    grad_w_back = product_low("rf,rd->fd", active_low, grad_second_low)
    grad_active = product_low("rd,fd->rf", grad_second_low, back_back)
    (grad_pre,) = gelu_back(grad_active)
    grad_pre_low = grad_pre.astype(jnp.bfloat16)
    grad_b_in = jnp.sum(grad_pre, axis=0)
    grad_w_in = product_low("rd,rf->df", normed_low, grad_pre_low)
    grad_normed = grad_second + product_low("rf,df->rd", grad_pre_low, in_back)
    grad_first, grad_gain_one, grad_shift_three = norm_one_back(grad_normed)
    grad_proj_low = grad_first.astype(jnp.bfloat16)
    grad_shift_two = jnp.sum(grad_first, axis=0)
    grad_w_out = product_low("rd,re->de", mix_low, grad_proj_low)
    grad_mix_low = (
        product_low("re,de->rd", grad_proj_low, out_back)
        .astype(jnp.bfloat16)
        .reshape(seq_count, slot_count, model_width)
    )
    grad_mix_heads = grad_mix_low.reshape(seq_count, slot_count, head_count, head_dim)
    grad_mixed_part = product_low("bshm,bshd->bhmd", first_low, grad_mix_heads)
    grad_first_kernel = product_low("bshd,bhmd->bshm", grad_mix_heads, mixed_low)
    inner_sum = jnp.sum(grad_first_kernel * first_score_kernel, axis=-1, keepdims=True)
    grad_first_low = (
        first_score_kernel * (grad_first_kernel - inner_sum) * score_scale_factor
    ).astype(jnp.bfloat16)
    part_grad_key = product_low("bshm,bshd->bmhd", grad_first_low, query_head_rows)
    grad_mixed, grad_mk_first = lax.psum((grad_mixed_part, part_grad_key), "tok")
    grad_mq_core, grad_mk_core, grad_numer, grad_denom = core_back(grad_mixed)
    grad_numer_low = grad_numer.astype(jnp.bfloat16)
    grad_third_exp = (
        product_low("bhmd,bshd->bhms", grad_numer_low, value_head_rows) + grad_denom[..., None]
    )
    grad_v_heads = product_low("bhms,bhmd->bshd", third_low, grad_numer_low)
    grad_third_low = (third_exponential * grad_third_exp * score_scale_factor).astype(jnp.bfloat16)
    part_grad_query = product_low("bhms,bshd->bmhd", grad_third_low, key_head_rows)
    grad_key_heads = product_low("bhms,bmhd->bshd", grad_third_low, mark_query)
    grad_mq_third = lax.psum(part_grad_query, "tok")
    grad_mq = (grad_mq_core + grad_mq_third).reshape(
        seq_count, mark_count, model_width
    ) / part_count[..., None]
    grad_mk = (grad_mk_core + grad_mk_first).reshape(
        seq_count, mark_count, model_width
    ) / part_count[..., None]
    grad_query = jnp.einsum(
        "bms,bmd->bsd", member, grad_mq, precision=EXACT_PRECISION
    ) + product_low("bshm,bmhd->bshd", grad_first_low, mark_key).reshape(
        seq_count, slot_count, model_width
    )
    grad_key = jnp.einsum(
        "bms,bmd->bsd", member, grad_mk, precision=EXACT_PRECISION
    ) + grad_key_heads.reshape(seq_count, slot_count, model_width)
    grad_padded = padded_2(grad_mix_low, (("tok", 1),), rim_width)
    grad_pad_heads = grad_padded.astype(jnp.float32).reshape(
        seq_count, slot_count + 2 * rim_width, head_count, head_dim
    )
    grad_mix_float = grad_mix_heads.astype(jnp.float32)
    grad_conv_v = jnp.zeros_like(grad_mix_float)
    conv_terms = []
    for offset in range(tap_count):
        start_at = 2 * rim_width - offset
        grad_conv_v = (
            grad_conv_v
            + w_conv[:, offset][None, None, :, None]
            * grad_pad_heads[:, start_at : start_at + slot_count]
        )
        conv_terms.append(
            jnp.sum(padded_heads[:, offset : offset + slot_count] * grad_mix_float, axis=(0, 1, 3))
        )
    grad_w_conv = lax.psum(jnp.stack(conv_terms, axis=1), ("seq", "tok"))
    grad_value = (grad_v_heads + grad_conv_v).reshape(
        seq_count, slot_count, model_width
    ) * valid_mask[..., None]
    grad_query_flat = grad_query.reshape(row_count, model_width)
    grad_key_flat = grad_key.reshape(row_count, model_width)
    grad_value_flat = grad_value.reshape(row_count, model_width)
    grad_query_low = grad_query_flat.astype(jnp.bfloat16)
    grad_key_low = grad_key_flat.astype(jnp.bfloat16)
    grad_value_low = grad_value_flat.astype(jnp.bfloat16)
    grad_w_query = product_low("rd,re->de", flat_rows, grad_query_low)
    grad_w_key = product_low("rd,re->de", flat_rows, grad_key_low)
    grad_w_value = product_low("rd,re->de", flat_rows, grad_value_low)
    grad_input = (
        grad_first
        + product_low("re,de->rd", grad_query_low, query_back)
        + product_low("re,de->rd", grad_key_low, key_back)
        + product_low("re,de->rd", grad_value_low, value_back)
    )
    grad_gains = jnp.stack([grad_gain_one, grad_gain_two], axis=0)
    grad_shifts = jnp.stack(
        [
            jnp.sum(grad_query_flat, axis=0),
            jnp.sum(grad_value_flat, axis=0),
            grad_shift_two,
            grad_shift_three,
            grad_shift_four,
            grad_shift_five,
        ],
        axis=0,
    )
    (
        owned_query,
        owned_key,
        owned_value,
        owned_out,
        owned_in,
        owned_back,
        owned_bias,
        owned_gains,
        owned_shifts,
    ) = (
        lax.psum_scatter(grad_w_query, ("seq", "tok"), scatter_dimension=0, tiled=True),
        lax.psum_scatter(grad_w_key, ("seq", "tok"), scatter_dimension=0, tiled=True),
        lax.psum_scatter(grad_w_value, ("seq", "tok"), scatter_dimension=0, tiled=True),
        lax.psum_scatter(grad_w_out, ("seq", "tok"), scatter_dimension=0, tiled=True),
        lax.psum_scatter(grad_w_in, ("seq", "tok"), scatter_dimension=0, tiled=True),
        lax.psum_scatter(grad_w_back, ("seq", "tok"), scatter_dimension=0, tiled=True),
        lax.psum_scatter(grad_b_in, ("seq", "tok"), scatter_dimension=0, tiled=True),
        lax.psum_scatter(grad_gains, ("seq", "tok"), scatter_dimension=1, tiled=True),
        lax.psum_scatter(grad_shifts, ("seq", "tok"), scatter_dimension=1, tiled=True),
    )
    return (
        result.reshape(seq_count, slot_count, model_width),
        grad_input.reshape(seq_count, slot_count, model_width),
        owned_query,
        owned_key,
        owned_value,
        owned_out,
        grad_w_conv,
        owned_in,
        owned_back,
        owned_bias,
        owned_gains,
        owned_shifts,
    )


F32 = jnp.float32
BF = jnp.bfloat16

def dot(a, b, ca=1, cb=0):
    return lax.dot_general(a, b, (((ca,), (cb,)), ((), ())), preferred_element_type=F32)

def lane_low(shape):
    return lax.broadcasted_iota(jnp.int32, shape, len(shape) - 1) % 128 < 64

def halves_diag(m):
    low = lane_low((64, 128))
    return jnp.where(low, m[:64], m[64:])

def spread_diag(v):
    low = lane_low(v.shape)
    zero = jnp.zeros_like(v)
    return jnp.concatenate([jnp.where(low, v, zero), jnp.where(low, zero, v)], axis=0)

def seg(op, v, fill):
    low = lane_low(v.shape)
    a = op(jnp.where(low, v, fill), axis=-1, keepdims=True)
    b = op(jnp.where(low, fill, v), axis=-1, keepdims=True)
    return jnp.where(low, a, b)

def split(v):
    hi = v.astype(BF)
    return hi, (v - hi.astype(F32)).astype(BF)

def norm_stats(h):
    center = h - jnp.mean(h, axis=-1, keepdims=True)
    spread = jnp.mean(center * center, axis=-1, keepdims=True)
    rstd = lax.rsqrt(spread + 1e-05)
    return center * rstd, rstd

def norm_back(dy, gain, xhat, rstd):
    d = dy * gain
    a = jnp.mean(d, axis=-1, keepdims=True)
    b = jnp.mean(d * xhat, axis=-1, keepdims=True)
    return rstd * (d - a - xhat * b)

def skew(row, width, count):
    return pltpu.roll(jnp.broadcast_to(row, (count, width)), 0, 1, stride=1, stride_axis=0)

def colsum(v):
    return jnp.sum(v, axis=0, keepdims=True)

TILE = 512

def layer_kernel(x_ref, cot_ref, valid_ref, r1_ref, p1_ref, wz_ref, km_ref, q_ref, vpad_ref, wc_ref, cv_ref, bias_ref, wo_hbm, win_hbm, wback_hbm,
                 res_ref, dh1_ref, da_ref, dwz_ref, dkm_ref, dq1_ref, gv_ref, gb_ref, gw_ref, dwo_ref, dwin_ref, dwback_ref,
                 wo, win, wback, ar, gr, gp, acc, xh1, yt, sems, osem, gwin, gwback, gwo):
    nseq, heads = vpad_ref.shape[0], wc_ref.shape[0]
    pairs = heads // 2
    slots = x_ref.shape[0] // nseq
    rows, width = x_ref.shape
    ff = bias_ref.shape[1]
    scale = 64 ** -0.5
    cps = [pltpu.make_async_copy(a, b, sems.at[i]) for i, (a, b) in enumerate(((wo_hbm.at[3], wo), (win_hbm, win), (wback_hbm, wback)))]
    for cp in cps: cp.start()
    def att(p, _):
        lanes = pl.ds(pl.multiple_of(p * 128, 128), 128)
        th = []
        for e in range(2):
            hi, lo = split(skew(wc_ref[pl.ds(2 * p + e, 1), :], 256, slots))
            th.append((hi, lo))
        low = lane_low((slots, 128))
        for b in range(nseq):
            u = b * pairs + p
            v = vpad_ref[b, :, lanes]
            c0 = dot(th[0][0], v) + dot(th[0][1], v)
            c1 = dot(th[1][0], v) + dot(th[1][1], v)
            a = dot(r1_ref[u], spread_diag(wz_ref[u]))
            ar[pl.ds(b * slots, slots), lanes] = (a + jnp.where(low, c0, c1)).astype(BF)
        return 0
    lax.fori_loop(0, pairs, att, 0)
    cps[0].wait()
    h1 = x_ref[...].astype(F32) + dot(ar[...], wo[...]) + cv_ref[4:5, :]
    xhat1, rstd1 = norm_stats(h1)
    xh1[...] = xhat1
    y = xhat1 * cv_ref[0:1, :] + cv_ref[5:6, :]
    yr = y.astype(BF)
    yt[...] = yr
    acc[...] = y + cv_ref[6:7, :]
    cps[1].wait(); cps[2].wait()
    def ffn(j, _):
        cols = pl.ds(pl.multiple_of(j * TILE, TILE), TILE)
        u = dot(yt[...], win[:, cols]) + bias_ref[:, cols]
        phi = 0.5 * (1.0 + lax.erf(u * (0.5 ** 0.5)))
        g = (u * phi).astype(BF)
        gr[:, cols] = g
        gp[:, cols] = phi + u * (jnp.exp(-0.5 * u * u) * 0.3989422804014327)
        acc[...] += dot(g, wback[cols, :])
        return 0
    lax.fori_loop(0, ff // TILE, ffn, 0)
    xhat2, rstd2 = norm_stats(acc[...])
    valid = valid_ref[...]
    res_ref[...] = (xhat2 * cv_ref[1:2, :] + cv_ref[7:8, :]) * valid
    dr = cot_ref[...].astype(F32) * valid
    gv_ref[1:2, :] = colsum(dr * xhat2)
    gv_ref[7:8, :] = colsum(dr)
    dh2 = norm_back(dr, cv_ref[1:2, :], xhat2, rstd2)
    gv_ref[6:7, :] = colsum(dh2)
    df = dh2.astype(BF)
    acc[...] = dh2
    def back(j, _):
        cols = pl.ds(pl.multiple_of(j * TILE, TILE), TILE)
        dg = dot(df, wback[cols, :], 1, 1)
        du = gp[:, cols] * dg
        gb_ref[:, cols] = colsum(du)
        dur = du.astype(BF)
        gwback[cols, :] = dot(gr[:, cols], df, 0, 0).astype(BF)
        gwin[:, cols] = dot(yt[...], dur, 0, 0).astype(BF)
        acc[...] += dot(dur, win[:, cols], 1, 1)
        return 0
    lax.fori_loop(0, ff // TILE, back, 0)
    o1 = pltpu.make_async_copy(gwback, dwback_ref, osem.at[0]); o1.start()
    o2 = pltpu.make_async_copy(gwin, dwin_ref, osem.at[1]); o2.start()
    dy = acc[...]
    xhat1 = xh1[...]
    gv_ref[0:1, :] = colsum(dy * xhat1)
    gv_ref[5:6, :] = colsum(dy)
    dh1 = norm_back(dy, cv_ref[0:1, :], xhat1, rstd1)
    gv_ref[4:5, :] = colsum(dh1)
    gv_ref[2:4, :] = jnp.zeros((2, width), F32)
    dh1_ref[...] = dh1
    do = dh1.astype(BF)
    gwo[...] = dot(ar[...], do, 0, 0).astype(BF)
    o3 = pltpu.make_async_copy(gwo, dwo_ref, osem.at[2]); o3.start()
    da_ref[...] = dot(do, wo[...], 1, 1).astype(BF)
    gw_ref[...] = jnp.zeros_like(gw_ref)
    def unit(u, _):
        b, p = u // pairs, u % pairs
        da = da_ref[pl.ds(pl.multiple_of(b * slots, slots), slots), pl.ds(pl.multiple_of(p * 128, 128), 128)]
        dwz_ref[u] = halves_diag(dot(r1_ref[u], da, 0, 0))
        dp1 = dot(da, spread_diag(wz_ref[u]), 1, 1)
        p1 = p1_ref[u]
        inner = seg(jnp.sum, dp1 * p1, 0.0)
        ds1 = (p1 * (dp1 - inner) * scale).astype(BF)
        dkm_ref[u] = halves_diag(dot(ds1, q_ref[u], 0, 0))
        dq1_ref[u] = dot(ds1, spread_diag(km_ref[u]))
        v = vpad_ref[b, :, pl.ds(pl.multiple_of(p * 128, 128), 128)]
        low = lane_low(da.shape)
        zero = jnp.zeros_like(da)
        i = lax.broadcasted_iota(jnp.int32, (slots, slots), 0)
        j = lax.broadcasted_iota(jnp.int32, (slots, slots), 1)
        da = dot(jnp.where(i + j == slots - 1, 1.0, 0.0).astype(BF), da).astype(BF)
        for e in range(2):
            m = dot(jnp.where(low, da, zero) if e == 0 else jnp.where(low, zero, da), v, 1, 1)
            m = pltpu.roll(m, m.shape[1] - slots + 1, 1, stride=1, stride_axis=0)
            gw_ref[pl.ds(2 * p + e, 1), :] += colsum(m)
        return 0
    lax.fori_loop(0, nseq * pairs, unit, 0)
    o1.wait(); o2.wait(); o3.wait()

def layer(x, cot, valid, r1, p1, wz, km, q, vpad, wc, cv, bias, wo, win, wback):
    S = jax.ShapeDtypeStruct
    rows, width = x.shape
    ff = bias.shape[1]
    n = r1.shape[0]
    V = pltpu.VMEM
    vm = pl.BlockSpec(memory_space=pltpu.VMEM)
    hb = pl.BlockSpec(memory_space=pl.ANY)
    return pl.pallas_call(
        layer_kernel,
        out_shape=(S((rows, width), F32), S((rows, width), F32), S((rows, width), BF), S((n, 64, 128), F32), S((n, 64, 128), F32), S((n, 128, 128), F32),
                   S((8, width), F32), S((1, ff), F32), S(wc.shape, F32), S((width, width), BF), S((width, ff), BF), S((ff, width), BF)),
        in_specs=[vm] * 12 + [hb] * 3,
        out_specs=(vm,) * 9 + (hb,) * 3,
        scratch_shapes=[V((width, width), BF), V((width, ff), BF), V((ff, width), BF), V((rows, width), BF), V((rows, ff), BF), V((rows, ff), F32),
                        V((rows, width), F32), V((rows, width), F32), V((rows, width), BF), pltpu.SemaphoreType.DMA((3,)), pltpu.SemaphoreType.DMA((3,)),
                        V((width, ff), BF), V((ff, width), BF), V((width, width), BF)],
        compiler_params=pltpu.CompilerParams(vmem_limit_bytes=60 * 1024 * 1024),
        cost_estimate=pl.CostEstimate(flops=9_000_000_000, bytes_accessed=30_000_000, transcendentals=2_000_000),
        name="layer_body",
    )(x, cot, valid, r1, p1, wz, km, q, vpad, wc, cv, bias, wo, win, wback)


MESH = pl.DeviceIdType.MESH
ITERS = 6

def place():
    s = lax.axis_index("seq"); t = lax.axis_index("tok")
    x, y, z, c = s % 2, s // 2, t // 2, t % 2
    px = s + 1 - 2 * x
    py = (s + 2) % 4
    p1 = px * (1 - c) + py * c
    p2 = py * (1 - c) + px * c
    return s, z, c, p1, p2

def remote(src, dst, send, recv, seq, tok):
    return pltpu.make_async_remote_copy(src_ref=src, dst_ref=dst, send_sem=send, recv_sem=recv,
                                        device_id={"seq": seq, "tok": tok}, device_id_type=MESH)

def entry(s, z, c, p1, p2):
    bar = pltpu.get_barrier_semaphore()
    def sig(seq, tok):
        pl.semaphore_signal(bar, inc=1, device_id={"seq": seq, "tok": tok}, device_id_type=MESH)
    t = 2 * z + c
    sig(p1, t); sig(p2, t); sig(s, 2 * z + 1 - c)
    for d in (1, 2, 3):
        sig(s, 2 * ((z + d) % 4) + c)
    @pl.when(((c == 1) & (z < 3)) | ((c == 0) & (z > 0)))
    def _(): sig(s, t + 2 * c - 1)
    edge = c * (6 - z) // 4 + (1 - c) * ((z + 3) // 4)
    pl.semaphore_wait(bar, 6 + edge)

class Gather:
    def __init__(self, chunks, owns, blk, recva, recvb, sz, s1, s2, sc, sl, alpha, beta, where):
        self.__dict__.update(locals())
        s, z, c, p1, p2 = where
        self.t = 2 * z + c
        self.events = sorted(((k_key + d + beta * part, k, d, part) for k, k_key in enumerate(alpha) for d in range(4) for part in range(3)))
    def rc(self, k, src, s_, z_, send, dev, recv):
        return remote(src, self.blk(k, s_, z_, self.where[2]), send, recv.at[k, s_, z_], *dev)
    def dests(self):
        s, z, c, p1, p2 = self.where
        t = self.t
        return (s, t + 2), (s, t - 2), (p1, t), (p2, t), (s, 2 * z + 1 - c)
    def run(self, k, d, part):
        s, z, c, p1, p2 = self.where
        right, left, d1, d2, dc = self.dests()
        blk, recva, recvb, sz, s1, s2, sc = self.blk, self.recva, self.recvb, self.sz, self.s1, self.s2, self.sc
        def to_core(src, s_, z_): self.rc(k, src, s_, z_, sc.at[k, s_, z_], dc, recvb).start()
        def to_p2(src, s_, z_, g): self.rc(k, src, s_, z_, s2.at[k, g, z_], d2, recva).start()
        def to_p1(src, s_, z_): self.rc(k, src, s_, z_, s1.at[k, z_], d1, recva).start()
        def wait_in(s_, z_): self.rc(k, blk(k, s_, z_, c), s_, z_, self.sl.at[k], dc, recva).wait_recv()
        def go_right(src, zz): self.rc(k, src, s, zz, sz.at[k, 0, zz], right, recva).start()
        def go_left(src, zz): self.rc(k, src, s, zz, sz.at[k, 1, zz], left, recva).start()
        def pair(f):
            if d == 0:
                f(z, None); return
            @pl.when(z >= d)
            def _(): f(z - d, 0)
            @pl.when(z + d <= 3)
            def _(): f(z + d, 1)
        if part == 0:
            def f(zz, side):
                if side is None:
                    src = self.owns(k)
                else:
                    wait_in(s, zz); src = blk(k, s, zz, c)
                if side != 1:
                    @pl.when(z < 3)
                    def _(): go_right(src, zz)
                if side != 0:
                    @pl.when(z > 0)
                    def _(): go_left(src, zz)
                to_p1(src, s, zz); to_p2(src, s, zz, 0); to_core(src, s, zz)
                if side is None:
                    pltpu.make_async_copy(src, blk(k, s, z, c), self.sl.at[k]).start()
        elif part == 1:
            def f(zz, side):
                wait_in(p1, zz); src = blk(k, p1, zz, c)
                to_p2(src, p1, zz, 1); to_core(src, p1, zz)
        else:
            def f(zz, side):
                for s_ in (p2, 3 - s):
                    wait_in(s_, zz); to_core(blk(k, s_, zz, c), s_, zz)
        pair(f)
    def arrive(self, k):
        s, z, c, p1, p2 = self.where
        dc = self.dests()[4]
        def rb(i, _):
            b = self.blk(k, i // 4, i % 4, 1 - c)
            remote(b, b, self.sc.at[k, i // 4, i % 4], self.recvb.at[k, i // 4, i % 4], *dc).wait_recv()
            return 0
        lax.fori_loop(0, 16, rb, 0)
        pltpu.make_async_copy(self.owns(k), self.blk(k, s, z, c), self.sl.at[k]).wait()
    def drain(self):
        s, z, c, p1, p2 = self.where
        right, left, d1, d2, dc = self.dests()
        for k in range(len(self.chunks)):
            o = self.owns(k)
            def ws(i, _):
                self.rc(k, o, s, z, self.s1.at[k, i], d1, self.recva).wait_send()
                for g in range(2): self.rc(k, o, s, z, self.s2.at[k, g, i], d2, self.recva).wait_send()
                for j in range(4): self.rc(k, o, s, z, self.sc.at[k, j, i], dc, self.recvb).wait_send()
                @pl.when((z < 3) & (i <= z))
                def _(): self.rc(k, o, s, z, self.sz.at[k, 0, i], right, self.recva).wait_send()
                @pl.when((z > 0) & (i >= z))
                def _(): self.rc(k, o, s, z, self.sz.at[k, 1, i], left, self.recva).wait_send()
                return 0
            lax.fori_loop(0, 4, ws, 0)

def each_slot(c, f):
    f(0)
    @pl.when(c == 0)
    def _(): f(1)

class UnitSum:
    def __init__(self, src, ra, rb, sems, where, combine):
        self.__dict__.update(locals())
        self.sa, self.qa, self.sb, self.qb = sems
    def cp_a(self, c):
        s, z, cc, _, _ = self.where
        if c == 0:
            return remote(self.src.at[:, pl.ds(2, 1)], self.ra.at[:, pl.ds(0, 1)], self.sa, self.qa, s, 2 * z + 1)
        return remote(self.src.at[:, pl.ds(0, 2)], self.ra, self.sa, self.qa, s, 2 * z)
    def cp_b(self, d, i):
        s, z, c, _, _ = self.where
        zz = (z + d) % 4
        return remote(self.src.at[zz, 2 * c + i], self.rb.at[z, i], self.sb.at[d, i], self.qb.at[z, i], s, 2 * zz + c)
    def start(self):
        for k in (0, 1):
            @pl.when(self.where[2] == k)
            def _(): self.cp_a(k).start()
    def mid(self):
        s, z, c, _, _ = self.where
        for k in (0, 1):
            @pl.when(c == k)
            def _(): self.cp_a(1 - k).wait_recv()
        def comb(zz):
            each_slot(c, lambda i: self.combine(self.src.at[zz, 2 * c + i], self.ra.at[zz, i]))
        for d in (2, 1, 3):
            comb((z + d) % 4)
            each_slot(c, lambda i: self.cp_b(d, i).start())
        comb(z)
    def end(self):
        s, z, c, _, _ = self.where
        for d in (1, 3, 2):
            zz = (z + d) % 4
            def f(i):
                remote(self.src.at[zz, 2 * c + i], self.rb.at[zz, i], self.sb.at[d, i], self.qb.at[zz, i], s, 2 * zz + c).wait_recv()
                self.combine(self.src.at[z, 2 * c + i], self.rb.at[zz, i])
            each_slot(c, f)
    def drain(self):
        c = self.where[2]
        for k in (0, 1):
            @pl.when(c == k)
            def _(): self.cp_a(k).wait_send()
        for d in (1, 2, 3):
            each_slot(c, lambda i: self.cp_b(d, i).wait_send())

class UnitShare:
    def __init__(self, buf, sems, where):
        self.__dict__.update(locals())
        self.sz, self.qz, self.sc, self.qc = sems
    def cp_z(self, d, i):
        s, z, c, _, _ = self.where
        b = self.buf.at[z, 2 * c + i]
        return remote(b, b, self.sz.at[d, i], self.qz.at[z, i], s, 2 * ((z + d) % 4) + c)
    def cp_c(self, zz, i):
        s, z, c, _, _ = self.where
        b = self.buf.at[zz, 2 * c + i]
        return remote(b, b, self.sc.at[zz, i], self.qc.at[zz, i], s, 2 * z + 1 - c)
    def start(self):
        z, c = self.where[1], self.where[2]
        def f(i):
            for d in (2, 1, 3): self.cp_z(d, i).start()
            self.cp_c(z, i).start()
        each_slot(c, f)
    def mid(self):
        s, z, c, _, _ = self.where
        for d in (1, 3, 2):
            zz = (z + d) % 4
            def f(i):
                b = self.buf.at[zz, 2 * c + i]
                remote(b, b, self.sz.at[d, i], self.qz.at[zz, i], s, 2 * zz + c).wait_recv()
                self.cp_c(zz, i).start()
            each_slot(c, f)
    def end(self):
        s, z, c, _, _ = self.where
        def f(i):
            for zz in range(4):
                b = self.buf.at[zz, 2 * (1 - c) + i]
                remote(b, b, self.sc.at[zz, i], self.qc.at[zz, i], s, 2 * z + 1 - c).wait_recv()
        each_slot(1 - c, f)
    def drain(self):
        z, c = self.where[1], self.where[2]
        def f(i):
            for d in (1, 2, 3): self.cp_z(d, i).wait_send()
            for zz in range(4): self.cp_c(zz, i).wait_send()
        each_slot(c, f)

class Halo:
    def __init__(self, buf, slots, send, recv, where):
        self.__dict__.update(locals())
        s, z, c, _, _ = where
        self.t = 2 * z + c
    def cps(self):
        s, n = self.where[0], self.slots
        up = remote(self.buf.at[:, pl.ds(n, 16)], self.buf.at[:, pl.ds(0, 16)], self.send.at[0], self.recv.at[0], s, self.t + 1)
        down = remote(self.buf.at[:, pl.ds(16, 16)], self.buf.at[:, pl.ds(16 + n, 16)], self.send.at[1], self.recv.at[1], s, self.t - 1)
        return up, down
    def zero(self):
        n = self.slots
        a, _, d = self.buf.shape
        self.buf[:, 16 + n:, :] = jnp.zeros((a, 256 - 16 - n, d), BF)
        self.buf[:, 0:16, :] = jnp.zeros((a, 16, d), BF)
    def start(self):
        up, down = self.cps()
        @pl.when(self.t < 7)
        def _(): up.start()
        @pl.when(self.t > 0)
        def _(): down.start()
    def end(self):
        up, down = self.cps()
        @pl.when(self.t > 0)
        def _(): up.wait_recv()
        @pl.when(self.t < 7)
        def _(): down.wait_recv()
    def drain(self):
        up, down = self.cps()
        @pl.when(self.t < 7)
        def _(): up.wait_send()
        @pl.when(self.t > 0)
        def _(): down.wait_send()

def exact3(a, b):
    return jnp.concatenate([a[0], a[0], a[1]], axis=1), b

def mm(a, b, flip=False):
    ah, al = split(a)
    bh, bl = split(spread_diag(b))
    if flip:
        return dot(ah, bh, 1, 1) + (dot(ah, bl, 1, 1) + dot(al, bh, 1, 1))
    return dot(jnp.concatenate([ah, ah, al], axis=1), jnp.concatenate([bh, bl, bh], axis=0))

def flip64(a):
    t = jnp.transpose(a)
    return jnp.concatenate([t[:64], t[64:]], axis=1)

def eye_pair():
    i = lax.broadcasted_iota(jnp.int32, (64, 128), 0)
    j = lax.broadcasted_iota(jnp.int32, (64, 128), 1)
    return jnp.where(i == j % 64, 1.0, 0.0).astype(F32)

def soft_combine(dst, other):
    m1, m2 = dst[64:65, :], other[64:65, :]
    m = jnp.maximum(m1, m2)
    a, b = jnp.exp(m1 - m), jnp.exp(m2 - m)
    dst[0:64, :] = dst[0:64, :] * a + other[0:64, :] * b
    dst[65:66, :] = dst[65:66, :] * a + other[65:66, :] * b
    dst[64:65, :] = m

def core_setup(qm, km):
    p2 = dot(qm, spread_diag(km), 1, 1) * (64 ** -0.5)
    e = jnp.exp(p2 - seg(jnp.max, p2, -jnp.inf))
    p2 = e / seg(jnp.sum, e, 0.0)
    factor = 1.0 / seg(jnp.max, colsum(p2), -jnp.inf)
    return p2, flip64(p2) * factor

def front_kernel(alpha, x_ref, memb_ref, cnt_ref, valid_ref, wq_ref, wk_ref, wv_ref, wo_ref, win_ref, wback_ref, bin_ref, gains_ref, shifts_ref,
                 w4, wi, wb, q_u, k_u, vpad, qm_u, km_u, p1_ref, r1_ref, e3_ref, ml_ref, wz, sv, p2s, z6, nts, mden, cv_ref, bias_ref,
                 own4, owni, ownb, ownv, vec, wqkv, lhs, xs, xa, xb, xm, nu, ra, rb,
                 recva, recvb, sz, s1, s2, sc, sl, lsem, e0s, e0q, ua, ub, ug, uh, hs):
    where = place()
    s, z, c, p1, p2 = where
    t = 2 * z + c
    nseq = vpad.shape[0]
    rows, width = x_ref.shape
    slots = rows // nseq
    heads = width // 64
    pairs = heads // 2
    sub = wq_ref.shape[0]
    scale = 64 ** -0.5
    for i, r in enumerate((wq_ref, wk_ref, wv_ref, wo_ref)): own4[i] = r[...].astype(BF)
    owni[...] = win_ref[...].astype(BF)
    ownb[...] = wback_ref[...].astype(BF)
    ownv[...] = jnp.zeros_like(ownv)
    ownv[0:2, 0:sub] = gains_ref[...]
    ownv[2:8, 0:sub] = shifts_ref[...]
    ownv[8:9, 0:4 * sub] = bin_ref[...]
    entry(*where)
    chunks = ["vec", "qkv", "o", "in", "back"]
    def owns(k):
        return (ownv, own4.at[pl.ds(0, 3)], own4.at[pl.ds(3, 1)], owni, ownb)[k]
    def blk(k, s_, z_, c_):
        i = s_ * 8 + z_ * 2 + c_
        if k == 0: return vec.at[i]
        at = pl.ds(pl.multiple_of(i * sub, 8), sub)
        if k == 1: return w4.at[pl.ds(0, 3), at]
        if k == 2: return w4.at[pl.ds(3, 1), at]
        if k == 3: return wi.at[at]
        return wb.at[pl.ds(pl.multiple_of(i * 4 * sub, 8), 4 * sub)]
    g = Gather(chunks, owns, blk, recva, recvb, sz, s1, s2, sc, sl, alpha, 1.0, where)
    e2 = UnitSum(nu, ra, rb, (ua.at[0], ua.at[1], ub.at[0], ub.at[1]), where, soft_combine)
    e3 = UnitShare(wz, (ug.at[0], ug.at[1], uh.at[0], uh.at[1]), where)
    halo = Halo(vpad, slots, hs.at[0], hs.at[1], where)
    def xm_part():
        for b in range(nseq):
            xs[b] = dot(memb_ref[pl.ds(64 * b, 64), :], x_ref[pl.ds(slots * b, slots), :])
        remote(xs.at[1 - c], xa, e0s.at[0], e0q.at[0], s, 2 * z + 1 - c).start()
    def cp_xb(d):
        zz = (z + d) % 4
        return remote(xs.at[c, pl.ds(pl.multiple_of(16 * zz, 16), 16)], xb.at[z], e0s.at[d], e0q.at[1 + z], s, 2 * zz + c)
    def cp_xm(d):
        return remote(xm.at[c, z], xm.at[c, z], e0s.at[3 + d], e0q.at[5 + z], s, 2 * ((z + d) % 4) + c)
    def cp_xc(zz):
        return remote(xm.at[c, zz], xm.at[c, zz], e0s.at[7 + zz], e0q.at[9 + zz], s, 2 * z + 1 - c)
    def xm_b():
        remote(xs.at[1 - c], xa, e0s.at[0], e0q.at[0], s, 2 * z + 1 - c).wait_recv()
        xs[c] = xs[c] + xa[...]
        for d in (2, 1, 3): cp_xb(d).start()
    def xm_c():
        tot = xs[c, pl.ds(pl.multiple_of(16 * z, 16), 16), :]
        for d in (1, 3, 2):
            zz = (z + d) % 4
            remote(xb.at[zz], xb.at[zz], e0s.at[d], e0q.at[1 + zz], s, 2 * zz + c).wait_recv()
            tot = tot + xb[zz]
        xm[c, z] = tot / cnt_ref[pl.ds(pl.multiple_of(64 * c + 16 * z, 16), 16), :]
        for d in (2, 1, 3): cp_xm(d).start()
        cp_xc(z).start()
    def xm_d():
        for d in (1, 3, 2):
            zz = (z + d) % 4
            remote(xm.at[c, zz], xm.at[c, zz], e0s.at[3 + d], e0q.at[5 + zz], s, 2 * zz + c).wait_recv()
            cp_xc(zz).start()
    def xm_e():
        for zz in range(4):
            b = xm.at[1 - c, zz]
            remote(b, b, e0s.at[7 + zz], e0q.at[9 + zz], s, 2 * z + 1 - c).wait_recv()
        m = xm[...].reshape(64 * nseq, width)
        hi, lo = split(m)
        lhs[pl.ds(0, rows), :] = x_ref[...]
        lhs[pl.ds(rows, 64 * nseq), :] = hi
        lhs[pl.ds(rows + 64 * nseq, 64 * nseq), :] = lo
    def vectors():
        g.arrive(0)
        i32 = jnp.int32
        v = vec[...]
        row = v[:, 0:8, :].reshape(8 * 32, 128).astype(BF)
        k = lax.broadcasted_iota(i32, (128, width), 0); l = lax.broadcasted_iota(i32, (128, width), 1)
        e = jnp.where((l % sub == k) & (k < sub), 1.0, 0.0).astype(BF)
        w = dot(row, e).reshape(32, 8, width)
        own = lax.broadcasted_iota(i32, (32, 8, width), 0) == lax.broadcasted_iota(i32, (32, 8, width), 2) // sub
        cv_ref[...] = jnp.sum(jnp.where(own, w, 0.0), axis=0)
        ff = bias_ref.shape[1]
        row = v[:, 8:16, :].reshape(8 * 32, 128).astype(BF)
        pick = lax.broadcasted_iota(i32, (256, 1), 0) % 8 == 0
        row = jnp.where(pick, row, jnp.zeros_like(row))
        f4 = 4 * sub
        for q in range(4):
            k = lax.broadcasted_iota(i32, (128, ff // 4), 0); l = lax.broadcasted_iota(i32, (128, ff // 4), 1) + q * (ff // 4)
            e = jnp.where((l % f4 == k) & (k < f4), 1.0, 0.0).astype(BF)
            w = dot(row, e)
            dev = lax.broadcasted_iota(i32, (256, ff // 4), 0) // 8
            own = dev == (lax.broadcasted_iota(i32, (256, ff // 4), 1) + q * (ff // 4)) // f4
            bias_ref[:, pl.ds(q * (ff // 4), ff // 4)] = colsum(jnp.where(own, w, 0.0))
    def load(i): return pltpu.make_async_copy(w4.at[i], wqkv.at[i], lsem.at[i])
    def projections():
        g.arrive(1)
        for i in (2, 1, 0): load(i).start()
        n = 64 * nseq
        load(2).wait()
        v = (dot(x_ref[...], wqkv[2]) + cv_ref[3:4, :]) * valid_ref[...]
        v = v.astype(BF)
        for b in range(nseq): vpad[b, pl.ds(16, slots), :] = v[b * slots:(b + 1) * slots]
        halo.start()
        for i, (dst, marks) in ((1, (k_u, km_u)), (0, (q_u, qm_u))):
            load(i).wait()
            r = dot(lhs[...], wqkv[i])
            a = r[:rows]
            m = r[rows:rows + n] + r[rows + n:]
            if i == 0:
                a = a + cv_ref[2:3, :]
                m = m + cv_ref[2:3, :]
            a = a.astype(BF); m = m.astype(BF)
            for b in range(nseq):
                for p in range(pairs):
                    dst[b * pairs + p] = a[b * slots:(b + 1) * slots, p * 128:(p + 1) * 128]
                    marks[b * pairs + p] = m[b * 64:(b + 1) * 64, p * 128:(p + 1) * 128]
    def third():
        def unit(u, _):
            b, p = u // pairs, u % pairs
            ok = valid_ref[pl.ds(pl.multiple_of(b * slots, slots), slots), :] > 0
            sc3 = dot(k_u[u], spread_diag(qm_u[u]), 1, 1) * scale
            sc3 = jnp.where(ok, sc3, -1e30)
            m = jnp.max(sc3, axis=0, keepdims=True)
            e = jnp.where(ok, jnp.exp(sc3 - m), 0.0)
            e3_ref[u] = e
            ml_ref[u] = jnp.broadcast_to(m, (8, 128))
            v = vpad[b, pl.ds(16, slots), pl.ds(pl.multiple_of(p * 128, 128), 128)]
            nu[u // 3, u % 3, 0:64, :] = halves_diag(dot(v, e.astype(BF), 0, 0))
            nu[u // 3, u % 3, 64:72, :] = jnp.broadcast_to(m, (8, 128))
            nu[u // 3, u % 3, 65:66, :] = colsum(e)
            return 0
        lax.fori_loop(0, nseq * pairs, unit, 0)
        e2.start()
    def first(lo, hi):
        def unit(u, _):
            sc1 = dot(q_u[u], spread_diag(km_u[u]), 1, 1) * scale
            e = jnp.exp(sc1 - seg(jnp.max, sc1, -jnp.inf))
            pr = e / seg(jnp.sum, e, 0.0)
            p1_ref[u] = pr
            r1_ref[u] = pr.astype(BF)
            return 0
        lax.fori_loop(lo, hi, unit, 0)
    st = {}
    def core_a():
        st["P"], st["Z"] = [], []
        for i in range(2):
            u = 3 * z + 2 * c + i * (1 - c)
            pp, zz = core_setup(qm_u[u], km_u[u])
            p2s[i] = pp
            st["P"].append(pp); st["Z"].append(zz)
    def newton(it):
        eye = eye_pair()
        P, Z = st["P"], st["Z"]
        R2 = range(2)
        pr = [mm(P[i], Z[i]) for i in R2]
        t2 = [15.0 * eye - mm(pr[i], 7.0 * eye - pr[i]) for i in R2]
        t3 = [13.0 * eye - mm(pr[i], t2[i]) for i in R2]
        for i in R2:
            sv[i, it, 0] = Z[i]; sv[i, it, 1] = pr[i]; sv[i, it, 2] = t2[i]; sv[i, it, 3] = t3[i]
        st["Z"] = [0.25 * mm(Z[i], t3[i]) for i in R2]
    def core_z():
        for i in range(2):
            k = 2 * c + i * (1 - c)
            z6[i] = st["Z"][i]
            den = nu[z, k, 65:66, :]
            nt = nu[z, k, 0:64, :] / den
            nts[i] = nt
            mden[i] = nu[z, k, 64:72, :]
            wz[z, k] = mm(st["Z"][i], nt, flip=True).astype(BF)
        e3.start()
    halo.zero()
    half = nseq * pairs // 2
    items = [(-1.0, xm_part), (0.6, xm_b), (1.6, xm_c), (2.6, xm_d), (4.6, xm_e), (6.1, vectors), (6.2, projections), (6.3, third),
             (6.4, lambda: first(0, half)), (6.5, core_a), (6.6, e2.mid), (6.7, lambda: newton(0)), (7.6, lambda: newton(1)), (8.1, lambda: newton(2)), (8.6, lambda: newton(3)),
             (9.1, lambda: newton(4)), (9.6, lambda: newton(5)), (9.7, e2.end), (9.8, core_z), (9.9, lambda: first(half, 2 * half)), (11.9, e3.mid), (12.9, e3.end)]
    for key, k, d, part in g.events:
        items.append((key, functools.partial(g.run, k, d, part)))
    items.sort(key=lambda e: e[0])
    for _, f in items: f()
    for k in (2, 3, 4): g.arrive(k)
    halo.end()
    g.drain(); e2.drain(); e3.drain(); halo.drain()
    remote(xs.at[1 - c], xa, e0s.at[0], e0q.at[0], s, 2 * z + 1 - c).wait_send()
    for d in (1, 2, 3):
        cp_xb(d).wait_send(); cp_xm(d).wait_send()
    for zz in range(4): cp_xc(zz).wait_send()

def front(x, memb, cnt, valid, shards, alpha=(0.0, 0.0, 3.0, 4.0, 6.0), cid=0):
    S = jax.ShapeDtypeStruct
    rows, width = x.shape
    wq, wk, wv, wo, win, wback, bin_, gains, shifts = shards
    nseq = 2
    slots = rows // nseq
    sub, ff = wq.shape[0], win.shape[1]
    n = nseq * width // 128
    V = pltpu.VMEM; DMA = pltpu.SemaphoreType.DMA
    vm = pl.BlockSpec(memory_space=pltpu.VMEM); hb = pl.BlockSpec(memory_space=pl.ANY)
    nk = 5
    return pl.pallas_call(
        functools.partial(front_kernel, alpha),
        out_shape=(S((4, width, width), BF), S((width, ff), BF), S((ff, width), BF), S((n, slots, 128), BF), S((n, slots, 128), BF), S((nseq, 256, width), BF),
                   S((n, 64, 128), BF), S((n, 64, 128), BF), S((n, slots, 128), F32), S((n, slots, 128), BF), S((n, slots, 128), F32), S((n, 8, 128), F32),
                   S((4, 3, 64, 128), BF), S((2, ITERS, 4, 64, 128), F32), S((2, 64, 128), F32), S((2, 64, 128), F32), S((2, 64, 128), F32), S((2, 8, 128), F32),
                   S((8, width), F32), S((1, ff), F32)),
        in_specs=[vm] * 13,
        out_specs=(hb,) * 3 + (vm,) * 17,
        scratch_shapes=[V((4, sub, width), BF), V((sub, ff), BF), V((4 * sub, width), BF), V((16, 128), F32), V((32, 16, 128), F32), V((3, width, width), BF),
                        V((rows + 128 * nseq, width), BF), V((2, 64, width), F32), V((64, width), F32), V((4, 16, width), F32), V((2, 4, 16, width), F32),
                        V((4, 3, 72, 128), F32), V((4, 2, 72, 128), F32), V((4, 2, 72, 128), F32),
                        DMA((nk, 4, 4)), DMA((nk, 4, 4)), DMA((nk, 2, 4)), DMA((nk, 4)), DMA((nk, 2, 4)), DMA((nk, 4, 4)), DMA((nk,)), DMA((3,)),
                        DMA((11,)), DMA((13,)), DMA((2,)), DMA((2, 4, 2)), DMA((2, 4, 2)), DMA((2, 4, 2)), DMA((2, 2))],
        compiler_params=pltpu.CompilerParams(collective_id=cid, has_side_effects=True, vmem_limit_bytes=60 * 1024 * 1024),
        name="front_body",
    )(x, memb, cnt, valid, wq, wk, wv, wo, win, wback, bin_, gains, shifts)


def plain_add(dst, other):
    dst[...] = dst[...] + other[...]

class Scatter:
    STAGES = 7
    def __init__(self, srcs, outs, bufs, sems, where):
        self.__dict__.update(locals())
        self.acc, self.rcb, self.r2, self.r1, self.rl, self.rr = bufs
        self.s_ld, self.s_c, self.q_c, self.s_2, self.q_2, self.s_1, self.q_1, self.s_z, self.q_z = sems
        s, z, c, p1, p2 = where
        t = 2 * z + c
        self.right, self.left, self.d1, self.d2, self.dc = (s, t + 2), (s, t - 2), (p1, t), (p2, t), (s, 2 * z + 1 - c)
    def cp_c(self, k): return remote(self.srcs(k, 1 - self.where[2]), self.rcb.at[k], self.s_c.at[k], self.q_c.at[k], *self.dc)
    def cp_ld(self, k): return pltpu.make_async_copy(self.srcs(k, self.where[2]), self.acc.at[k], self.s_ld.at[k])
    def cp_2(self, k, g):
        b = self.where[4] if g == 0 else 3 - self.where[0]
        return remote(self.acc.at[k, b], self.r2.at[k, g], self.s_2.at[k, g], self.q_2.at[k, g], *self.d2)
    def cp_1(self, k): return remote(self.acc.at[k, self.where[3]], self.r1.at[k], self.s_1.at[k], self.q_1.at[k], *self.d1)
    def cp_r(self, k, zz): return remote(self.acc.at[k, self.where[0], zz], self.rl.at[k, zz], self.s_z.at[k, 0, zz], self.q_z.at[k, 0, zz], *self.right)
    def cp_l(self, k, zz): return remote(self.acc.at[k, self.where[0], zz], self.rr.at[k, zz], self.s_z.at[k, 1, zz], self.q_z.at[k, 1, zz], *self.left)
    def add(self, k, i, j, val):
        a = self.acc
        a[k, i, j] = (a[k, i, j].astype(F32) + val.astype(F32)).astype(BF)
    def add4(self, k, i, f):
        def body(j, _):
            self.add(k, i, j, f(j)); return 0
        lax.fori_loop(0, 4, body, 0)
    def run(self, k, i):
        s, z, c, p1, p2 = self.where
        if i == 0:
            self.cp_c(k).start(); self.cp_ld(k).start()
        elif i == 1:
            self.cp_ld(k).wait(); self.cp_c(k).wait_recv()
            for g, b in enumerate((p2, 3 - s)):
                self.add4(k, b, lambda j: self.rcb[k, b, j])
                self.cp_2(k, g).start()
            for b in (p1, s): self.add4(k, b, lambda j: self.rcb[k, b, j])
        elif i == 2:
            self.cp_2(k, 1).wait_recv()
            self.add4(k, p1, lambda j: self.r2[k, 1, j])
            self.cp_1(k).start()
            self.cp_2(k, 0).wait_recv()
            self.add4(k, s, lambda j: self.r2[k, 0, j])
        elif i == 3:
            self.cp_1(k).wait_recv()
            self.add4(k, s, lambda j: self.r1[k, j])
            @pl.when(z == 0)
            def _():
                for zz in (3, 2, 1): self.cp_r(k, zz).start()
            @pl.when(z == 3)
            def _():
                for zz in (0, 1, 2): self.cp_l(k, zz).start()
        elif i in (4, 5):
            h = i - 3
            @pl.when(z == h)
            def _():
                for zz in range(3, h, -1):
                    self.cp_r(k, zz).wait_recv(); self.add(k, s, zz, self.rl[k, zz]); self.cp_r(k, zz).start()
            @pl.when(z == 3 - h)
            def _():
                for zz in range(0, 3 - h):
                    self.cp_l(k, zz).wait_recv(); self.add(k, s, zz, self.rr[k, zz]); self.cp_l(k, zz).start()
        else:
            dst = self.outs(k)
            dst[...] = self.acc[k, s, z].astype(F32)
            @pl.when(z > 0)
            def _():
                self.cp_r(k, z).wait_recv(); dst[...] = dst[...] + self.rl[k, z].astype(F32)
            @pl.when(z < 3)
            def _():
                self.cp_l(k, z).wait_recv(); dst[...] = dst[...] + self.rr[k, z].astype(F32)
    def drain(self, n):
        z = self.where[1]
        for k in range(n):
            self.cp_c(k).wait_send()
            for g in range(2): self.cp_2(k, g).wait_send()
            self.cp_1(k).wait_send()
            def body(zz, _):
                @pl.when(z < zz)
                def _(): self.cp_r(k, zz).wait_send()
                @pl.when(z > zz)
                def _(): self.cp_l(k, zz).wait_send()
                return 0
            lax.fori_loop(0, 4, body, 0)

def back_kernel(keys, x_ref, memb_ref, cnt_ref, valid_ref, da_ref, dwz_ref, dkm1_ref, dq1_ref, e3_ref, ml_ref, k_u, vpad, qm_u, km_u, sv, p2s, z6, nts, mden,
                wr_ref, dh1_ref, gv_ref, gb_ref, gw_ref, w4, g_o, g_in, g_back,
                oq, ok_, ov, oo, oi, ob, gx_ref, sums,
                dpad, e4, ra4, rb4, sh5, e6, ra6, rb6, core_g, sh7, dv1, dk1, dqr, dkr, dvr, gq, gk, gvv, wqkv, acc, rcb, r2, r1, rl, rr, vr, va, vx, vy, vz,
                s_ld, s_c, q_c, s_2, q_2, s_1, q_1, s_z, q_z, ua, ub, u6a, u6b, ug, uh, u7, u7h, hs, lsem, vs, vq):
    where = place()
    s, z, c, p1, p2 = where
    t = 2 * z + c
    rows, width = x_ref.shape
    nseq = vpad.shape[0]
    slots = rows // nseq
    pairs = width // 128
    n = nseq * pairs
    scale = 64 ** -0.5
    sub = oq.shape[0]
    for i in range(3): pltpu.make_async_copy(w4.at[i], wqkv.at[i], lsem.at[i]).start()
    dpad[...] = jnp.zeros_like(dpad)
    for b in range(nseq): dpad[b, pl.ds(16, slots), :] = da_ref[pl.ds(b * slots, slots), :]
    for u in range(n):
        e4[u // 3, u % 3, 0:64, :] = dwz_ref[u]
        e4[u // 3, u % 3, 64:128, :] = dkm1_ref[u]
    entry(*where)
    halo = Halo(dpad, slots, hs.at[0], hs.at[1], where)
    sum4 = UnitSum(e4, ra4, rb4, (ua.at[0], ua.at[1], ub.at[0], ub.at[1]), where, plain_add)
    share5 = UnitShare(sh5, (ug.at[0], ug.at[1], uh.at[0], uh.at[1]), where)
    sum6 = UnitSum(e6, ra6, rb6, (u6a.at[0], u6a.at[1], u6b.at[0], u6b.at[1]), where, plain_add)
    share7 = UnitShare(sh7, (u7.at[0], u7.at[1], u7h.at[0], u7h.at[1]), where)
    def srcs(k, c_):
        if k < 4: return g_back.at[:, :, c_, pl.ds(k * sub, sub), :]
        if k < 8: return g_in.at[:, :, c_, :, pl.ds((k - 4) * width, width)]
        if k == 8: return g_o.at[:, :, c_]
        return (gvv, gk, gq)[k - 9].at[:, :, c_]
    def outs(k):
        if k < 4: return ob.at[pl.ds(k * sub, sub), :]
        if k < 8: return oi.at[:, pl.ds((k - 4) * width, width)]
        return (oo, ov, ok_, oq)[k - 8]
    rs = Scatter(srcs, outs, (acc, rcb, r2, r1, rl, rr), (s_ld, s_c, q_c, s_2, q_2, s_1, q_1, s_z, q_z), where)
    st = {}
    R2 = range(2)
    def core_a():
        st["G"], st["DP"] = [], []
        for i in R2:
            k = 2 * c + i * (1 - c)
            dwz = e4[z, k, 0:64, :]
            nt = nts[i]
            den = mden[i, 1:2, :]
            dnt = mm(flip64(dwz), z6[i])
            dden = -colsum(dnt * nt) / den
            m = mden[i, 0:1, :]
            m1 = m.astype(BF); mr = m - m1.astype(F32); m2 = mr.astype(BF); m3 = (mr - m2.astype(F32)).astype(BF)
            d1 = dden.astype(BF); dr = dden - d1.astype(F32); d2 = dr.astype(BF); d3 = (dr - d2.astype(F32)).astype(BF)
            sh5[z, k, 0:64, :] = (dnt / den).astype(BF)
            row = lax.broadcasted_iota(jnp.int32, (16, 128), 0)
            tile = jnp.zeros((16, 128), F32)
            for j, v in enumerate((m1, m2, m3, d1, d2, d3)):
                tile = jnp.where(row == j, v.astype(F32), tile)
            sh5[z, k, 64:80, :] = tile.astype(BF)
            st["G"].append(mm(flip64(nt), dwz, flip=True))
            st["DP"].append(jnp.zeros((64, 128), F32))
        share5.start()
    def core_it(it):
        eye = eye_pair()
        G, DP = st["G"], st["DP"]
        Z = [sv[i, it, 0] for i in R2]; Pr = [sv[i, it, 1] for i in R2]; T2 = [sv[i, it, 2] for i in R2]; T3 = [sv[i, it, 3] for i in R2]
        d3 = [0.25 * mm(G[i], Z[i]) for i in R2]
        dz = [0.25 * mm(T3[i], G[i]) for i in R2]
        d2 = [-mm(d3[i], Pr[i]) for i in R2]
        dp = [-mm(T2[i], d3[i]) for i in R2]
        d1 = [-mm(d2[i], Pr[i]) for i in R2]
        dp = [dp[i] - mm(7.0 * eye - Pr[i], d2[i]) - d1[i] for i in R2]
        st["DP"] = [DP[i] + mm(Z[i], dp[i]) for i in R2]
        st["G"] = [dz[i] + mm(dp[i], p2s[i]) for i in R2]
    def core_z():
        for i in R2:
            k = 2 * c + i * (1 - c)
            u = 3 * z + k
            p, g0 = p2s[i], st["G"][i]
            col = colsum(p)
            top = seg(jnp.max, col, -jnp.inf)
            f = 1.0 / top
            df = seg(jnp.sum, colsum(g0 * p), 0.0)
            hit = (col == top).astype(F32)
            dcol = -f * f * df * hit / seg(jnp.sum, hit, 0.0)
            dp = flip64(st["DP"][i]) + f * g0 + dcol
            ds = p * (dp - seg(jnp.sum, dp * p, 0.0)) * scale
            hi, lo = split(ds)
            b = spread_diag(km_u[u])
            core_g[i, 0:64, :] = dot(hi, b) + dot(lo, b)
            hi, lo = split(flip64(ds))
            b = spread_diag(qm_u[u])
            core_g[i, 64:128, :] = dot(hi, b) + dot(lo, b)
    def third():
        def unit(u, _):
            b, p = u // pairs, u % pairs
            tile = sh5[u // 3, u % 3, 64:80, :].astype(F32)
            m = tile[0:1] + tile[1:2] + tile[2:3]
            dden = tile[3:4] + tile[4:5] + tile[5:6]
            e = e3_ref[u] * jnp.exp(ml_ref[u, 0:1, :] - m)
            dn = spread_diag(sh5[u // 3, u % 3, 0:64, :])
            v = vpad[b, pl.ds(16, slots), pl.ds(pl.multiple_of(p * 128, 128), 128)]
            de = dot(v, dn) + dden
            dv1[u] = dot(e.astype(BF), dn, 1, 1)
            ds = (e * de * scale).astype(BF)
            e6[u // 3, u % 3] = halves_diag(dot(ds, k_u[u], 0, 0))
            dk1[u] = dot(ds, spread_diag(qm_u[u]))
            return 0
        lax.fori_loop(0, n, unit, 0)
        sum6.start()
    def conv():
        def per(p, _):
            lanes = pl.ds(pl.multiple_of(p * 128, 128), 128)
            th = [split(skew(wr_ref[pl.ds(2 * p + e, 1), :], 256, slots)) for e in range(2)]
            low = lane_low((slots, 128))
            for b in range(nseq):
                u = b * pairs + p
                d = dpad[b, :, lanes]
                c0 = dot(th[0][0], d) + dot(th[0][1], d)
                c1 = dot(th[1][0], d) + dot(th[1][1], d)
                at = pl.ds(b * slots, slots)
                v = (dv1[u] + jnp.where(low, c0, c1)) * valid_ref[at, :]
                dv1[u] = v
                dvr[at, lanes] = v.astype(BF)
            vr[3:4, lanes] = sum(colsum(dv1[b * pairs + p]) for b in range(nseq))
            return 0
        halo.end()
        lax.fori_loop(0, pairs, per, 0)
    def weight_grad(dst, src):
        def tile(j, _):
            cols = pl.ds(pl.multiple_of(j * 256, 256), 256)
            dst[:, :, :, :, cols] = dot(x_ref[...], src[:, cols], 0, 0).astype(BF).reshape(4, 4, 2, sub, 256)
            return 0
        lax.fori_loop(0, width // 256, tile, 0)
    def own_marks():
        for i in R2:
            k = 2 * c + i * (1 - c)
            q = core_g[i, 0:64, :] + e6[z, k]
            kk = core_g[i, 64:128, :] + e4[z, k, 64:128, :]
            cn = cnt_ref[pl.ds(pl.multiple_of(64 * (z // 2), 64), 64), :]
            sh7[z, k, 0:64, :] = (q / cn).astype(BF)
            sh7[z, k, 64:128, :] = (kk / cn).astype(BF)
        share7.start()
    def queries():
        def unit(u, _):
            b, p = u // pairs, u % pairs
            lanes = pl.ds(pl.multiple_of(p * 128, 128), 128)
            at = pl.ds(pl.multiple_of(b * slots, slots), slots)
            mb = memb_ref[pl.ds(pl.multiple_of(64 * b, 64), 64), :]
            q = dot(mb, sh7[u // 3, u % 3, 0:64, :], 0, 0) + dq1_ref[u]
            k = dot(mb, sh7[u // 3, u % 3, 64:128, :], 0, 0) + dk1[u]
            dqr[at, lanes] = q.astype(BF)
            dkr[at, lanes] = k.astype(BF)
            vr[2:3, lanes] += colsum(q)
            return 0
        vr[2:3, :] = jnp.zeros((1, width), F32)
        lax.fori_loop(0, n, unit, 0)
    y_of = s // 2
    px = s + 1 - 2 * (s % 2)
    py = (s + 2) % 4
    def cp_v(i):
        dst, dev = ((va, (s, 2 * z + 1 - c)), (vx, (px, t)), (vy, (py, t)))[i]
        return remote(vr, dst, vs.at[i], vq.at[i], *dev)
    def vec_0():
        vr[0:2, :] = gv_ref[0:2, :]
        vr[4:8, :] = gv_ref[4:8, :]
        for i in range(4): vr[8 + i:9 + i, :] = gb_ref[:, pl.ds(i * width, width)]
        vr[12:24, :] = jnp.zeros((12, width), F32)
        vr[12:24, 0:128] = gw_ref[:, 0:128]
        cp_v(0).start()
    def vec_step(i):
        cp_v(i).wait()
        vr[...] = vr[...] + (va, vx, vy)[i][...]
        if i < 2: cp_v(i + 1).start()
        else:
            for d in (1, 2, 3): cp_vz(d).start()
    def cp_vz(d): return remote(vr, vz.at[z], vs.at[2 + d], vq.at[3 + z], s, 2 * ((z + d) % 4) + c)
    def vec_z():
        for d in (1, 2, 3):
            zz = (z + d) % 4
            remote(vr, vz.at[zz], vs.at[2 + d], vq.at[3 + zz], s, 2 * zz + c).wait_recv()
        for d in (1, 2, 3): cp_vz(d).wait_send()
        vz[z] = vr[...]
        sums[...] = ((vz[0] + vz[1]) + vz[2]) + vz[3]
    def grad_x(first_):
        if first_:
            for i in range(3): pltpu.make_async_copy(w4.at[i], wqkv.at[i], lsem.at[i]).wait()
            gx_ref[...] = dh1_ref[...] + dot(dvr[...], wqkv[2], 1, 1)
        else:
            gx_ref[...] = gx_ref[...] + dot(dqr[...], wqkv[0], 1, 1) + dot(dkr[...], wqkv[1], 1, 1)
    chunk_keys, K = keys
    items = [(-2, sum4.start), (-1.9, halo.start), (K[0], sum4.mid), (K[1], sum4.end), (K[2], core_a), (K[3], share5.mid), (K[4], core_z), (K[5], share5.end), (K[5] + .001, third),
             (K[6], conv), (K[6] + .001, lambda: weight_grad(gvv, dvr)), (K[7], sum6.mid), (K[8], sum6.end), (K[8] + .001, own_marks), (K[9], lambda: grad_x(True)),
             (K[10], share7.mid), (K[11], share7.end), (K[11] + .001, queries), (K[11] + .002, lambda: weight_grad(gk, dkr)), (K[12], lambda: weight_grad(gq, dqr)),
             (K[13], vec_0), (K[14], lambda: grad_x(False)), (K[15], lambda: vec_step(0)), (K[16], lambda: vec_step(1)), (K[17], lambda: vec_step(2)), (K[18], vec_z)]
    for j in range(ITERS):
        items.append((K[2] + .01 + (K[4] - K[2] - .02) * j / ITERS, functools.partial(core_it, ITERS - 1 - j)))
    for k, base in enumerate(chunk_keys):
        for i in range(Scatter.STAGES): items.append((base + i, functools.partial(rs.run, k, i)))
    items.sort(key=lambda e: e[0])
    for _, f in items: f()
    rs.drain(len(chunk_keys)); sum4.drain(); share5.drain(); sum6.drain(); share7.drain(); halo.drain()

KEYS = ((0.0, 0.5, 1.0, 1.5, 2.0, 2.5, 3.0, 3.5, 4.0, 5.01, 6.31, 6.33),
        (0.4, 0.9, 1.0, 1.8, 4.0, 4.3, 4.6, 4.9, 5.3, 5.4, 5.8, 6.2, 6.32, 6.34, 6.9, 7.3, 8.3, 9.3, 10.3))

def back(x, memb, cnt, valid, da, dwz, dkm1, dq1, e3, ml, k_u, vpad, qm_u, km_u, sv, p2s, z6, nts, mden, wr, dh1, gv, gb, gw, w4, g_o, g_in, g_back, keys=KEYS, cid=1):
    S = jax.ShapeDtypeStruct
    rows, width = x.shape
    ff = gb.shape[1]
    nseq = vpad.shape[0]
    slots = rows // nseq
    sub = width // 32
    n = nseq * width // 128
    V = pltpu.VMEM; DMA = pltpu.SemaphoreType.DMA
    vm = pl.BlockSpec(memory_space=pltpu.VMEM); hb = pl.BlockSpec(memory_space=pl.ANY)
    five = lambda a: a.reshape(4, 4, 2, a.shape[0] // 32, a.shape[1])
    nk = 12
    return pl.pallas_call(
        functools.partial(back_kernel, keys),
        out_shape=(S((sub, width), F32),) * 4 + (S((sub, ff), F32), S((4 * sub, width), F32), S((rows, width), F32), S((24, width), F32)),
        in_specs=[vm] * 24 + [hb] * 4,
        out_specs=(vm,) * 8,
        scratch_shapes=[V((nseq, 256, width), BF), V((4, 3, 128, 128), F32), V((4, 2, 128, 128), F32), V((4, 2, 128, 128), F32), V((4, 3, 80, 128), BF),
                        V((4, 3, 64, 128), F32), V((4, 2, 64, 128), F32), V((4, 2, 64, 128), F32), V((2, 128, 128), F32), V((4, 3, 128, 128), BF),
                        V((n, slots, 128), F32), V((n, slots, 128), F32), V((rows, width), BF), V((rows, width), BF), V((rows, width), BF),
                        V((4, 4, 2, sub, width), BF), V((4, 4, 2, sub, width), BF), V((4, 4, 2, sub, width), BF), V((3, width, width), BF),
                        V((nk, 4, 4, sub, width), BF), V((nk, 4, 4, sub, width), BF), V((nk, 2, 4, sub, width), BF), V((nk, 4, sub, width), BF),
                        V((nk, 4, sub, width), BF), V((nk, 4, sub, width), BF),
                        V((24, width), F32), V((24, width), F32), V((24, width), F32), V((24, width), F32), V((4, 24, width), F32),
                        DMA((nk,)), DMA((nk,)), DMA((nk,)), DMA((nk, 2)), DMA((nk, 2)), DMA((nk,)), DMA((nk,)), DMA((nk, 2, 4)), DMA((nk, 2, 4)),
                        DMA((2,)), DMA((2, 4, 2)), DMA((2,)), DMA((2, 4, 2)), DMA((2, 4, 2)), DMA((2, 4, 2)), DMA((2, 4, 2)), DMA((2, 4, 2)), DMA((2, 2)), DMA((3,)),
                        DMA((6,)), DMA((7,))],
        compiler_params=pltpu.CompilerParams(collective_id=cid, has_side_effects=True, vmem_limit_bytes=62 * 1024 * 1024),
        name="back_body",
    )(x, memb, cnt, valid, da, dwz, dkm1, dq1, e3, ml, k_u, vpad, qm_u, km_u, sv, p2s, z6, nts, mden, wr, dh1, gv, gb, gw, w4, five(g_o), five(g_in), five(g_back))


def fast_shards(inputs, lengths, bounds, w_query, w_key, w_value, w_out, w_conv, w_in, w_back, b_in, gains, shifts, cotangent):
    nseq, slots, width = inputs.shape
    rows = nseq * slots
    ff = w_in.shape[1]
    taps = w_conv.shape[1]
    position = lax.axis_index("tok") * slots + jnp.arange(slots, dtype=jnp.int32)
    valid = (position[None, :] < lengths[:, None]).astype(F32).reshape(rows, 1)
    member = ((position[None, None] >= bounds[:, :-1, None]) & (position[None, None] < bounds[:, 1:, None])).astype(BF)
    member = member.reshape(-1, slots)
    count = (bounds[:, 1:] - bounds[:, :-1]).astype(F32).reshape(-1, 1)
    x = inputs.reshape(rows, width)
    taps_row = jnp.pad(w_conv, ((0, 0), (0, 256 - taps)))
    taps_back = jnp.pad(w_conv[:, ::-1], ((0, 0), (0, 256 - taps)))
    shards_in = (w_query, w_key, w_value, w_out, w_in, w_back, b_in.reshape(1, -1), gains, shifts)
    (w4, wi, wb, q_u, k_u, vpad, qm_u, km_u, p1, r1, e3, ml, wz, sv, p2s, z6, nts, mden, cv, bias) = front(x, member, count, valid, shards_in)
    (res, dh1, da, dwz, dkm, dq1, gv, gb, gw, g_o, g_in, g_back) = layer(
        x, cotangent.reshape(rows, width), valid, r1, p1, wz.reshape(-1, 64, 128), km_u, q_u, vpad, taps_row, cv, bias, w4, wi, wb)
    (oq, ok, ov, oo, oi, ob, gx, sums) = back(
        x, member, count, valid, da, dwz, dkm, dq1, e3, ml, k_u, vpad, qm_u, km_u, sv, p2s, z6, nts, mden, taps_back, dh1, gv, gb, gw, w4, g_o, g_in, g_back)
    me = lax.axis_index("seq") * 8 + lax.axis_index("tok")
    sub = width // 32
    vec = lax.dynamic_slice(sums, (0, me * sub), (8, sub))
    bias_grad = lax.dynamic_slice(sums[8:12].reshape(ff), (me * (ff // 32),), (ff // 32,))
    return (res.reshape(inputs.shape), gx.reshape(inputs.shape), oq, ok, ov, oo, sums[12:24, :taps], oi, ob, bias_grad, vec[:2], vec[2:])


def solution(mesh):
    placed = (
        P("seq", "tok", None),
        P("seq"),
        P("seq", None),
        P(("seq", "tok"), None),
        P(("seq", "tok"), None),
        P(("seq", "tok"), None),
        P(("seq", "tok"), None),
        P(),
        P(("seq", "tok"), None),
        P(("seq", "tok"), None),
        P(("seq", "tok")),
        P(None, ("seq", "tok")),
        P(None, ("seq", "tok")),
        P("seq", "tok", None),
    )
    return jax.shard_map(
        fast_shards if (mesh.shape["seq"], mesh.shape["tok"]) == (4, 8) else shards,
        mesh=mesh,
        in_specs=placed,
        out_specs=(
            P("seq", "tok", None),
            P("seq", "tok", None),
            P(("seq", "tok"), None),
            P(("seq", "tok"), None),
            P(("seq", "tok"), None),
            P(("seq", "tok"), None),
            P(),
            P(("seq", "tok"), None),
            P(("seq", "tok"), None),
            P(("seq", "tok")),
            P(None, ("seq", "tok")),
            P(None, ("seq", "tok")),
        ),
        check_vma=False,
    )
```

```python
import functools

import jax
import jax.numpy as jnp
from jax import lax
from jax.experimental import pallas as pl
from jax.experimental.pallas import tpu as pltpu
from jax.sharding import PartitionSpec as P

ITERS = 6


EPSILON = 1e-05
EXACT_PRECISION = lax.Precision.HIGHEST


def padded_2(cells, sides, width):
    for axis, dim in sides:
        count = lax.axis_size(axis)
        ends = count - 1
        head = lax.slice_in_dim(cells, 0, width, axis=dim)
        tail = lax.slice_in_dim(cells, cells.shape[dim] - width, cells.shape[dim], axis=dim)
        cells = jnp.concatenate(
            [
                lax.ppermute(tail, axis, [(i, (i + 1) % count) for i in range(ends)]),
                cells,
                lax.ppermute(head, axis, [((i + 1) % count, i) for i in range(ends)]),
            ],
            axis=dim,
        )
    return cells


def layer_norm(hidden, gain_row, shift_row):
    center = hidden - jnp.mean(hidden, axis=-1, keepdims=True)
    spread = jnp.mean(center * center, axis=-1, keepdims=True)
    return center * lax.rsqrt(spread + EPSILON) * gain_row + shift_row


def newton_inverse(kernel):
    column_sum = jnp.sum(kernel, axis=-2)
    factor = 1.0 / jnp.max(column_sum, axis=-1)
    approx = jnp.swapaxes(kernel, -1, -2) * factor[..., None, None]
    identity = jnp.eye(kernel.shape[-1], dtype=jnp.float32)
    for sweep_index in range(ITERS):
        product = jnp.matmul(kernel, approx, precision=EXACT_PRECISION)
        inner_term = 7.0 * identity - product
        inner_term = 15.0 * identity - jnp.matmul(product, inner_term, precision=EXACT_PRECISION)
        inner_term = 13.0 * identity - jnp.matmul(product, inner_term, precision=EXACT_PRECISION)
        approx = 0.25 * jnp.matmul(approx, inner_term, precision=EXACT_PRECISION)
    return approx


def mixer_core(query_marks, key_marks, numerator, denom):
    score_scale_factor = query_marks.shape[-1] ** (-0.5)
    scores = (
        jnp.einsum("bihd,bjhd->bhij", query_marks, key_marks, precision=EXACT_PRECISION)
        * score_scale_factor
    )
    middle = jax.nn.softmax(scores, axis=-1)
    pseudo = newton_inverse(middle)
    summary = numerator / denom[..., None]
    return jnp.einsum("bhij,bhjd->bhid", pseudo, summary, precision=EXACT_PRECISION)


def gelu_exact(pre_act):
    return jax.nn.gelu(pre_act, approximate=False)


def product_low(pattern, left, right):
    return jnp.einsum(pattern, left, right, preferred_element_type=jnp.float32)


def shards(
    inputs,
    lengths,
    bounds,
    w_query,
    w_key,
    w_value,
    w_out,
    w_conv,
    w_in,
    w_back,
    b_in,
    gains,
    shifts,
    cotangent,
):
    seq_count, slot_count, model_width = inputs.shape
    head_count, tap_count = w_conv.shape
    head_dim = model_width // head_count
    rim_width = tap_count // 2
    mark_count = bounds.shape[1] - 1
    row_count = seq_count * slot_count
    score_scale_factor = head_dim ** (-0.5)
    first_slot = lax.axis_index("tok") * slot_count
    position = first_slot + jnp.arange(slot_count, dtype=jnp.int32)
    valid_mask = (position[None, :] < lengths[:, None]).astype(jnp.float32)
    member = (
        (position[None, None, :] >= bounds[:, :-1, None])
        & (position[None, None, :] < bounds[:, 1:, None])
    ).astype(jnp.float32)
    part_count = (bounds[:, 1:] - bounds[:, :-1]).astype(jnp.float32)
    gathered = (
        lax.all_gather(w_query.astype(jnp.bfloat16), ("seq", "tok"), axis=0, tiled=True),
        lax.all_gather(w_key.astype(jnp.bfloat16), ("seq", "tok"), axis=0, tiled=True),
        lax.all_gather(w_value.astype(jnp.bfloat16), ("seq", "tok"), axis=0, tiled=True),
        lax.all_gather(w_out.astype(jnp.bfloat16), ("seq", "tok"), axis=0, tiled=True),
        lax.all_gather(w_in.astype(jnp.bfloat16), ("seq", "tok"), axis=0, tiled=True),
        lax.all_gather(w_back.astype(jnp.bfloat16), ("seq", "tok"), axis=0, tiled=True),
        lax.all_gather(b_in.astype(jnp.bfloat16), ("seq", "tok"), axis=0, tiled=True),
        lax.all_gather(gains.astype(jnp.bfloat16), ("seq", "tok"), axis=1, tiled=True),
        lax.all_gather(shifts.astype(jnp.bfloat16), ("seq", "tok"), axis=1, tiled=True),
    )
    query_mat, key_mat, value_mat, out_mat, in_mat, back_mat, bias_vec, gain_vec, shift_vec = (
        gathered
    )
    bias_rows = bias_vec.astype(jnp.float32)
    gain_rows = gain_vec.astype(jnp.float32)
    shift_rows = shift_vec.astype(jnp.float32)
    flat_rows = inputs.reshape(row_count, model_width)
    query_rows = jnp.dot(flat_rows, query_mat, preferred_element_type=jnp.float32) + shift_rows[0]
    key_rows = jnp.dot(flat_rows, key_mat, preferred_element_type=jnp.float32)
    value_rows = jnp.dot(flat_rows, value_mat, preferred_element_type=jnp.float32) + shift_rows[1]
    part_query = jnp.einsum(
        "bms,bsd->bmd",
        member,
        query_rows.reshape(seq_count, slot_count, model_width),
        precision=EXACT_PRECISION,
    )
    part_key = jnp.einsum(
        "bms,bsd->bmd",
        member,
        key_rows.reshape(seq_count, slot_count, model_width),
        precision=EXACT_PRECISION,
    )
    sum_query, sum_key = lax.psum((part_query, part_key), "tok")
    mark_query = (
        (sum_query / part_count[..., None])
        .astype(jnp.bfloat16)
        .reshape(seq_count, mark_count, head_count, head_dim)
    )
    mark_key = (
        (sum_key / part_count[..., None])
        .astype(jnp.bfloat16)
        .reshape(seq_count, mark_count, head_count, head_dim)
    )
    query_head_rows = query_rows.astype(jnp.bfloat16).reshape(
        seq_count, slot_count, head_count, head_dim
    )
    key_head_rows = key_rows.astype(jnp.bfloat16).reshape(
        seq_count, slot_count, head_count, head_dim
    )
    v_low = (value_rows.reshape(seq_count, slot_count, model_width) * valid_mask[..., None]).astype(
        jnp.bfloat16
    )
    value_head_rows = v_low.reshape(seq_count, slot_count, head_count, head_dim)
    first_score_matrix = (
        product_low("bshd,bmhd->bshm", query_head_rows, mark_key) * score_scale_factor
    )
    first_score_kernel = jax.nn.softmax(first_score_matrix, axis=-1)
    first_low = first_score_kernel.astype(jnp.bfloat16)
    third_score_matrix = (
        product_low("bmhd,bshd->bhms", mark_query, key_head_rows) * score_scale_factor
    )
    third_score_matrix = jnp.where(valid_mask[:, None, None, :] > 0, third_score_matrix, -1e30)
    score_top = lax.pmax(jnp.max(third_score_matrix, axis=-1), "tok")
    third_exponential = jnp.exp(third_score_matrix - score_top[..., None])
    third_low = third_exponential.astype(jnp.bfloat16)
    numerator, denom = lax.psum(
        (
            product_low("bhms,bshd->bhmd", third_low, value_head_rows),
            jnp.sum(third_exponential, axis=-1),
        ),
        "tok",
    )
    mixed_output, core_back = jax.vjp(
        mixer_core, mark_query.astype(jnp.float32), mark_key.astype(jnp.float32), numerator, denom
    )
    mixed_low = mixed_output.astype(jnp.bfloat16)
    attention_forward = product_low("bshm,bhmd->bshd", first_low, mixed_low)
    padded = padded_2(v_low, (("tok", 1),), rim_width)
    padded_heads = padded.astype(jnp.float32).reshape(
        seq_count, slot_count + 2 * rim_width, head_count, head_dim
    )
    conv_out = jnp.zeros_like(attention_forward)
    for offset in range(tap_count):
        conv_out = (
            conv_out
            + w_conv[:, offset][None, None, :, None] * padded_heads[:, offset : offset + slot_count]
        )
    mix_low = (attention_forward + conv_out).reshape(row_count, model_width).astype(jnp.bfloat16)
    first_sum = (
        flat_rows.astype(jnp.float32)
        + jnp.dot(mix_low, out_mat, preferred_element_type=jnp.float32)
        + shift_rows[2]
    )
    normed, norm_one_back = jax.vjp(layer_norm, first_sum, gain_rows[0], shift_rows[3])
    normed_low = normed.astype(jnp.bfloat16)
    pre_act = jnp.dot(normed_low, in_mat, preferred_element_type=jnp.float32) + bias_rows
    active, gelu_back = jax.vjp(gelu_exact, pre_act)
    active_low = active.astype(jnp.bfloat16)
    second_sum = (
        normed + jnp.dot(active_low, back_mat, preferred_element_type=jnp.float32) + shift_rows[4]
    )
    final_raw, norm_two_back = jax.vjp(layer_norm, second_sum, gain_rows[1], shift_rows[5])
    valid_rows = valid_mask.reshape(row_count, 1)
    result = final_raw * valid_rows
    back_weights = (
        lax.all_gather(w_query.astype(jnp.bfloat16), ("seq", "tok"), axis=0, tiled=True),
        lax.all_gather(w_key.astype(jnp.bfloat16), ("seq", "tok"), axis=0, tiled=True),
        lax.all_gather(w_value.astype(jnp.bfloat16), ("seq", "tok"), axis=0, tiled=True),
        lax.all_gather(w_out.astype(jnp.bfloat16), ("seq", "tok"), axis=0, tiled=True),
        lax.all_gather(w_in.astype(jnp.bfloat16), ("seq", "tok"), axis=0, tiled=True),
        lax.all_gather(w_back.astype(jnp.bfloat16), ("seq", "tok"), axis=0, tiled=True),
    )
    query_back, key_back, value_back, out_back, in_back, back_back = back_weights
    grad_out = cotangent.reshape(row_count, model_width).astype(jnp.float32) * valid_rows
    grad_second, grad_gain_two, grad_shift_five = norm_two_back(grad_out)
    grad_second_low = grad_second.astype(jnp.bfloat16)
    grad_shift_four = jnp.sum(grad_second, axis=0)
    grad_w_back = product_low("rf,rd->fd", active_low, grad_second_low)
    grad_active = product_low("rd,fd->rf", grad_second_low, back_back)
    (grad_pre,) = gelu_back(grad_active)
    grad_pre_low = grad_pre.astype(jnp.bfloat16)
    grad_b_in = jnp.sum(grad_pre, axis=0)
    grad_w_in = product_low("rd,rf->df", normed_low, grad_pre_low)
    grad_normed = grad_second + product_low("rf,df->rd", grad_pre_low, in_back)
    grad_first, grad_gain_one, grad_shift_three = norm_one_back(grad_normed)
    grad_proj_low = grad_first.astype(jnp.bfloat16)
    grad_shift_two = jnp.sum(grad_first, axis=0)
    grad_w_out = product_low("rd,re->de", mix_low, grad_proj_low)
    grad_mix_low = (
        product_low("re,de->rd", grad_proj_low, out_back)
        .astype(jnp.bfloat16)
        .reshape(seq_count, slot_count, model_width)
    )
    grad_mix_heads = grad_mix_low.reshape(seq_count, slot_count, head_count, head_dim)
    grad_mixed_part = product_low("bshm,bshd->bhmd", first_low, grad_mix_heads)
    grad_first_kernel = product_low("bshd,bhmd->bshm", grad_mix_heads, mixed_low)
    inner_sum = jnp.sum(grad_first_kernel * first_score_kernel, axis=-1, keepdims=True)
    grad_first_low = (
        first_score_kernel * (grad_first_kernel - inner_sum) * score_scale_factor
    ).astype(jnp.bfloat16)
    part_grad_key = product_low("bshm,bshd->bmhd", grad_first_low, query_head_rows)
    grad_mixed, grad_mk_first = lax.psum((grad_mixed_part, part_grad_key), "tok")
    grad_mq_core, grad_mk_core, grad_numer, grad_denom = core_back(grad_mixed)
    grad_numer_low = grad_numer.astype(jnp.bfloat16)
    grad_third_exp = (
        product_low("bhmd,bshd->bhms", grad_numer_low, value_head_rows) + grad_denom[..., None]
    )
    grad_v_heads = product_low("bhms,bhmd->bshd", third_low, grad_numer_low)
    grad_third_low = (third_exponential * grad_third_exp * score_scale_factor).astype(jnp.bfloat16)
    part_grad_query = product_low("bhms,bshd->bmhd", grad_third_low, key_head_rows)
    grad_key_heads = product_low("bhms,bmhd->bshd", grad_third_low, mark_query)
    grad_mq_third = lax.psum(part_grad_query, "tok")
    grad_mq = (grad_mq_core + grad_mq_third).reshape(
        seq_count, mark_count, model_width
    ) / part_count[..., None]
    grad_mk = (grad_mk_core + grad_mk_first).reshape(
        seq_count, mark_count, model_width
    ) / part_count[..., None]
    grad_query = jnp.einsum(
        "bms,bmd->bsd", member, grad_mq, precision=EXACT_PRECISION
    ) + product_low("bshm,bmhd->bshd", grad_first_low, mark_key).reshape(
        seq_count, slot_count, model_width
    )
    grad_key = jnp.einsum(
        "bms,bmd->bsd", member, grad_mk, precision=EXACT_PRECISION
    ) + grad_key_heads.reshape(seq_count, slot_count, model_width)
    grad_padded = padded_2(grad_mix_low, (("tok", 1),), rim_width)
    grad_pad_heads = grad_padded.astype(jnp.float32).reshape(
        seq_count, slot_count + 2 * rim_width, head_count, head_dim
    )
    grad_mix_float = grad_mix_heads.astype(jnp.float32)
    grad_conv_v = jnp.zeros_like(grad_mix_float)
    conv_terms = []
    for offset in range(tap_count):
        start_at = 2 * rim_width - offset
        grad_conv_v = (
            grad_conv_v
            + w_conv[:, offset][None, None, :, None]
            * grad_pad_heads[:, start_at : start_at + slot_count]
        )
        conv_terms.append(
            jnp.sum(padded_heads[:, offset : offset + slot_count] * grad_mix_float, axis=(0, 1, 3))
        )
    grad_w_conv = lax.psum(jnp.stack(conv_terms, axis=1), ("seq", "tok"))
    grad_value = (grad_v_heads + grad_conv_v).reshape(
        seq_count, slot_count, model_width
    ) * valid_mask[..., None]
    grad_query_flat = grad_query.reshape(row_count, model_width)
    grad_key_flat = grad_key.reshape(row_count, model_width)
    grad_value_flat = grad_value.reshape(row_count, model_width)
    grad_query_low = grad_query_flat.astype(jnp.bfloat16)
    grad_key_low = grad_key_flat.astype(jnp.bfloat16)
    grad_value_low = grad_value_flat.astype(jnp.bfloat16)
    grad_w_query = product_low("rd,re->de", flat_rows, grad_query_low)
    grad_w_key = product_low("rd,re->de", flat_rows, grad_key_low)
    grad_w_value = product_low("rd,re->de", flat_rows, grad_value_low)
    grad_input = (
        grad_first
        + product_low("re,de->rd", grad_query_low, query_back)
        + product_low("re,de->rd", grad_key_low, key_back)
        + product_low("re,de->rd", grad_value_low, value_back)
    )
    grad_gains = jnp.stack([grad_gain_one, grad_gain_two], axis=0)
    grad_shifts = jnp.stack(
        [
            jnp.sum(grad_query_flat, axis=0),
            jnp.sum(grad_value_flat, axis=0),
            grad_shift_two,
            grad_shift_three,
            grad_shift_four,
            grad_shift_five,
        ],
        axis=0,
    )
    (
        owned_query,
        owned_key,
        owned_value,
        owned_out,
        owned_in,
        owned_back,
        owned_bias,
        owned_gains,
        owned_shifts,
    ) = (
        lax.psum_scatter(grad_w_query, ("seq", "tok"), scatter_dimension=0, tiled=True),
        lax.psum_scatter(grad_w_key, ("seq", "tok"), scatter_dimension=0, tiled=True),
        lax.psum_scatter(grad_w_value, ("seq", "tok"), scatter_dimension=0, tiled=True),
        lax.psum_scatter(grad_w_out, ("seq", "tok"), scatter_dimension=0, tiled=True),
        lax.psum_scatter(grad_w_in, ("seq", "tok"), scatter_dimension=0, tiled=True),
        lax.psum_scatter(grad_w_back, ("seq", "tok"), scatter_dimension=0, tiled=True),
        lax.psum_scatter(grad_b_in, ("seq", "tok"), scatter_dimension=0, tiled=True),
        lax.psum_scatter(grad_gains, ("seq", "tok"), scatter_dimension=1, tiled=True),
        lax.psum_scatter(grad_shifts, ("seq", "tok"), scatter_dimension=1, tiled=True),
    )
    return (
        result.reshape(seq_count, slot_count, model_width),
        grad_input.reshape(seq_count, slot_count, model_width),
        owned_query,
        owned_key,
        owned_value,
        owned_out,
        grad_w_conv,
        owned_in,
        owned_back,
        owned_bias,
        owned_gains,
        owned_shifts,
    )


F32 = jnp.float32


BF = jnp.bfloat16


def dot(a, b, ca=1, cb=0):
    return lax.dot_general(a, b, (((ca,), (cb,)), ((), ())), preferred_element_type=F32)


def lane_low(shape):
    return lax.broadcasted_iota(jnp.int32, shape, len(shape) - 1) % 128 < 64


def halves_diag(m):
    low = lane_low((64, 128))
    return jnp.where(low, m[:64], m[64:])


def spread_diag(v):
    low = lane_low(v.shape)
    zero = jnp.zeros_like(v)
    return jnp.concatenate([jnp.where(low, v, zero), jnp.where(low, zero, v)], axis=0)


def seg(op, v, fill):
    low = lane_low(v.shape)
    a = op(jnp.where(low, v, fill), axis=-1, keepdims=True)
    b = op(jnp.where(low, fill, v), axis=-1, keepdims=True)
    return jnp.where(low, a, b)


def split(v):
    hi = v.astype(BF)
    return hi, (v - hi.astype(F32)).astype(BF)


def norm_stats(h):
    center = h - jnp.mean(h, axis=-1, keepdims=True)
    spread = jnp.mean(center * center, axis=-1, keepdims=True)
    rstd = lax.rsqrt(spread + 1e-05)
    return center * rstd, rstd


def norm_back(dy, gain, xhat, rstd):
    d = dy * gain
    a = jnp.mean(d, axis=-1, keepdims=True)
    b = jnp.mean(d * xhat, axis=-1, keepdims=True)
    return rstd * (d - a - xhat * b)


def skew(row, width, count):
    return pltpu.roll(jnp.broadcast_to(row, (count, width)), 0, 1, stride=1, stride_axis=0)


def colsum(v):
    return jnp.sum(v, axis=0, keepdims=True)


MESH = pl.DeviceIdType.MESH


FIRST = 0


def place():
    s = lax.axis_index("seq"); t = lax.axis_index("tok")
    x, y, z, c = s % 2, s // 2, t // 2, t % 2
    px = s + 1 - 2 * x
    py = (s + 2) % 4
    p1 = px * (1 - c) + py * c
    p2 = py * (1 - c) + px * c
    return s, z, c, p1, p2


def remote(src, dst, send, recv, seq, tok):
    return pltpu.make_async_remote_copy(src_ref=src, dst_ref=dst, send_sem=send, recv_sem=recv,
                                        device_id={"seq": seq, "tok": tok}, device_id_type=MESH)


def entry(s, z, c, p1, p2):
    bar = pltpu.get_barrier_semaphore()
    def sig(seq, tok):
        pl.semaphore_signal(bar, inc=1, device_id={"seq": seq, "tok": tok}, device_id_type=MESH)
    t = 2 * z + c
    sig(p1, t); sig(p2, t); sig(s, 2 * z + 1 - c)
    for d in (1, 2, 3):
        sig(s, 2 * ((z + d) % 4) + c)
    @pl.when(((c == 1) & (z < 3)) | ((c == 0) & (z > 0)))
    def _(): sig(s, t + 2 * c - 1)
    edge = c * (6 - z) // 4 + (1 - c) * ((z + 3) // 4)
    pl.semaphore_wait(bar, 6 + edge)


def each_slot(c, f):
    f(0)
    @pl.when(c == 0)
    def _(): f(1)


class UnitSum:
    def __init__(self, src, ra, rb, sems, where, combine):
        self.__dict__.update(locals())
        self.sa, self.qa, self.sb, self.qb = sems
    def cp_a(self, c):
        s, z, cc, _, _ = self.where
        if c == 0:
            return remote(self.src.at[:, pl.ds(2, 1)], self.ra.at[:, pl.ds(0, 1)], self.sa, self.qa, s, 2 * z + 1)
        return remote(self.src.at[:, pl.ds(0, 2)], self.ra, self.sa, self.qa, s, 2 * z)
    def cp_b(self, d, i):
        s, z, c, _, _ = self.where
        zz = (z + d) % 4
        return remote(self.src.at[zz, 2 * c + i], self.rb.at[z, i], self.sb.at[d, i], self.qb.at[z, i], s, 2 * zz + c)
    def start(self):
        for k in (0, 1):
            @pl.when(self.where[2] == k)
            def _(): self.cp_a(k).start(FIRST)
    def mid(self):
        s, z, c, _, _ = self.where
        for k in (0, 1):
            @pl.when(c == k)
            def _(): self.cp_a(1 - k).wait_recv()
        def comb(zz):
            each_slot(c, lambda i: self.combine(self.src.at[zz, 2 * c + i], self.ra.at[zz, i]))
        for d in (2, 1, 3):
            comb((z + d) % 4)
            each_slot(c, lambda i: self.cp_b(d, i).start(FIRST))
        comb(z)
    def end(self):
        s, z, c, _, _ = self.where
        for d in (1, 3, 2):
            zz = (z + d) % 4
            def f(i):
                remote(self.src.at[zz, 2 * c + i], self.rb.at[zz, i], self.sb.at[d, i], self.qb.at[zz, i], s, 2 * zz + c).wait_recv()
                self.combine(self.src.at[z, 2 * c + i], self.rb.at[zz, i])
            each_slot(c, f)
    def drain(self):
        c = self.where[2]
        for k in (0, 1):
            @pl.when(c == k)
            def _(): self.cp_a(k).wait_send()
        for d in (1, 2, 3):
            each_slot(c, lambda i: self.cp_b(d, i).wait_send())


class UnitShare:
    def __init__(self, buf, sems, where):
        self.__dict__.update(locals())
        self.sz, self.qz, self.sc, self.qc = sems
    def cp_z(self, d, i):
        s, z, c, _, _ = self.where
        b = self.buf.at[z, 2 * c + i]
        return remote(b, b, self.sz.at[d, i], self.qz.at[z, i], s, 2 * ((z + d) % 4) + c)
    def cp_c(self, zz, i):
        s, z, c, _, _ = self.where
        b = self.buf.at[zz, 2 * c + i]
        return remote(b, b, self.sc.at[zz, i], self.qc.at[zz, i], s, 2 * z + 1 - c)
    def start(self):
        z, c = self.where[1], self.where[2]
        def f(i):
            for d in (2, 1, 3): self.cp_z(d, i).start(FIRST)
            self.cp_c(z, i).start(FIRST)
        each_slot(c, f)
    def mid(self):
        s, z, c, _, _ = self.where
        for d in (1, 3, 2):
            zz = (z + d) % 4
            def f(i):
                b = self.buf.at[zz, 2 * c + i]
                remote(b, b, self.sz.at[d, i], self.qz.at[zz, i], s, 2 * zz + c).wait_recv()
                self.cp_c(zz, i).start(FIRST)
            each_slot(c, f)
    def end(self):
        s, z, c, _, _ = self.where
        def f(i):
            for zz in range(4):
                b = self.buf.at[zz, 2 * (1 - c) + i]
                remote(b, b, self.sc.at[zz, i], self.qc.at[zz, i], s, 2 * z + 1 - c).wait_recv()
        each_slot(1 - c, f)
    def drain(self):
        z, c = self.where[1], self.where[2]
        def f(i):
            for d in (1, 2, 3): self.cp_z(d, i).wait_send()
            for zz in range(4): self.cp_c(zz, i).wait_send()
        each_slot(c, f)


class Halo:
    def __init__(self, buf, slots, send, recv, where):
        self.__dict__.update(locals())
        s, z, c, _, _ = where
        self.t = 2 * z + c
    def cps(self):
        s, n = self.where[0], self.slots
        up = remote(self.buf.at[:, pl.ds(n, 16)], self.buf.at[:, pl.ds(0, 16)], self.send.at[0], self.recv.at[0], s, self.t + 1)
        down = remote(self.buf.at[:, pl.ds(16, 16)], self.buf.at[:, pl.ds(16 + n, 16)], self.send.at[1], self.recv.at[1], s, self.t - 1)
        return up, down
    def zero(self):
        n = self.slots
        a, _, d = self.buf.shape
        self.buf[:, 16 + n:, :] = jnp.zeros((a, 256 - 16 - n, d), BF)
        self.buf[:, 0:16, :] = jnp.zeros((a, 16, d), BF)
    def start(self):
        up, down = self.cps()
        @pl.when(self.t < 7)
        def _(): up.start(FIRST)
        @pl.when(self.t > 0)
        def _(): down.start(FIRST)
    def end(self):
        up, down = self.cps()
        @pl.when(self.t > 0)
        def _(): up.wait_recv()
        @pl.when(self.t < 7)
        def _(): down.wait_recv()
    def drain(self):
        up, down = self.cps()
        @pl.when(self.t < 7)
        def _(): up.wait_send()
        @pl.when(self.t > 0)
        def _(): down.wait_send()


def mm(a, b, flip=False):
    ah, al = split(a)
    bh, bl = split(spread_diag(b))
    if flip:
        return dot(ah, bh, 1, 1) + (dot(ah, bl, 1, 1) + dot(al, bh, 1, 1))
    return dot(jnp.concatenate([ah, ah, al], axis=1), jnp.concatenate([bh, bl, bh], axis=0))


def flip64(a):
    t = jnp.transpose(a)
    return jnp.concatenate([t[:64], t[64:]], axis=1)


def eye_pair():
    i = lax.broadcasted_iota(jnp.int32, (64, 128), 0)
    j = lax.broadcasted_iota(jnp.int32, (64, 128), 1)
    return jnp.where(i == j % 64, 1.0, 0.0).astype(F32)


def soft_combine(dst, other):
    m1, m2 = dst[64:65, :], other[64:65, :]
    m = jnp.maximum(m1, m2)
    a, b = jnp.exp(m1 - m), jnp.exp(m2 - m)
    dst[0:64, :] = dst[0:64, :] * a + other[0:64, :] * b
    dst[65:66, :] = dst[65:66, :] * a + other[65:66, :] * b
    dst[64:65, :] = m


def core_setup(qm, km):
    p2 = dot(qm, spread_diag(km), 1, 1) * (64 ** -0.5)
    e = jnp.exp(p2 - seg(jnp.max, p2, -jnp.inf))
    p2 = e / seg(jnp.sum, e, 0.0)
    factor = 1.0 / seg(jnp.max, colsum(p2), -jnp.inf)
    return p2, flip64(p2) * factor


def plain_add(dst, other):
    dst[...] = (dst[...].astype(F32) + other[...].astype(F32)).astype(dst.dtype)

class Gather:
    STAGES = 9
    def __init__(self, views, owns, sems, where):
        self.__dict__.update(locals())
        self.qa, self.qb, self.sz, self.s1, self.s2, self.sc, self.sl = sems
        s, z, c, p1, p2 = where
        t = 2 * z + c
        self.line = ((s, t + 2), (s, t - 2))
        self.d1, self.d2, self.dc = (p1, t), (p2, t), (s, 2 * z + 1 - c)
    def at(self, k, s_, z_, c_):
        return self.views[k](s_, z_, c_)
    def cp(self, k, s_, zz, send, dev, src=None):
        dst = self.at(k, s_, zz, self.where[2])
        return remote(dst if src is None else src, dst, send, self.qa.at[k, s_, zz], *dev)
    def to_z(self, k, zz, way, src=None): return self.cp(k, self.where[0], zz, self.sz.at[k, way, zz], self.line[way], src)
    def to_1(self, k, zz, src=None): return self.cp(k, self.where[0], zz, self.s1.at[k, zz], self.d1, src)
    def to_2(self, k, g, zz, src=None): return self.cp(k, self.where[3 if g else 0], zz, self.s2.at[k, g, zz], self.d2, src)
    def got(self, k, s_, zz): self.cp(k, s_, zz, self.s1.at[k, 0], self.dc).wait_recv()
    def local(self, k):
        s, z, c, _, _ = self.where
        return pltpu.make_async_copy(self.owns(k), self.at(k, s, z, c), self.sl.at[k])
    def col(self, k, s_):
        b = self.at(k, s_, slice(None), self.where[2])
        return remote(b, b, self.sc.at[k, s_], self.qb.at[k, s_], *self.dc)
    def pair(self, d, f):
        z = self.where[1]
        if d == 0:
            f(z, 2); return
        @pl.when(z >= d)
        def _(): f(z - d, 0)
        @pl.when(z + d <= 3)
        def _(): f(z + d, 1)
    def run(self, k, i):
        s, z, c, p1, p2 = self.where
        if i < 4:
            def f(zz, side):
                src = None
                if side == 2:
                    src = self.owns(k)
                    self.local(k).start()
                else:
                    self.got(k, s, zz)
                if side != 1 and i < 3:
                    @pl.when(z < 3)
                    def _(): self.to_z(k, zz, 0, src).start()
                if side != 0 and i < 3:
                    @pl.when(z > 0)
                    def _(): self.to_z(k, zz, 1, src).start()
                self.to_2(k, 0, zz, src).start(); self.to_1(k, zz, src).start()
            self.pair(i, f)
            if i == 3:
                self.local(k).wait()
                self.col(k, s).start()
        elif i < 8:
            def f(zz, side):
                self.got(k, p1, zz)
                self.to_2(k, 1, zz).start()
            self.pair(i - 4, f)
            if i == 7: self.col(k, p1).start()
        else:
            for s_ in (p2, 3 - s):
                for zz in range(4): self.got(k, s_, zz)
                self.col(k, s_).start()
    def arrive(self, k):
        for s_ in range(4):
            b = self.at(k, s_, slice(None), 1 - self.where[2])
            remote(b, b, self.sc.at[k, s_], self.qb.at[k, s_], *self.dc).wait_recv()
    def drain(self):
        s, z, c, p1, p2 = self.where
        for k in range(len(self.views)):
            def ws(i, _):
                self.col(k, i).wait_send()
                self.to_1(k, i).wait_send()
                for g in range(2): self.to_2(k, g, i).wait_send()
                @pl.when((z < 3) & (i <= z))
                def _(): self.to_z(k, i, 0).wait_send()
                @pl.when((z > 0) & (i >= z))
                def _(): self.to_z(k, i, 1).wait_send()
                return 0
            lax.fori_loop(0, 4, ws, 0)

class Scatter:
    STAGES = 5
    def __init__(self, part, outs, bufs, sems, where):
        self.__dict__.update(locals())
        self.rcb, self.r2, self.r1, self.rz = bufs
        self.s_c, self.q_c, self.s_2, self.q_2, self.s_1, self.q_1, self.s_z, self.q_z = sems
        s, z, c, p1, p2 = where
        t = 2 * z + c
        self.d1, self.d2, self.dc = (p1, t), (p2, t), (s, 2 * z + 1 - c)
    def own(self, k, *at): return self.part(k, self.where[2], *at)
    def cp_c(self, k): return remote(self.part(k, 1 - self.where[2]), self.rcb.at[k], self.s_c.at[k], self.q_c.at[k], *self.dc)
    def cp_2(self, k, g):
        b = self.where[4] if g == 0 else 3 - self.where[0]
        return remote(self.own(k, b), self.r2.at[k, g], self.s_2.at[k, g], self.q_2.at[k, g], *self.d2)
    def cp_1(self, k): return remote(self.own(k, self.where[3]), self.r1.at[k], self.s_1.at[k], self.q_1.at[k], *self.d1)
    def cp_z(self, k, d):
        s, z, c, p1, p2 = self.where
        zz = (z + d) % 4
        return remote(self.own(k, s, zz), self.rz.at[k, z], self.s_z.at[k, d], self.q_z.at[k, z], s, 2 * zz + c)
    def add4(self, k, i, v):
        a = self.own(k, i)
        a[...] = a[...] + v
    def run(self, k, i):
        s, z, c, p1, p2 = self.where
        if i == 0:
            self.cp_c(k).start()
        elif i == 1:
            self.cp_c(k).wait_recv()
            for g, b in ((1, 3 - s), (0, p2)):
                self.add4(k, b, self.rcb[k, b])
                self.cp_2(k, g).start()
            for b in (p1, s): self.add4(k, b, self.rcb[k, b])
        elif i == 2:
            self.cp_2(k, 1).wait_recv()
            self.add4(k, p1, self.r2[k, 1])
            self.cp_1(k).start()
            self.cp_2(k, 0).wait_recv()
            self.add4(k, s, self.r2[k, 0])
        elif i == 3:
            self.cp_1(k).wait_recv()
            self.add4(k, s, self.r1[k])
            for d in (2, 1, 3): self.cp_z(k, d).start()
        else:
            tot = self.own(k, s, z)[...].astype(F32)
            for d in (1, 3, 2):
                zz = (z + d) % 4
                b = self.rz.at[k, zz]
                remote(b, b, self.s_z.at[k, d], self.q_z.at[k, zz], s, 2 * zz + c).wait_recv()
                tot = tot + b[...].astype(F32)
            self.outs(k)[...] = tot
    def drain(self, n):
        for k in range(n):
            self.cp_c(k).wait_send()
            for g in range(2): self.cp_2(k, g).wait_send()
            self.cp_1(k).wait_send()
            for d in (1, 2, 3): self.cp_z(k, d).wait_send()

CHUNKS = (("w", 1, 1), ("w", 0, 1), ("w", 2, 1), ("w", 3, 1), ("i", 0, 2), ("i", 1, 2), ("b", 0, 2), ("b", 1, 2))
ORDER = (
    0, 9, 18, 27, 173, 36, 1, 4, 10, 19, 28, 31, 2, 11, 20, 29, 3, 5, 32, 12, 21, 30, 6, 22, 13, 33, 7, 23,
    14, 24, 15, 25, 34, 16, 174, 45, 8, 54, 37, 40, 81, 26, 35, 17, 175, 63, 46, 178, 72, 55, 84, 83, 82, 38, 176, 41,
    58, 49, 67, 64, 177, 179, 73, 76, 56, 47, 180, 65, 39, 183, 150, 74, 42, 59, 57, 50, 184, 48, 151, 77, 66, 68, 152, 75,
    60, 153, 51, 154, 69, 43, 155, 78, 185, 186, 182, 61, 181, 52, 187, 70, 188, 189, 79, 44, 62, 53, 80, 71, 85, 190, 87, 165,
    86, 164, 163, 162, 89, 88, 191, 192, 193, 105, 100, 95, 90, 169, 106, 101, 168, 96, 91, 107, 125, 167, 126, 102, 120, 166, 121, 97,
    115, 194, 116, 92, 110, 108, 195, 111, 127, 103, 109, 197, 122, 104, 98, 198, 196, 130, 199, 131, 117, 93, 99, 200, 201, 112, 156, 128,
    94, 123, 202, 157, 129, 132, 204, 205, 118, 113, 124, 133, 158, 159, 119, 114, 207, 160, 134, 161, 203, 209, 210, 206, 211, 135, 212, 208,
    136, 213, 214, 216, 145, 215, 140, 137, 217, 146, 218, 141, 138, 170, 147, 139, 142, 171, 148, 143, 172, 149, 144, 219,
)

def body(order, lens, x_ref, cot_ref, wc_ref, wq_ref, wk_ref, wv_ref, wo_ref, win_ref, wback_ref, bin_ref, gains_ref, shifts_ref,
         res_o, gx_o, oq_o, ok_o, ov_o, oo_o, oi_o, ob_o, sums_o,
         own4, owni, ownb, ownv, vec, w4, wi, wb, lhs, xs, xa, xb, xm, nu, ra, rb, q_u, k_u, vpad, qm_u, km_u, p1_s, e3_s, ml_s, wz, sv, p2s, z6, nts, mden, cv, bias, wcp, wrp,
         ar, yt, gr, gp, gbs, rs1, acc, xh1, gb5, gi5, g4, dpad, e4, ra4, rb4, e6, ra6, rb6, sh5, core_g, sh7, dq1, memb, rcb, r2, r1b, rz, vr, va, vx, vy, vz, sums,
         qa, qb, sz, s1, s2, sc, sl, e0s, e0q, ua, ub, ug, uh, hs, s_c, q_c, s_2, q_2, s_1, q_1, s_z, q_z, va4, vb4, v6a, v6b, ug5, uh5, u7, u7h, hs2, vs, vq, osem, rsem):
    where = place()
    s, z, c, p1, p2 = where
    t = 2 * z + c
    nseq = vpad.shape[0]
    rows, width = x_ref.shape
    slots = rows // nseq
    pairs = width // 128
    n = nseq * pairs
    heads = 2 * pairs
    taps = wc_ref.shape[1]
    ff = wi.shape[1]
    nff = ff // width
    sub = wq_ref.shape[0]
    scale = 64 ** -0.5
    i32 = jnp.int32
    iota = lambda shape, d: lax.broadcasted_iota(i32, shape, d)
    four = [pltpu.make_async_copy(r, gp.at[pl.ds(sub, sub), pl.ds(i * width, width)], osem.at[i]) for i, r in enumerate((wq_ref, wk_ref, wv_ref, wo_ref))]
    four.append(pltpu.make_async_copy(win_ref, gp.at[pl.ds(0, sub)], osem.at[4]))
    four.append(pltpu.make_async_copy(wback_ref, gp.at[pl.ds(2 * sub, 4 * sub), pl.ds(0, width)], osem.at[5]))
    for cp in four: cp.start()
    for cp in four: cp.wait()
    for i in range(4): own4[i] = gp[pl.ds(sub, sub), pl.ds(i * width, width)].astype(BF)
    owni[...] = gp[pl.ds(0, sub), :].astype(BF)
    ownb[...] = gp[pl.ds(2 * sub, 4 * sub), pl.ds(0, width)].astype(BF)
    ownv[...] = jnp.zeros_like(ownv)
    ownv[0:2, 0:sub] = gains_ref[...]
    ownv[2:8, 0:sub] = shifts_ref[...]
    ownv[8:9, 0:4 * sub] = bin_ref[...]
    def edges(b, first, count):
        j = iota((count, 1), 0) + first
        return lax.shift_right_logical(j * lens[b], 6), lax.shift_right_logical((j + 1) * lens[b], 6)
    def counts(b, first, count):
        lo, hi = edges(b, first, count)
        return (hi - lo).astype(F32)
    def valid_of(b): return iota((slots, 1), 0) + t * slots < lens[b]
    def valid_all(): return jnp.concatenate([valid_of(b).astype(F32) for b in range(nseq)], axis=0)
    for b in range(nseq):
        lo, hi = edges(b, 0, 64)
        pos = iota((64, slots), 1) + t * slots
        memb[pl.ds(64 * b, 64), :] = jnp.where((pos >= lo) & (pos < hi), 1.0, 0.0).astype(BF)
    wcp[...] = jnp.zeros_like(wcp); wrp[...] = jnp.zeros_like(wrp)
    wcp[:, 0:taps] = wc_ref[...]
    w0 = wcp[:, 0:128]
    a1 = w0.astype(BF); rest = w0 - a1.astype(F32); a2 = rest.astype(BF); a3 = (rest - a2.astype(F32)).astype(BF)
    turn = jnp.where(iota((128, 128), 0) + iota((128, 128), 1) == taps - 1, 1.0, 0.0).astype(BF)
    wrp[:, 0:128] = (dot(a1, turn) + dot(a2, turn)) + dot(a3, turn)
    entry(*where)
    chip = 2 * sub
    wv, iv, bv = w4.reshape(4, 4, 4, chip, width), wi.reshape(4, 4, chip, ff), wb.reshape(4, 4, 4 * chip, width)
    giv, gbv, gwv = gi5.reshape(4, 4, chip, ff), gb5.reshape(4, 4, 4 * chip, width), g4.reshape(4, 4, 4, chip, width)
    def span(c_, step, lo, cnt): return pl.ds(pl.multiple_of(c_ * step + lo, 8), cnt)
    views, srcs = [lambda s_, z_, c_: vec.at[s_, z_, c_]], [ownv]
    for kind, lo, cnt in CHUNKS:
        if kind == "w":
            views.append(lambda s_, z_, c_, lo=lo, cnt=cnt: wv.at[pl.ds(lo, cnt), s_, z_, span(c_, sub, 0, sub)])
            srcs.append(own4.at[pl.ds(lo, cnt)])
        elif kind == "i":
            m = ff // cnt
            views.append(lambda s_, z_, c_, lo=lo, m=m: iv.at[s_, z_, span(c_, sub, 0, sub), pl.ds(lo * m, m)])
            srcs.append(owni.at[:, pl.ds(lo * m, m)])
        else:
            m = 4 * sub // cnt
            views.append(lambda s_, z_, c_, lo=lo, m=m: bv.at[s_, z_, span(c_, 4 * sub, lo * m, m)])
            srcs.append(ownb.at[pl.ds(lo * m, m)])
    g = Gather(views, lambda k: srcs[k], (qa, qb, sz, s1, s2, sc, sl), where)
    e2 = UnitSum(nu, ra, rb, (ua.at[0], ua.at[1], ub.at[0], ub.at[1]), where, soft_combine)
    e3 = UnitShare(wz, (ug.at[0], ug.at[1], uh.at[0], uh.at[1]), where)
    halo = Halo(vpad, slots, hs.at[0], hs.at[1], where)
    dhalo = Halo(dpad, slots, hs2.at[0], hs2.at[1], where)
    sum4 = UnitSum(e4, ra4, rb4, (va4.at[0], va4.at[1], vb4.at[0], vb4.at[1]), where, plain_add)
    share5 = UnitShare(sh5, (ug5.at[0], ug5.at[1], uh5.at[0], uh5.at[1]), where)
    sum6 = UnitSum(e6, ra6, rb6, (v6a.at[0], v6a.at[1], v6b.at[0], v6b.at[1]), where, plain_add)
    share7 = UnitShare(sh7, (u7.at[0], u7.at[1], u7h.at[0], u7h.at[1]), where)
    def part(k, c_, *at):
        at = (*at, *((slice(None),) * (2 - len(at))))
        if k < 4: return gbv.at[(*at, span(c_, 4 * sub, k * sub, sub))]
        if k < 4 + nff: return giv.at[(*at, span(c_, sub, 0, sub), pl.ds((k - 4) * width, width))]
        return gwv.at[(k - 4 - nff, *at, span(c_, sub, 0, sub))]
    def outs(k):
        if k < 4: return gp.at[pl.ds(k * sub, sub), pl.ds(0, width)]
        if k < 4 + nff: return gp.at[pl.ds(4 * sub, sub), pl.ds((k - 4) * width, width)]
        return gp.at[pl.ds(5 * sub, sub), pl.ds((k - 4 - nff) * width, width)]
    rs = Scatter(part, outs, (rcb, r2, r1b, rz), (s_c, q_c, s_2, q_2, s_1, q_1, s_z, q_z), where)
    def xm_part():
        for b in range(nseq):
            xs[b] = dot(memb[pl.ds(64 * b, 64), :], x_ref[pl.ds(slots * b, slots), :])
        cp_xa().start(FIRST)
    def cp_xa(): return remote(xs.at[1 - c], xa, e0s.at[0], e0q.at[0], s, 2 * z + 1 - c)
    def cp_xb(d):
        zz = (z + d) % 4
        return remote(xs.at[c, pl.ds(pl.multiple_of(16 * zz, 16), 16)], xb.at[z], e0s.at[d], e0q.at[1 + z], s, 2 * zz + c)
    def cp_xm(d):
        return remote(xm.at[c, z], xm.at[c, z], e0s.at[3 + d], e0q.at[5 + z], s, 2 * ((z + d) % 4) + c)
    def cp_xc(zz):
        return remote(xm.at[c, zz], xm.at[c, zz], e0s.at[7 + zz], e0q.at[9 + zz], s, 2 * z + 1 - c)
    def xm_b():
        cp_xa().wait_recv()
        xs[c] = xs[c] + xa[...]
        for d in (2, 1, 3): cp_xb(d).start(FIRST)
    def xm_c():
        tot = xs[c, pl.ds(pl.multiple_of(16 * z, 16), 16), :]
        for d in (1, 3, 2):
            zz = (z + d) % 4
            remote(xb.at[zz], xb.at[zz], e0s.at[d], e0q.at[1 + zz], s, 2 * zz + c).wait_recv()
            tot = tot + xb[zz]
        xm[c, z] = tot / counts(c, 16 * z, 16)
        for d in (2, 1, 3): cp_xm(d).start(FIRST)
        cp_xc(z).start(FIRST)
    def xm_d():
        for d in (1, 3, 2):
            zz = (z + d) % 4
            remote(xm.at[c, zz], xm.at[c, zz], e0s.at[3 + d], e0q.at[5 + zz], s, 2 * zz + c).wait_recv()
            cp_xc(zz).start(FIRST)
    def xm_e():
        for zz in range(4):
            b = xm.at[1 - c, zz]
            remote(b, b, e0s.at[7 + zz], e0q.at[9 + zz], s, 2 * z + 1 - c).wait_recv()
        hi, lo = split(xm[...].reshape(64 * nseq, width))
        lhs[pl.ds(0, rows), :] = x_ref[...]
        lhs[pl.ds(rows, 64 * nseq), :] = hi
        lhs[pl.ds(rows + 64 * nseq, 64 * nseq), :] = lo
    def vectors():
        v = vec[...].reshape(32, 16, 128)
        def spread_rows(row, group, dst, at, count):
            for h in range(0, count, 256):
                k = iota((128, 256), 0); l = iota((128, 256), 1) + h
                w = dot(row, jnp.where((l % group == k) & (k < group), 1.0, 0.0).astype(BF)).reshape(32, 8, 256)
                mine = iota((32, 8, 256), 0) == (iota((32, 8, 256), 2) + h) // group
                dst(h, jnp.sum(jnp.where(mine, w, 0.0), axis=0))
        def to_cv(h, w): cv[:, pl.ds(h, 256)] = w
        def to_bias(h, w): bias[:, pl.ds(h, 256)] = w[0:1]
        spread_rows(v[:, 0:8, :].reshape(256, 128).astype(BF), sub, to_cv, 0, width)
        spread_rows(v[:, 8:16, :].reshape(256, 128).astype(BF), 4 * sub, to_bias, 0, ff)
    def projections():
        m_n = 64 * nseq
        valid = valid_all()
        for h in range(0, width, 256):
            cols = pl.ds(h, 256)
            v = ((dot(x_ref[...], w4[2, :, cols]) + cv[3:4, cols]) * valid).astype(BF)
            for b in range(nseq): vpad[b, pl.ds(16, slots), cols] = v[b * slots:(b + 1) * slots]
        halo.start()
        for i, (dst, marks) in ((1, (k_u, km_u)), (0, (q_u, qm_u))):
            for h in range(0, width, 256):
                cols = pl.ds(h, 256)
                r = dot(lhs[...], w4[i, :, cols])
                a = r[:rows]
                m = r[rows:rows + m_n] + r[rows + m_n:]
                if i == 0:
                    a = a + cv[2:3, cols]
                    m = m + cv[2:3, cols]
                a = a.astype(BF); m = m.astype(BF)
                for b in range(nseq):
                    for q in range(2):
                        u = b * pairs + h // 128 + q
                        dst[u] = a[b * slots:(b + 1) * slots, q * 128:(q + 1) * 128]
                        marks[u] = m[b * 64:(b + 1) * 64, q * 128:(q + 1) * 128]
    def cp_cot(): return pltpu.make_async_copy(cot_ref, lhs.at[pl.ds(rows, rows)], osem.at[0])
    def third():
        cp_cot().start()
        def unit(u, _):
            b, p = u // pairs, u % pairs
            ok = valid_of(b)
            sc3 = jnp.where(ok, dot(k_u[u], spread_diag(qm_u[u]), 1, 1) * scale, -1e30)
            m = jnp.max(sc3, axis=0, keepdims=True)
            e = jnp.where(ok, jnp.exp(sc3 - m), 0.0)
            e3_s[u] = e
            ml_s[u] = jnp.broadcast_to(m, (8, 128))
            v = vpad[b, pl.ds(16, slots), pl.ds(pl.multiple_of(p * 128, 128), 128)]
            nu[u // 3, u % 3, 0:64, :] = halves_diag(dot(v, e.astype(BF), 0, 0))
            nu[u // 3, u % 3, 64:72, :] = jnp.broadcast_to(m, (8, 128))
            nu[u // 3, u % 3, 65:66, :] = colsum(e)
            return 0
        lax.fori_loop(0, n, unit, 0)
        e2.start()
    def first(lo, hi):
        def unit(u, _):
            sc1 = dot(q_u[u], spread_diag(km_u[u]), 1, 1) * scale
            e = jnp.exp(sc1 - seg(jnp.max, sc1, -jnp.inf))
            pr = e / seg(jnp.sum, e, 0.0)
            p1_s[u] = pr
            return 0
        lax.fori_loop(lo, hi, unit, 0)
    st = {}
    R2 = range(2)
    def slot(i): return 2 * c + i * (1 - c)
    def core_a():
        st["P"], st["Z"] = [], []
        for i in R2:
            pp, zz = core_setup(qm_u[3 * z + slot(i)], km_u[3 * z + slot(i)])
            p2s[i] = pp
            st["P"].append(pp); st["Z"].append(zz)
    def newton(it):
        eye = eye_pair()
        P, Z = st["P"], st["Z"]
        pr = [mm(P[i], Z[i]) for i in R2]
        t2 = [15.0 * eye - mm(pr[i], 7.0 * eye - pr[i]) for i in R2]
        t3 = [13.0 * eye - mm(pr[i], t2[i]) for i in R2]
        for i in R2:
            sv[i, it, 0] = Z[i]; sv[i, it, 1] = pr[i]; sv[i, it, 2] = t2[i]; sv[i, it, 3] = t3[i]
        st["Z"] = [0.25 * mm(Z[i], t3[i]) for i in R2]
    def core_z():
        for i in R2:
            k = slot(i)
            z6[i] = st["Z"][i]
            nt = nu[z, k, 0:64, :] / nu[z, k, 65:66, :]
            nts[i] = nt
            mden[i] = nu[z, k, 64:72, :]
            wz[z, k] = mm(st["Z"][i], nt, flip=True).astype(BF)
        e3.start()
    def attention():
        halo.end()
        def per(p, _):
            lanes = pl.ds(pl.multiple_of(p * 128, 128), 128)
            th = [split(skew(wcp[pl.ds(2 * p + e, 1), :], 256, slots)) for e in range(2)]
            low = lane_low((slots, 128))
            for b in range(nseq):
                u = b * pairs + p
                v = vpad[b, :, lanes]
                c0 = dot(th[0][0], v) + dot(th[0][1], v)
                c1 = dot(th[1][0], v) + dot(th[1][1], v)
                a = dot(p1_s[u].astype(BF), spread_diag(wz[u // 3, u % 3]))
                ar[pl.ds(b * slots, slots), lanes] = (a + jnp.where(low, c0, c1)).astype(BF)
            return 0
        lax.fori_loop(0, pairs, per, 0)
    def col_tiles(f):
        def tile(j, _):
            f(pl.ds(pl.multiple_of(j * 256, 256), 256)); return 0
        lax.fori_loop(0, width // 256, tile, 0)
    RB = 64
    def row_tiles(f):
        def tile(j, _):
            r0 = pl.multiple_of(j * RB, RB)
            f(pl.ds(r0, RB), r0); return 0
        lax.fori_loop(0, rows // RB, tile, 0)
    def valid_rows(r0):
        per = slots // RB
        b = r0 // slots
        return (iota((RB, 1), 0) + (r0 - b * slots + t * slots) < lens[b]).astype(F32)
    def out_proj():
        def proj(cols):
            acc[:, cols] = x_ref[:, cols].astype(F32) + dot(ar[...], w4[3, :, cols]) + cv[4:5, cols]
        col_tiles(proj)
        def norm(at, r0):
            xhat, rstd = norm_stats(acc[at, :])
            rs1[at, :] = rstd
            xh1[at, :] = xhat
            y = xhat * cv[0:1, :] + cv[5:6, :]
            yt[at, :] = y.astype(BF)
            acc[at, :] = y + cv[6:7, :]
        row_tiles(norm)
    def up(j):
        def tile(h, _):
            cols = pl.ds(pl.multiple_of(j * width + h * 256, 256), 256)
            u = dot(yt[...], wi[:, cols]) + bias[:, cols]
            phi = 0.5 * (1.0 + lax.erf(u * (0.5 ** 0.5)))
            gr[:, cols] = (u * phi).astype(BF)
            gp[:, cols] = phi + u * (jnp.exp(-0.5 * u * u) * 0.3989422804014327)
            return 0
        lax.fori_loop(0, width // 256, tile, 0)
    def down():
        def tile(cols): acc[:, cols] += dot(gr[...], wb[:, cols])
        col_tiles(tile)
    def cp_res(u):
        b, p = u // pairs, u % pairs
        return pltpu.make_async_copy(dq1.at[u], res_o.at[pl.ds(b * slots, slots), pl.ds(p * 128, 128)], rsem.at[u])
    def norm2():
        cp_cot().wait()
        vr[...] = jnp.zeros_like(vr)
        def norm(at, r0):
            xhat, rstd = norm_stats(acc[at, :])
            valid = valid_rows(r0)
            out = (xhat * cv[1:2, :] + cv[7:8, :]) * valid
            b = r0 // slots
            for p in range(pairs): dq1[b * pairs + p, pl.ds(pl.multiple_of(r0 - b * slots, RB), RB), :] = out[:, p * 128:(p + 1) * 128]
            dr = lhs[pl.ds(pl.multiple_of(rows + r0, RB), RB), :].astype(F32) * valid
            vr[1:2, :] += colsum(dr * xhat)
            vr[7:8, :] += colsum(dr)
            dh2 = norm_back(dr, cv[1:2, :], xhat, rstd)
            vr[6:7, :] += colsum(dh2)
            lhs[at, :] = dh2.astype(BF)
            acc[at, :] = dh2
        row_tiles(norm)
        for u in range(n): cp_res(u).start()
    def outer(dst, left, right):
        def tile(i, _):
            rows_ = pl.ds(pl.multiple_of(i * 256, 256), 256)
            lt = jnp.transpose(left[:, rows_])
            for h in range(0, width, 256): dst[rows_, pl.ds(h, 256)] = dot(lt, right[:, h:h + 256]).astype(BF)
            return 0
        lax.fori_loop(0, left.shape[1] // 256, tile, 0)
    def grad_back():
        outer(gb5, gr, lhs.at[pl.ds(0, rows)])
        for i in range(width // 256): lhs[pl.ds(rows, 256), pl.ds(256 * i, 256)] = jnp.transpose(yt[:, pl.ds(256 * i, 256)])
    def bwd(j):
        def tile(h, _):
            cols = pl.ds(pl.multiple_of(j * width + h * 256, 256), 256)
            du = gp[:, cols] * dot(lhs[pl.ds(0, rows), :], wb[cols, :], 1, 1)
            gbs[:, cols] = colsum(du)
            dur = du.astype(BF)
            gr[:, cols] = dur
            for i in range(width // 256): gi5[pl.ds(256 * i, 256), cols] = dot(lhs[pl.ds(rows, 256), pl.ds(256 * i, 256)], dur).astype(BF)
            return 0
        lax.fori_loop(0, width // 256, tile, 0)
    def dy():
        def tile(cols): acc[:, cols] += dot(gr[...], wi[cols, :], 1, 1)
        col_tiles(tile)
    def weight_grad(i, left, right): outer(g4.at[i], left, right)
    def norm1():
        def norm(at, r0):
            dy, xhat = acc[at, :], xh1[at, :]
            vr[0:1, :] += colsum(dy * xhat)
            vr[5:6, :] += colsum(dy)
            d = norm_back(dy, cv[0:1, :], xhat, rs1[at, :])
            vr[4:5, :] += colsum(d)
            acc[at, :] = d
            lhs[pl.ds(pl.multiple_of(rows + r0, RB), RB), :] = d.astype(BF)
        row_tiles(norm)
        def da_tile(cols):
            da = dot(lhs[pl.ds(rows, rows), :], w4[3, cols, :], 1, 1).astype(BF)
            for b in range(nseq): dpad[b, pl.ds(16, slots), cols] = da[b * slots:(b + 1) * slots]
        col_tiles(da_tile)
        dhalo.start()
    def units():
        for u in range(n): cp_res(u).wait()
        def unit(u, _):
            b, p = u // pairs, u % pairs
            lanes = pl.ds(pl.multiple_of(p * 128, 128), 128)
            da = dpad[b, pl.ds(16, slots), lanes]
            pr = p1_s[u]
            e4[u // 3, u % 3, 0:64, :] = halves_diag(dot(pr.astype(BF), da, 0, 0))
            dp1 = dot(da, spread_diag(wz[u // 3, u % 3]), 1, 1)
            ds1 = (pr * (dp1 - seg(jnp.sum, dp1 * pr, 0.0)) * scale).astype(BF)
            e6[u // 3, u % 3, 64:128, :] = halves_diag(dot(ds1, q_u[u], 0, 0)).astype(BF)
            dq1[u] = dot(ds1, spread_diag(km_u[u]))
            return 0
        lax.fori_loop(0, n, unit, 0)
        sum4.start()
    def grad_conv():
        wcp[...] = jnp.zeros_like(wcp)
        def unit(u, _):
            b, p = u // pairs, u % pairs
            lanes = pl.ds(pl.multiple_of(p * 128, 128), 128)
            v = vpad[b, :, lanes]
            turn = jnp.where(iota((slots, slots), 0) + iota((slots, slots), 1) == slots - 1, 1.0, 0.0).astype(BF)
            da = dot(turn, dpad[b, pl.ds(16, slots), lanes]).astype(BF)
            low = lane_low(da.shape)
            zero = jnp.zeros_like(da)
            for e in range(2):
                m = dot(jnp.where(low, da, zero) if e == 0 else jnp.where(low, zero, da), v, 1, 1)
                m = pltpu.roll(m, m.shape[1] - slots + 1, 1, stride=1, stride_axis=0)
                wcp[pl.ds(2 * p + e, 1), :] += colsum(m)
            return 0
        lax.fori_loop(0, n, unit, 0)
        vr[12:24, 0:128] = wcp[:, 0:128]
    def cb_a():
        st["G"], st["DP"] = [], []
        for i in R2:
            k = slot(i)
            dwz = e4[z, k, 0:64, :]
            nt = nts[i]
            den = mden[i, 1:2, :]
            dnt = mm(flip64(dwz), z6[i])
            dden = -colsum(dnt * nt) / den
            tile = jnp.zeros((16, 128), F32)
            row = iota((16, 128), 0)
            for j, v in enumerate((mden[i, 0:1, :], dden)):
                for q in range(3):
                    h = v.astype(BF).astype(F32)
                    tile = jnp.where(row == 3 * j + q, h, tile)
                    v = v - h
            sh5[z, k, 0:64, :] = (dnt / den).astype(BF)
            sh5[z, k, 64:80, :] = tile.astype(BF)
            st["G"].append(mm(flip64(nt), dwz, flip=True))
            st["DP"].append(jnp.zeros((64, 128), F32))
        share5.start()
    def cb(it):
        eye = eye_pair()
        G, DP = st["G"], st["DP"]
        Z = [sv[i, it, 0] for i in R2]; Pr = [sv[i, it, 1] for i in R2]; T2 = [sv[i, it, 2] for i in R2]; T3 = [sv[i, it, 3] for i in R2]
        d3 = [0.25 * mm(G[i], Z[i]) for i in R2]
        d2 = [-mm(d3[i], Pr[i]) for i in R2]
        dz = [0.25 * mm(T3[i], G[i]) for i in R2]
        dp = [-mm(T2[i], d3[i]) for i in R2]
        d1 = [-mm(d2[i], Pr[i]) for i in R2]
        dp = [dp[i] - mm(7.0 * eye - Pr[i], d2[i]) - d1[i] for i in R2]
        st["G"] = [dz[i] + mm(dp[i], p2s[i]) for i in R2]
        st["DP"] = [DP[i] + mm(Z[i], dp[i]) for i in R2]
    def cb_z():
        for i in R2:
            u = 3 * z + slot(i)
            p, g0 = p2s[i], st["G"][i]
            col = colsum(p)
            top = seg(jnp.max, col, -jnp.inf)
            f = 1.0 / top
            df = seg(jnp.sum, colsum(g0 * p), 0.0)
            hit = (col == top).astype(F32)
            dcol = -f * f * df * hit / seg(jnp.sum, hit, 0.0)
            dp = flip64(st["DP"][i]) + f * g0 + dcol
            ds = p * (dp - seg(jnp.sum, dp * p, 0.0)) * scale
            hi, lo = split(ds)
            b = spread_diag(km_u[u])
            core_g[i, 0:64, :] = dot(hi, b) + dot(lo, b)
            hi, lo = split(flip64(ds))
            b = spread_diag(qm_u[u])
            core_g[i, 64:128, :] = dot(hi, b) + dot(lo, b)
    def third_b():
        def unit(u, _):
            b, p = u // pairs, u % pairs
            tile = sh5[u // 3, u % 3, 64:80, :].astype(F32)
            m = tile[0:1] + tile[1:2] + tile[2:3]
            dden = tile[3:4] + tile[4:5] + tile[5:6]
            e = e3_s[u] * jnp.exp(ml_s[u, 0:1, :] - m)
            dn = spread_diag(sh5[u // 3, u % 3, 0:64, :])
            v = vpad[b, pl.ds(16, slots), pl.ds(pl.multiple_of(p * 128, 128), 128)]
            de = dot(v, dn) + dden
            p1_s[u] = dot(e.astype(BF), dn, 1, 1)
            ds = (e * de * scale).astype(BF)
            e6[u // 3, u % 3, 0:64, :] = halves_diag(dot(ds, k_u[u], 0, 0)).astype(BF)
            e3_s[u] = dot(ds, spread_diag(qm_u[u]))
            return 0
        lax.fori_loop(0, n, unit, 0)
        sum6.start()
    def conv():
        dhalo.end()
        def per(p, _):
            lanes = pl.ds(pl.multiple_of(p * 128, 128), 128)
            th = [split(skew(wrp[pl.ds(2 * p + e, 1), :], 256, slots)) for e in range(2)]
            low = lane_low((slots, 128))
            tot = jnp.zeros((1, 128), F32)
            for b in range(nseq):
                u = b * pairs + p
                d = dpad[b, :, lanes]
                c0 = dot(th[0][0], d) + dot(th[0][1], d)
                c1 = dot(th[1][0], d) + dot(th[1][1], d)
                v = (p1_s[u] + jnp.where(low, c0, c1)) * valid_of(b).astype(F32)
                tot = tot + colsum(v)
                yt[pl.ds(b * slots, slots), lanes] = v.astype(BF)
            vr[3:4, lanes] = tot
            return 0
        lax.fori_loop(0, pairs, per, 0)
    def own_marks():
        cn = counts(z // 2, 0, 64)
        for i in R2:
            k = slot(i)
            sh7[z, k, 0:64, :] = ((core_g[i, 0:64, :] + e6[z, k, 0:64, :].astype(F32)) / cn).astype(BF)
            sh7[z, k, 64:128, :] = ((core_g[i, 64:128, :] + e6[z, k, 64:128, :].astype(F32)) / cn).astype(BF)
        share7.start()
    def queries():
        def unit(u, _):
            b, p = u // pairs, u % pairs
            lanes = pl.ds(pl.multiple_of(p * 128, 128), 128)
            r0 = pl.multiple_of(b * slots, slots)
            mb = memb[pl.ds(pl.multiple_of(64 * b, 64), 64), :]
            q = dot(mb, sh7[u // 3, u % 3, 0:64, :], 0, 0) + dq1[u]
            k = dot(mb, sh7[u // 3, u % 3, 64:128, :], 0, 0) + e3_s[u]
            lhs[pl.ds(r0, slots), lanes] = q.astype(BF)
            lhs[pl.ds(rows + r0, slots), lanes] = k.astype(BF)
            vr[2:3, lanes] += colsum(q)
            return 0
        lax.fori_loop(0, n, unit, 0)
    def gx1():
        def tile(cols): acc[:, cols] += dot(yt[...], w4[2, cols, :], 1, 1)
        col_tiles(tile)
    def cp_gx(): return pltpu.make_async_copy(acc, gx_o, osem.at[1])
    def gx2():
        def tile(cols):
            acc[:, cols] += dot(lhs[pl.ds(0, rows), :], w4[0, cols, :], 1, 1) + dot(lhs[pl.ds(rows, rows), :], w4[1, cols, :], 1, 1)
        col_tiles(tile)
        cp_gx().start()
    px = s + 1 - 2 * (s % 2)
    py = (s + 2) % 4
    def cp_v(i):
        dst, dev = ((va, (s, 2 * z + 1 - c)), (vx, (px, t)), (vy, (py, t)))[i]
        return remote(vr, dst, vs.at[i], vq.at[i], *dev)
    def cp_vz(d): return remote(vr, vz.at[z], vs.at[2 + d], vq.at[3 + z], s, 2 * ((z + d) % 4) + c)
    def vec_0():
        for i in range(nff): vr[8 + i:9 + i, :] = gbs[:, pl.ds(i * width, width)]
        cp_v(0).start(FIRST)
    def vec_step(i):
        cp_v(i).wait()
        vr[...] = vr[...] + (va, vx, vy)[i][...]
        if i < 2: cp_v(i + 1).start(FIRST)
        else:
            for d in (1, 2, 3): cp_vz(d).start(FIRST)
    def vec_z():
        for d in (1, 2, 3):
            zz = (z + d) % 4
            remote(vr, vz.at[zz], vs.at[2 + d], vq.at[3 + zz], s, 2 * zz + c).wait_recv()
        for d in (1, 2, 3): cp_vz(d).wait_send()
        vz[z] = vr[...]
        sums[...] = ((vz[0] + vz[1]) + vz[2]) + vz[3]
    halo.zero(); dhalo.zero()
    half = n // 2
    P_ = functools.partial
    steps = [P_(g.run, k, i) for k in range(len(views)) for i in range(Gather.STAGES)] + [P_(g.arrive, k) for k in range(len(views))]
    nk = 8 + nff
    steps += [P_(rs.run, k, i) for k in range(nk) for i in range(Scatter.STAGES)]
    steps += [P_(newton, i) for i in range(ITERS)] + [P_(cb, ITERS - 1 - i) for i in range(ITERS)] + [P_(up, j) for j in range(nff)] + [P_(bwd, j) for j in range(nff)]
    steps += [P_(vec_step, i) for i in range(3)]
    steps += [xm_part, xm_b, xm_c, xm_d, xm_e, vectors, projections, third, P_(first, 0, half), P_(first, half, n), core_a, e2.mid, e2.end, core_z, e3.mid, e3.end, attention, out_proj,
              down, norm2, grad_back, dy, norm1, P_(weight_grad, 0, ar, lhs.at[pl.ds(rows, rows)]), units, sum4.mid, grad_conv, sum4.end, cb_a, share5.mid, cb_z, share5.end, third_b,
              conv, sum6.mid, gx1, sum6.end, own_marks, P_(weight_grad, 1, x_ref, yt), share7.mid, share7.end, queries, P_(weight_grad, 2, x_ref, lhs.at[pl.ds(rows, rows)]),
              P_(weight_grad, 3, x_ref, lhs.at[pl.ds(0, rows)]), vec_0, gx2, vec_z]
    for i in order: steps[i]()
    o = [pltpu.make_async_copy(gp.at[pl.ds(a, m), pl.ds(b, w)], dst, osem.at[2 + i]) for i, (a, m, b, w, dst) in enumerate((
        (0, 4 * sub, 0, width, ob_o), (4 * sub, sub, 0, ff, oi_o), (5 * sub, sub, 0, width, oo_o), (5 * sub, sub, width, width, ov_o),
        (5 * sub, sub, 2 * width, width, ok_o), (5 * sub, sub, 3 * width, width, oq_o)))]
    o.append(pltpu.make_async_copy(sums, sums_o, osem.at[8]))
    for cp in o: cp.start()
    g.drain(); e2.drain(); e3.drain(); halo.drain()
    cp_xa().wait_send()
    for d in (1, 2, 3):
        cp_xb(d).wait_send(); cp_xm(d).wait_send()
    for zz in range(4): cp_xc(zz).wait_send()
    rs.drain(nk)
    sum4.drain(); share5.drain(); sum6.drain(); share7.drain(); dhalo.drain()
    cp_gx().wait()
    for cp in o: cp.wait()

def whole(lengths, x, cot, wc, shards, order=ORDER):
    S = jax.ShapeDtypeStruct
    rows, width = x.shape
    wq, wk, wv, wo, win, wback, bin_, gains, shifts = shards
    nseq = lengths.shape[0]
    slots = rows // nseq
    sub, ff = wq.shape[0], win.shape[1]
    n = nseq * width // 128
    nk = 8 + ff // width
    na = 1 + len(CHUNKS)
    V = lambda *sh: pltpu.VMEM(sh, F32)
    B = lambda *sh: pltpu.VMEM(sh, BF)
    D = lambda *sh: pltpu.SemaphoreType.DMA(sh)
    vm = pl.BlockSpec(memory_space=pltpu.VMEM); hb = pl.BlockSpec(memory_space=pl.ANY)
    return pl.pallas_call(
        functools.partial(body, tuple(order)),
        out_shape=(S((rows, width), F32),) * 2 + (S((sub, width), F32),) * 4 + (S((sub, ff), F32), S((4 * sub, width), F32), S((24, width), F32)),
        in_specs=[pl.BlockSpec(memory_space=pltpu.SMEM), vm, hb, vm] + [hb] * 6 + [vm] * 3,
        out_specs=(hb,) * 9,
        scratch_shapes=[B(4, sub, width), B(sub, ff), B(4 * sub, width), V(16, 128), V(4, 4, 2, 16, 128), B(4, width, width), B(width, ff), B(ff, width), B(rows + 128 * nseq, width),
                        V(2, 64, width), V(64, width), V(4, 16, width), V(2, 4, 16, width), V(4, 3, 72, 128), V(4, 2, 72, 128), V(4, 2, 72, 128),
                        B(n, slots, 128), B(n, slots, 128), B(nseq, 256, width), B(n, 64, 128), B(n, 64, 128), V(n, slots, 128), V(n, slots, 128), V(n, 8, 128),
                        B(4, 3, 64, 128), V(2, ITERS, 4, 64, 128), V(2, 64, 128), V(2, 64, 128), V(2, 64, 128), V(2, 8, 128), V(8, width), V(1, ff), V(wc.shape[0], 256), V(wc.shape[0], 256),
                        B(rows, width), B(rows, width), B(rows, ff), V(rows, ff), V(1, ff), V(rows, 1), V(rows, width), V(rows, width),
                        B(ff, width), B(width, ff), B(4, width, width), B(nseq, 256, width), V(4, 3, 64, 128), V(4, 2, 64, 128), V(4, 2, 64, 128), B(4, 3, 128, 128), B(4, 2, 128, 128), B(4, 2, 128, 128), B(4, 3, 80, 128),
                        V(2, 128, 128), B(4, 3, 128, 128), V(n, slots, 128), B(64 * nseq, slots),
                        B(nk, 4, 4, sub, width), B(nk, 2, 4, sub, width), B(nk, 4, sub, width), B(nk, 4, sub, width),
                        V(24, width), V(24, width), V(24, width), V(24, width), V(4, 24, width), V(24, width),
                        D(na, 4, 4), D(na, 4), D(na, 2, 4), D(na, 4), D(na, 2, 4), D(na, 4), D(na), D(11), D(13), D(2), D(2, 4, 2), D(2, 4, 2), D(2, 4, 2), D(2, 2),
                        D(nk), D(nk), D(nk, 2), D(nk, 2), D(nk), D(nk), D(nk, 4), D(nk, 4), D(2), D(2, 4, 2), D(2), D(2, 4, 2), D(2, 4, 2), D(2, 4, 2), D(2, 4, 2), D(2, 4, 2), D(2, 2),
                        D(6), D(7), D(9), D(n)],
        compiler_params=pltpu.CompilerParams(collective_id=0, has_side_effects=True, vmem_limit_bytes=67043328),
        name="layer_whole",
    )(lengths, x, cot, wc, wq, wk, wv, wo, win, wback, bin_, gains, shifts)


def hand_out(taps, *refs):
    big, sums_ref = refs[:8], refs[8]
    outs, (conv_o, bias_o, gains_o, shifts_o) = refs[9:17], refs[17:21]
    bufs, sums, sin, sout = refs[21:29], refs[29], refs[30], refs[31]
    a = [pltpu.make_async_copy(r, b, sin.at[i]) for i, (r, b) in enumerate(zip((*big, sums_ref), (*bufs, sums)))]
    o = [pltpu.make_async_copy(b, r, sout.at[i]) for i, (r, b) in enumerate(zip(outs, bufs))]
    for cp in a: cp.start()
    me = lax.axis_index("seq") * 8 + lax.axis_index("tok")
    sub = gains_o.shape[1]
    width = sums.shape[1]
    a[8].wait()
    v = pltpu.roll(sums[0:8, :], (width - sub * me) % width, 1)
    gains_o[...] = v[0:2, 0:sub]
    shifts_o[...] = v[2:8, 0:sub]
    f4 = bias_o.shape[1]
    per = width // f4
    row = lax.broadcasted_iota(jnp.int32, (4, width), 0)
    b = jnp.sum(jnp.where(row == me // per, sums[8:12, :], 0.0), axis=0, keepdims=True)
    b = pltpu.roll(jnp.broadcast_to(b, (8, width)), (width - f4 * (me % per)) % width, 1)
    bias_o[...] = b[0:1, 0:f4]
    conv_o[...] = sums[12:24, 0:taps]
    for i in range(8):
        a[i].wait()
        o[i].start()
    for cp in o: cp.wait()

def finish(big, sums, taps):
    S = jax.ShapeDtypeStruct
    width = sums.shape[1]
    sub = width // 32
    vm = pl.BlockSpec(memory_space=pltpu.VMEM); hb = pl.BlockSpec(memory_space=pl.ANY)
    return pl.pallas_call(
        functools.partial(hand_out, taps),
        out_shape=tuple(S(b.shape, F32) for b in big) + (S((12, taps), F32), S((1, 4 * sub), F32), S((2, sub), F32), S((6, sub), F32)),
        in_specs=[hb] * 9,
        out_specs=(hb,) * 8 + (vm,) * 4,
        scratch_shapes=[pltpu.VMEM(b.shape, F32) for b in big] + [pltpu.VMEM(sums.shape, F32), pltpu.SemaphoreType.DMA((9,)), pltpu.SemaphoreType.DMA((8,))],
        name="hand_out",
    )(*big, sums)


def fast_shards(inputs, lengths, bounds, w_query, w_key, w_value, w_out, w_conv, w_in, w_back, b_in, gains, shifts, cotangent):
    shape = inputs.shape
    x = inputs.reshape(-1, shape[2])
    owned = (w_query, w_key, w_value, w_out, w_in, w_back, b_in.reshape(1, -1), gains, shifts)
    *big, sums = whole(lengths, x, cotangent.reshape(x.shape), w_conv, owned)
    res, gx, gq, gk, gv, go, gi, gb, conv, bias, gain, shift = finish(big, sums, w_conv.shape[1])
    return (res.reshape(shape), gx.reshape(shape), gq, gk, gv, go, conv, gi, gb, bias.reshape(-1), gain, shift)


def solution(mesh):
    placed = (
        P("seq", "tok", None),
        P("seq"),
        P("seq", None),
        P(("seq", "tok"), None),
        P(("seq", "tok"), None),
        P(("seq", "tok"), None),
        P(("seq", "tok"), None),
        P(),
        P(("seq", "tok"), None),
        P(("seq", "tok"), None),
        P(("seq", "tok")),
        P(None, ("seq", "tok")),
        P(None, ("seq", "tok")),
        P("seq", "tok", None),
    )
    return jax.shard_map(
        fast_shards if (mesh.shape["seq"], mesh.shape["tok"]) == (4, 8) else shards,
        mesh=mesh,
        in_specs=placed,
        out_specs=(
            P("seq", "tok", None),
            P("seq", "tok", None),
            P(("seq", "tok"), None),
            P(("seq", "tok"), None),
            P(("seq", "tok"), None),
            P(("seq", "tok"), None),
            P(),
            P(("seq", "tok"), None),
            P(("seq", "tok"), None),
            P(("seq", "tok")),
            P(None, ("seq", "tok")),
            P(None, ("seq", "tok")),
        ),
        check_vma=False,
    )
```

```python
import functools

import jax
import jax.numpy as jnp
from jax import lax
from jax.experimental import pallas as pl
from jax.experimental.pallas import tpu as pltpu
from jax.sharding import PartitionSpec as P

ITERS = 6


EPSILON = 1e-05
EXACT_PRECISION = lax.Precision.HIGHEST


def padded_2(cells, sides, width):
    for axis, dim in sides:
        count = lax.axis_size(axis)
        ends = count - 1
        head = lax.slice_in_dim(cells, 0, width, axis=dim)
        tail = lax.slice_in_dim(cells, cells.shape[dim] - width, cells.shape[dim], axis=dim)
        cells = jnp.concatenate(
            [
                lax.ppermute(tail, axis, [(i, (i + 1) % count) for i in range(ends)]),
                cells,
                lax.ppermute(head, axis, [((i + 1) % count, i) for i in range(ends)]),
            ],
            axis=dim,
        )
    return cells


def layer_norm(hidden, gain_row, shift_row):
    center = hidden - jnp.mean(hidden, axis=-1, keepdims=True)
    spread = jnp.mean(center * center, axis=-1, keepdims=True)
    return center * lax.rsqrt(spread + EPSILON) * gain_row + shift_row


def newton_inverse(kernel):
    column_sum = jnp.sum(kernel, axis=-2)
    factor = 1.0 / jnp.max(column_sum, axis=-1)
    approx = jnp.swapaxes(kernel, -1, -2) * factor[..., None, None]
    identity = jnp.eye(kernel.shape[-1], dtype=jnp.float32)
    for sweep_index in range(ITERS):
        product = jnp.matmul(kernel, approx, precision=EXACT_PRECISION)
        inner_term = 7.0 * identity - product
        inner_term = 15.0 * identity - jnp.matmul(product, inner_term, precision=EXACT_PRECISION)
        inner_term = 13.0 * identity - jnp.matmul(product, inner_term, precision=EXACT_PRECISION)
        approx = 0.25 * jnp.matmul(approx, inner_term, precision=EXACT_PRECISION)
    return approx


def mixer_core(query_marks, key_marks, numerator, denom):
    score_scale_factor = query_marks.shape[-1] ** (-0.5)
    scores = (
        jnp.einsum("bihd,bjhd->bhij", query_marks, key_marks, precision=EXACT_PRECISION)
        * score_scale_factor
    )
    middle = jax.nn.softmax(scores, axis=-1)
    pseudo = newton_inverse(middle)
    summary = numerator / denom[..., None]
    return jnp.einsum("bhij,bhjd->bhid", pseudo, summary, precision=EXACT_PRECISION)


def gelu_exact(pre_act):
    return jax.nn.gelu(pre_act, approximate=False)


def product_low(pattern, left, right):
    return jnp.einsum(pattern, left, right, preferred_element_type=jnp.float32)


def shards(
    inputs,
    lengths,
    bounds,
    w_query,
    w_key,
    w_value,
    w_out,
    w_conv,
    w_in,
    w_back,
    b_in,
    gains,
    shifts,
    cotangent,
):
    seq_count, slot_count, model_width = inputs.shape
    head_count, tap_count = w_conv.shape
    head_dim = model_width // head_count
    rim_width = tap_count // 2
    mark_count = bounds.shape[1] - 1
    row_count = seq_count * slot_count
    score_scale_factor = head_dim ** (-0.5)
    first_slot = lax.axis_index("tok") * slot_count
    position = first_slot + jnp.arange(slot_count, dtype=jnp.int32)
    valid_mask = (position[None, :] < lengths[:, None]).astype(jnp.float32)
    member = (
        (position[None, None, :] >= bounds[:, :-1, None])
        & (position[None, None, :] < bounds[:, 1:, None])
    ).astype(jnp.float32)
    part_count = (bounds[:, 1:] - bounds[:, :-1]).astype(jnp.float32)
    gathered = (
        lax.all_gather(w_query.astype(jnp.bfloat16), ("seq", "tok"), axis=0, tiled=True),
        lax.all_gather(w_key.astype(jnp.bfloat16), ("seq", "tok"), axis=0, tiled=True),
        lax.all_gather(w_value.astype(jnp.bfloat16), ("seq", "tok"), axis=0, tiled=True),
        lax.all_gather(w_out.astype(jnp.bfloat16), ("seq", "tok"), axis=0, tiled=True),
        lax.all_gather(w_in.astype(jnp.bfloat16), ("seq", "tok"), axis=0, tiled=True),
        lax.all_gather(w_back.astype(jnp.bfloat16), ("seq", "tok"), axis=0, tiled=True),
        lax.all_gather(b_in.astype(jnp.bfloat16), ("seq", "tok"), axis=0, tiled=True),
        lax.all_gather(gains.astype(jnp.bfloat16), ("seq", "tok"), axis=1, tiled=True),
        lax.all_gather(shifts.astype(jnp.bfloat16), ("seq", "tok"), axis=1, tiled=True),
    )
    query_mat, key_mat, value_mat, out_mat, in_mat, back_mat, bias_vec, gain_vec, shift_vec = (
        gathered
    )
    bias_rows = bias_vec.astype(jnp.float32)
    gain_rows = gain_vec.astype(jnp.float32)
    shift_rows = shift_vec.astype(jnp.float32)
    flat_rows = inputs.reshape(row_count, model_width)
    query_rows = jnp.dot(flat_rows, query_mat, preferred_element_type=jnp.float32) + shift_rows[0]
    key_rows = jnp.dot(flat_rows, key_mat, preferred_element_type=jnp.float32)
    value_rows = jnp.dot(flat_rows, value_mat, preferred_element_type=jnp.float32) + shift_rows[1]
    part_query = jnp.einsum(
        "bms,bsd->bmd",
        member,
        query_rows.reshape(seq_count, slot_count, model_width),
        precision=EXACT_PRECISION,
    )
    part_key = jnp.einsum(
        "bms,bsd->bmd",
        member,
        key_rows.reshape(seq_count, slot_count, model_width),
        precision=EXACT_PRECISION,
    )
    sum_query, sum_key = lax.psum((part_query, part_key), "tok")
    mark_query = (
        (sum_query / part_count[..., None])
        .astype(jnp.bfloat16)
        .reshape(seq_count, mark_count, head_count, head_dim)
    )
    mark_key = (
        (sum_key / part_count[..., None])
        .astype(jnp.bfloat16)
        .reshape(seq_count, mark_count, head_count, head_dim)
    )
    query_head_rows = query_rows.astype(jnp.bfloat16).reshape(
        seq_count, slot_count, head_count, head_dim
    )
    key_head_rows = key_rows.astype(jnp.bfloat16).reshape(
        seq_count, slot_count, head_count, head_dim
    )
    v_low = (value_rows.reshape(seq_count, slot_count, model_width) * valid_mask[..., None]).astype(
        jnp.bfloat16
    )
    value_head_rows = v_low.reshape(seq_count, slot_count, head_count, head_dim)
    first_score_matrix = (
        product_low("bshd,bmhd->bshm", query_head_rows, mark_key) * score_scale_factor
    )
    first_score_kernel = jax.nn.softmax(first_score_matrix, axis=-1)
    first_low = first_score_kernel.astype(jnp.bfloat16)
    third_score_matrix = (
        product_low("bmhd,bshd->bhms", mark_query, key_head_rows) * score_scale_factor
    )
    third_score_matrix = jnp.where(valid_mask[:, None, None, :] > 0, third_score_matrix, -1e30)
    score_top = lax.pmax(jnp.max(third_score_matrix, axis=-1), "tok")
    third_exponential = jnp.exp(third_score_matrix - score_top[..., None])
    third_low = third_exponential.astype(jnp.bfloat16)
    numerator, denom = lax.psum(
        (
            product_low("bhms,bshd->bhmd", third_low, value_head_rows),
            jnp.sum(third_exponential, axis=-1),
        ),
        "tok",
    )
    mixed_output, core_back = jax.vjp(
        mixer_core, mark_query.astype(jnp.float32), mark_key.astype(jnp.float32), numerator, denom
    )
    mixed_low = mixed_output.astype(jnp.bfloat16)
    attention_forward = product_low("bshm,bhmd->bshd", first_low, mixed_low)
    padded = padded_2(v_low, (("tok", 1),), rim_width)
    padded_heads = padded.astype(jnp.float32).reshape(
        seq_count, slot_count + 2 * rim_width, head_count, head_dim
    )
    conv_out = jnp.zeros_like(attention_forward)
    for offset in range(tap_count):
        conv_out = (
            conv_out
            + w_conv[:, offset][None, None, :, None] * padded_heads[:, offset : offset + slot_count]
        )
    mix_low = (attention_forward + conv_out).reshape(row_count, model_width).astype(jnp.bfloat16)
    first_sum = (
        flat_rows.astype(jnp.float32)
        + jnp.dot(mix_low, out_mat, preferred_element_type=jnp.float32)
        + shift_rows[2]
    )
    normed, norm_one_back = jax.vjp(layer_norm, first_sum, gain_rows[0], shift_rows[3])
    normed_low = normed.astype(jnp.bfloat16)
    pre_act = jnp.dot(normed_low, in_mat, preferred_element_type=jnp.float32) + bias_rows
    active, gelu_back = jax.vjp(gelu_exact, pre_act)
    active_low = active.astype(jnp.bfloat16)
    second_sum = (
        normed + jnp.dot(active_low, back_mat, preferred_element_type=jnp.float32) + shift_rows[4]
    )
    final_raw, norm_two_back = jax.vjp(layer_norm, second_sum, gain_rows[1], shift_rows[5])
    valid_rows = valid_mask.reshape(row_count, 1)
    result = final_raw * valid_rows
    back_weights = (
        lax.all_gather(w_query.astype(jnp.bfloat16), ("seq", "tok"), axis=0, tiled=True),
        lax.all_gather(w_key.astype(jnp.bfloat16), ("seq", "tok"), axis=0, tiled=True),
        lax.all_gather(w_value.astype(jnp.bfloat16), ("seq", "tok"), axis=0, tiled=True),
        lax.all_gather(w_out.astype(jnp.bfloat16), ("seq", "tok"), axis=0, tiled=True),
        lax.all_gather(w_in.astype(jnp.bfloat16), ("seq", "tok"), axis=0, tiled=True),
        lax.all_gather(w_back.astype(jnp.bfloat16), ("seq", "tok"), axis=0, tiled=True),
    )
    query_back, key_back, value_back, out_back, in_back, back_back = back_weights
    grad_out = cotangent.reshape(row_count, model_width).astype(jnp.float32) * valid_rows
    grad_second, grad_gain_two, grad_shift_five = norm_two_back(grad_out)
    grad_second_low = grad_second.astype(jnp.bfloat16)
    grad_shift_four = jnp.sum(grad_second, axis=0)
    grad_w_back = product_low("rf,rd->fd", active_low, grad_second_low)
    grad_active = product_low("rd,fd->rf", grad_second_low, back_back)
    (grad_pre,) = gelu_back(grad_active)
    grad_pre_low = grad_pre.astype(jnp.bfloat16)
    grad_b_in = jnp.sum(grad_pre, axis=0)
    grad_w_in = product_low("rd,rf->df", normed_low, grad_pre_low)
    grad_normed = grad_second + product_low("rf,df->rd", grad_pre_low, in_back)
    grad_first, grad_gain_one, grad_shift_three = norm_one_back(grad_normed)
    grad_proj_low = grad_first.astype(jnp.bfloat16)
    grad_shift_two = jnp.sum(grad_first, axis=0)
    grad_w_out = product_low("rd,re->de", mix_low, grad_proj_low)
    grad_mix_low = (
        product_low("re,de->rd", grad_proj_low, out_back)
        .astype(jnp.bfloat16)
        .reshape(seq_count, slot_count, model_width)
    )
    grad_mix_heads = grad_mix_low.reshape(seq_count, slot_count, head_count, head_dim)
    grad_mixed_part = product_low("bshm,bshd->bhmd", first_low, grad_mix_heads)
    grad_first_kernel = product_low("bshd,bhmd->bshm", grad_mix_heads, mixed_low)
    inner_sum = jnp.sum(grad_first_kernel * first_score_kernel, axis=-1, keepdims=True)
    grad_first_low = (
        first_score_kernel * (grad_first_kernel - inner_sum) * score_scale_factor
    ).astype(jnp.bfloat16)
    part_grad_key = product_low("bshm,bshd->bmhd", grad_first_low, query_head_rows)
    grad_mixed, grad_mk_first = lax.psum((grad_mixed_part, part_grad_key), "tok")
    grad_mq_core, grad_mk_core, grad_numer, grad_denom = core_back(grad_mixed)
    grad_numer_low = grad_numer.astype(jnp.bfloat16)
    grad_third_exp = (
        product_low("bhmd,bshd->bhms", grad_numer_low, value_head_rows) + grad_denom[..., None]
    )
    grad_v_heads = product_low("bhms,bhmd->bshd", third_low, grad_numer_low)
    grad_third_low = (third_exponential * grad_third_exp * score_scale_factor).astype(jnp.bfloat16)
    part_grad_query = product_low("bhms,bshd->bmhd", grad_third_low, key_head_rows)
    grad_key_heads = product_low("bhms,bmhd->bshd", grad_third_low, mark_query)
    grad_mq_third = lax.psum(part_grad_query, "tok")
    grad_mq = (grad_mq_core + grad_mq_third).reshape(
        seq_count, mark_count, model_width
    ) / part_count[..., None]
    grad_mk = (grad_mk_core + grad_mk_first).reshape(
        seq_count, mark_count, model_width
    ) / part_count[..., None]
    grad_query = jnp.einsum(
        "bms,bmd->bsd", member, grad_mq, precision=EXACT_PRECISION
    ) + product_low("bshm,bmhd->bshd", grad_first_low, mark_key).reshape(
        seq_count, slot_count, model_width
    )
    grad_key = jnp.einsum(
        "bms,bmd->bsd", member, grad_mk, precision=EXACT_PRECISION
    ) + grad_key_heads.reshape(seq_count, slot_count, model_width)
    grad_padded = padded_2(grad_mix_low, (("tok", 1),), rim_width)
    grad_pad_heads = grad_padded.astype(jnp.float32).reshape(
        seq_count, slot_count + 2 * rim_width, head_count, head_dim
    )
    grad_mix_float = grad_mix_heads.astype(jnp.float32)
    grad_conv_v = jnp.zeros_like(grad_mix_float)
    conv_terms = []
    for offset in range(tap_count):
        start_at = 2 * rim_width - offset
        grad_conv_v = (
            grad_conv_v
            + w_conv[:, offset][None, None, :, None]
            * grad_pad_heads[:, start_at : start_at + slot_count]
        )
        conv_terms.append(
            jnp.sum(padded_heads[:, offset : offset + slot_count] * grad_mix_float, axis=(0, 1, 3))
        )
    grad_w_conv = lax.psum(jnp.stack(conv_terms, axis=1), ("seq", "tok"))
    grad_value = (grad_v_heads + grad_conv_v).reshape(
        seq_count, slot_count, model_width
    ) * valid_mask[..., None]
    grad_query_flat = grad_query.reshape(row_count, model_width)
    grad_key_flat = grad_key.reshape(row_count, model_width)
    grad_value_flat = grad_value.reshape(row_count, model_width)
    grad_query_low = grad_query_flat.astype(jnp.bfloat16)
    grad_key_low = grad_key_flat.astype(jnp.bfloat16)
    grad_value_low = grad_value_flat.astype(jnp.bfloat16)
    grad_w_query = product_low("rd,re->de", flat_rows, grad_query_low)
    grad_w_key = product_low("rd,re->de", flat_rows, grad_key_low)
    grad_w_value = product_low("rd,re->de", flat_rows, grad_value_low)
    grad_input = (
        grad_first
        + product_low("re,de->rd", grad_query_low, query_back)
        + product_low("re,de->rd", grad_key_low, key_back)
        + product_low("re,de->rd", grad_value_low, value_back)
    )
    grad_gains = jnp.stack([grad_gain_one, grad_gain_two], axis=0)
    grad_shifts = jnp.stack(
        [
            jnp.sum(grad_query_flat, axis=0),
            jnp.sum(grad_value_flat, axis=0),
            grad_shift_two,
            grad_shift_three,
            grad_shift_four,
            grad_shift_five,
        ],
        axis=0,
    )
    (
        owned_query,
        owned_key,
        owned_value,
        owned_out,
        owned_in,
        owned_back,
        owned_bias,
        owned_gains,
        owned_shifts,
    ) = (
        lax.psum_scatter(grad_w_query, ("seq", "tok"), scatter_dimension=0, tiled=True),
        lax.psum_scatter(grad_w_key, ("seq", "tok"), scatter_dimension=0, tiled=True),
        lax.psum_scatter(grad_w_value, ("seq", "tok"), scatter_dimension=0, tiled=True),
        lax.psum_scatter(grad_w_out, ("seq", "tok"), scatter_dimension=0, tiled=True),
        lax.psum_scatter(grad_w_in, ("seq", "tok"), scatter_dimension=0, tiled=True),
        lax.psum_scatter(grad_w_back, ("seq", "tok"), scatter_dimension=0, tiled=True),
        lax.psum_scatter(grad_b_in, ("seq", "tok"), scatter_dimension=0, tiled=True),
        lax.psum_scatter(grad_gains, ("seq", "tok"), scatter_dimension=1, tiled=True),
        lax.psum_scatter(grad_shifts, ("seq", "tok"), scatter_dimension=1, tiled=True),
    )
    return (
        result.reshape(seq_count, slot_count, model_width),
        grad_input.reshape(seq_count, slot_count, model_width),
        owned_query,
        owned_key,
        owned_value,
        owned_out,
        grad_w_conv,
        owned_in,
        owned_back,
        owned_bias,
        owned_gains,
        owned_shifts,
    )


F32 = jnp.float32


BF = jnp.bfloat16


def dot(a, b, ca=1, cb=0):
    return lax.dot_general(a, b, (((ca,), (cb,)), ((), ())), preferred_element_type=F32)


def lane_low(shape):
    return lax.broadcasted_iota(jnp.int32, shape, len(shape) - 1) % 128 < 64


def halves_diag(m):
    low = lane_low((64, 128))
    return jnp.where(low, m[:64], m[64:])


def spread_diag(v):
    low = lane_low(v.shape)
    zero = jnp.zeros_like(v)
    return jnp.concatenate([jnp.where(low, v, zero), jnp.where(low, zero, v)], axis=0)


def seg(op, v, fill):
    low = lane_low(v.shape)
    a = op(jnp.where(low, v, fill), axis=-1, keepdims=True)
    b = op(jnp.where(low, fill, v), axis=-1, keepdims=True)
    return jnp.where(low, a, b)


def split(v):
    hi = v.astype(BF)
    return hi, (v - hi.astype(F32)).astype(BF)


def norm_stats(h):
    center = h - jnp.mean(h, axis=-1, keepdims=True)
    spread = jnp.mean(center * center, axis=-1, keepdims=True)
    rstd = lax.rsqrt(spread + 1e-05)
    return center * rstd, rstd


def norm_back(dy, gain, xhat, rstd):
    d = dy * gain
    a = jnp.mean(d, axis=-1, keepdims=True)
    b = jnp.mean(d * xhat, axis=-1, keepdims=True)
    return rstd * (d - a - xhat * b)


def skew(row, width, count):
    return pltpu.roll(jnp.broadcast_to(row, (count, width)), 0, 1, stride=1, stride_axis=0)


def colsum(v):
    return jnp.sum(v, axis=0, keepdims=True)


MESH = pl.DeviceIdType.MESH


FIRST = 0


def place():
    s = lax.axis_index("seq"); t = lax.axis_index("tok")
    x, y, z, c = s % 2, s // 2, t // 2, t % 2
    px = s + 1 - 2 * x
    py = (s + 2) % 4
    p1 = px * (1 - c) + py * c
    p2 = py * (1 - c) + px * c
    return s, z, c, p1, p2


def remote(src, dst, send, recv, seq, tok):
    return pltpu.make_async_remote_copy(src_ref=src, dst_ref=dst, send_sem=send, recv_sem=recv,
                                        device_id={"seq": seq, "tok": tok}, device_id_type=MESH)


def entry(s, z, c, p1, p2):
    bar = pltpu.get_barrier_semaphore()
    def sig(seq, tok):
        pl.semaphore_signal(bar, inc=1, device_id={"seq": seq, "tok": tok}, device_id_type=MESH)
    t = 2 * z + c
    sig(p1, t); sig(p2, t); sig(s, 2 * z + 1 - c)
    for d in (1, 2, 3):
        sig(s, 2 * ((z + d) % 4) + c)
    @pl.when(((c == 1) & (z < 3)) | ((c == 0) & (z > 0)))
    def _(): sig(s, t + 2 * c - 1)
    edge = c * (6 - z) // 4 + (1 - c) * ((z + 3) // 4)
    pl.semaphore_wait(bar, 6 + edge)


def each_slot(c, f):
    f(0)
    @pl.when(c == 0)
    def _(): f(1)


class UnitSum:
    def __init__(self, src, ra, rb, sems, where, combine):
        self.__dict__.update(locals())
        self.sa, self.qa, self.sb, self.qb = sems
    def cp_a(self, c):
        s, z, cc, _, _ = self.where
        if c == 0:
            return remote(self.src.at[:, pl.ds(2, 1)], self.ra.at[:, pl.ds(0, 1)], self.sa, self.qa, s, 2 * z + 1)
        return remote(self.src.at[:, pl.ds(0, 2)], self.ra, self.sa, self.qa, s, 2 * z)
    def cp_b(self, d, i):
        s, z, c, _, _ = self.where
        zz = (z + d) % 4
        return remote(self.src.at[zz, 2 * c + i], self.rb.at[z, i], self.sb.at[i], self.qb.at[i], s, 2 * zz + c)
    def start(self):
        for k in (0, 1):
            @pl.when(self.where[2] == k)
            def _(): self.cp_a(k).start(FIRST)
    def mid(self):
        s, z, c, _, _ = self.where
        for k in (0, 1):
            @pl.when(c == k)
            def _(): self.cp_a(1 - k).wait_recv()
        def comb(zz):
            each_slot(c, lambda i: self.combine(self.src.at[zz, 2 * c + i], self.ra.at[zz, i]))
        for d in (2, 1, 3):
            comb((z + d) % 4)
            each_slot(c, lambda i: self.cp_b(d, i).start(FIRST))
        comb(z)
    def three(self, i):
        s, z, c, _, _ = self.where
        return remote(self.src.at[pl.ds(0, 3), 2 * c + i], self.rb.at[pl.ds(0, 3), i], self.sb.at[i], self.qb.at[i], s, 2 * z + 1 - c)
    def end(self):
        s, z, c, _, _ = self.where
        def f(i):
            self.three(i).wait_recv()
            for d in (1, 3, 2): self.combine(self.src.at[z, 2 * c + i], self.rb.at[(z + d) % 4, i])
        each_slot(c, f)
    def drain(self):
        c = self.where[2]
        for k in (0, 1):
            @pl.when(c == k)
            def _(): self.cp_a(k).wait_send()
        each_slot(c, lambda i: self.three(i).wait_send())


class UnitShare:
    def __init__(self, buf, sems, where):
        self.__dict__.update(locals())
        self.sz, self.qz, self.sc, self.qc = sems
    def cp_z(self, d, i):
        s, z, c, _, _ = self.where
        b = self.buf.at[z, 2 * c + i]
        return remote(b, b, self.sz.at[i], self.qz.at[z, i], s, 2 * ((z + d) % 4) + c)
    def cp_c(self, zz, i):
        s, z, c, _, _ = self.where
        b = self.buf.at[zz, 2 * c + i]
        return remote(b, b, self.sc.at[i], self.qc.at[i], s, 2 * z + 1 - c)
    def start(self):
        z, c = self.where[1], self.where[2]
        def f(i):
            for d in (2, 1, 3): self.cp_z(d, i).start(FIRST)
            self.cp_c(z, i).start(FIRST)
        each_slot(c, f)
    def mid(self):
        s, z, c, _, _ = self.where
        for d in (1, 3, 2):
            zz = (z + d) % 4
            def f(i):
                b = self.buf.at[zz, 2 * c + i]
                remote(b, b, self.sz.at[i], self.qz.at[zz, i], s, 2 * zz + c).wait_recv()
                self.cp_c(zz, i).start(FIRST)
            each_slot(c, f)
    def end(self):
        s, z, c, _, _ = self.where
        def f(i):
            b = self.buf.at[:, 2 * (1 - c) + i]
            remote(b, b, self.sc.at[i], self.qc.at[i], s, 2 * z + 1 - c).wait_recv()
        each_slot(1 - c, f)
    def drain(self):
        s, z, c, _, _ = self.where
        def f(i):
            b = self.buf.at[pl.ds(0, 3), 2 * c + i]
            remote(b, b, self.sz.at[i], self.qc.at[i], s, 2 * z + 1 - c).wait_send()
            b = self.buf.at[:, 2 * c + i]
            remote(b, b, self.sc.at[i], self.qc.at[i], s, 2 * z + 1 - c).wait_send()
        each_slot(c, f)


class Halo:
    def __init__(self, buf, slots, send, recv, where):
        self.__dict__.update(locals())
        s, z, c, _, _ = where
        self.t = 2 * z + c
    def cps(self):
        s, n = self.where[0], self.slots
        up = remote(self.buf.at[:, pl.ds(n, 16)], self.buf.at[:, pl.ds(0, 16)], self.send.at[0], self.recv.at[0], s, self.t + 1)
        down = remote(self.buf.at[:, pl.ds(16, 16)], self.buf.at[:, pl.ds(16 + n, 16)], self.send.at[1], self.recv.at[1], s, self.t - 1)
        return up, down
    def zero(self):
        n = self.slots
        a, _, d = self.buf.shape
        self.buf[:, 16 + n:, :] = jnp.zeros((a, 256 - 16 - n, d), BF)
        self.buf[:, 0:16, :] = jnp.zeros((a, 16, d), BF)
    def start(self):
        up, down = self.cps()
        @pl.when(self.t < 7)
        def _(): up.start(FIRST)
        @pl.when(self.t > 0)
        def _(): down.start(FIRST)
    def end(self):
        up, down = self.cps()
        @pl.when(self.t > 0)
        def _(): up.wait_recv()
        @pl.when(self.t < 7)
        def _(): down.wait_recv()
    def drain(self):
        up, down = self.cps()
        @pl.when(self.t < 7)
        def _(): up.wait_send()
        @pl.when(self.t > 0)
        def _(): down.wait_send()


def mm(a, b, flip=False):
    ah, al = split(a)
    bh, bl = split(spread_diag(b))
    if flip:
        return dot(ah, bh, 1, 1) + (dot(ah, bl, 1, 1) + dot(al, bh, 1, 1))
    return dot(jnp.concatenate([ah, ah, al], axis=1), jnp.concatenate([bh, bl, bh], axis=0))


def flip64(a):
    t = jnp.transpose(a)
    return jnp.concatenate([t[:64], t[64:]], axis=1)


def eye_pair():
    i = lax.broadcasted_iota(jnp.int32, (64, 128), 0)
    j = lax.broadcasted_iota(jnp.int32, (64, 128), 1)
    return jnp.where(i == j % 64, 1.0, 0.0).astype(F32)


def soft_combine(dst, other):
    m1, m2 = dst[64:65, :], other[64:65, :]
    m = jnp.maximum(m1, m2)
    a, b = jnp.exp(m1 - m), jnp.exp(m2 - m)
    dst[0:64, :] = dst[0:64, :] * a + other[0:64, :] * b
    dst[65:66, :] = dst[65:66, :] * a + other[65:66, :] * b
    dst[64:65, :] = m


def core_setup(qm, km):
    p2 = dot(qm, spread_diag(km), 1, 1) * (64 ** -0.5)
    e = jnp.exp(p2 - seg(jnp.max, p2, -jnp.inf))
    p2 = e / seg(jnp.sum, e, 0.0)
    factor = 1.0 / seg(jnp.max, colsum(p2), -jnp.inf)
    return p2, flip64(p2) * factor


def seg_sum(v):
    i = lax.broadcasted_iota(jnp.int32, (128, 128), 0)
    j = lax.broadcasted_iota(jnp.int32, (128, 128), 1)
    ones = jnp.where(i // 64 == j // 64, 1.0, 0.0).astype(BF)
    hi, lo = split(v)
    return dot(hi, ones) + dot(lo, ones)

def plain_add(dst, other):
    dst[...] = (dst[...].astype(F32) + other[...].astype(F32)).astype(dst.dtype)

class Gather:
    STAGES = 9
    def __init__(self, views, owns, last, sems, where):
        self.__dict__.update(locals())
        self.qa, self.qb, self.sz, self.s1, self.s2, self.sc, self.sl = sems
        s, z, c, p1, p2 = where
        t = 2 * z + c
        self.line = ((s, t + 2), (s, t - 2))
        self.d1, self.d2, self.dc = (p1, t), (p2, t), (s, 2 * z + 1 - c)
    def at(self, k, s_, z_, c_):
        return self.views[k](s_, z_, c_)
    def cp(self, k, s_, zz, send, got, dev, src=None):
        dst = self.at(k, s_, zz, self.where[2])
        return remote(dst if src is None else src, dst, send, self.qa.at[k, got], *dev)
    def to_z(self, k, zz, way, src=None): return self.cp(k, self.where[0], zz, self.sz.at[k, way], zz, self.line[way], src)
    def to_1(self, k, zz, src=None): return self.cp(k, self.where[0], zz, self.s1.at[k], 4 + zz, self.d1, src)
    def to_2(self, k, g, zz, src=None): return self.cp(k, self.where[3 if g else 0], zz, self.s2.at[k], 8, self.d2, src)
    def several(self, k, s_, zz, send, got): return self.cp(k, s_, zz, send, got, self.dc)
    def local(self, k):
        s, z, c, _, _ = self.where
        return pltpu.make_async_copy(self.owns(k), self.at(k, s, z, c), self.sl.at[k])
    def col(self, k, s_):
        b = self.at(k, s_, slice(None), self.where[2])
        return remote(b, b, self.sc.at[k], self.qb.at[k], *self.dc)
    def pair(self, d, f):
        z = self.where[1]
        if d == 0:
            f(z, 2); return
        @pl.when(z >= d)
        def _(): f(z - d, 0)
        @pl.when(z + d <= 3)
        def _(): f(z + d, 1)
    def plane_z(self, k, zz, way):
        return self.cp(k, slice(None), zz, self.sz.at[k, way], zz, self.line[way])
    def run_last(self, k, i):
        s, z, c, p1, p2 = self.where
        every = slice(None)
        if i == 0:
            self.local(k).start()
            self.to_2(k, 0, z, self.owns(k)).start(); self.to_1(k, z, self.owns(k)).start()
        elif i == 1:
            self.several(k, p1, z, self.s1.at[k], 4 + z).wait_recv()
            self.to_2(k, 1, z).start()
        elif i == 2:
            self.several(k, pl.ds(0, 2), z, self.s2.at[k], 8).wait_recv()
            self.local(k).wait()
            @pl.when(z < 3)
            def _(): self.plane_z(k, z, 0).start()
            @pl.when(z > 0)
            def _(): self.plane_z(k, z, 1).start()
        elif i < 6:
            def f(zz, side):
                self.several(k, every, zz, self.sz.at[k, 0], zz).wait_recv()
                if side == 0 and i < 5:
                    @pl.when(z < 3)
                    def _(): self.plane_z(k, zz, 0).start()
                if side == 1 and i < 5:
                    @pl.when(z > 0)
                    def _(): self.plane_z(k, zz, 1).start()
            self.pair(i - 2, f)
            if i == 5:
                b = self.at(k, every, every, c)
                remote(b, b, self.sc.at[k], self.qb.at[k], *self.dc).start()
    def run(self, k, i):
        if k in self.last: return self.run_last(k, i)
        s, z, c, p1, p2 = self.where
        if i < 4:
            def f(zz, side):
                src = None
                if side == 2:
                    src = self.owns(k)
                    self.local(k).start()
                else:
                    self.several(k, s, zz, self.s1.at[k], zz).wait_recv()
                if side != 1 and i < 3:
                    @pl.when(z < 3)
                    def _(): self.to_z(k, zz, 0, src).start()
                if side != 0 and i < 3:
                    @pl.when(z > 0)
                    def _(): self.to_z(k, zz, 1, src).start()
                self.to_2(k, 0, zz, src).start(); self.to_1(k, zz, src).start()
            self.pair(i, f)
            if i == 3:
                self.local(k).wait()
                self.col(k, s).start()
        elif i < 8:
            def f(zz, side):
                self.several(k, p1, zz, self.s1.at[k], 4 + zz).wait_recv()
                self.to_2(k, 1, zz).start()
            self.pair(i - 4, f)
            if i == 7: self.col(k, p1).start()
        else:
            self.several(k, pl.ds(0, 2), slice(None), self.s2.at[k], 8).wait_recv()
            for s_ in (p2, 3 - s): self.col(k, s_).start()
    def arrive(self, k):
        b = self.at(k, slice(None), slice(None), 1 - self.where[2])
        remote(b, b, self.sc.at[k], self.qb.at[k], *self.dc).wait_recv()
    def drain(self):
        s, z, c, p1, p2 = self.where
        every = slice(None)
        for k in range(len(self.views)):
            self.several(k, every, every, self.sc.at[k], 8).wait_send()
            last = k in self.last
            self.several(k, s, z if last else every, self.s1.at[k], 8).wait_send()
            self.several(k, pl.ds(0, 2), z if last else every, self.s2.at[k], 8).wait_send()
            line = every if last else s
            for q in range(3):
                @pl.when(z == q)
                def _(): self.several(k, line, pl.ds(0, q + 1), self.sz.at[k, 0], 8).wait_send()
                @pl.when(z == 3 - q)
                def _(): self.several(k, line, pl.ds(0, q + 1), self.sz.at[k, 1], 8).wait_send()

class Scatter:
    STAGES = 5
    def __init__(self, part, outs, zfirst, bufs, sems, where):
        self.__dict__.update(locals())
        self.rcb, self.r2, self.r1, self.rz = bufs
        self.s_c, self.q_c, self.s_2, self.q_2, self.s_1, self.q_1, self.s_z, self.q_z = sems
        s, z, c, p1, p2 = where
        t = 2 * z + c
        self.d1, self.d2, self.dc = (p1, t), (p2, t), (s, 2 * z + 1 - c)
    def own(self, k, *at): return self.part(k, self.where[2], *at)
    def cp_c(self, k): return remote(self.part(k, 1 - self.where[2]), self.rcb.at[k], self.s_c.at[k], self.q_c.at[k], *self.dc)
    def cp_2(self, k, g):
        b = self.where[4] if g == 0 else 3 - self.where[0]
        return remote(self.own(k, b), self.r2.at[k, g], self.s_2.at[k], self.q_2.at[k, g], *self.d2)
    def cp_1(self, k): return remote(self.own(k, self.where[3]), self.r1.at[k], self.s_1.at[k], self.q_1.at[k], *self.d1)
    def cp_z(self, k, d):
        s, z, c, p1, p2 = self.where
        zz = (z + d) % 4
        return remote(self.own(k, s, zz), self.rz.at[k, z], self.s_z.at[k], self.q_z.at[k], s, 2 * zz + c)
    def three(self, k):
        return remote(self.own(k, self.where[0], pl.ds(0, 3)), self.rz.at[k, pl.ds(0, 3)], self.s_z.at[k], self.q_z.at[k], *self.dc)
    def add4(self, k, i, v):
        a = self.own(k, i)
        a[...] = a[...] + v
    def first_z(self, k, d):
        s, z, c, p1, p2 = self.where
        dst = self.r1.at[k] if d == 3 else self.r2.at[k, d - 1]
        return remote(self.own(k, slice(None), (z + d) % 4), dst, self.s_z.at[k], self.q_z.at[k], s, 2 * ((z + d) % 4) + c)
    def first_2(self, k, g):
        b = self.where[4] if g == 0 else 3 - self.where[0]
        return remote(self.own(k, b, self.where[1]), self.rz.at[k, g], self.s_2.at[k], self.q_2.at[k, g], *self.d2)
    def first_1(self, k): return remote(self.own(k, self.where[3], self.where[1]), self.rz.at[k, 2], self.s_1.at[k], self.q_1.at[k], *self.d1)
    def twelve(self, k): return remote(self.own(k, pl.ds(0, 3)), self.rcb.at[k, pl.ds(0, 3)], self.s_z.at[k], self.q_z.at[k], *self.dc)
    def run_first(self, k, i):
        s, z, c, p1, p2 = self.where
        if i == 0:
            self.cp_c(k).start()
        elif i == 1:
            self.cp_c(k).wait_recv()
            for j in range(4): self.add4(k, j, self.rcb[k, j])
            for d in (2, 1, 3): self.first_z(k, d).start()
        elif i == 2:
            self.twelve(k).wait_recv()
            a = self.own(k, slice(None), z)
            tot = (a[...].astype(F32) + self.r2[k, 0].astype(F32)) + (self.r2[k, 1].astype(F32) + self.r1[k].astype(F32))
            a[...] = tot.astype(BF)
            for g in (1, 0): self.first_2(k, g).start()
        elif i == 3:
            for g, b in ((1, p1), (0, s)):
                self.first_2(k, g).wait_recv()
                a = self.own(k, b, z)
                a[...] = a[...] + self.rz[k, g]
                if g: self.first_1(k).start()
        else:
            self.first_1(k).wait_recv()
            self.outs(k)[...] = self.own(k, s, z)[...].astype(F32) + self.rz[k, 2].astype(F32)
    def run(self, k, i):
        if k in self.zfirst: return self.run_first(k, i)
        s, z, c, p1, p2 = self.where
        if i == 0:
            self.cp_c(k).start()
        elif i == 1:
            self.cp_c(k).wait_recv()
            for g, b in ((1, 3 - s), (0, p2)):
                self.add4(k, b, self.rcb[k, b])
                self.cp_2(k, g).start()
            for b in (p1, s): self.add4(k, b, self.rcb[k, b])
        elif i == 2:
            self.cp_2(k, 1).wait_recv()
            self.add4(k, p1, self.r2[k, 1])
            self.cp_1(k).start()
            self.cp_2(k, 0).wait_recv()
            self.add4(k, s, self.r2[k, 0])
        elif i == 3:
            self.cp_1(k).wait_recv()
            self.add4(k, s, self.r1[k])
            for d in (2, 1, 3): self.cp_z(k, d).start()
        else:
            self.three(k).wait_recv()
            tot = self.own(k, s, z)[...].astype(F32)
            for d in (1, 3, 2): tot = tot + self.rz[k, (z + d) % 4].astype(F32)
            self.outs(k)[...] = tot
    def drain(self, n):
        for k in range(n):
            self.cp_c(k).wait_send()
            if k in self.zfirst:
                self.twelve(k).wait_send(); self.first_1(k).wait_send()
                remote(self.own(k, 0, pl.ds(0, 2)), self.rz.at[k, pl.ds(0, 2)], self.s_2.at[k], self.q_2.at[k, 0], *self.d2).wait_send()
                continue
            remote(self.own(k, pl.ds(0, 2)), self.r2.at[k], self.s_2.at[k], self.q_2.at[k, 0], *self.d2).wait_send()
            self.cp_1(k).wait_send()
            self.three(k).wait_send()

CHUNKS = (("w", 1, 1), ("w", 0, 1), ("w", 2, 1), ("w", 3, 1), ("i", 0, 2), ("i", 1, 2), ("b", 0, 2), ("b", 1, 2))
LINE_LAST = (4,)
LINE_FIRST = (2,)
ORDER = (
    0, 9, 173, 18, 27, 4, 1, 36, 174, 10, 13, 22, 19, 31, 2, 5, 28, 37, 175, 14, 11, 20, 3, 23, 29, 6, 176, 45,
    12, 38, 32, 21, 15, 30, 24, 7, 177, 46, 33, 49, 16, 54, 39, 25, 34, 8, 47, 81, 178, 55, 50, 17, 40, 58, 26, 35,
    82, 48, 51, 83, 56, 84, 179, 59, 183, 180, 63, 41, 42, 43, 57, 44, 150, 151, 60, 72, 184, 52, 181, 64, 85, 182, 67, 152,
    61, 73, 153, 154, 155, 53, 185, 186, 76, 65, 68, 86, 74, 62, 187, 66, 77, 87, 188, 189, 75, 190, 69, 163, 165, 70, 78, 162,
    164, 79, 71, 80, 88, 89, 191, 192, 193, 90, 100, 169, 125, 167, 91, 101, 115, 166, 110, 126, 168, 194, 111, 92, 116, 105, 195, 127,
    102, 197, 112, 93, 106, 196, 130, 120, 95, 198, 199, 131, 128, 94, 103, 117, 121, 200, 201, 113, 156, 96, 157, 129, 158, 159, 202, 107,
    160, 161, 114, 204, 205, 132, 104, 206, 211, 135, 207, 118, 208, 203, 122, 136, 209, 210, 97, 119, 108, 133, 212, 123, 213, 214, 217, 216,
    145, 215, 134, 170, 109, 137, 218, 146, 124, 98, 171, 140, 138, 141, 99, 147, 139, 172, 142, 219, 148, 143, 149, 144,
)
UNROLL = True
UNROLL_T = 3

def body(order, lens, x_ref, cot_ref, wc_ref, wq_ref, wk_ref, wv_ref, wo_ref, win_ref, wback_ref, bin_ref, gains_ref, shifts_ref,
         res_o, gx_o, oq_o, ok_o, ov_o, oo_o, oi_o, ob_o, sums_o,
         own4, owni, ownb, ownv, vec, w4, wi, wb, lhs, xs, xa, xb, xm, nu, ra, rb, q_u, k_u, vpad, qm_u, km_u, p1_s, e3_s, ml_s, wz, sv, p2s, z6, nts, mden, cv, bias, wcp, wrp,
         ar, yt, gr, gp, gbs, rs1, acc, xh1, gb5, gi5, g4, dpad, e4, ra4, rb4, e6, ra6, rb6, sh5, core_g, sh7, dq1, memb, rcb, r2, r1b, rz, vr, va, vx, vy, vz, sums,
         qa, qb, sz, s1, s2, sc, sl, e0s, e0q, ua, ub, ug, uh, hs, s_c, q_c, s_2, q_2, s_1, q_1, s_z, q_z, va4, vb4, v6a, v6b, ug5, uh5, u7, u7h, hs2, vs, vq, osem, rsem):
    where = place()
    s, z, c, p1, p2 = where
    t = 2 * z + c
    nseq = vpad.shape[0]
    rows, width = x_ref.shape
    slots = rows // nseq
    pairs = width // 128
    n = nseq * pairs
    heads = 2 * pairs
    taps = wc_ref.shape[1]
    ff = wi.shape[1]
    nff = ff // width
    sub = wq_ref.shape[0]
    scale = 64 ** -0.5
    i32 = jnp.int32
    iota = lambda shape, d: lax.broadcasted_iota(i32, shape, d)
    four = [pltpu.make_async_copy(r, gp.at[pl.ds(sub, sub), pl.ds(i * width, width)], osem.at[i]) for i, r in enumerate((wq_ref, wk_ref, wv_ref, wo_ref))]
    four.append(pltpu.make_async_copy(win_ref, gp.at[pl.ds(0, sub)], osem.at[4]))
    four.append(pltpu.make_async_copy(wback_ref, gp.at[pl.ds(2 * sub, 4 * sub), pl.ds(0, width)], osem.at[5]))
    for cp in four: cp.start()
    for cp in four: cp.wait()
    for i in range(4): own4[i] = gp[pl.ds(sub, sub), pl.ds(i * width, width)].astype(BF)
    owni[...] = gp[pl.ds(0, sub), :].astype(BF)
    ownb[...] = gp[pl.ds(2 * sub, 4 * sub), pl.ds(0, width)].astype(BF)
    ownv[...] = jnp.zeros_like(ownv)
    ownv[0:2, 0:sub] = gains_ref[...]
    ownv[2:8, 0:sub] = shifts_ref[...]
    ownv[8:9, 0:4 * sub] = bin_ref[...]
    def edges(b, first, count):
        j = iota((count, 1), 0) + first
        return lax.shift_right_logical(j * lens[b], 6), lax.shift_right_logical((j + 1) * lens[b], 6)
    def counts(b, first, count):
        lo, hi = edges(b, first, count)
        return (hi - lo).astype(F32)
    def valid_of(b): return iota((slots, 1), 0) + t * slots < lens[b]
    def valid_all(): return jnp.concatenate([valid_of(b).astype(F32) for b in range(nseq)], axis=0)
    for b in range(nseq):
        lo, hi = edges(b, 0, 64)
        pos = iota((64, slots), 1) + t * slots
        memb[pl.ds(64 * b, 64), :] = jnp.where((pos >= lo) & (pos < hi), 1.0, 0.0).astype(BF)
    wcp[...] = jnp.zeros_like(wcp); wrp[...] = jnp.zeros_like(wrp)
    wcp[:, 0:taps] = wc_ref[...]
    w0 = wcp[:, 0:128]
    a1 = w0.astype(BF); rest = w0 - a1.astype(F32); a2 = rest.astype(BF); a3 = (rest - a2.astype(F32)).astype(BF)
    turn = jnp.where(iota((128, 128), 0) + iota((128, 128), 1) == taps - 1, 1.0, 0.0).astype(BF)
    wrp[:, 0:128] = (dot(a1, turn) + dot(a2, turn)) + dot(a3, turn)
    entry(*where)
    chip = 2 * sub
    wv, iv, bv = w4.reshape(4, 4, 4, chip, width), wi.reshape(4, 4, chip, ff), wb.reshape(4, 4, 4 * chip, width)
    giv, gbv, gwv = gi5.reshape(4, 4, chip, ff), gb5.reshape(4, 4, 4 * chip, width), g4.reshape(4, 4, 4, chip, width)
    def span(c_, step, lo, cnt): return pl.ds(pl.multiple_of(c_ * step + lo, 8), cnt)
    views, srcs = [lambda s_, z_, c_: vec.at[s_, z_, c_]], [ownv]
    for kind, lo, cnt in CHUNKS:
        if kind == "w":
            views.append(lambda s_, z_, c_, lo=lo, cnt=cnt: wv.at[pl.ds(lo, cnt), s_, z_, span(c_, sub, 0, sub)])
            srcs.append(own4.at[pl.ds(lo, cnt)])
        elif kind == "i":
            m = ff // cnt
            views.append(lambda s_, z_, c_, lo=lo, m=m: iv.at[s_, z_, span(c_, sub, 0, sub), pl.ds(lo * m, m)])
            srcs.append(owni.at[:, pl.ds(lo * m, m)])
        else:
            m = 4 * sub // cnt
            views.append(lambda s_, z_, c_, lo=lo, m=m: bv.at[s_, z_, span(c_, 4 * sub, lo * m, m)])
            srcs.append(ownb.at[pl.ds(lo * m, m)])
    g = Gather(views, lambda k: srcs[k], LINE_LAST, (qa, qb, sz, s1, s2, sc, sl), where)
    e2 = UnitSum(nu, ra, rb, (ua.at[0], ua.at[1], ub.at[0], ub.at[1]), where, soft_combine)
    e3 = UnitShare(wz, (ug.at[0], uh, ug.at[1], ug.at[2]), where)
    halo = Halo(vpad, slots, hs.at[0], hs.at[1], where)
    dhalo = Halo(dpad, slots, hs2.at[0], hs2.at[1], where)
    sum4 = UnitSum(e4, ra4, rb4, (va4.at[0], va4.at[1], vb4.at[0], vb4.at[1]), where, plain_add)
    share5 = UnitShare(sh5, (ug5.at[0], uh5, ug5.at[1], ug5.at[2]), where)
    sum6 = UnitSum(e6, ra6, rb6, (v6a.at[0], v6a.at[1], v6b.at[0], v6b.at[1]), where, plain_add)
    share7 = UnitShare(sh7, (u7.at[0], u7h, u7.at[1], u7.at[2]), where)
    def part(k, c_, *at):
        at = (*at, *((slice(None),) * (2 - len(at))))
        if k < 4: return gbv.at[(*at, span(c_, 4 * sub, k * sub, sub))]
        if k < 4 + nff: return giv.at[(*at, span(c_, sub, 0, sub), pl.ds((k - 4) * width, width))]
        return gwv.at[(k - 4 - nff, *at, span(c_, sub, 0, sub))]
    def outs(k):
        if k < 4: return gp.at[pl.ds(k * sub, sub), pl.ds(0, width)]
        if k < 4 + nff: return gp.at[pl.ds(4 * sub, sub), pl.ds((k - 4) * width, width)]
        return gp.at[pl.ds(5 * sub, sub), pl.ds((k - 4 - nff) * width, width)]
    rs = Scatter(part, outs, LINE_FIRST, (rcb, r2, r1b, rz), (s_c, q_c, s_2, q_2, s_1, q_1, s_z, q_z), where)
    def xm_part():
        for b in range(nseq):
            xs[b] = dot(memb[pl.ds(64 * b, 64), :], x_ref[pl.ds(slots * b, slots), :])
        cp_xa().start(FIRST)
    def cp_xa(): return remote(xs.at[1 - c], xa, e0s.at[0], e0q.at[0], s, 2 * z + 1 - c)
    def cp_xb(d):
        zz = (z + d) % 4
        return remote(xs.at[c, pl.ds(pl.multiple_of(16 * zz, 16), 16)], xb.at[z], e0s.at[d], e0q.at[1 + z], s, 2 * zz + c)
    def cp_xm(d):
        return remote(xm.at[c, z], xm.at[c, z], e0s.at[3 + d], e0q.at[5 + z], s, 2 * ((z + d) % 4) + c)
    def cp_xc(zz):
        return remote(xm.at[c, zz], xm.at[c, zz], e0s.at[7 + zz], e0q.at[9 + zz], s, 2 * z + 1 - c)
    def xm_b():
        cp_xa().wait_recv()
        xs[c] = xs[c] + xa[...]
        for d in (2, 1, 3): cp_xb(d).start(FIRST)
    def xm_c():
        tot = xs[c, pl.ds(pl.multiple_of(16 * z, 16), 16), :]
        for d in (1, 3, 2):
            zz = (z + d) % 4
            remote(xb.at[zz], xb.at[zz], e0s.at[d], e0q.at[1 + zz], s, 2 * zz + c).wait_recv()
            tot = tot + xb[zz]
        xm[c, z] = tot / counts(c, 16 * z, 16)
        for d in (2, 1, 3): cp_xm(d).start(FIRST)
        cp_xc(z).start(FIRST)
    def xm_d():
        for d in (1, 3, 2):
            zz = (z + d) % 4
            remote(xm.at[c, zz], xm.at[c, zz], e0s.at[3 + d], e0q.at[5 + zz], s, 2 * zz + c).wait_recv()
            cp_xc(zz).start(FIRST)
    def xm_e():
        for zz in range(4):
            b = xm.at[1 - c, zz]
            remote(b, b, e0s.at[7 + zz], e0q.at[9 + zz], s, 2 * z + 1 - c).wait_recv()
        hi, lo = split(xm[...].reshape(64 * nseq, width))
        lhs[pl.ds(0, rows), :] = x_ref[...]
        lhs[pl.ds(rows, 64 * nseq), :] = hi
        lhs[pl.ds(rows + 64 * nseq, 64 * nseq), :] = lo
    def vectors():
        v = vec[...].reshape(32, 16, 128)
        def spread_rows(row, group, dst, at, count):
            for h in range(0, count, 256):
                k = iota((128, 256), 0); l = iota((128, 256), 1) + h
                w = dot(row, jnp.where((l % group == k) & (k < group), 1.0, 0.0).astype(BF)).reshape(32, 8, 256)
                mine = iota((32, 8, 256), 0) == (iota((32, 8, 256), 2) + h) // group
                dst(h, jnp.sum(jnp.where(mine, w, 0.0), axis=0))
        def to_cv(h, w): cv[:, pl.ds(h, 256)] = w
        def to_bias(h, w): bias[:, pl.ds(h, 256)] = w[0:1]
        spread_rows(v[:, 0:8, :].reshape(256, 128).astype(BF), sub, to_cv, 0, width)
        spread_rows(v[:, 8:16, :].reshape(256, 128).astype(BF), 4 * sub, to_bias, 0, ff)
    def projections():
        m_n = 64 * nseq
        valid = valid_all()
        for h in range(0, width, 256):
            cols = pl.ds(h, 256)
            v = ((dot(x_ref[...], w4[2, :, cols]) + cv[3:4, cols]) * valid).astype(BF)
            for b in range(nseq): vpad[b, pl.ds(16, slots), cols] = v[b * slots:(b + 1) * slots]
        halo.start()
        for i, (dst, marks) in ((1, (k_u, km_u)), (0, (q_u, qm_u))):
            for h in range(0, width, 256):
                cols = pl.ds(h, 256)
                r = dot(lhs[...], w4[i, :, cols])
                a = r[:rows]
                m = r[rows:rows + m_n] + r[rows + m_n:]
                if i == 0:
                    a = a + cv[2:3, cols]
                    m = m + cv[2:3, cols]
                a = a.astype(BF); m = m.astype(BF)
                for b in range(nseq):
                    for q in range(2):
                        u = b * pairs + h // 128 + q
                        dst[u] = a[b * slots:(b + 1) * slots, q * 128:(q + 1) * 128]
                        marks[u] = m[b * 64:(b + 1) * 64, q * 128:(q + 1) * 128]
    def cp_cot(): return pltpu.make_async_copy(cot_ref, lhs.at[pl.ds(rows, rows)], osem.at[0])
    def third():
        cp_cot().start()
        def unit(u, _):
            b, p = u // pairs, u % pairs
            ok = valid_of(b)
            sc3 = jnp.where(ok, dot(k_u[u], spread_diag(qm_u[u]), 1, 1) * scale, -1e30)
            m = jnp.max(sc3, axis=0, keepdims=True)
            e = jnp.where(ok, jnp.exp(sc3 - m), 0.0)
            e3_s[u] = e
            ml_s[u] = jnp.broadcast_to(m, (8, 128))
            v = vpad[b, pl.ds(16, slots), pl.ds(pl.multiple_of(p * 128, 128), 128)]
            nu[u // 3, u % 3, 0:64, :] = halves_diag(dot(v, e.astype(BF), 0, 0))
            nu[u // 3, u % 3, 64:72, :] = jnp.broadcast_to(m, (8, 128))
            nu[u // 3, u % 3, 65:66, :] = colsum(e)
            return 0
        lax.fori_loop(0, n, unit, 0, unroll=UNROLL)
        e2.start()
    def first(lo, hi):
        def unit(u, _):
            sc1 = dot(q_u[u], spread_diag(km_u[u]), 1, 1) * scale
            e = jnp.exp(sc1 - seg(jnp.max, sc1, -jnp.inf))
            pr = e / seg_sum(e)
            p1_s[u] = pr
            return 0
        lax.fori_loop(lo, hi, unit, 0, unroll=UNROLL)
    st = {}
    R2 = range(2)
    def slot(i): return 2 * c + i * (1 - c)
    def core_a():
        st["P"], st["Z"] = [], []
        for i in R2:
            pp, zz = core_setup(qm_u[3 * z + slot(i)], km_u[3 * z + slot(i)])
            p2s[i] = pp
            st["P"].append(pp); st["Z"].append(zz)
    def newton(it):
        eye = eye_pair()
        P, Z = st["P"], st["Z"]
        pr = [mm(P[i], Z[i]) for i in R2]
        t2 = [15.0 * eye - mm(pr[i], 7.0 * eye - pr[i]) for i in R2]
        t3 = [13.0 * eye - mm(pr[i], t2[i]) for i in R2]
        for i in R2:
            sv[i, it, 0] = Z[i]; sv[i, it, 1] = pr[i]; sv[i, it, 2] = t2[i]; sv[i, it, 3] = t3[i]
        st["Z"] = [0.25 * mm(Z[i], t3[i]) for i in R2]
    def core_z():
        for i in R2:
            k = slot(i)
            z6[i] = st["Z"][i]
            nt = nu[z, k, 0:64, :] / nu[z, k, 65:66, :]
            nts[i] = nt
            mden[i] = nu[z, k, 64:72, :]
            wz[z, k] = mm(st["Z"][i], nt, flip=True).astype(BF)
        e3.start()
    def attention():
        halo.end()
        def per(p, _):
            lanes = pl.ds(pl.multiple_of(p * 128, 128), 128)
            th = [split(skew(wcp[pl.ds(2 * p + e, 1), :], 256, slots)) for e in range(2)]
            low = lane_low((slots, 128))
            for b in range(nseq):
                u = b * pairs + p
                v = vpad[b, :, lanes]
                c0 = dot(th[0][0], v) + dot(th[0][1], v)
                c1 = dot(th[1][0], v) + dot(th[1][1], v)
                a = dot(p1_s[u].astype(BF), spread_diag(wz[u // 3, u % 3]))
                ar[pl.ds(b * slots, slots), lanes] = (a + jnp.where(low, c0, c1)).astype(BF)
            return 0
        lax.fori_loop(0, pairs, per, 0, unroll=UNROLL)
    def col_tiles(f):
        def tile(j, _):
            f(pl.ds(pl.multiple_of(j * 256, 256), 256)); return 0
        lax.fori_loop(0, width // 256, tile, 0, unroll=UNROLL)
    RB = 64
    def row_tiles(f):
        def tile(j, _):
            r0 = pl.multiple_of(j * RB, RB)
            f(pl.ds(r0, RB), r0); return 0
        lax.fori_loop(0, rows // RB, tile, 0)
    def valid_rows(r0):
        per = slots // RB
        b = r0 // slots
        return (iota((RB, 1), 0) + (r0 - b * slots + t * slots) < lens[b]).astype(F32)
    def out_proj():
        def proj(cols):
            acc[:, cols] = x_ref[:, cols].astype(F32) + dot(ar[...], w4[3, :, cols]) + cv[4:5, cols]
        col_tiles(proj)
        def norm(at, r0):
            xhat, rstd = norm_stats(acc[at, :])
            rs1[at, :] = rstd
            xh1[at, :] = xhat
            y = xhat * cv[0:1, :] + cv[5:6, :]
            yt[at, :] = y.astype(BF)
            acc[at, :] = y + cv[6:7, :]
        row_tiles(norm)
    def up(j):
        def tile(h, _):
            cols = pl.ds(pl.multiple_of(j * width + h * 256, 256), 256)
            u = dot(yt[...], wi[:, cols]) + bias[:, cols]
            phi = 0.5 * (1.0 + lax.erf(u * (0.5 ** 0.5)))
            gr[:, cols] = (u * phi).astype(BF)
            gp[:, cols] = phi + u * (jnp.exp(-0.5 * u * u) * 0.3989422804014327)
            return 0
        lax.fori_loop(0, width // 256, tile, 0, unroll=UNROLL)
    def down():
        def tile(cols): acc[:, cols] += dot(gr[...], wb[:, cols])
        col_tiles(tile)
    def cp_res(u):
        b, p = u // pairs, u % pairs
        return pltpu.make_async_copy(dq1.at[u], res_o.at[pl.ds(b * slots, slots), pl.ds(p * 128, 128)], rsem.at[0])
    def norm2():
        cp_cot().wait()
        vr[...] = jnp.zeros_like(vr)
        def norm(at, r0):
            xhat, rstd = norm_stats(acc[at, :])
            valid = valid_rows(r0)
            out = (xhat * cv[1:2, :] + cv[7:8, :]) * valid
            b = r0 // slots
            for p in range(pairs): dq1[b * pairs + p, pl.ds(pl.multiple_of(r0 - b * slots, RB), RB), :] = out[:, p * 128:(p + 1) * 128]
            dr = lhs[pl.ds(pl.multiple_of(rows + r0, RB), RB), :].astype(F32) * valid
            vr[1:2, :] += colsum(dr * xhat)
            vr[7:8, :] += colsum(dr)
            dh2 = norm_back(dr, cv[1:2, :], xhat, rstd)
            vr[6:7, :] += colsum(dh2)
            lhs[at, :] = dh2.astype(BF)
            acc[at, :] = dh2
        row_tiles(norm)
        for u in range(n): cp_res(u).start()
    def outer(dst, left, right):
        def tile(i, _):
            rows_ = pl.ds(pl.multiple_of(i * 256, 256), 256)
            lt = jnp.transpose(left[:, rows_])
            for h in range(0, width, 256): dst[rows_, pl.ds(h, 256)] = dot(lt, right[:, h:h + 256]).astype(BF)
            return 0
        lax.fori_loop(0, left.shape[1] // 256, tile, 0, unroll=UNROLL_T)
    def grad_back():
        outer(gb5, gr, lhs.at[pl.ds(0, rows)])
        for i in range(width // 256): lhs[pl.ds(rows, 256), pl.ds(256 * i, 256)] = jnp.transpose(yt[:, pl.ds(256 * i, 256)])
    def bwd(j):
        def tile(h, _):
            cols = pl.ds(pl.multiple_of(j * width + h * 256, 256), 256)
            du = gp[:, cols] * dot(lhs[pl.ds(0, rows), :], wb[cols, :], 1, 1)
            gbs[:, cols] = colsum(du)
            dur = du.astype(BF)
            gr[:, cols] = dur
            for i in range(width // 256): gi5[pl.ds(256 * i, 256), cols] = dot(lhs[pl.ds(rows, 256), pl.ds(256 * i, 256)], dur).astype(BF)
            return 0
        lax.fori_loop(0, width // 256, tile, 0, unroll=UNROLL)
    def dy():
        def tile(cols): acc[:, cols] += dot(gr[...], wi[cols, :], 1, 1)
        col_tiles(tile)
    def weight_grad(i, left, right): outer(g4.at[i], left, right)
    def norm1():
        def norm(at, r0):
            dy, xhat = acc[at, :], xh1[at, :]
            vr[0:1, :] += colsum(dy * xhat)
            vr[5:6, :] += colsum(dy)
            d = norm_back(dy, cv[0:1, :], xhat, rs1[at, :])
            vr[4:5, :] += colsum(d)
            acc[at, :] = d
            lhs[pl.ds(pl.multiple_of(rows + r0, RB), RB), :] = d.astype(BF)
        row_tiles(norm)
        def da_tile(cols):
            da = dot(lhs[pl.ds(rows, rows), :], w4[3, cols, :], 1, 1).astype(BF)
            for b in range(nseq): dpad[b, pl.ds(16, slots), cols] = da[b * slots:(b + 1) * slots]
        col_tiles(da_tile)
        dhalo.start()
    def units():
        pltpu.make_async_copy(dq1, dq1, rsem.at[0]).wait()
        def unit(u, _):
            b, p = u // pairs, u % pairs
            lanes = pl.ds(pl.multiple_of(p * 128, 128), 128)
            da = dpad[b, pl.ds(16, slots), lanes]
            pr = p1_s[u]
            e4[u // 3, u % 3, 0:64, :] = halves_diag(dot(pr.astype(BF), da, 0, 0))
            dp1 = dot(da, spread_diag(wz[u // 3, u % 3]), 1, 1)
            ds1 = (pr * (dp1 - seg_sum(dp1 * pr)) * scale).astype(BF)
            e6[u // 3, u % 3, 64:128, :] = halves_diag(dot(ds1, q_u[u], 0, 0)).astype(BF)
            dq1[u] = dot(ds1, spread_diag(km_u[u]))
            return 0
        lax.fori_loop(0, n, unit, 0, unroll=UNROLL)
        sum4.start()
    def grad_conv():
        wcp[...] = jnp.zeros_like(wcp)
        def unit(u, _):
            b, p = u // pairs, u % pairs
            lanes = pl.ds(pl.multiple_of(p * 128, 128), 128)
            v = vpad[b, :, lanes]
            turn = jnp.where(iota((slots, slots), 0) + iota((slots, slots), 1) == slots - 1, 1.0, 0.0).astype(BF)
            da = dot(turn, dpad[b, pl.ds(16, slots), lanes]).astype(BF)
            low = lane_low(da.shape)
            zero = jnp.zeros_like(da)
            for e in range(2):
                m = dot(jnp.where(low, da, zero) if e == 0 else jnp.where(low, zero, da), v, 1, 1)
                m = pltpu.roll(m, m.shape[1] - slots + 1, 1, stride=1, stride_axis=0)
                wcp[pl.ds(2 * p + e, 1), :] += colsum(m)
            return 0
        lax.fori_loop(0, n, unit, 0, unroll=UNROLL)
        vr[12:24, 0:128] = wcp[:, 0:128]
    def cb_a():
        st["G"], st["DP"] = [], []
        for i in R2:
            k = slot(i)
            dwz = e4[z, k, 0:64, :]
            nt = nts[i]
            den = mden[i, 1:2, :]
            dnt = mm(flip64(dwz), z6[i])
            dden = -colsum(dnt * nt) / den
            tile = jnp.zeros((16, 128), F32)
            row = iota((16, 128), 0)
            for j, v in enumerate((mden[i, 0:1, :], dden)):
                for q in range(3):
                    h = v.astype(BF).astype(F32)
                    tile = jnp.where(row == 3 * j + q, h, tile)
                    v = v - h
            sh5[z, k, 0:64, :] = (dnt / den).astype(BF)
            sh5[z, k, 64:80, :] = tile.astype(BF)
            st["G"].append(mm(flip64(nt), dwz, flip=True))
            st["DP"].append(jnp.zeros((64, 128), F32))
        share5.start()
    def cb(it):
        eye = eye_pair()
        G, DP = st["G"], st["DP"]
        Z = [sv[i, it, 0] for i in R2]; Pr = [sv[i, it, 1] for i in R2]; T2 = [sv[i, it, 2] for i in R2]; T3 = [sv[i, it, 3] for i in R2]
        d3 = [0.25 * mm(G[i], Z[i]) for i in R2]
        d2 = [-mm(d3[i], Pr[i]) for i in R2]
        dz = [0.25 * mm(T3[i], G[i]) for i in R2]
        dp = [-mm(T2[i], d3[i]) for i in R2]
        d1 = [-mm(d2[i], Pr[i]) for i in R2]
        dp = [dp[i] - mm(7.0 * eye - Pr[i], d2[i]) - d1[i] for i in R2]
        st["G"] = [dz[i] + mm(dp[i], p2s[i]) for i in R2]
        st["DP"] = [DP[i] + mm(Z[i], dp[i]) for i in R2]
    def cb_z():
        for i in R2:
            u = 3 * z + slot(i)
            p, g0 = p2s[i], st["G"][i]
            col = colsum(p)
            top = seg(jnp.max, col, -jnp.inf)
            f = 1.0 / top
            df = seg(jnp.sum, colsum(g0 * p), 0.0)
            hit = (col == top).astype(F32)
            dcol = -f * f * df * hit / seg(jnp.sum, hit, 0.0)
            dp = flip64(st["DP"][i]) + f * g0 + dcol
            ds = p * (dp - seg(jnp.sum, dp * p, 0.0)) * scale
            hi, lo = split(ds)
            b = spread_diag(km_u[u])
            core_g[i, 0:64, :] = dot(hi, b) + dot(lo, b)
            hi, lo = split(flip64(ds))
            b = spread_diag(qm_u[u])
            core_g[i, 64:128, :] = dot(hi, b) + dot(lo, b)
    def third_b():
        def unit(u, _):
            b, p = u // pairs, u % pairs
            tile = sh5[u // 3, u % 3, 64:80, :].astype(F32)
            m = tile[0:1] + tile[1:2] + tile[2:3]
            dden = tile[3:4] + tile[4:5] + tile[5:6]
            e = e3_s[u] * jnp.exp(ml_s[u, 0:1, :] - m)
            dn = spread_diag(sh5[u // 3, u % 3, 0:64, :])
            v = vpad[b, pl.ds(16, slots), pl.ds(pl.multiple_of(p * 128, 128), 128)]
            de = dot(v, dn) + dden
            p1_s[u] = dot(e.astype(BF), dn, 1, 1)
            ds = (e * de * scale).astype(BF)
            e6[u // 3, u % 3, 0:64, :] = halves_diag(dot(ds, k_u[u], 0, 0)).astype(BF)
            e3_s[u] = dot(ds, spread_diag(qm_u[u]))
            return 0
        lax.fori_loop(0, n, unit, 0, unroll=UNROLL)
        sum6.start()
    def conv():
        dhalo.end()
        def per(p, _):
            lanes = pl.ds(pl.multiple_of(p * 128, 128), 128)
            th = [split(skew(wrp[pl.ds(2 * p + e, 1), :], 256, slots)) for e in range(2)]
            low = lane_low((slots, 128))
            tot = jnp.zeros((1, 128), F32)
            for b in range(nseq):
                u = b * pairs + p
                d = dpad[b, :, lanes]
                c0 = dot(th[0][0], d) + dot(th[0][1], d)
                c1 = dot(th[1][0], d) + dot(th[1][1], d)
                v = (p1_s[u] + jnp.where(low, c0, c1)) * valid_of(b).astype(F32)
                tot = tot + colsum(v)
                yt[pl.ds(b * slots, slots), lanes] = v.astype(BF)
            vr[3:4, lanes] = tot
            return 0
        lax.fori_loop(0, pairs, per, 0, unroll=UNROLL)
    def own_marks():
        cn = counts(z // 2, 0, 64)
        for i in R2:
            k = slot(i)
            sh7[z, k, 0:64, :] = ((core_g[i, 0:64, :] + e6[z, k, 0:64, :].astype(F32)) / cn).astype(BF)
            sh7[z, k, 64:128, :] = ((core_g[i, 64:128, :] + e6[z, k, 64:128, :].astype(F32)) / cn).astype(BF)
        share7.start()
    def queries():
        def unit(u, _):
            b, p = u // pairs, u % pairs
            lanes = pl.ds(pl.multiple_of(p * 128, 128), 128)
            r0 = pl.multiple_of(b * slots, slots)
            mb = memb[pl.ds(pl.multiple_of(64 * b, 64), 64), :]
            q = dot(mb, sh7[u // 3, u % 3, 0:64, :], 0, 0) + dq1[u]
            k = dot(mb, sh7[u // 3, u % 3, 64:128, :], 0, 0) + e3_s[u]
            lhs[pl.ds(r0, slots), lanes] = q.astype(BF)
            lhs[pl.ds(rows + r0, slots), lanes] = k.astype(BF)
            vr[2:3, lanes] += colsum(q)
            return 0
        lax.fori_loop(0, n, unit, 0, unroll=UNROLL)
    def gx1():
        def tile(cols): acc[:, cols] += dot(yt[...], w4[2, cols, :], 1, 1)
        col_tiles(tile)
    def cp_gx(): return pltpu.make_async_copy(acc, gx_o, osem.at[1])
    def gx2():
        def tile(cols):
            acc[:, cols] += dot(lhs[pl.ds(0, rows), :], w4[0, cols, :], 1, 1) + dot(lhs[pl.ds(rows, rows), :], w4[1, cols, :], 1, 1)
        col_tiles(tile)
        cp_gx().start()
    px = s + 1 - 2 * (s % 2)
    py = (s + 2) % 4
    def cp_v(i):
        dst, dev = ((va, (s, 2 * z + 1 - c)), (vx, (px, t)), (vy, (py, t)))[i]
        return remote(vr, dst, vs.at[i], vq.at[i], *dev)
    def cp_vz(d): return remote(vr, vz.at[z], vs.at[2 + d], vq.at[3 + z], s, 2 * ((z + d) % 4) + c)
    def vec_0():
        for i in range(nff): vr[8 + i:9 + i, :] = gbs[:, pl.ds(i * width, width)]
        cp_v(0).start(FIRST)
    def vec_step(i):
        cp_v(i).wait()
        vr[...] = vr[...] + (va, vx, vy)[i][...]
        if i < 2: cp_v(i + 1).start(FIRST)
        else:
            for d in (1, 2, 3): cp_vz(d).start(FIRST)
    def vec_z():
        for d in (1, 2, 3):
            zz = (z + d) % 4
            remote(vr, vz.at[zz], vs.at[2 + d], vq.at[3 + zz], s, 2 * zz + c).wait_recv()
        for d in (1, 2, 3): cp_vz(d).wait_send()
        vz[z] = vr[...]
        sums[...] = ((vz[0] + vz[1]) + vz[2]) + vz[3]
    halo.zero(); dhalo.zero()
    half = n // 2
    P_ = functools.partial
    steps = [P_(g.run, k, i) for k in range(len(views)) for i in range(Gather.STAGES)] + [P_(g.arrive, k) for k in range(len(views))]
    nk = 8 + nff
    steps += [P_(rs.run, k, i) for k in range(nk) for i in range(Scatter.STAGES)]
    steps += [P_(newton, i) for i in range(ITERS)] + [P_(cb, ITERS - 1 - i) for i in range(ITERS)] + [P_(up, j) for j in range(nff)] + [P_(bwd, j) for j in range(nff)]
    steps += [P_(vec_step, i) for i in range(3)]
    steps += [xm_part, xm_b, xm_c, xm_d, xm_e, vectors, projections, third, P_(first, 0, half), P_(first, half, n), core_a, e2.mid, e2.end, core_z, e3.mid, e3.end, attention, out_proj,
              down, norm2, grad_back, dy, norm1, P_(weight_grad, 0, ar, lhs.at[pl.ds(rows, rows)]), units, sum4.mid, grad_conv, sum4.end, cb_a, share5.mid, cb_z, share5.end, third_b,
              conv, sum6.mid, gx1, sum6.end, own_marks, P_(weight_grad, 1, x_ref, yt), share7.mid, share7.end, queries, P_(weight_grad, 2, x_ref, lhs.at[pl.ds(rows, rows)]),
              P_(weight_grad, 3, x_ref, lhs.at[pl.ds(0, rows)]), vec_0, gx2, vec_z]
    for i in order: steps[i]()
    o = [pltpu.make_async_copy(gp.at[pl.ds(a, m), pl.ds(b, w)], dst, osem.at[2 + i]) for i, (a, m, b, w, dst) in enumerate((
        (0, 4 * sub, 0, width, ob_o), (4 * sub, sub, 0, ff, oi_o), (5 * sub, sub, 0, width, oo_o), (5 * sub, sub, width, width, ov_o),
        (5 * sub, sub, 2 * width, width, ok_o), (5 * sub, sub, 3 * width, width, oq_o)))]
    o.append(pltpu.make_async_copy(sums, sums_o, osem.at[8]))
    for cp in o: cp.start()
    g.drain(); e2.drain(); e3.drain(); halo.drain()
    cp_xa().wait_send()
    for d in (1, 2, 3):
        cp_xb(d).wait_send(); cp_xm(d).wait_send()
    for zz in range(4): cp_xc(zz).wait_send()
    rs.drain(nk)
    sum4.drain(); share5.drain(); sum6.drain(); share7.drain(); dhalo.drain()
    cp_gx().wait()
    for cp in o: cp.wait()

def whole(lengths, x, cot, wc, shards, order=ORDER):
    S = jax.ShapeDtypeStruct
    rows, width = x.shape
    wq, wk, wv, wo, win, wback, bin_, gains, shifts = shards
    nseq = lengths.shape[0]
    slots = rows // nseq
    sub, ff = wq.shape[0], win.shape[1]
    n = nseq * width // 128
    nk = 8 + ff // width
    na = 1 + len(CHUNKS)
    V = lambda *sh: pltpu.VMEM(sh, F32)
    B = lambda *sh: pltpu.VMEM(sh, BF)
    D = lambda *sh: pltpu.SemaphoreType.DMA(sh)
    vm = pl.BlockSpec(memory_space=pltpu.VMEM); hb = pl.BlockSpec(memory_space=pl.ANY)
    return pl.pallas_call(
        functools.partial(body, tuple(order)),
        out_shape=(S((rows, width), F32),) * 2 + (S((sub, width), F32),) * 4 + (S((sub, ff), F32), S((4 * sub, width), F32), S((24, width), F32)),
        in_specs=[pl.BlockSpec(memory_space=pltpu.SMEM), vm, hb, vm] + [hb] * 6 + [vm] * 3,
        out_specs=(hb,) * 9,
        scratch_shapes=[B(4, sub, width), B(sub, ff), B(4 * sub, width), V(16, 128), V(4, 4, 2, 16, 128), B(4, width, width), B(width, ff), B(ff, width), B(rows + 128 * nseq, width),
                        V(2, 64, width), V(64, width), V(4, 16, width), V(2, 4, 16, width), V(4, 3, 72, 128), V(4, 2, 72, 128), V(4, 2, 72, 128),
                        B(n, slots, 128), B(n, slots, 128), B(nseq, 256, width), B(n, 64, 128), B(n, 64, 128), V(n, slots, 128), V(n, slots, 128), V(n, 8, 128),
                        B(4, 3, 64, 128), V(2, ITERS, 4, 64, 128), V(2, 64, 128), V(2, 64, 128), V(2, 64, 128), V(2, 8, 128), V(8, width), V(1, ff), V(wc.shape[0], 256), V(wc.shape[0], 256),
                        B(rows, width), B(rows, width), B(rows, ff), V(rows, ff), V(1, ff), V(rows, 1), V(rows, width), V(rows, width),
                        B(ff, width), B(width, ff), B(4, width, width), B(nseq, 256, width), V(4, 3, 64, 128), V(4, 2, 64, 128), V(4, 2, 64, 128), B(4, 3, 128, 128), B(4, 2, 128, 128), B(4, 2, 128, 128), B(4, 3, 80, 128),
                        V(2, 128, 128), B(4, 3, 128, 128), V(n, slots, 128), B(64 * nseq, slots),
                        B(nk, 4, 4, sub, width), B(nk, 2, 4, sub, width), B(nk, 4, sub, width), B(nk, 4, sub, width),
                        V(24, width), V(24, width), V(24, width), V(24, width), V(4, 24, width), V(24, width),
                        D(na, 9), D(na), D(na, 2), D(na), D(na), D(na), D(na), D(11), D(13), D(2), D(2, 2), D(3, 2), D(4, 2), D(2, 2),
                        D(nk), D(nk), D(nk), D(nk, 2), D(nk), D(nk), D(nk), D(nk), D(2), D(2, 2), D(2), D(2, 2), D(3, 2), D(4, 2), D(3, 2), D(4, 2), D(2, 2),
                        D(6), D(7), D(9), D(1)],
        compiler_params=pltpu.CompilerParams(collective_id=0, has_side_effects=True, vmem_limit_bytes=67043328),
        name="layer_whole",
    )(lengths, x, cot, wc, wq, wk, wv, wo, win, wback, bin_, gains, shifts)


def hand_out(taps, *refs):
    big, sums_ref = refs[:8], refs[8]
    outs, (conv_o, bias_o, gains_o, shifts_o) = refs[9:17], refs[17:21]
    bufs, sums, sin, sout = refs[21:29], refs[29], refs[30], refs[31]
    a = [pltpu.make_async_copy(r, b, sin.at[i]) for i, (r, b) in enumerate(zip((*big, sums_ref), (*bufs, sums)))]
    o = [pltpu.make_async_copy(b, r, sout.at[i]) for i, (r, b) in enumerate(zip(outs, bufs))]
    for cp in a: cp.start()
    me = lax.axis_index("seq") * 8 + lax.axis_index("tok")
    sub = gains_o.shape[1]
    width = sums.shape[1]
    a[8].wait()
    v = pltpu.roll(sums[0:8, :], (width - sub * me) % width, 1)
    gains_o[...] = v[0:2, 0:sub]
    shifts_o[...] = v[2:8, 0:sub]
    f4 = bias_o.shape[1]
    per = width // f4
    row = lax.broadcasted_iota(jnp.int32, (4, width), 0)
    b = jnp.sum(jnp.where(row == me // per, sums[8:12, :], 0.0), axis=0, keepdims=True)
    b = pltpu.roll(jnp.broadcast_to(b, (8, width)), (width - f4 * (me % per)) % width, 1)
    bias_o[...] = b[0:1, 0:f4]
    conv_o[...] = sums[12:24, 0:taps]
    for i in range(8):
        a[i].wait()
        o[i].start()
    for cp in o: cp.wait()

def finish(big, sums, taps):
    S = jax.ShapeDtypeStruct
    width = sums.shape[1]
    sub = width // 32
    vm = pl.BlockSpec(memory_space=pltpu.VMEM); hb = pl.BlockSpec(memory_space=pl.ANY)
    return pl.pallas_call(
        functools.partial(hand_out, taps),
        out_shape=tuple(S(b.shape, F32) for b in big) + (S((12, taps), F32), S((1, 4 * sub), F32), S((2, sub), F32), S((6, sub), F32)),
        in_specs=[hb] * 9,
        out_specs=(hb,) * 8 + (vm,) * 4,
        scratch_shapes=[pltpu.VMEM(b.shape, F32) for b in big] + [pltpu.VMEM(sums.shape, F32), pltpu.SemaphoreType.DMA((9,)), pltpu.SemaphoreType.DMA((8,))],
        name="hand_out",
    )(*big, sums)


def fast_shards(inputs, lengths, bounds, w_query, w_key, w_value, w_out, w_conv, w_in, w_back, b_in, gains, shifts, cotangent):
    shape = inputs.shape
    x = inputs.reshape(-1, shape[2])
    owned = (w_query, w_key, w_value, w_out, w_in, w_back, b_in.reshape(1, -1), gains, shifts)
    *big, sums = whole(lengths, x, cotangent.reshape(x.shape), w_conv, owned)
    res, gx, gq, gk, gv, go, gi, gb, conv, bias, gain, shift = finish(big, sums, w_conv.shape[1])
    return (res.reshape(shape), gx.reshape(shape), gq, gk, gv, go, conv, gi, gb, bias.reshape(-1), gain, shift)


def solution(mesh):
    placed = (
        P("seq", "tok", None),
        P("seq"),
        P("seq", None),
        P(("seq", "tok"), None),
        P(("seq", "tok"), None),
        P(("seq", "tok"), None),
        P(("seq", "tok"), None),
        P(),
        P(("seq", "tok"), None),
        P(("seq", "tok"), None),
        P(("seq", "tok")),
        P(None, ("seq", "tok")),
        P(None, ("seq", "tok")),
        P("seq", "tok", None),
    )
    return jax.shard_map(
        fast_shards if (mesh.shape["seq"], mesh.shape["tok"]) == (4, 8) else shards,
        mesh=mesh,
        in_specs=placed,
        out_specs=(
            P("seq", "tok", None),
            P("seq", "tok", None),
            P(("seq", "tok"), None),
            P(("seq", "tok"), None),
            P(("seq", "tok"), None),
            P(("seq", "tok"), None),
            P(),
            P(("seq", "tok"), None),
            P(("seq", "tok"), None),
            P(("seq", "tok")),
            P(None, ("seq", "tok")),
            P(None, ("seq", "tok")),
        ),
        check_vma=False,
    )
```

```python
import functools

import jax
import jax.numpy as jnp
from jax import lax
from jax.experimental import pallas as pl
from jax.experimental.pallas import tpu as pltpu
from jax.sharding import PartitionSpec as P

ITERS = 6


EPSILON = 1e-05
EXACT_PRECISION = lax.Precision.HIGHEST


def padded_2(cells, sides, width):
    for axis, dim in sides:
        count = lax.axis_size(axis)
        ends = count - 1
        head = lax.slice_in_dim(cells, 0, width, axis=dim)
        tail = lax.slice_in_dim(cells, cells.shape[dim] - width, cells.shape[dim], axis=dim)
        cells = jnp.concatenate(
            [
                lax.ppermute(tail, axis, [(i, (i + 1) % count) for i in range(ends)]),
                cells,
                lax.ppermute(head, axis, [((i + 1) % count, i) for i in range(ends)]),
            ],
            axis=dim,
        )
    return cells


def layer_norm(hidden, gain_row, shift_row):
    center = hidden - jnp.mean(hidden, axis=-1, keepdims=True)
    spread = jnp.mean(center * center, axis=-1, keepdims=True)
    return center * lax.rsqrt(spread + EPSILON) * gain_row + shift_row


def newton_inverse(kernel):
    column_sum = jnp.sum(kernel, axis=-2)
    factor = 1.0 / jnp.max(column_sum, axis=-1)
    approx = jnp.swapaxes(kernel, -1, -2) * factor[..., None, None]
    identity = jnp.eye(kernel.shape[-1], dtype=jnp.float32)
    for sweep_index in range(ITERS):
        product = jnp.matmul(kernel, approx, precision=EXACT_PRECISION)
        inner_term = 7.0 * identity - product
        inner_term = 15.0 * identity - jnp.matmul(product, inner_term, precision=EXACT_PRECISION)
        inner_term = 13.0 * identity - jnp.matmul(product, inner_term, precision=EXACT_PRECISION)
        approx = 0.25 * jnp.matmul(approx, inner_term, precision=EXACT_PRECISION)
    return approx


def mixer_core(query_marks, key_marks, numerator, denom):
    score_scale_factor = query_marks.shape[-1] ** (-0.5)
    scores = (
        jnp.einsum("bihd,bjhd->bhij", query_marks, key_marks, precision=EXACT_PRECISION)
        * score_scale_factor
    )
    middle = jax.nn.softmax(scores, axis=-1)
    pseudo = newton_inverse(middle)
    summary = numerator / denom[..., None]
    return jnp.einsum("bhij,bhjd->bhid", pseudo, summary, precision=EXACT_PRECISION)


def gelu_exact(pre_act):
    return jax.nn.gelu(pre_act, approximate=False)


def product_low(pattern, left, right):
    return jnp.einsum(pattern, left, right, preferred_element_type=jnp.float32)


def shards(
    inputs,
    lengths,
    bounds,
    w_query,
    w_key,
    w_value,
    w_out,
    w_conv,
    w_in,
    w_back,
    b_in,
    gains,
    shifts,
    cotangent,
):
    seq_count, slot_count, model_width = inputs.shape
    head_count, tap_count = w_conv.shape
    head_dim = model_width // head_count
    rim_width = tap_count // 2
    mark_count = bounds.shape[1] - 1
    row_count = seq_count * slot_count
    score_scale_factor = head_dim ** (-0.5)
    first_slot = lax.axis_index("tok") * slot_count
    position = first_slot + jnp.arange(slot_count, dtype=jnp.int32)
    valid_mask = (position[None, :] < lengths[:, None]).astype(jnp.float32)
    member = (
        (position[None, None, :] >= bounds[:, :-1, None])
        & (position[None, None, :] < bounds[:, 1:, None])
    ).astype(jnp.float32)
    part_count = (bounds[:, 1:] - bounds[:, :-1]).astype(jnp.float32)
    gathered = (
        lax.all_gather(w_query.astype(jnp.bfloat16), ("seq", "tok"), axis=0, tiled=True),
        lax.all_gather(w_key.astype(jnp.bfloat16), ("seq", "tok"), axis=0, tiled=True),
        lax.all_gather(w_value.astype(jnp.bfloat16), ("seq", "tok"), axis=0, tiled=True),
        lax.all_gather(w_out.astype(jnp.bfloat16), ("seq", "tok"), axis=0, tiled=True),
        lax.all_gather(w_in.astype(jnp.bfloat16), ("seq", "tok"), axis=0, tiled=True),
        lax.all_gather(w_back.astype(jnp.bfloat16), ("seq", "tok"), axis=0, tiled=True),
        lax.all_gather(b_in.astype(jnp.bfloat16), ("seq", "tok"), axis=0, tiled=True),
        lax.all_gather(gains.astype(jnp.bfloat16), ("seq", "tok"), axis=1, tiled=True),
        lax.all_gather(shifts.astype(jnp.bfloat16), ("seq", "tok"), axis=1, tiled=True),
    )
    query_mat, key_mat, value_mat, out_mat, in_mat, back_mat, bias_vec, gain_vec, shift_vec = (
        gathered
    )
    bias_rows = bias_vec.astype(jnp.float32)
    gain_rows = gain_vec.astype(jnp.float32)
    shift_rows = shift_vec.astype(jnp.float32)
    flat_rows = inputs.reshape(row_count, model_width)
    query_rows = jnp.dot(flat_rows, query_mat, preferred_element_type=jnp.float32) + shift_rows[0]
    key_rows = jnp.dot(flat_rows, key_mat, preferred_element_type=jnp.float32)
    value_rows = jnp.dot(flat_rows, value_mat, preferred_element_type=jnp.float32) + shift_rows[1]
    part_query = jnp.einsum(
        "bms,bsd->bmd",
        member,
        query_rows.reshape(seq_count, slot_count, model_width),
        precision=EXACT_PRECISION,
    )
    part_key = jnp.einsum(
        "bms,bsd->bmd",
        member,
        key_rows.reshape(seq_count, slot_count, model_width),
        precision=EXACT_PRECISION,
    )
    sum_query, sum_key = lax.psum((part_query, part_key), "tok")
    mark_query = (
        (sum_query / part_count[..., None])
        .astype(jnp.bfloat16)
        .reshape(seq_count, mark_count, head_count, head_dim)
    )
    mark_key = (
        (sum_key / part_count[..., None])
        .astype(jnp.bfloat16)
        .reshape(seq_count, mark_count, head_count, head_dim)
    )
    query_head_rows = query_rows.astype(jnp.bfloat16).reshape(
        seq_count, slot_count, head_count, head_dim
    )
    key_head_rows = key_rows.astype(jnp.bfloat16).reshape(
        seq_count, slot_count, head_count, head_dim
    )
    v_low = (value_rows.reshape(seq_count, slot_count, model_width) * valid_mask[..., None]).astype(
        jnp.bfloat16
    )
    value_head_rows = v_low.reshape(seq_count, slot_count, head_count, head_dim)
    first_score_matrix = (
        product_low("bshd,bmhd->bshm", query_head_rows, mark_key) * score_scale_factor
    )
    first_score_kernel = jax.nn.softmax(first_score_matrix, axis=-1)
    first_low = first_score_kernel.astype(jnp.bfloat16)
    third_score_matrix = (
        product_low("bmhd,bshd->bhms", mark_query, key_head_rows) * score_scale_factor
    )
    third_score_matrix = jnp.where(valid_mask[:, None, None, :] > 0, third_score_matrix, -1e30)
    score_top = lax.pmax(jnp.max(third_score_matrix, axis=-1), "tok")
    third_exponential = jnp.exp(third_score_matrix - score_top[..., None])
    third_low = third_exponential.astype(jnp.bfloat16)
    numerator, denom = lax.psum(
        (
            product_low("bhms,bshd->bhmd", third_low, value_head_rows),
            jnp.sum(third_exponential, axis=-1),
        ),
        "tok",
    )
    mixed_output, core_back = jax.vjp(
        mixer_core, mark_query.astype(jnp.float32), mark_key.astype(jnp.float32), numerator, denom
    )
    mixed_low = mixed_output.astype(jnp.bfloat16)
    attention_forward = product_low("bshm,bhmd->bshd", first_low, mixed_low)
    padded = padded_2(v_low, (("tok", 1),), rim_width)
    padded_heads = padded.astype(jnp.float32).reshape(
        seq_count, slot_count + 2 * rim_width, head_count, head_dim
    )
    conv_out = jnp.zeros_like(attention_forward)
    for offset in range(tap_count):
        conv_out = (
            conv_out
            + w_conv[:, offset][None, None, :, None] * padded_heads[:, offset : offset + slot_count]
        )
    mix_low = (attention_forward + conv_out).reshape(row_count, model_width).astype(jnp.bfloat16)
    first_sum = (
        flat_rows.astype(jnp.float32)
        + jnp.dot(mix_low, out_mat, preferred_element_type=jnp.float32)
        + shift_rows[2]
    )
    normed, norm_one_back = jax.vjp(layer_norm, first_sum, gain_rows[0], shift_rows[3])
    normed_low = normed.astype(jnp.bfloat16)
    pre_act = jnp.dot(normed_low, in_mat, preferred_element_type=jnp.float32) + bias_rows
    active, gelu_back = jax.vjp(gelu_exact, pre_act)
    active_low = active.astype(jnp.bfloat16)
    second_sum = (
        normed + jnp.dot(active_low, back_mat, preferred_element_type=jnp.float32) + shift_rows[4]
    )
    final_raw, norm_two_back = jax.vjp(layer_norm, second_sum, gain_rows[1], shift_rows[5])
    valid_rows = valid_mask.reshape(row_count, 1)
    result = final_raw * valid_rows
    back_weights = (
        lax.all_gather(w_query.astype(jnp.bfloat16), ("seq", "tok"), axis=0, tiled=True),
        lax.all_gather(w_key.astype(jnp.bfloat16), ("seq", "tok"), axis=0, tiled=True),
        lax.all_gather(w_value.astype(jnp.bfloat16), ("seq", "tok"), axis=0, tiled=True),
        lax.all_gather(w_out.astype(jnp.bfloat16), ("seq", "tok"), axis=0, tiled=True),
        lax.all_gather(w_in.astype(jnp.bfloat16), ("seq", "tok"), axis=0, tiled=True),
        lax.all_gather(w_back.astype(jnp.bfloat16), ("seq", "tok"), axis=0, tiled=True),
    )
    query_back, key_back, value_back, out_back, in_back, back_back = back_weights
    grad_out = cotangent.reshape(row_count, model_width).astype(jnp.float32) * valid_rows
    grad_second, grad_gain_two, grad_shift_five = norm_two_back(grad_out)
    grad_second_low = grad_second.astype(jnp.bfloat16)
    grad_shift_four = jnp.sum(grad_second, axis=0)
    grad_w_back = product_low("rf,rd->fd", active_low, grad_second_low)
    grad_active = product_low("rd,fd->rf", grad_second_low, back_back)
    (grad_pre,) = gelu_back(grad_active)
    grad_pre_low = grad_pre.astype(jnp.bfloat16)
    grad_b_in = jnp.sum(grad_pre, axis=0)
    grad_w_in = product_low("rd,rf->df", normed_low, grad_pre_low)
    grad_normed = grad_second + product_low("rf,df->rd", grad_pre_low, in_back)
    grad_first, grad_gain_one, grad_shift_three = norm_one_back(grad_normed)
    grad_proj_low = grad_first.astype(jnp.bfloat16)
    grad_shift_two = jnp.sum(grad_first, axis=0)
    grad_w_out = product_low("rd,re->de", mix_low, grad_proj_low)
    grad_mix_low = (
        product_low("re,de->rd", grad_proj_low, out_back)
        .astype(jnp.bfloat16)
        .reshape(seq_count, slot_count, model_width)
    )
    grad_mix_heads = grad_mix_low.reshape(seq_count, slot_count, head_count, head_dim)
    grad_mixed_part = product_low("bshm,bshd->bhmd", first_low, grad_mix_heads)
    grad_first_kernel = product_low("bshd,bhmd->bshm", grad_mix_heads, mixed_low)
    inner_sum = jnp.sum(grad_first_kernel * first_score_kernel, axis=-1, keepdims=True)
    grad_first_low = (
        first_score_kernel * (grad_first_kernel - inner_sum) * score_scale_factor
    ).astype(jnp.bfloat16)
    part_grad_key = product_low("bshm,bshd->bmhd", grad_first_low, query_head_rows)
    grad_mixed, grad_mk_first = lax.psum((grad_mixed_part, part_grad_key), "tok")
    grad_mq_core, grad_mk_core, grad_numer, grad_denom = core_back(grad_mixed)
    grad_numer_low = grad_numer.astype(jnp.bfloat16)
    grad_third_exp = (
        product_low("bhmd,bshd->bhms", grad_numer_low, value_head_rows) + grad_denom[..., None]
    )
    grad_v_heads = product_low("bhms,bhmd->bshd", third_low, grad_numer_low)
    grad_third_low = (third_exponential * grad_third_exp * score_scale_factor).astype(jnp.bfloat16)
    part_grad_query = product_low("bhms,bshd->bmhd", grad_third_low, key_head_rows)
    grad_key_heads = product_low("bhms,bmhd->bshd", grad_third_low, mark_query)
    grad_mq_third = lax.psum(part_grad_query, "tok")
    grad_mq = (grad_mq_core + grad_mq_third).reshape(
        seq_count, mark_count, model_width
    ) / part_count[..., None]
    grad_mk = (grad_mk_core + grad_mk_first).reshape(
        seq_count, mark_count, model_width
    ) / part_count[..., None]
    grad_query = jnp.einsum(
        "bms,bmd->bsd", member, grad_mq, precision=EXACT_PRECISION
    ) + product_low("bshm,bmhd->bshd", grad_first_low, mark_key).reshape(
        seq_count, slot_count, model_width
    )
    grad_key = jnp.einsum(
        "bms,bmd->bsd", member, grad_mk, precision=EXACT_PRECISION
    ) + grad_key_heads.reshape(seq_count, slot_count, model_width)
    grad_padded = padded_2(grad_mix_low, (("tok", 1),), rim_width)
    grad_pad_heads = grad_padded.astype(jnp.float32).reshape(
        seq_count, slot_count + 2 * rim_width, head_count, head_dim
    )
    grad_mix_float = grad_mix_heads.astype(jnp.float32)
    grad_conv_v = jnp.zeros_like(grad_mix_float)
    conv_terms = []
    for offset in range(tap_count):
        start_at = 2 * rim_width - offset
        grad_conv_v = (
            grad_conv_v
            + w_conv[:, offset][None, None, :, None]
            * grad_pad_heads[:, start_at : start_at + slot_count]
        )
        conv_terms.append(
            jnp.sum(padded_heads[:, offset : offset + slot_count] * grad_mix_float, axis=(0, 1, 3))
        )
    grad_w_conv = lax.psum(jnp.stack(conv_terms, axis=1), ("seq", "tok"))
    grad_value = (grad_v_heads + grad_conv_v).reshape(
        seq_count, slot_count, model_width
    ) * valid_mask[..., None]
    grad_query_flat = grad_query.reshape(row_count, model_width)
    grad_key_flat = grad_key.reshape(row_count, model_width)
    grad_value_flat = grad_value.reshape(row_count, model_width)
    grad_query_low = grad_query_flat.astype(jnp.bfloat16)
    grad_key_low = grad_key_flat.astype(jnp.bfloat16)
    grad_value_low = grad_value_flat.astype(jnp.bfloat16)
    grad_w_query = product_low("rd,re->de", flat_rows, grad_query_low)
    grad_w_key = product_low("rd,re->de", flat_rows, grad_key_low)
    grad_w_value = product_low("rd,re->de", flat_rows, grad_value_low)
    grad_input = (
        grad_first
        + product_low("re,de->rd", grad_query_low, query_back)
        + product_low("re,de->rd", grad_key_low, key_back)
        + product_low("re,de->rd", grad_value_low, value_back)
    )
    grad_gains = jnp.stack([grad_gain_one, grad_gain_two], axis=0)
    grad_shifts = jnp.stack(
        [
            jnp.sum(grad_query_flat, axis=0),
            jnp.sum(grad_value_flat, axis=0),
            grad_shift_two,
            grad_shift_three,
            grad_shift_four,
            grad_shift_five,
        ],
        axis=0,
    )
    (
        owned_query,
        owned_key,
        owned_value,
        owned_out,
        owned_in,
        owned_back,
        owned_bias,
        owned_gains,
        owned_shifts,
    ) = (
        lax.psum_scatter(grad_w_query, ("seq", "tok"), scatter_dimension=0, tiled=True),
        lax.psum_scatter(grad_w_key, ("seq", "tok"), scatter_dimension=0, tiled=True),
        lax.psum_scatter(grad_w_value, ("seq", "tok"), scatter_dimension=0, tiled=True),
        lax.psum_scatter(grad_w_out, ("seq", "tok"), scatter_dimension=0, tiled=True),
        lax.psum_scatter(grad_w_in, ("seq", "tok"), scatter_dimension=0, tiled=True),
        lax.psum_scatter(grad_w_back, ("seq", "tok"), scatter_dimension=0, tiled=True),
        lax.psum_scatter(grad_b_in, ("seq", "tok"), scatter_dimension=0, tiled=True),
        lax.psum_scatter(grad_gains, ("seq", "tok"), scatter_dimension=1, tiled=True),
        lax.psum_scatter(grad_shifts, ("seq", "tok"), scatter_dimension=1, tiled=True),
    )
    return (
        result.reshape(seq_count, slot_count, model_width),
        grad_input.reshape(seq_count, slot_count, model_width),
        owned_query,
        owned_key,
        owned_value,
        owned_out,
        grad_w_conv,
        owned_in,
        owned_back,
        owned_bias,
        owned_gains,
        owned_shifts,
    )


F32 = jnp.float32


BF = jnp.bfloat16


def dot(a, b, ca=1, cb=0):
    return lax.dot_general(a, b, (((ca,), (cb,)), ((), ())), preferred_element_type=F32)


def lane_low(shape):
    return lax.broadcasted_iota(jnp.int32, shape, len(shape) - 1) % 128 < 64


def halves_diag(m):
    low = lane_low((64, 128))
    return jnp.where(low, m[:64], m[64:])


def spread_diag(v):
    low = lane_low(v.shape)
    zero = jnp.zeros_like(v)
    return jnp.concatenate([jnp.where(low, v, zero), jnp.where(low, zero, v)], axis=0)


def seg(op, v, fill):
    low = lane_low(v.shape)
    a = op(jnp.where(low, v, fill), axis=-1, keepdims=True)
    b = op(jnp.where(low, fill, v), axis=-1, keepdims=True)
    return jnp.where(low, a, b)


def split(v):
    hi = v.astype(BF)
    return hi, (v - hi.astype(F32)).astype(BF)


def norm_stats(h):
    center = h - jnp.mean(h, axis=-1, keepdims=True)
    spread = jnp.mean(center * center, axis=-1, keepdims=True)
    rstd = lax.rsqrt(spread + 1e-05)
    return center * rstd, rstd


def norm_back(dy, gain, xhat, rstd):
    d = dy * gain
    a = jnp.mean(d, axis=-1, keepdims=True)
    b = jnp.mean(d * xhat, axis=-1, keepdims=True)
    return rstd * (d - a - xhat * b)


def skew(row, width, count):
    return pltpu.roll(jnp.broadcast_to(row, (count, width)), 0, 1, stride=1, stride_axis=0)


def colsum(v):
    return jnp.sum(v, axis=0, keepdims=True)


MESH = pl.DeviceIdType.MESH


FIRST = 0


def place():
    s = lax.axis_index("seq"); t = lax.axis_index("tok")
    x, y, z, c = s % 2, s // 2, t // 2, t % 2
    px = s + 1 - 2 * x
    py = (s + 2) % 4
    p1 = px * (1 - c) + py * c
    p2 = py * (1 - c) + px * c
    return s, z, c, p1, p2


def remote(src, dst, send, recv, seq, tok):
    return pltpu.make_async_remote_copy(src_ref=src, dst_ref=dst, send_sem=send, recv_sem=recv,
                                        device_id={"seq": seq, "tok": tok}, device_id_type=MESH)


def greet(s, z, c, p1, p2):
    bar = pltpu.get_barrier_semaphore()
    def sig(seq, tok):
        pl.semaphore_signal(bar, inc=1, device_id={"seq": seq, "tok": tok}, device_id_type=MESH)
    t = 2 * z + c
    sig(p1, t); sig(p2, t); sig(s, 2 * z + 1 - c)
    for d in (1, 2, 3):
        sig(s, 2 * ((z + d) % 4) + c)
    @pl.when(((c == 1) & (z < 3)) | ((c == 0) & (z > 0)))
    def _(): sig(s, t + 2 * c - 1)
    edge = c * (6 - z) // 4 + (1 - c) * ((z + 3) // 4)
    return 6 + edge


def each_slot(c, f):
    f(0)
    @pl.when(c == 0)
    def _(): f(1)


class UnitSum:
    def __init__(self, src, ra, rb, sems, where, combine):
        self.__dict__.update(locals())
        self.sa, self.qa, self.sb, self.qb = sems
    def cp_a(self, c):
        s, z, cc, _, _ = self.where
        if c == 0:
            return remote(self.src.at[:, pl.ds(2, 1)], self.ra.at[:, pl.ds(0, 1)], self.sa, self.qa, s, 2 * z + 1)
        return remote(self.src.at[:, pl.ds(0, 2)], self.ra, self.sa, self.qa, s, 2 * z)
    def cp_b(self, d, i):
        s, z, c, _, _ = self.where
        zz = (z + d) % 4
        return remote(self.src.at[zz, 2 * c + i], self.rb.at[z, i], self.sb.at[i], self.qb.at[i], s, 2 * zz + c)
    def start(self):
        for k in (0, 1):
            @pl.when(self.where[2] == k)
            def _(): self.cp_a(k).start(FIRST)
    def mid(self):
        s, z, c, _, _ = self.where
        for k in (0, 1):
            @pl.when(c == k)
            def _(): self.cp_a(1 - k).wait_recv()
        def comb(zz):
            each_slot(c, lambda i: self.combine(self.src.at[zz, 2 * c + i], self.ra.at[zz, i]))
        for d in (2, 1, 3):
            comb((z + d) % 4)
            each_slot(c, lambda i: self.cp_b(d, i).start(FIRST))
        comb(z)
    def three(self, i):
        s, z, c, _, _ = self.where
        return remote(self.src.at[pl.ds(0, 3), 2 * c + i], self.rb.at[pl.ds(0, 3), i], self.sb.at[i], self.qb.at[i], s, 2 * z + 1 - c)
    def end(self):
        s, z, c, _, _ = self.where
        def f(i):
            self.three(i).wait_recv()
            for d in (1, 3, 2): self.combine(self.src.at[z, 2 * c + i], self.rb.at[(z + d) % 4, i])
        each_slot(c, f)
    def drain(self):
        c = self.where[2]
        for k in (0, 1):
            @pl.when(c == k)
            def _(): self.cp_a(k).wait_send()
        each_slot(c, lambda i: self.three(i).wait_send())


class UnitShare:
    def __init__(self, buf, sems, where):
        self.__dict__.update(locals())
        self.sz, self.qz, self.sc, self.qc = sems
    def cp_z(self, d, i):
        s, z, c, _, _ = self.where
        b = self.buf.at[z, 2 * c + i]
        return remote(b, b, self.sz.at[i], self.qz.at[z, i], s, 2 * ((z + d) % 4) + c)
    def cp_c(self, zz, i):
        s, z, c, _, _ = self.where
        b = self.buf.at[zz, 2 * c + i]
        return remote(b, b, self.sc.at[i], self.qc.at[i], s, 2 * z + 1 - c)
    def start(self):
        z, c = self.where[1], self.where[2]
        def f(i):
            for d in (2, 1, 3): self.cp_z(d, i).start(FIRST)
            self.cp_c(z, i).start(FIRST)
        each_slot(c, f)
    def mid(self):
        s, z, c, _, _ = self.where
        for d in (1, 3, 2):
            zz = (z + d) % 4
            def f(i):
                b = self.buf.at[zz, 2 * c + i]
                remote(b, b, self.sz.at[i], self.qz.at[zz, i], s, 2 * zz + c).wait_recv()
                self.cp_c(zz, i).start(FIRST)
            each_slot(c, f)
    def end(self):
        s, z, c, _, _ = self.where
        def f(i):
            b = self.buf.at[:, 2 * (1 - c) + i]
            remote(b, b, self.sc.at[i], self.qc.at[i], s, 2 * z + 1 - c).wait_recv()
        each_slot(1 - c, f)
    def drain(self):
        s, z, c, _, _ = self.where
        def f(i):
            b = self.buf.at[pl.ds(0, 3), 2 * c + i]
            remote(b, b, self.sz.at[i], self.qc.at[i], s, 2 * z + 1 - c).wait_send()
            b = self.buf.at[:, 2 * c + i]
            remote(b, b, self.sc.at[i], self.qc.at[i], s, 2 * z + 1 - c).wait_send()
        each_slot(c, f)


class Halo:
    def __init__(self, buf, slots, send, recv, where):
        self.__dict__.update(locals())
        s, z, c, _, _ = where
        self.t = 2 * z + c
    def cps(self):
        s, n = self.where[0], self.slots
        up = remote(self.buf.at[:, pl.ds(n, 16)], self.buf.at[:, pl.ds(0, 16)], self.send.at[0], self.recv.at[0], s, self.t + 1)
        down = remote(self.buf.at[:, pl.ds(16, 16)], self.buf.at[:, pl.ds(16 + n, 16)], self.send.at[1], self.recv.at[1], s, self.t - 1)
        return up, down
    def zero(self):
        n = self.slots
        a, _, d = self.buf.shape
        self.buf[:, 16 + n:, :] = jnp.zeros((a, 256 - 16 - n, d), BF)
        self.buf[:, 0:16, :] = jnp.zeros((a, 16, d), BF)
    def start(self):
        up, down = self.cps()
        @pl.when(self.t < 7)
        def _(): up.start(FIRST)
        @pl.when(self.t > 0)
        def _(): down.start(FIRST)
    def end(self):
        up, down = self.cps()
        @pl.when(self.t > 0)
        def _(): up.wait_recv()
        @pl.when(self.t < 7)
        def _(): down.wait_recv()
    def drain(self):
        up, down = self.cps()
        @pl.when(self.t < 7)
        def _(): up.wait_send()
        @pl.when(self.t > 0)
        def _(): down.wait_send()


def mm(a, b, flip=False):
    ah, al = split(a)
    bh, bl = split(spread_diag(b))
    if flip:
        return dot(ah, bh, 1, 1) + (dot(ah, bl, 1, 1) + dot(al, bh, 1, 1))
    return dot(jnp.concatenate([ah, ah, al], axis=1), jnp.concatenate([bh, bl, bh], axis=0))


def flip64(a):
    t = jnp.transpose(a)
    return jnp.concatenate([t[:64], t[64:]], axis=1)


def eye_pair():
    i = lax.broadcasted_iota(jnp.int32, (64, 128), 0)
    j = lax.broadcasted_iota(jnp.int32, (64, 128), 1)
    return jnp.where(i == j % 64, 1.0, 0.0).astype(F32)


def soft_combine(dst, other):
    m1, m2 = dst[64:65, :], other[64:65, :]
    m = jnp.maximum(m1, m2)
    a, b = jnp.exp(m1 - m), jnp.exp(m2 - m)
    dst[0:64, :] = dst[0:64, :] * a + other[0:64, :] * b
    dst[65:66, :] = dst[65:66, :] * a + other[65:66, :] * b
    dst[64:65, :] = m


def core_setup(qm, km):
    p2 = dot(qm, spread_diag(km), 1, 1) * (64 ** -0.5)
    e = jnp.exp(p2 - seg(jnp.max, p2, -jnp.inf))
    p2 = e / seg(jnp.sum, e, 0.0)
    factor = 1.0 / seg(jnp.max, colsum(p2), -jnp.inf)
    return p2, flip64(p2) * factor


def seg_sum(v):
    i = lax.broadcasted_iota(jnp.int32, (128, 128), 0)
    j = lax.broadcasted_iota(jnp.int32, (128, 128), 1)
    ones = jnp.where(i // 64 == j // 64, 1.0, 0.0).astype(BF)
    hi, lo = split(v)
    return dot(hi, ones) + dot(lo, ones)

def plain_add(dst, other):
    dst[...] = (dst[...].astype(F32) + other[...].astype(F32)).astype(dst.dtype)

class Gather:
    STAGES = 9
    def __init__(self, views, owns, last, sems, where):
        self.__dict__.update(locals())
        self.qa, self.qb, self.sz, self.s1, self.s2, self.sc, self.sl = sems
        s, z, c, p1, p2 = where
        t = 2 * z + c
        self.line = ((s, t + 2), (s, t - 2))
        self.d1, self.d2, self.dc = (p1, t), (p2, t), (s, 2 * z + 1 - c)
    def at(self, k, s_, z_, c_):
        return self.views[k](s_, z_, c_)
    def cp(self, k, s_, zz, send, got, dev, src=None):
        dst = self.at(k, s_, zz, self.where[2])
        return remote(dst if src is None else src, dst, send, self.qa.at[k, got], *dev)
    def to_z(self, k, zz, way, src=None): return self.cp(k, self.where[0], zz, self.sz.at[k, way], zz, self.line[way], src)
    def to_1(self, k, zz, src=None): return self.cp(k, self.where[0], zz, self.s1.at[k], 4 + zz, self.d1, src)
    def to_2(self, k, g, zz, src=None): return self.cp(k, self.where[3 if g else 0], zz, self.s2.at[k], 8, self.d2, src)
    def several(self, k, s_, zz, send, got): return self.cp(k, s_, zz, send, got, self.dc)
    def local(self, k):
        s, z, c, _, _ = self.where
        return pltpu.make_async_copy(self.owns(k), self.at(k, s, z, c), self.sl.at[k])
    def col(self, k, s_):
        b = self.at(k, s_, slice(None), self.where[2])
        return remote(b, b, self.sc.at[k], self.qb.at[k], *self.dc)
    def pair(self, d, f):
        z = self.where[1]
        if d == 0:
            f(z, 2); return
        @pl.when(z >= d)
        def _(): f(z - d, 0)
        @pl.when(z + d <= 3)
        def _(): f(z + d, 1)
    def plane_z(self, k, zz, way):
        return self.cp(k, slice(None), zz, self.sz.at[k, way], zz, self.line[way])
    def run_last(self, k, i):
        s, z, c, p1, p2 = self.where
        every = slice(None)
        if i == 0:
            self.local(k).start()
            self.to_2(k, 0, z, self.owns(k)).start(); self.to_1(k, z, self.owns(k)).start()
        elif i == 1:
            self.several(k, p1, z, self.s1.at[k], 4 + z).wait_recv()
            self.to_2(k, 1, z).start()
        elif i == 2:
            self.several(k, pl.ds(0, 2), z, self.s2.at[k], 8).wait_recv()
            self.local(k).wait()
            @pl.when(z < 3)
            def _(): self.plane_z(k, z, 0).start()
            @pl.when(z > 0)
            def _(): self.plane_z(k, z, 1).start()
        elif i < 6:
            def f(zz, side):
                self.several(k, every, zz, self.sz.at[k, 0], zz).wait_recv()
                if side == 0 and i < 5:
                    @pl.when(z < 3)
                    def _(): self.plane_z(k, zz, 0).start()
                if side == 1 and i < 5:
                    @pl.when(z > 0)
                    def _(): self.plane_z(k, zz, 1).start()
            self.pair(i - 2, f)
            if i == 5:
                b = self.at(k, every, every, c)
                remote(b, b, self.sc.at[k], self.qb.at[k], *self.dc).start()
    def run(self, k, i):
        if k in self.last: return self.run_last(k, i)
        s, z, c, p1, p2 = self.where
        if i < 4:
            def f(zz, side):
                src = None
                if side == 2:
                    src = self.owns(k)
                    self.local(k).start()
                else:
                    self.several(k, s, zz, self.s1.at[k], zz).wait_recv()
                if side != 1 and i < 3:
                    @pl.when(z < 3)
                    def _(): self.to_z(k, zz, 0, src).start()
                if side != 0 and i < 3:
                    @pl.when(z > 0)
                    def _(): self.to_z(k, zz, 1, src).start()
                self.to_2(k, 0, zz, src).start(); self.to_1(k, zz, src).start()
            self.pair(i, f)
            if i == 3:
                self.local(k).wait()
                self.col(k, s).start()
        elif i < 8:
            def f(zz, side):
                self.several(k, p1, zz, self.s1.at[k], 4 + zz).wait_recv()
                self.to_2(k, 1, zz).start()
            self.pair(i - 4, f)
            if i == 7: self.col(k, p1).start()
        else:
            self.several(k, pl.ds(0, 2), slice(None), self.s2.at[k], 8).wait_recv()
            for s_ in (p2, 3 - s): self.col(k, s_).start()
    def arrive(self, k):
        b = self.at(k, slice(None), slice(None), 1 - self.where[2])
        remote(b, b, self.sc.at[k], self.qb.at[k], *self.dc).wait_recv()
    def drain(self):
        s, z, c, p1, p2 = self.where
        every = slice(None)
        for k in range(len(self.views)):
            self.several(k, every, every, self.sc.at[k], 8).wait_send()
            last = k in self.last
            self.several(k, s, z if last else every, self.s1.at[k], 8).wait_send()
            self.several(k, pl.ds(0, 2), z if last else every, self.s2.at[k], 8).wait_send()
            line = every if last else s
            for q in range(3):
                @pl.when(z == q)
                def _(): self.several(k, line, pl.ds(0, q + 1), self.sz.at[k, 0], 8).wait_send()
                @pl.when(z == 3 - q)
                def _(): self.several(k, line, pl.ds(0, q + 1), self.sz.at[k, 1], 8).wait_send()

class Scatter:
    STAGES = 5
    def __init__(self, part, outs, zfirst, bufs, sems, where):
        self.__dict__.update(locals())
        self.rcb, self.r2, self.r1, self.rz = bufs
        self.s_c, self.q_c, self.s_2, self.q_2, self.s_1, self.q_1, self.s_z, self.q_z = sems
        s, z, c, p1, p2 = where
        t = 2 * z + c
        self.d1, self.d2, self.dc = (p1, t), (p2, t), (s, 2 * z + 1 - c)
    def own(self, k, *at): return self.part(k, self.where[2], *at)
    def cp_c(self, k): return remote(self.part(k, 1 - self.where[2]), self.rcb.at[k], self.s_c.at[k], self.q_c.at[k], *self.dc)
    def cp_2(self, k, g):
        b = self.where[4] if g == 0 else 3 - self.where[0]
        return remote(self.own(k, b), self.r2.at[k, g], self.s_2.at[k], self.q_2.at[k, g], *self.d2)
    def cp_1(self, k): return remote(self.own(k, self.where[3]), self.r1.at[k], self.s_1.at[k], self.q_1.at[k], *self.d1)
    def cp_z(self, k, d):
        s, z, c, p1, p2 = self.where
        zz = (z + d) % 4
        return remote(self.own(k, s, zz), self.rz.at[k, z], self.s_z.at[k], self.q_z.at[k], s, 2 * zz + c)
    def three(self, k):
        return remote(self.own(k, self.where[0], pl.ds(0, 3)), self.rz.at[k, pl.ds(0, 3)], self.s_z.at[k], self.q_z.at[k], *self.dc)
    def add4(self, k, i, v):
        a = self.own(k, i)
        a[...] = a[...] + v
    def first_z(self, k, d):
        s, z, c, p1, p2 = self.where
        dst = self.r1.at[k] if d == 3 else self.r2.at[k, d - 1]
        return remote(self.own(k, slice(None), (z + d) % 4), dst, self.s_z.at[k], self.q_z.at[k], s, 2 * ((z + d) % 4) + c)
    def first_2(self, k, g):
        b = self.where[4] if g == 0 else 3 - self.where[0]
        return remote(self.own(k, b, self.where[1]), self.rz.at[k, g], self.s_2.at[k], self.q_2.at[k, g], *self.d2)
    def first_1(self, k): return remote(self.own(k, self.where[3], self.where[1]), self.rz.at[k, 2], self.s_1.at[k], self.q_1.at[k], *self.d1)
    def twelve(self, k): return remote(self.own(k, pl.ds(0, 3)), self.rcb.at[k, pl.ds(0, 3)], self.s_z.at[k], self.q_z.at[k], *self.dc)
    def run_first(self, k, i):
        s, z, c, p1, p2 = self.where
        if i == 0:
            self.cp_c(k).start()
        elif i == 1:
            self.cp_c(k).wait_recv()
            for j in range(4): self.add4(k, j, self.rcb[k, j])
            for d in (2, 1, 3): self.first_z(k, d).start()
        elif i == 2:
            self.twelve(k).wait_recv()
            a = self.own(k, slice(None), z)
            tot = (a[...].astype(F32) + self.r2[k, 0].astype(F32)) + (self.r2[k, 1].astype(F32) + self.r1[k].astype(F32))
            a[...] = tot.astype(BF)
            for g in (1, 0): self.first_2(k, g).start()
        elif i == 3:
            for g, b in ((1, p1), (0, s)):
                self.first_2(k, g).wait_recv()
                a = self.own(k, b, z)
                a[...] = a[...] + self.rz[k, g]
                if g: self.first_1(k).start()
        else:
            self.first_1(k).wait_recv()
            self.outs(k)[...] = self.own(k, s, z)[...].astype(F32) + self.rz[k, 2].astype(F32)
    def run(self, k, i):
        if k in self.zfirst: return self.run_first(k, i)
        s, z, c, p1, p2 = self.where
        if i == 0:
            self.cp_c(k).start()
        elif i == 1:
            self.cp_c(k).wait_recv()
            for g, b in ((1, 3 - s), (0, p2)):
                self.add4(k, b, self.rcb[k, b])
                self.cp_2(k, g).start()
            for b in (p1, s): self.add4(k, b, self.rcb[k, b])
        elif i == 2:
            self.cp_2(k, 1).wait_recv()
            self.add4(k, p1, self.r2[k, 1])
            self.cp_1(k).start()
            self.cp_2(k, 0).wait_recv()
            self.add4(k, s, self.r2[k, 0])
        elif i == 3:
            self.cp_1(k).wait_recv()
            self.add4(k, s, self.r1[k])
            for d in (2, 1, 3): self.cp_z(k, d).start()
        else:
            self.three(k).wait_recv()
            tot = self.own(k, s, z)[...].astype(F32)
            for d in (1, 3, 2): tot = tot + self.rz[k, (z + d) % 4].astype(F32)
            self.outs(k)[...] = tot
    def drain(self, n):
        for k in range(n):
            self.cp_c(k).wait_send()
            if k in self.zfirst:
                self.twelve(k).wait_send(); self.first_1(k).wait_send()
                remote(self.own(k, 0, pl.ds(0, 2)), self.rz.at[k, pl.ds(0, 2)], self.s_2.at[k], self.q_2.at[k, 0], *self.d2).wait_send()
                continue
            remote(self.own(k, pl.ds(0, 2)), self.r2.at[k], self.s_2.at[k], self.q_2.at[k, 0], *self.d2).wait_send()
            self.cp_1(k).wait_send()
            self.three(k).wait_send()

CHUNKS = (("w", 1, 1), ("w", 0, 1), ("w", 2, 1), ("w", 3, 1), ("i", 0, 1), ("b", 0, 2), ("b", 1, 2))
LINE_LAST = (4,)
LINE_FIRST = ()
ORDER = (
    0, 9, 167, 18, 27, 4, 1, 36, 13, 10, 19, 22, 28, 2, 5, 168, 37, 11, 31, 20, 14, 3, 29, 45, 23, 32, 12, 15,
    21, 6, 7, 30, 33, 24, 54, 169, 38, 16, 25, 46, 34, 49, 55, 58, 170, 171, 39, 50, 17, 8, 47, 26, 73, 35, 72, 172,
    56, 59, 74, 63, 75, 173, 174, 51, 177, 67, 140, 178, 48, 40, 175, 64, 57, 141, 142, 143, 144, 145, 52, 176, 60, 68, 179, 180,
    61, 41, 42, 43, 44, 65, 76, 181, 66, 69, 53, 182, 183, 184, 70, 62, 77, 154, 155, 71, 78, 152, 153, 79, 185, 186, 187, 80,
    85, 156, 157, 95, 158, 81, 159, 86, 188, 189, 82, 191, 192, 87, 83, 193, 162, 110, 90, 161, 105, 96, 88, 163, 111, 190, 194, 84,
    91, 97, 120, 106, 160, 195, 196, 146, 147, 112, 100, 148, 149, 89, 150, 98, 101, 151, 197, 198, 92, 113, 115, 199, 200, 201, 116, 202,
    203, 93, 206, 107, 114, 121, 99, 102, 125, 126, 204, 205, 108, 117, 94, 103, 122, 118, 207, 208, 209, 212, 213, 164, 109, 123, 211, 127,
    210, 130, 135, 104, 165, 131, 128, 166, 119, 136, 124, 132, 129, 137, 133, 138, 214, 134, 139,
)
UNROLL = True
UNROLL_T = 3

def body(order, lens, x_ref, cot_ref, wc_ref, wq_ref, wk_ref, wv_ref, wo_ref, win_ref, wback_ref, bin_ref, gains_ref, shifts_ref,
         res_o, gx_o, oq_o, ok_o, ov_o, oo_o, oi_o, ob_o, sums_o,
         own4, owni, ownb, ownv, vec, w4, wi, wb, lhs, xs, xa, xb, xm, nu, ra, rb, q_u, k_u, vpad, qm_u, km_u, p1_s, e3_s, ml_s, wz, sv, p2s, z6, nts, mden, cv, bias, wcp, wrp,
         ar, yt, gr, gp, gbs, rs1, acc, xh1, gb5, gi5, g4, dpad, e4, ra4, rb4, e6, ra6, rb6, sh5, core_g, sh7, dq1, memb, rcb, r2, r1b, rz, vr, va, vx, vy, vz, sums,
         qa, qb, sz, s1, s2, sc, sl, e0s, e0q, ua, ub, ug, uh, hs, s_c, q_c, s_2, q_2, s_1, q_1, s_z, q_z, va4, vb4, v6a, v6b, ug5, uh5, u7, u7h, hs2, vs, vq, osem, rsem):
    where = place()
    s, z, c, p1, p2 = where
    t = 2 * z + c
    nseq = vpad.shape[0]
    rows, width = x_ref.shape
    slots = rows // nseq
    pairs = width // 128
    n = nseq * pairs
    heads = 2 * pairs
    taps = wc_ref.shape[1]
    ff = wi.shape[1]
    nff = ff // width
    sub = wq_ref.shape[0]
    scale = 64 ** -0.5
    i32 = jnp.int32
    iota = lambda shape, d: lax.broadcasted_iota(i32, shape, d)
    four = [pltpu.make_async_copy(r, gp.at[pl.ds(sub, sub), pl.ds(i * width, width)], osem.at[i]) for i, r in enumerate((wq_ref, wk_ref, wv_ref, wo_ref))]
    four.append(pltpu.make_async_copy(win_ref, gp.at[pl.ds(0, sub)], osem.at[4]))
    four.append(pltpu.make_async_copy(wback_ref, gp.at[pl.ds(2 * sub, 4 * sub), pl.ds(0, width)], osem.at[5]))
    for cp in four: cp.start()
    greeted = greet(*where)
    for pad in (vpad, dpad):
        pad[:, 16 + slots:, :] = jnp.zeros((nseq, pad.shape[1] - 16 - slots, width), BF)
        pad[:, 0:16, :] = jnp.zeros((nseq, 16, width), BF)
    ownv[...] = jnp.zeros_like(ownv)
    ownv[0:2, 0:sub] = gains_ref[...]
    ownv[2:8, 0:sub] = shifts_ref[...]
    ownv[8:9, 0:4 * sub] = bin_ref[...]
    def edges(b, first, count):
        j = iota((count, 1), 0) + first
        return lax.shift_right_logical(j * lens[b], 6), lax.shift_right_logical((j + 1) * lens[b], 6)
    def counts(b, first, count):
        lo, hi = edges(b, first, count)
        return (hi - lo).astype(F32)
    def valid_of(b): return iota((slots, 1), 0) + t * slots < lens[b]
    def valid_all(): return jnp.concatenate([valid_of(b).astype(F32) for b in range(nseq)], axis=0)
    for b in range(nseq):
        lo, hi = edges(b, 0, 64)
        pos = iota((64, slots), 1) + t * slots
        memb[pl.ds(64 * b, 64), :] = jnp.where((pos >= lo) & (pos < hi), 1.0, 0.0).astype(BF)
    wcp[...] = jnp.zeros_like(wcp); wrp[...] = jnp.zeros_like(wrp)
    wcp[:, 0:taps] = wc_ref[...]
    w0 = wcp[:, 0:128]
    a1 = w0.astype(BF); rest = w0 - a1.astype(F32); a2 = rest.astype(BF); a3 = (rest - a2.astype(F32)).astype(BF)
    turn = jnp.where(iota((128, 128), 0) + iota((128, 128), 1) == taps - 1, 1.0, 0.0).astype(BF)
    wrp[:, 0:128] = (dot(a1, turn) + dot(a2, turn)) + dot(a3, turn)
    for cp in four: cp.wait()
    for i in range(4): own4[i] = gp[pl.ds(sub, sub), pl.ds(i * width, width)].astype(BF)
    owni[...] = gp[pl.ds(0, sub), :].astype(BF)
    ownb[...] = gp[pl.ds(2 * sub, 4 * sub), pl.ds(0, width)].astype(BF)
    pl.semaphore_wait(pltpu.get_barrier_semaphore(), greeted)
    chip = 2 * sub
    wv, iv, bv = w4.reshape(4, 4, 4, chip, width), wi.reshape(4, 4, chip, ff), wb.reshape(4, 4, 4 * chip, width)
    giv, gbv, gwv = gi5.reshape(4, 4, chip, ff), gb5.reshape(4, 4, 4 * chip, width), g4.reshape(4, 4, 4, chip, width)
    def span(c_, step, lo, cnt): return pl.ds(pl.multiple_of(c_ * step + lo, 8), cnt)
    views, srcs = [lambda s_, z_, c_: vec.at[s_, z_, c_]], [ownv]
    for kind, lo, cnt in CHUNKS:
        if kind == "w":
            views.append(lambda s_, z_, c_, lo=lo, cnt=cnt: wv.at[pl.ds(lo, cnt), s_, z_, span(c_, sub, 0, sub)])
            srcs.append(own4.at[pl.ds(lo, cnt)])
        elif kind == "i":
            m = ff // cnt
            views.append(lambda s_, z_, c_, lo=lo, m=m: iv.at[s_, z_, span(c_, sub, 0, sub), pl.ds(lo * m, m)])
            srcs.append(owni.at[:, pl.ds(lo * m, m)])
        else:
            m = 4 * sub // cnt
            views.append(lambda s_, z_, c_, lo=lo, m=m: bv.at[s_, z_, span(c_, 4 * sub, lo * m, m)])
            srcs.append(ownb.at[pl.ds(lo * m, m)])
    g = Gather(views, lambda k: srcs[k], LINE_LAST, (qa, qb, sz, s1, s2, sc, sl), where)
    e2 = UnitSum(nu, ra, rb, (ua.at[0], ua.at[1], ub.at[0], ub.at[1]), where, soft_combine)
    e3 = UnitShare(wz, (ug.at[0], uh, ug.at[1], ug.at[2]), where)
    halo = Halo(vpad, slots, hs.at[0], hs.at[1], where)
    dhalo = Halo(dpad, slots, hs2.at[0], hs2.at[1], where)
    sum4 = UnitSum(e4, ra4, rb4, (va4.at[0], va4.at[1], vb4.at[0], vb4.at[1]), where, plain_add)
    share5 = UnitShare(sh5, (ug5.at[0], uh5, ug5.at[1], ug5.at[2]), where)
    sum6 = UnitSum(e6, ra6, rb6, (v6a.at[0], v6a.at[1], v6b.at[0], v6b.at[1]), where, plain_add)
    share7 = UnitShare(sh7, (u7.at[0], u7h, u7.at[1], u7.at[2]), where)
    def part(k, c_, *at):
        at = (*at, *((slice(None),) * (2 - len(at))))
        if k < 4: return gbv.at[(*at, span(c_, 4 * sub, k * sub, sub))]
        if k < 4 + nff: return giv.at[(*at, span(c_, sub, 0, sub), pl.ds((k - 4) * width, width))]
        return gwv.at[(k - 4 - nff, *at, span(c_, sub, 0, sub))]
    def outs(k):
        if k < 4: return gp.at[pl.ds(k * sub, sub), pl.ds(0, width)]
        if k < 4 + nff: return gp.at[pl.ds(4 * sub, sub), pl.ds((k - 4) * width, width)]
        return gp.at[pl.ds(5 * sub, sub), pl.ds((k - 4 - nff) * width, width)]
    rs = Scatter(part, outs, LINE_FIRST, (rcb, r2, r1b, rz), (s_c, q_c, s_2, q_2, s_1, q_1, s_z, q_z), where)
    def xm_part():
        for b in range(nseq):
            xs[b] = dot(memb[pl.ds(64 * b, 64), :], x_ref[pl.ds(slots * b, slots), :])
        cp_xa().start(FIRST)
    def cp_xa(): return remote(xs.at[1 - c], xa, e0s.at[0], e0q.at[0], s, 2 * z + 1 - c)
    def cp_xb(d):
        zz = (z + d) % 4
        return remote(xs.at[c, pl.ds(pl.multiple_of(16 * zz, 16), 16)], xb.at[z], e0s.at[d], e0q.at[1 + z], s, 2 * zz + c)
    def cp_xm(d):
        return remote(xm.at[c, z], xm.at[c, z], e0s.at[3 + d], e0q.at[5 + z], s, 2 * ((z + d) % 4) + c)
    def cp_xc(zz):
        return remote(xm.at[c, zz], xm.at[c, zz], e0s.at[7 + zz], e0q.at[9 + zz], s, 2 * z + 1 - c)
    def xm_b():
        cp_xa().wait_recv()
        xs[c] = xs[c] + xa[...]
        for d in (2, 1, 3): cp_xb(d).start(FIRST)
    def xm_c():
        tot = xs[c, pl.ds(pl.multiple_of(16 * z, 16), 16), :]
        for d in (1, 3, 2):
            zz = (z + d) % 4
            remote(xb.at[zz], xb.at[zz], e0s.at[d], e0q.at[1 + zz], s, 2 * zz + c).wait_recv()
            tot = tot + xb[zz]
        xm[c, z] = tot / counts(c, 16 * z, 16)
        for d in (2, 1, 3): cp_xm(d).start(FIRST)
        cp_xc(z).start(FIRST)
    def xm_d():
        for d in (1, 3, 2):
            zz = (z + d) % 4
            remote(xm.at[c, zz], xm.at[c, zz], e0s.at[3 + d], e0q.at[5 + zz], s, 2 * zz + c).wait_recv()
            cp_xc(zz).start(FIRST)
    def xm_e():
        for zz in range(4):
            b = xm.at[1 - c, zz]
            remote(b, b, e0s.at[7 + zz], e0q.at[9 + zz], s, 2 * z + 1 - c).wait_recv()
        hi, lo = split(xm[...].reshape(64 * nseq, width))
        lhs[pl.ds(0, rows), :] = x_ref[...]
        lhs[pl.ds(rows, 64 * nseq), :] = hi
        lhs[pl.ds(rows + 64 * nseq, 64 * nseq), :] = lo
    def vectors():
        v = vec[...].reshape(32, 16, 128)
        def spread_rows(row, group, dst, at, count):
            for h in range(0, count, 256):
                k = iota((128, 256), 0); l = iota((128, 256), 1) + h
                w = dot(row, jnp.where((l % group == k) & (k < group), 1.0, 0.0).astype(BF)).reshape(32, 8, 256)
                mine = iota((32, 8, 256), 0) == (iota((32, 8, 256), 2) + h) // group
                dst(h, jnp.sum(jnp.where(mine, w, 0.0), axis=0))
        def to_cv(h, w): cv[:, pl.ds(h, 256)] = w
        def to_bias(h, w): bias[:, pl.ds(h, 256)] = w[0:1]
        spread_rows(v[:, 0:8, :].reshape(256, 128).astype(BF), sub, to_cv, 0, width)
        spread_rows(v[:, 8:16, :].reshape(256, 128).astype(BF), 4 * sub, to_bias, 0, ff)
    def projections():
        m_n = 64 * nseq
        valid = valid_all()
        for h in range(0, width, 256):
            cols = pl.ds(h, 256)
            v = ((dot(x_ref[...], w4[2, :, cols]) + cv[3:4, cols]) * valid).astype(BF)
            for b in range(nseq): vpad[b, pl.ds(16, slots), cols] = v[b * slots:(b + 1) * slots]
        halo.start()
        for i, (dst, marks) in ((1, (k_u, km_u)), (0, (q_u, qm_u))):
            for h in range(0, width, 256):
                cols = pl.ds(h, 256)
                r = dot(lhs[...], w4[i, :, cols])
                a = r[:rows]
                m = r[rows:rows + m_n] + r[rows + m_n:]
                if i == 0:
                    a = a + cv[2:3, cols]
                    m = m + cv[2:3, cols]
                a = a.astype(BF); m = m.astype(BF)
                for b in range(nseq):
                    for q in range(2):
                        u = b * pairs + h // 128 + q
                        dst[u] = a[b * slots:(b + 1) * slots, q * 128:(q + 1) * 128]
                        marks[u] = m[b * 64:(b + 1) * 64, q * 128:(q + 1) * 128]
    def cp_cot(): return pltpu.make_async_copy(cot_ref, lhs.at[pl.ds(rows, rows)], osem.at[0])
    def third():
        cp_cot().start()
        def unit(u, _):
            b, p = u // pairs, u % pairs
            ok = valid_of(b)
            sc3 = jnp.where(ok, dot(k_u[u], spread_diag(qm_u[u]), 1, 1) * scale, -1e30)
            m = jnp.max(sc3, axis=0, keepdims=True)
            e = jnp.where(ok, jnp.exp(sc3 - m), 0.0)
            e3_s[u] = e
            ml_s[u] = jnp.broadcast_to(m, (8, 128))
            v = vpad[b, pl.ds(16, slots), pl.ds(pl.multiple_of(p * 128, 128), 128)]
            nu[u // 3, u % 3, 0:64, :] = halves_diag(dot(v, e.astype(BF), 0, 0))
            nu[u // 3, u % 3, 64:72, :] = jnp.broadcast_to(m, (8, 128))
            nu[u // 3, u % 3, 65:66, :] = colsum(e)
            return 0
        lax.fori_loop(0, n, unit, 0, unroll=UNROLL)
        e2.start()
    def first(lo, hi):
        def unit(u, _):
            sc1 = dot(q_u[u], spread_diag(km_u[u]), 1, 1) * scale
            e = jnp.exp(sc1 - seg(jnp.max, sc1, -jnp.inf))
            pr = e / seg_sum(e)
            p1_s[u] = pr
            return 0
        lax.fori_loop(lo, hi, unit, 0, unroll=UNROLL)
    st = {}
    R2 = range(2)
    def slot(i): return 2 * c + i * (1 - c)
    def core_a():
        st["P"], st["Z"] = [], []
        for i in R2:
            pp, zz = core_setup(qm_u[3 * z + slot(i)], km_u[3 * z + slot(i)])
            p2s[i] = pp
            st["P"].append(pp); st["Z"].append(zz)
    def newton(it):
        eye = eye_pair()
        P, Z = st["P"], st["Z"]
        pr = [mm(P[i], Z[i]) for i in R2]
        t2 = [15.0 * eye - mm(pr[i], 7.0 * eye - pr[i]) for i in R2]
        t3 = [13.0 * eye - mm(pr[i], t2[i]) for i in R2]
        for i in R2:
            sv[i, it, 0] = Z[i]; sv[i, it, 1] = pr[i]; sv[i, it, 2] = t2[i]; sv[i, it, 3] = t3[i]
        st["Z"] = [0.25 * mm(Z[i], t3[i]) for i in R2]
    def core_z():
        for i in R2:
            k = slot(i)
            z6[i] = st["Z"][i]
            nt = nu[z, k, 0:64, :] / nu[z, k, 65:66, :]
            nts[i] = nt
            mden[i] = nu[z, k, 64:72, :]
            wz[z, k] = mm(st["Z"][i], nt, flip=True).astype(BF)
        e3.start()
    def attention():
        halo.end()
        def per(p, _):
            lanes = pl.ds(pl.multiple_of(p * 128, 128), 128)
            th = [split(skew(wcp[pl.ds(2 * p + e, 1), :], 256, slots)) for e in range(2)]
            low = lane_low((slots, 128))
            for b in range(nseq):
                u = b * pairs + p
                v = vpad[b, :, lanes]
                c0 = dot(th[0][0], v) + dot(th[0][1], v)
                c1 = dot(th[1][0], v) + dot(th[1][1], v)
                a = dot(p1_s[u].astype(BF), spread_diag(wz[u // 3, u % 3]))
                ar[pl.ds(b * slots, slots), lanes] = (a + jnp.where(low, c0, c1)).astype(BF)
            return 0
        lax.fori_loop(0, pairs, per, 0, unroll=UNROLL)
    def col_tiles(f):
        def tile(j, _):
            f(pl.ds(pl.multiple_of(j * 256, 256), 256)); return 0
        lax.fori_loop(0, width // 256, tile, 0, unroll=UNROLL)
    RB = 64
    def row_tiles(f):
        def tile(j, _):
            r0 = pl.multiple_of(j * RB, RB)
            f(pl.ds(r0, RB), r0); return 0
        lax.fori_loop(0, rows // RB, tile, 0)
    def valid_rows(r0):
        per = slots // RB
        b = r0 // slots
        return (iota((RB, 1), 0) + (r0 - b * slots + t * slots) < lens[b]).astype(F32)
    def out_proj():
        def proj(cols):
            acc[:, cols] = x_ref[:, cols].astype(F32) + dot(ar[...], w4[3, :, cols]) + cv[4:5, cols]
        col_tiles(proj)
        def norm(at, r0):
            xhat, rstd = norm_stats(acc[at, :])
            rs1[at, :] = rstd
            xh1[at, :] = xhat
            y = xhat * cv[0:1, :] + cv[5:6, :]
            yt[at, :] = y.astype(BF)
            acc[at, :] = y + cv[6:7, :]
        row_tiles(norm)
    def up(j):
        def tile(h, _):
            cols = pl.ds(pl.multiple_of(j * width + h * 256, 256), 256)
            u = dot(yt[...], wi[:, cols]) + bias[:, cols]
            phi = 0.5 * (1.0 + lax.erf(u * (0.5 ** 0.5)))
            gr[:, cols] = (u * phi).astype(BF)
            gp[:, cols] = phi + u * (jnp.exp(-0.5 * u * u) * 0.3989422804014327)
            return 0
        lax.fori_loop(0, width // 256, tile, 0, unroll=UNROLL)
    def down():
        def tile(cols): acc[:, cols] += dot(gr[...], wb[:, cols])
        col_tiles(tile)
    def cp_res(u):
        b, p = u // pairs, u % pairs
        return pltpu.make_async_copy(dq1.at[u], res_o.at[pl.ds(b * slots, slots), pl.ds(p * 128, 128)], rsem.at[0])
    def norm2():
        cp_cot().wait()
        vr[...] = jnp.zeros_like(vr)
        def norm(at, r0):
            xhat, rstd = norm_stats(acc[at, :])
            valid = valid_rows(r0)
            out = (xhat * cv[1:2, :] + cv[7:8, :]) * valid
            b = r0 // slots
            for p in range(pairs): dq1[b * pairs + p, pl.ds(pl.multiple_of(r0 - b * slots, RB), RB), :] = out[:, p * 128:(p + 1) * 128]
            dr = lhs[pl.ds(pl.multiple_of(rows + r0, RB), RB), :].astype(F32) * valid
            vr[1:2, :] += colsum(dr * xhat)
            vr[7:8, :] += colsum(dr)
            dh2 = norm_back(dr, cv[1:2, :], xhat, rstd)
            vr[6:7, :] += colsum(dh2)
            lhs[at, :] = dh2.astype(BF)
            acc[at, :] = dh2
        row_tiles(norm)
        for u in range(n): cp_res(u).start()
    def outer(dst, left, right):
        def tile(i, _):
            rows_ = pl.ds(pl.multiple_of(i * 256, 256), 256)
            lt = jnp.transpose(left[:, rows_])
            for h in range(0, width, 256): dst[rows_, pl.ds(h, 256)] = dot(lt, right[:, h:h + 256]).astype(BF)
            return 0
        lax.fori_loop(0, left.shape[1] // 256, tile, 0, unroll=UNROLL_T)
    def grad_back():
        outer(gb5, gr, lhs.at[pl.ds(0, rows)])
        for i in range(width // 256): yt[:, pl.ds(256 * i, 256)] = jnp.transpose(yt[:, pl.ds(256 * i, 256)])
    def bwd(j):
        def tile(h, _):
            cols = pl.ds(pl.multiple_of(j * width + h * 256, 256), 256)
            du = gp[:, cols] * dot(lhs[pl.ds(0, rows), :], wb[cols, :], 1, 1)
            gbs[:, cols] = colsum(du)
            dur = du.astype(BF)
            gr[:, cols] = dur
            return 0
        lax.fori_loop(0, width // 256, tile, 0, unroll=UNROLL)
    def grad_in(j):
        def tile(h, _):
            cols = pl.ds(pl.multiple_of(j * width + h * 256, 256), 256)
            for i in range(width // 256): gi5[pl.ds(256 * i, 256), cols] = dot(yt[:, pl.ds(256 * i, 256)], gr[:, cols]).astype(BF)
            return 0
        lax.fori_loop(0, width // 256, tile, 0, unroll=UNROLL)
    def dy():
        def tile(cols): acc[:, cols] += dot(gr[...], wi[cols, :], 1, 1)
        col_tiles(tile)
    def weight_grad(i, left, right): outer(g4.at[i], left, right)
    def norm1():
        def norm(at, r0):
            dy, xhat = acc[at, :], xh1[at, :]
            vr[0:1, :] += colsum(dy * xhat)
            vr[5:6, :] += colsum(dy)
            d = norm_back(dy, cv[0:1, :], xhat, rs1[at, :])
            vr[4:5, :] += colsum(d)
            acc[at, :] = d
            lhs[pl.ds(pl.multiple_of(rows + r0, RB), RB), :] = d.astype(BF)
        row_tiles(norm)
        def da_tile(cols):
            da = dot(lhs[pl.ds(rows, rows), :], w4[3, cols, :], 1, 1).astype(BF)
            for b in range(nseq): dpad[b, pl.ds(16, slots), cols] = da[b * slots:(b + 1) * slots]
        col_tiles(da_tile)
        dhalo.start()
    def units_a():
        pltpu.make_async_copy(dq1, dq1, rsem.at[0]).wait()
        def unit(u, _):
            b, p = u // pairs, u % pairs
            da = dpad[b, pl.ds(16, slots), pl.ds(p * 128, 128)]
            e4[u // 3, u % 3, 0:64, :] = halves_diag(dot(p1_s[u].astype(BF), da, 0, 0))
            return 0
        for u in range(n): unit(u, 0)
        sum4.start()
    def units_b():
        def unit(u, _):
            b, p = u // pairs, u % pairs
            da = dpad[b, pl.ds(16, slots), pl.ds(p * 128, 128)]
            pr = p1_s[u]
            dp1 = dot(da, spread_diag(wz[u // 3, u % 3]), 1, 1)
            ds1 = (pr * (dp1 - seg_sum(dp1 * pr)) * scale).astype(BF)
            e6[u // 3, u % 3, 64:128, :] = halves_diag(dot(ds1, q_u[u], 0, 0)).astype(BF)
            dq1[u] = dot(ds1, spread_diag(km_u[u]))
            return 0
        for u in range(n): unit(u, 0)
    def grad_conv():
        wcp[...] = jnp.zeros_like(wcp)
        def unit(u, _):
            b, p = u // pairs, u % pairs
            lanes = pl.ds(pl.multiple_of(p * 128, 128), 128)
            v = vpad[b, :, lanes]
            turn = jnp.where(iota((slots, slots), 0) + iota((slots, slots), 1) == slots - 1, 1.0, 0.0).astype(BF)
            da = dot(turn, dpad[b, pl.ds(16, slots), lanes]).astype(BF)
            low = lane_low(da.shape)
            zero = jnp.zeros_like(da)
            for e in range(2):
                m = dot(jnp.where(low, da, zero) if e == 0 else jnp.where(low, zero, da), v, 1, 1)
                m = pltpu.roll(m, m.shape[1] - slots + 1, 1, stride=1, stride_axis=0)
                wcp[pl.ds(2 * p + e, 1), :] += colsum(m)
            return 0
        lax.fori_loop(0, n, unit, 0, unroll=UNROLL)
        vr[12:24, 0:128] = wcp[:, 0:128]
    def cb_a():
        st["G"], st["DP"] = [], []
        for i in R2:
            k = slot(i)
            dwz = e4[z, k, 0:64, :]
            nt = nts[i]
            den = mden[i, 1:2, :]
            dnt = mm(flip64(dwz), z6[i])
            dden = -colsum(dnt * nt) / den
            tile = jnp.zeros((16, 128), F32)
            row = iota((16, 128), 0)
            for j, v in enumerate((mden[i, 0:1, :], dden)):
                for q in range(3):
                    h = v.astype(BF).astype(F32)
                    tile = jnp.where(row == 3 * j + q, h, tile)
                    v = v - h
            sh5[z, k, 0:64, :] = (dnt / den).astype(BF)
            sh5[z, k, 64:80, :] = tile.astype(BF)
            st["G"].append(mm(flip64(nt), dwz, flip=True))
            st["DP"].append(jnp.zeros((64, 128), F32))
        share5.start()
    def cb(it):
        eye = eye_pair()
        G, DP = st["G"], st["DP"]
        Z = [sv[i, it, 0] for i in R2]; Pr = [sv[i, it, 1] for i in R2]; T2 = [sv[i, it, 2] for i in R2]; T3 = [sv[i, it, 3] for i in R2]
        d3 = [0.25 * mm(G[i], Z[i]) for i in R2]
        d2 = [-mm(d3[i], Pr[i]) for i in R2]
        dz = [0.25 * mm(T3[i], G[i]) for i in R2]
        dp = [-mm(T2[i], d3[i]) for i in R2]
        d1 = [-mm(d2[i], Pr[i]) for i in R2]
        dp = [dp[i] - mm(7.0 * eye - Pr[i], d2[i]) - d1[i] for i in R2]
        st["G"] = [dz[i] + mm(dp[i], p2s[i]) for i in R2]
        st["DP"] = [DP[i] + mm(Z[i], dp[i]) for i in R2]
    def cb_z():
        for i in R2:
            u = 3 * z + slot(i)
            p, g0 = p2s[i], st["G"][i]
            col = colsum(p)
            top = seg(jnp.max, col, -jnp.inf)
            f = 1.0 / top
            df = seg(jnp.sum, colsum(g0 * p), 0.0)
            hit = (col == top).astype(F32)
            dcol = -f * f * df * hit / seg(jnp.sum, hit, 0.0)
            dp = flip64(st["DP"][i]) + f * g0 + dcol
            ds = p * (dp - seg(jnp.sum, dp * p, 0.0)) * scale
            hi, lo = split(ds)
            b = spread_diag(km_u[u])
            core_g[i, 0:64, :] = dot(hi, b) + dot(lo, b)
            hi, lo = split(flip64(ds))
            b = spread_diag(qm_u[u])
            core_g[i, 64:128, :] = dot(hi, b) + dot(lo, b)
    def third_b():
        def unit(u, _):
            b, p = u // pairs, u % pairs
            tile = sh5[u // 3, u % 3, 64:80, :].astype(F32)
            m = tile[0:1] + tile[1:2] + tile[2:3]
            dden = tile[3:4] + tile[4:5] + tile[5:6]
            e = e3_s[u] * jnp.exp(ml_s[u, 0:1, :] - m)
            dn = spread_diag(sh5[u // 3, u % 3, 0:64, :])
            v = vpad[b, pl.ds(16, slots), pl.ds(pl.multiple_of(p * 128, 128), 128)]
            de = dot(v, dn) + dden
            p1_s[u] = dot(e.astype(BF), dn, 1, 1)
            ds = (e * de * scale).astype(BF)
            e6[u // 3, u % 3, 0:64, :] = halves_diag(dot(ds, k_u[u], 0, 0)).astype(BF)
            e3_s[u] = dot(ds, spread_diag(qm_u[u]))
            return 0
        lax.fori_loop(0, n, unit, 0, unroll=UNROLL)
        sum6.start()
    def conv():
        dhalo.end()
        def per(p, _):
            lanes = pl.ds(pl.multiple_of(p * 128, 128), 128)
            th = [split(skew(wrp[pl.ds(2 * p + e, 1), :], 256, slots)) for e in range(2)]
            low = lane_low((slots, 128))
            tot = jnp.zeros((1, 128), F32)
            for b in range(nseq):
                u = b * pairs + p
                d = dpad[b, :, lanes]
                c0 = dot(th[0][0], d) + dot(th[0][1], d)
                c1 = dot(th[1][0], d) + dot(th[1][1], d)
                v = (p1_s[u] + jnp.where(low, c0, c1)) * valid_of(b).astype(F32)
                tot = tot + colsum(v)
                yt[pl.ds(b * slots, slots), lanes] = v.astype(BF)
            vr[3:4, lanes] = tot
            return 0
        lax.fori_loop(0, pairs, per, 0, unroll=UNROLL)
    def own_marks():
        cn = counts(z // 2, 0, 64)
        for i in R2:
            k = slot(i)
            sh7[z, k, 0:64, :] = ((core_g[i, 0:64, :] + e6[z, k, 0:64, :].astype(F32)) / cn).astype(BF)
            sh7[z, k, 64:128, :] = ((core_g[i, 64:128, :] + e6[z, k, 64:128, :].astype(F32)) / cn).astype(BF)
        share7.start()
    def queries():
        def unit(u, _):
            b, p = u // pairs, u % pairs
            lanes = pl.ds(pl.multiple_of(p * 128, 128), 128)
            r0 = pl.multiple_of(b * slots, slots)
            mb = memb[pl.ds(pl.multiple_of(64 * b, 64), 64), :]
            q = dot(mb, sh7[u // 3, u % 3, 0:64, :], 0, 0) + dq1[u]
            k = dot(mb, sh7[u // 3, u % 3, 64:128, :], 0, 0) + e3_s[u]
            lhs[pl.ds(r0, slots), lanes] = q.astype(BF)
            lhs[pl.ds(rows + r0, slots), lanes] = k.astype(BF)
            vr[2:3, lanes] += colsum(q)
            return 0
        lax.fori_loop(0, n, unit, 0, unroll=UNROLL)
    def gx1():
        def tile(cols): acc[:, cols] += dot(yt[...], w4[2, cols, :], 1, 1)
        col_tiles(tile)
    def cp_gx(): return pltpu.make_async_copy(acc, gx_o, osem.at[1])
    def gx2():
        def tile(cols):
            acc[:, cols] += dot(lhs[pl.ds(0, rows), :], w4[0, cols, :], 1, 1) + dot(lhs[pl.ds(rows, rows), :], w4[1, cols, :], 1, 1)
        col_tiles(tile)
        cp_gx().start()
    px = s + 1 - 2 * (s % 2)
    py = (s + 2) % 4
    def cp_v(i):
        dst, dev = ((va, (s, 2 * z + 1 - c)), (vx, (px, t)), (vy, (py, t)))[i]
        return remote(vr, dst, vs.at[i], vq.at[i], *dev)
    def cp_vz(d): return remote(vr, vz.at[z], vs.at[2 + d], vq.at[3 + z], s, 2 * ((z + d) % 4) + c)
    def vec_0():
        for i in range(nff): vr[8 + i:9 + i, :] = gbs[:, pl.ds(i * width, width)]
        cp_v(0).start(FIRST)
    def vec_step(i):
        cp_v(i).wait()
        vr[...] = vr[...] + (va, vx, vy)[i][...]
        if i < 2: cp_v(i + 1).start(FIRST)
        else:
            for d in (1, 2, 3): cp_vz(d).start(FIRST)
    def vec_z():
        for d in (1, 2, 3):
            zz = (z + d) % 4
            remote(vr, vz.at[zz], vs.at[2 + d], vq.at[3 + zz], s, 2 * zz + c).wait_recv()
        for d in (1, 2, 3): cp_vz(d).wait_send()
        vz[z] = vr[...]
        sums[...] = ((vz[0] + vz[1]) + vz[2]) + vz[3]
    half = n // 2
    P_ = functools.partial
    steps = [P_(g.run, k, i) for k in range(len(views)) for i in range(Gather.STAGES)] + [P_(g.arrive, k) for k in range(len(views))]
    nk = 8 + nff
    steps += [P_(rs.run, k, i) for k in range(nk) for i in range(Scatter.STAGES)]
    steps += [P_(newton, i) for i in range(ITERS)] + [P_(cb, ITERS - 1 - i) for i in range(ITERS)] + [P_(up, j) for j in range(nff)] + [P_(bwd, j) for j in range(nff)] + [P_(grad_in, j) for j in range(nff)]
    steps += [P_(vec_step, i) for i in range(3)]
    steps += [xm_part, xm_b, xm_c, xm_d, xm_e, vectors, projections, third, P_(first, 0, half), P_(first, half, n), core_a, e2.mid, e2.end, core_z, e3.mid, e3.end, attention, out_proj,
              down, norm2, grad_back, dy, norm1, P_(weight_grad, 0, ar, lhs.at[pl.ds(rows, rows)]), units_a, units_b, sum4.mid, grad_conv, sum4.end, cb_a, share5.mid, cb_z, share5.end, third_b,
              conv, sum6.mid, gx1, sum6.end, own_marks, P_(weight_grad, 1, x_ref, yt), share7.mid, share7.end, queries, P_(weight_grad, 2, x_ref, lhs.at[pl.ds(rows, rows)]),
              P_(weight_grad, 3, x_ref, lhs.at[pl.ds(0, rows)]), vec_0, gx2, vec_z]
    for i in order: steps[i]()
    o = [pltpu.make_async_copy(gp.at[pl.ds(a, m), pl.ds(b, w)], dst, osem.at[2 + i]) for i, (a, m, b, w, dst) in enumerate((
        (0, 4 * sub, 0, width, ob_o), (4 * sub, sub, 0, ff, oi_o), (5 * sub, sub, 0, width, oo_o), (5 * sub, sub, width, width, ov_o),
        (5 * sub, sub, 2 * width, width, ok_o), (5 * sub, sub, 3 * width, width, oq_o)))]
    o.append(pltpu.make_async_copy(sums, sums_o, osem.at[8]))
    for cp in o: cp.start()
    g.drain(); e2.drain(); e3.drain(); halo.drain()
    cp_xa().wait_send()
    for d in (1, 2, 3):
        cp_xb(d).wait_send(); cp_xm(d).wait_send()
    for zz in range(4): cp_xc(zz).wait_send()
    rs.drain(nk)
    sum4.drain(); share5.drain(); sum6.drain(); share7.drain(); dhalo.drain()
    cp_gx().wait()
    for cp in o: cp.wait()

def whole(lengths, x, cot, wc, shards, order=ORDER):
    S = jax.ShapeDtypeStruct
    rows, width = x.shape
    wq, wk, wv, wo, win, wback, bin_, gains, shifts = shards
    nseq = lengths.shape[0]
    slots = rows // nseq
    sub, ff = wq.shape[0], win.shape[1]
    n = nseq * width // 128
    nk = 8 + ff // width
    na = 1 + len(CHUNKS)
    V = lambda *sh: pltpu.VMEM(sh, F32)
    B = lambda *sh: pltpu.VMEM(sh, BF)
    D = lambda *sh: pltpu.SemaphoreType.DMA(sh)
    vm = pl.BlockSpec(memory_space=pltpu.VMEM); hb = pl.BlockSpec(memory_space=pl.ANY)
    return pl.pallas_call(
        functools.partial(body, tuple(order)),
        out_shape=(S((rows, width), F32),) * 2 + (S((sub, width), F32),) * 4 + (S((sub, ff), F32), S((4 * sub, width), F32), S((24, width), F32)),
        in_specs=[pl.BlockSpec(memory_space=pltpu.SMEM), vm, hb, vm] + [hb] * 6 + [vm] * 3,
        out_specs=(hb,) * 9,
        scratch_shapes=[B(4, sub, width), B(sub, ff), B(4 * sub, width), V(16, 128), V(4, 4, 2, 16, 128), B(4, width, width), B(width, ff), B(ff, width), B(rows + 128 * nseq, width),
                        V(2, 64, width), V(64, width), V(4, 16, width), V(2, 4, 16, width), V(4, 3, 72, 128), V(4, 2, 72, 128), V(4, 2, 72, 128),
                        B(n, slots, 128), B(n, slots, 128), B(nseq, 256, width), B(n, 64, 128), B(n, 64, 128), V(n, slots, 128), V(n, slots, 128), V(n, 8, 128),
                        B(4, 3, 64, 128), V(2, ITERS, 4, 64, 128), V(2, 64, 128), V(2, 64, 128), V(2, 64, 128), V(2, 8, 128), V(8, width), V(1, ff), V(wc.shape[0], 256), V(wc.shape[0], 256),
                        B(rows, width), B(rows, width), B(rows, ff), V(rows, ff), V(1, ff), V(rows, 1), V(rows, width), V(rows, width),
                        B(ff, width), B(width, ff), B(4, width, width), B(nseq, 256, width), V(4, 3, 64, 128), V(4, 2, 64, 128), V(4, 2, 64, 128), B(4, 3, 128, 128), B(4, 2, 128, 128), B(4, 2, 128, 128), B(4, 3, 80, 128),
                        V(2, 128, 128), B(4, 3, 128, 128), V(n, slots, 128), B(64 * nseq, slots),
                        B(nk, 4, 4, sub, width), B(nk, 2, 4, sub, width), B(nk, 4, sub, width), B(nk, 4, sub, width),
                        V(24, width), V(24, width), V(24, width), V(24, width), V(4, 24, width), V(24, width),
                        D(na, 9), D(na), D(na, 2), D(na), D(na), D(na), D(na), D(11), D(13), D(2), D(2, 2), D(3, 2), D(4, 2), D(2, 2),
                        D(nk), D(nk), D(nk), D(nk, 2), D(nk), D(nk), D(nk), D(nk), D(2), D(2, 2), D(2), D(2, 2), D(3, 2), D(4, 2), D(3, 2), D(4, 2), D(2, 2),
                        D(6), D(7), D(9), D(1)],
        compiler_params=pltpu.CompilerParams(collective_id=0, has_side_effects=True, vmem_limit_bytes=67043328),
        name="layer_whole",
    )(lengths, x, cot, wc, wq, wk, wv, wo, win, wback, bin_, gains, shifts)


def hand_out(taps, *refs):
    big, sums_ref = refs[:8], refs[8]
    outs, (conv_o, bias_o, gains_o, shifts_o) = refs[9:17], refs[17:21]
    bufs, sums, sin, sout = refs[21:29], refs[29], refs[30], refs[31]
    a = [pltpu.make_async_copy(r, b, sin.at[i]) for i, (r, b) in enumerate(zip((*big, sums_ref), (*bufs, sums)))]
    o = [pltpu.make_async_copy(b, r, sout.at[i]) for i, (r, b) in enumerate(zip(outs, bufs))]
    for cp in a: cp.start()
    me = lax.axis_index("seq") * 8 + lax.axis_index("tok")
    sub = gains_o.shape[1]
    width = sums.shape[1]
    a[8].wait()
    v = pltpu.roll(sums[0:8, :], (width - sub * me) % width, 1)
    gains_o[...] = v[0:2, 0:sub]
    shifts_o[...] = v[2:8, 0:sub]
    f4 = bias_o.shape[1]
    per = width // f4
    row = lax.broadcasted_iota(jnp.int32, (4, width), 0)
    b = jnp.sum(jnp.where(row == me // per, sums[8:12, :], 0.0), axis=0, keepdims=True)
    b = pltpu.roll(jnp.broadcast_to(b, (8, width)), (width - f4 * (me % per)) % width, 1)
    bias_o[...] = b[0:1, 0:f4]
    conv_o[...] = sums[12:24, 0:taps]
    for i in range(8):
        a[i].wait()
        o[i].start()
    for cp in o: cp.wait()

def finish(big, sums, taps):
    S = jax.ShapeDtypeStruct
    width = sums.shape[1]
    sub = width // 32
    vm = pl.BlockSpec(memory_space=pltpu.VMEM); hb = pl.BlockSpec(memory_space=pl.ANY)
    return pl.pallas_call(
        functools.partial(hand_out, taps),
        out_shape=tuple(S(b.shape, F32) for b in big) + (S((12, taps), F32), S((1, 4 * sub), F32), S((2, sub), F32), S((6, sub), F32)),
        in_specs=[hb] * 9,
        out_specs=(hb,) * 8 + (vm,) * 4,
        scratch_shapes=[pltpu.VMEM(b.shape, F32) for b in big] + [pltpu.VMEM(sums.shape, F32), pltpu.SemaphoreType.DMA((9,)), pltpu.SemaphoreType.DMA((8,))],
        name="hand_out",
    )(*big, sums)


def fast_shards(inputs, lengths, bounds, w_query, w_key, w_value, w_out, w_conv, w_in, w_back, b_in, gains, shifts, cotangent):
    shape = inputs.shape
    x = inputs.reshape(-1, shape[2])
    owned = (w_query, w_key, w_value, w_out, w_in, w_back, b_in.reshape(1, -1), gains, shifts)
    *big, sums = whole(lengths, x, cotangent.reshape(x.shape), w_conv, owned)
    res, gx, gq, gk, gv, go, gi, gb, conv, bias, gain, shift = finish(big, sums, w_conv.shape[1])
    return (res.reshape(shape), gx.reshape(shape), gq, gk, gv, go, conv, gi, gb, bias.reshape(-1), gain, shift)


def solution(mesh):
    placed = (
        P("seq", "tok", None),
        P("seq"),
        P("seq", None),
        P(("seq", "tok"), None),
        P(("seq", "tok"), None),
        P(("seq", "tok"), None),
        P(("seq", "tok"), None),
        P(),
        P(("seq", "tok"), None),
        P(("seq", "tok"), None),
        P(("seq", "tok")),
        P(None, ("seq", "tok")),
        P(None, ("seq", "tok")),
        P("seq", "tok", None),
    )
    return jax.shard_map(
        fast_shards if (mesh.shape["seq"], mesh.shape["tok"]) == (4, 8) else shards,
        mesh=mesh,
        in_specs=placed,
        out_specs=(
            P("seq", "tok", None),
            P("seq", "tok", None),
            P(("seq", "tok"), None),
            P(("seq", "tok"), None),
            P(("seq", "tok"), None),
            P(("seq", "tok"), None),
            P(),
            P(("seq", "tok"), None),
            P(("seq", "tok"), None),
            P(("seq", "tok")),
            P(None, ("seq", "tok")),
            P(None, ("seq", "tok")),
        ),
        check_vma=False,
    )
```

```python
import functools

import jax
import jax.numpy as jnp
from jax import lax
from jax.experimental import pallas as pl
from jax.experimental.pallas import tpu as pltpu
from jax.sharding import PartitionSpec as P

ITERS = 6


EPSILON = 1e-05
EXACT_PRECISION = lax.Precision.HIGHEST


def padded_2(cells, sides, width):
    for axis, dim in sides:
        count = lax.axis_size(axis)
        ends = count - 1
        head = lax.slice_in_dim(cells, 0, width, axis=dim)
        tail = lax.slice_in_dim(cells, cells.shape[dim] - width, cells.shape[dim], axis=dim)
        cells = jnp.concatenate(
            [
                lax.ppermute(tail, axis, [(i, (i + 1) % count) for i in range(ends)]),
                cells,
                lax.ppermute(head, axis, [((i + 1) % count, i) for i in range(ends)]),
            ],
            axis=dim,
        )
    return cells


def layer_norm(hidden, gain_row, shift_row):
    center = hidden - jnp.mean(hidden, axis=-1, keepdims=True)
    spread = jnp.mean(center * center, axis=-1, keepdims=True)
    return center * lax.rsqrt(spread + EPSILON) * gain_row + shift_row


def newton_inverse(kernel):
    column_sum = jnp.sum(kernel, axis=-2)
    factor = 1.0 / jnp.max(column_sum, axis=-1)
    approx = jnp.swapaxes(kernel, -1, -2) * factor[..., None, None]
    identity = jnp.eye(kernel.shape[-1], dtype=jnp.float32)
    for sweep_index in range(ITERS):
        product = jnp.matmul(kernel, approx, precision=EXACT_PRECISION)
        inner_term = 7.0 * identity - product
        inner_term = 15.0 * identity - jnp.matmul(product, inner_term, precision=EXACT_PRECISION)
        inner_term = 13.0 * identity - jnp.matmul(product, inner_term, precision=EXACT_PRECISION)
        approx = 0.25 * jnp.matmul(approx, inner_term, precision=EXACT_PRECISION)
    return approx


def mixer_core(query_marks, key_marks, numerator, denom):
    score_scale_factor = query_marks.shape[-1] ** (-0.5)
    scores = (
        jnp.einsum("bihd,bjhd->bhij", query_marks, key_marks, precision=EXACT_PRECISION)
        * score_scale_factor
    )
    middle = jax.nn.softmax(scores, axis=-1)
    pseudo = newton_inverse(middle)
    summary = numerator / denom[..., None]
    return jnp.einsum("bhij,bhjd->bhid", pseudo, summary, precision=EXACT_PRECISION)


def gelu_exact(pre_act):
    return jax.nn.gelu(pre_act, approximate=False)


def product_low(pattern, left, right):
    return jnp.einsum(pattern, left, right, preferred_element_type=jnp.float32)


def shards(
    inputs,
    lengths,
    bounds,
    w_query,
    w_key,
    w_value,
    w_out,
    w_conv,
    w_in,
    w_back,
    b_in,
    gains,
    shifts,
    cotangent,
):
    seq_count, slot_count, model_width = inputs.shape
    head_count, tap_count = w_conv.shape
    head_dim = model_width // head_count
    rim_width = tap_count // 2
    mark_count = bounds.shape[1] - 1
    row_count = seq_count * slot_count
    score_scale_factor = head_dim ** (-0.5)
    first_slot = lax.axis_index("tok") * slot_count
    position = first_slot + jnp.arange(slot_count, dtype=jnp.int32)
    valid_mask = (position[None, :] < lengths[:, None]).astype(jnp.float32)
    member = (
        (position[None, None, :] >= bounds[:, :-1, None])
        & (position[None, None, :] < bounds[:, 1:, None])
    ).astype(jnp.float32)
    part_count = (bounds[:, 1:] - bounds[:, :-1]).astype(jnp.float32)
    gathered = (
        lax.all_gather(w_query.astype(jnp.bfloat16), ("seq", "tok"), axis=0, tiled=True),
        lax.all_gather(w_key.astype(jnp.bfloat16), ("seq", "tok"), axis=0, tiled=True),
        lax.all_gather(w_value.astype(jnp.bfloat16), ("seq", "tok"), axis=0, tiled=True),
        lax.all_gather(w_out.astype(jnp.bfloat16), ("seq", "tok"), axis=0, tiled=True),
        lax.all_gather(w_in.astype(jnp.bfloat16), ("seq", "tok"), axis=0, tiled=True),
        lax.all_gather(w_back.astype(jnp.bfloat16), ("seq", "tok"), axis=0, tiled=True),
        lax.all_gather(b_in.astype(jnp.bfloat16), ("seq", "tok"), axis=0, tiled=True),
        lax.all_gather(gains.astype(jnp.bfloat16), ("seq", "tok"), axis=1, tiled=True),
        lax.all_gather(shifts.astype(jnp.bfloat16), ("seq", "tok"), axis=1, tiled=True),
    )
    query_mat, key_mat, value_mat, out_mat, in_mat, back_mat, bias_vec, gain_vec, shift_vec = (
        gathered
    )
    bias_rows = bias_vec.astype(jnp.float32)
    gain_rows = gain_vec.astype(jnp.float32)
    shift_rows = shift_vec.astype(jnp.float32)
    flat_rows = inputs.reshape(row_count, model_width)
    query_rows = jnp.dot(flat_rows, query_mat, preferred_element_type=jnp.float32) + shift_rows[0]
    key_rows = jnp.dot(flat_rows, key_mat, preferred_element_type=jnp.float32)
    value_rows = jnp.dot(flat_rows, value_mat, preferred_element_type=jnp.float32) + shift_rows[1]
    part_query = jnp.einsum(
        "bms,bsd->bmd",
        member,
        query_rows.reshape(seq_count, slot_count, model_width),
        precision=EXACT_PRECISION,
    )
    part_key = jnp.einsum(
        "bms,bsd->bmd",
        member,
        key_rows.reshape(seq_count, slot_count, model_width),
        precision=EXACT_PRECISION,
    )
    sum_query, sum_key = lax.psum((part_query, part_key), "tok")
    mark_query = (
        (sum_query / part_count[..., None])
        .astype(jnp.bfloat16)
        .reshape(seq_count, mark_count, head_count, head_dim)
    )
    mark_key = (
        (sum_key / part_count[..., None])
        .astype(jnp.bfloat16)
        .reshape(seq_count, mark_count, head_count, head_dim)
    )
    query_head_rows = query_rows.astype(jnp.bfloat16).reshape(
        seq_count, slot_count, head_count, head_dim
    )
    key_head_rows = key_rows.astype(jnp.bfloat16).reshape(
        seq_count, slot_count, head_count, head_dim
    )
    v_low = (value_rows.reshape(seq_count, slot_count, model_width) * valid_mask[..., None]).astype(
        jnp.bfloat16
    )
    value_head_rows = v_low.reshape(seq_count, slot_count, head_count, head_dim)
    first_score_matrix = (
        product_low("bshd,bmhd->bshm", query_head_rows, mark_key) * score_scale_factor
    )
    first_score_kernel = jax.nn.softmax(first_score_matrix, axis=-1)
    first_low = first_score_kernel.astype(jnp.bfloat16)
    third_score_matrix = (
        product_low("bmhd,bshd->bhms", mark_query, key_head_rows) * score_scale_factor
    )
    third_score_matrix = jnp.where(valid_mask[:, None, None, :] > 0, third_score_matrix, -1e30)
    score_top = lax.pmax(jnp.max(third_score_matrix, axis=-1), "tok")
    third_exponential = jnp.exp(third_score_matrix - score_top[..., None])
    third_low = third_exponential.astype(jnp.bfloat16)
    numerator, denom = lax.psum(
        (
            product_low("bhms,bshd->bhmd", third_low, value_head_rows),
            jnp.sum(third_exponential, axis=-1),
        ),
        "tok",
    )
    mixed_output, core_back = jax.vjp(
        mixer_core, mark_query.astype(jnp.float32), mark_key.astype(jnp.float32), numerator, denom
    )
    mixed_low = mixed_output.astype(jnp.bfloat16)
    attention_forward = product_low("bshm,bhmd->bshd", first_low, mixed_low)
    padded = padded_2(v_low, (("tok", 1),), rim_width)
    padded_heads = padded.astype(jnp.float32).reshape(
        seq_count, slot_count + 2 * rim_width, head_count, head_dim
    )
    conv_out = jnp.zeros_like(attention_forward)
    for offset in range(tap_count):
        conv_out = (
            conv_out
            + w_conv[:, offset][None, None, :, None] * padded_heads[:, offset : offset + slot_count]
        )
    mix_low = (attention_forward + conv_out).reshape(row_count, model_width).astype(jnp.bfloat16)
    first_sum = (
        flat_rows.astype(jnp.float32)
        + jnp.dot(mix_low, out_mat, preferred_element_type=jnp.float32)
        + shift_rows[2]
    )
    normed, norm_one_back = jax.vjp(layer_norm, first_sum, gain_rows[0], shift_rows[3])
    normed_low = normed.astype(jnp.bfloat16)
    pre_act = jnp.dot(normed_low, in_mat, preferred_element_type=jnp.float32) + bias_rows
    active, gelu_back = jax.vjp(gelu_exact, pre_act)
    active_low = active.astype(jnp.bfloat16)
    second_sum = (
        normed + jnp.dot(active_low, back_mat, preferred_element_type=jnp.float32) + shift_rows[4]
    )
    final_raw, norm_two_back = jax.vjp(layer_norm, second_sum, gain_rows[1], shift_rows[5])
    valid_rows = valid_mask.reshape(row_count, 1)
    result = final_raw * valid_rows
    back_weights = (
        lax.all_gather(w_query.astype(jnp.bfloat16), ("seq", "tok"), axis=0, tiled=True),
        lax.all_gather(w_key.astype(jnp.bfloat16), ("seq", "tok"), axis=0, tiled=True),
        lax.all_gather(w_value.astype(jnp.bfloat16), ("seq", "tok"), axis=0, tiled=True),
        lax.all_gather(w_out.astype(jnp.bfloat16), ("seq", "tok"), axis=0, tiled=True),
        lax.all_gather(w_in.astype(jnp.bfloat16), ("seq", "tok"), axis=0, tiled=True),
        lax.all_gather(w_back.astype(jnp.bfloat16), ("seq", "tok"), axis=0, tiled=True),
    )
    query_back, key_back, value_back, out_back, in_back, back_back = back_weights
    grad_out = cotangent.reshape(row_count, model_width).astype(jnp.float32) * valid_rows
    grad_second, grad_gain_two, grad_shift_five = norm_two_back(grad_out)
    grad_second_low = grad_second.astype(jnp.bfloat16)
    grad_shift_four = jnp.sum(grad_second, axis=0)
    grad_w_back = product_low("rf,rd->fd", active_low, grad_second_low)
    grad_active = product_low("rd,fd->rf", grad_second_low, back_back)
    (grad_pre,) = gelu_back(grad_active)
    grad_pre_low = grad_pre.astype(jnp.bfloat16)
    grad_b_in = jnp.sum(grad_pre, axis=0)
    grad_w_in = product_low("rd,rf->df", normed_low, grad_pre_low)
    grad_normed = grad_second + product_low("rf,df->rd", grad_pre_low, in_back)
    grad_first, grad_gain_one, grad_shift_three = norm_one_back(grad_normed)
    grad_proj_low = grad_first.astype(jnp.bfloat16)
    grad_shift_two = jnp.sum(grad_first, axis=0)
    grad_w_out = product_low("rd,re->de", mix_low, grad_proj_low)
    grad_mix_low = (
        product_low("re,de->rd", grad_proj_low, out_back)
        .astype(jnp.bfloat16)
        .reshape(seq_count, slot_count, model_width)
    )
    grad_mix_heads = grad_mix_low.reshape(seq_count, slot_count, head_count, head_dim)
    grad_mixed_part = product_low("bshm,bshd->bhmd", first_low, grad_mix_heads)
    grad_first_kernel = product_low("bshd,bhmd->bshm", grad_mix_heads, mixed_low)
    inner_sum = jnp.sum(grad_first_kernel * first_score_kernel, axis=-1, keepdims=True)
    grad_first_low = (
        first_score_kernel * (grad_first_kernel - inner_sum) * score_scale_factor
    ).astype(jnp.bfloat16)
    part_grad_key = product_low("bshm,bshd->bmhd", grad_first_low, query_head_rows)
    grad_mixed, grad_mk_first = lax.psum((grad_mixed_part, part_grad_key), "tok")
    grad_mq_core, grad_mk_core, grad_numer, grad_denom = core_back(grad_mixed)
    grad_numer_low = grad_numer.astype(jnp.bfloat16)
    grad_third_exp = (
        product_low("bhmd,bshd->bhms", grad_numer_low, value_head_rows) + grad_denom[..., None]
    )
    grad_v_heads = product_low("bhms,bhmd->bshd", third_low, grad_numer_low)
    grad_third_low = (third_exponential * grad_third_exp * score_scale_factor).astype(jnp.bfloat16)
    part_grad_query = product_low("bhms,bshd->bmhd", grad_third_low, key_head_rows)
    grad_key_heads = product_low("bhms,bmhd->bshd", grad_third_low, mark_query)
    grad_mq_third = lax.psum(part_grad_query, "tok")
    grad_mq = (grad_mq_core + grad_mq_third).reshape(
        seq_count, mark_count, model_width
    ) / part_count[..., None]
    grad_mk = (grad_mk_core + grad_mk_first).reshape(
        seq_count, mark_count, model_width
    ) / part_count[..., None]
    grad_query = jnp.einsum(
        "bms,bmd->bsd", member, grad_mq, precision=EXACT_PRECISION
    ) + product_low("bshm,bmhd->bshd", grad_first_low, mark_key).reshape(
        seq_count, slot_count, model_width
    )
    grad_key = jnp.einsum(
        "bms,bmd->bsd", member, grad_mk, precision=EXACT_PRECISION
    ) + grad_key_heads.reshape(seq_count, slot_count, model_width)
    grad_padded = padded_2(grad_mix_low, (("tok", 1),), rim_width)
    grad_pad_heads = grad_padded.astype(jnp.float32).reshape(
        seq_count, slot_count + 2 * rim_width, head_count, head_dim
    )
    grad_mix_float = grad_mix_heads.astype(jnp.float32)
    grad_conv_v = jnp.zeros_like(grad_mix_float)
    conv_terms = []
    for offset in range(tap_count):
        start_at = 2 * rim_width - offset
        grad_conv_v = (
            grad_conv_v
            + w_conv[:, offset][None, None, :, None]
            * grad_pad_heads[:, start_at : start_at + slot_count]
        )
        conv_terms.append(
            jnp.sum(padded_heads[:, offset : offset + slot_count] * grad_mix_float, axis=(0, 1, 3))
        )
    grad_w_conv = lax.psum(jnp.stack(conv_terms, axis=1), ("seq", "tok"))
    grad_value = (grad_v_heads + grad_conv_v).reshape(
        seq_count, slot_count, model_width
    ) * valid_mask[..., None]
    grad_query_flat = grad_query.reshape(row_count, model_width)
    grad_key_flat = grad_key.reshape(row_count, model_width)
    grad_value_flat = grad_value.reshape(row_count, model_width)
    grad_query_low = grad_query_flat.astype(jnp.bfloat16)
    grad_key_low = grad_key_flat.astype(jnp.bfloat16)
    grad_value_low = grad_value_flat.astype(jnp.bfloat16)
    grad_w_query = product_low("rd,re->de", flat_rows, grad_query_low)
    grad_w_key = product_low("rd,re->de", flat_rows, grad_key_low)
    grad_w_value = product_low("rd,re->de", flat_rows, grad_value_low)
    grad_input = (
        grad_first
        + product_low("re,de->rd", grad_query_low, query_back)
        + product_low("re,de->rd", grad_key_low, key_back)
        + product_low("re,de->rd", grad_value_low, value_back)
    )
    grad_gains = jnp.stack([grad_gain_one, grad_gain_two], axis=0)
    grad_shifts = jnp.stack(
        [
            jnp.sum(grad_query_flat, axis=0),
            jnp.sum(grad_value_flat, axis=0),
            grad_shift_two,
            grad_shift_three,
            grad_shift_four,
            grad_shift_five,
        ],
        axis=0,
    )
    (
        owned_query,
        owned_key,
        owned_value,
        owned_out,
        owned_in,
        owned_back,
        owned_bias,
        owned_gains,
        owned_shifts,
    ) = (
        lax.psum_scatter(grad_w_query, ("seq", "tok"), scatter_dimension=0, tiled=True),
        lax.psum_scatter(grad_w_key, ("seq", "tok"), scatter_dimension=0, tiled=True),
        lax.psum_scatter(grad_w_value, ("seq", "tok"), scatter_dimension=0, tiled=True),
        lax.psum_scatter(grad_w_out, ("seq", "tok"), scatter_dimension=0, tiled=True),
        lax.psum_scatter(grad_w_in, ("seq", "tok"), scatter_dimension=0, tiled=True),
        lax.psum_scatter(grad_w_back, ("seq", "tok"), scatter_dimension=0, tiled=True),
        lax.psum_scatter(grad_b_in, ("seq", "tok"), scatter_dimension=0, tiled=True),
        lax.psum_scatter(grad_gains, ("seq", "tok"), scatter_dimension=1, tiled=True),
        lax.psum_scatter(grad_shifts, ("seq", "tok"), scatter_dimension=1, tiled=True),
    )
    return (
        result.reshape(seq_count, slot_count, model_width),
        grad_input.reshape(seq_count, slot_count, model_width),
        owned_query,
        owned_key,
        owned_value,
        owned_out,
        grad_w_conv,
        owned_in,
        owned_back,
        owned_bias,
        owned_gains,
        owned_shifts,
    )


F32 = jnp.float32


BF = jnp.bfloat16


def dot(a, b, ca=1, cb=0):
    return lax.dot_general(a, b, (((ca,), (cb,)), ((), ())), preferred_element_type=F32)


def lane_low(shape):
    return lax.broadcasted_iota(jnp.int32, shape, len(shape) - 1) % 128 < 64


def halves_diag(m):
    low = lane_low((64, 128))
    return jnp.where(low, m[:64], m[64:])


def spread_diag(v):
    low = lane_low(v.shape)
    zero = jnp.zeros_like(v)
    return jnp.concatenate([jnp.where(low, v, zero), jnp.where(low, zero, v)], axis=0)


def seg(op, v, fill):
    low = lane_low(v.shape)
    a = op(jnp.where(low, v, fill), axis=-1, keepdims=True)
    b = op(jnp.where(low, fill, v), axis=-1, keepdims=True)
    return jnp.where(low, a, b)


def split(v):
    hi = v.astype(BF)
    return hi, (v - hi.astype(F32)).astype(BF)


def norm_stats(h):
    center = h - jnp.mean(h, axis=-1, keepdims=True)
    spread = jnp.mean(center * center, axis=-1, keepdims=True)
    rstd = lax.rsqrt(spread + 1e-05)
    return center * rstd, rstd


def norm_back(dy, gain, xhat, rstd):
    d = dy * gain
    a = jnp.mean(d, axis=-1, keepdims=True)
    b = jnp.mean(d * xhat, axis=-1, keepdims=True)
    return rstd * (d - a - xhat * b)


def skew(row, width, count):
    return pltpu.roll(jnp.broadcast_to(row, (count, width)), 0, 1, stride=1, stride_axis=0)


def colsum(v):
    return jnp.sum(v, axis=0, keepdims=True)


MESH = pl.DeviceIdType.MESH


FIRST = 0


def place():
    s = lax.axis_index("seq"); t = lax.axis_index("tok")
    x, y, z, c = s % 2, s // 2, t // 2, t % 2
    px = s + 1 - 2 * x
    py = (s + 2) % 4
    p1 = px * (1 - c) + py * c
    p2 = py * (1 - c) + px * c
    return s, z, c, p1, p2


def remote(src, dst, send, recv, seq, tok):
    return pltpu.make_async_remote_copy(src_ref=src, dst_ref=dst, send_sem=send, recv_sem=recv,
                                        device_id={"seq": seq, "tok": tok}, device_id_type=MESH)


def greet(s, z, c, p1, p2):
    bar = pltpu.get_barrier_semaphore()
    def sig(seq, tok):
        pl.semaphore_signal(bar, inc=1, device_id={"seq": seq, "tok": tok}, device_id_type=MESH)
    t = 2 * z + c
    sig(p1, t); sig(p2, t); sig(s, 2 * z + 1 - c)
    for d in (1, 2, 3):
        sig(s, 2 * ((z + d) % 4) + c)
    @pl.when(((c == 1) & (z < 3)) | ((c == 0) & (z > 0)))
    def _(): sig(s, t + 2 * c - 1)
    edge = c * (6 - z) // 4 + (1 - c) * ((z + 3) // 4)
    return 6 + edge


def each_slot(c, f):
    f(0)
    @pl.when(c == 0)
    def _(): f(1)


class UnitSum:
    def __init__(self, src, ra, rb, sems, where, combine):
        self.__dict__.update(locals())
        self.sa, self.qa, self.sb, self.qb = sems
    def cp_a(self, c):
        s, z, cc, _, _ = self.where
        if c == 0:
            return remote(self.src.at[:, pl.ds(2, 1)], self.ra.at[:, pl.ds(0, 1)], self.sa, self.qa, s, 2 * z + 1)
        return remote(self.src.at[:, pl.ds(0, 2)], self.ra, self.sa, self.qa, s, 2 * z)
    def cp_b(self, d, i):
        s, z, c, _, _ = self.where
        zz = (z + d) % 4
        return remote(self.src.at[zz, 2 * c + i], self.rb.at[z, i], self.sb.at[i], self.qb.at[i], s, 2 * zz + c)
    def start(self):
        for k in (0, 1):
            @pl.when(self.where[2] == k)
            def _(): self.cp_a(k).start(FIRST)
    def mid(self):
        s, z, c, _, _ = self.where
        for k in (0, 1):
            @pl.when(c == k)
            def _(): self.cp_a(1 - k).wait_recv()
        def comb(zz):
            each_slot(c, lambda i: self.combine(self.src.at[zz, 2 * c + i], self.ra.at[zz, i]))
        for d in (2, 1, 3):
            comb((z + d) % 4)
            each_slot(c, lambda i: self.cp_b(d, i).start(FIRST))
        comb(z)
    def three(self, i):
        s, z, c, _, _ = self.where
        return remote(self.src.at[pl.ds(0, 3), 2 * c + i], self.rb.at[pl.ds(0, 3), i], self.sb.at[i], self.qb.at[i], s, 2 * z + 1 - c)
    def end(self):
        s, z, c, _, _ = self.where
        def f(i):
            self.three(i).wait_recv()
            for d in (1, 3, 2): self.combine(self.src.at[z, 2 * c + i], self.rb.at[(z + d) % 4, i])
        each_slot(c, f)
    def drain(self):
        c = self.where[2]
        for k in (0, 1):
            @pl.when(c == k)
            def _(): self.cp_a(k).wait_send()
        each_slot(c, lambda i: self.three(i).wait_send())


class UnitShare:
    def __init__(self, buf, sems, where):
        self.__dict__.update(locals())
        self.sz, self.qz, self.sc, self.qc = sems
    def cp_z(self, d, i):
        s, z, c, _, _ = self.where
        b = self.buf.at[z, 2 * c + i]
        return remote(b, b, self.sz.at[i], self.qz.at[z, i], s, 2 * ((z + d) % 4) + c)
    def cp_c(self, zz, i):
        s, z, c, _, _ = self.where
        b = self.buf.at[zz, 2 * c + i]
        return remote(b, b, self.sc.at[i], self.qc.at[i], s, 2 * z + 1 - c)
    def start(self):
        z, c = self.where[1], self.where[2]
        def f(i):
            for d in (2, 1, 3): self.cp_z(d, i).start(FIRST)
            self.cp_c(z, i).start(FIRST)
        each_slot(c, f)
    def mid(self):
        s, z, c, _, _ = self.where
        for d in (1, 3, 2):
            zz = (z + d) % 4
            def f(i):
                b = self.buf.at[zz, 2 * c + i]
                remote(b, b, self.sz.at[i], self.qz.at[zz, i], s, 2 * zz + c).wait_recv()
                self.cp_c(zz, i).start(FIRST)
            each_slot(c, f)
    def end(self):
        s, z, c, _, _ = self.where
        def f(i):
            b = self.buf.at[:, 2 * (1 - c) + i]
            remote(b, b, self.sc.at[i], self.qc.at[i], s, 2 * z + 1 - c).wait_recv()
        each_slot(1 - c, f)
    def drain(self):
        s, z, c, _, _ = self.where
        def f(i):
            b = self.buf.at[pl.ds(0, 3), 2 * c + i]
            remote(b, b, self.sz.at[i], self.qc.at[i], s, 2 * z + 1 - c).wait_send()
            b = self.buf.at[:, 2 * c + i]
            remote(b, b, self.sc.at[i], self.qc.at[i], s, 2 * z + 1 - c).wait_send()
        each_slot(c, f)


class Halo:
    def __init__(self, buf, slots, send, recv, where):
        self.__dict__.update(locals())
        s, z, c, _, _ = where
        self.t = 2 * z + c
    def cps(self):
        s, n = self.where[0], self.slots
        up = remote(self.buf.at[:, pl.ds(n, 16)], self.buf.at[:, pl.ds(0, 16)], self.send.at[0], self.recv.at[0], s, self.t + 1)
        down = remote(self.buf.at[:, pl.ds(16, 16)], self.buf.at[:, pl.ds(16 + n, 16)], self.send.at[1], self.recv.at[1], s, self.t - 1)
        return up, down
    def zero(self):
        n = self.slots
        a, _, d = self.buf.shape
        self.buf[:, 16 + n:, :] = jnp.zeros((a, 256 - 16 - n, d), BF)
        self.buf[:, 0:16, :] = jnp.zeros((a, 16, d), BF)
    def start(self):
        up, down = self.cps()
        @pl.when(self.t < 7)
        def _(): up.start(FIRST)
        @pl.when(self.t > 0)
        def _(): down.start(FIRST)
    def end(self):
        up, down = self.cps()
        @pl.when(self.t > 0)
        def _(): up.wait_recv()
        @pl.when(self.t < 7)
        def _(): down.wait_recv()
    def drain(self):
        up, down = self.cps()
        @pl.when(self.t < 7)
        def _(): up.wait_send()
        @pl.when(self.t > 0)
        def _(): down.wait_send()


def mm(a, b, flip=False):
    ah, al = split(a)
    bh, bl = split(spread_diag(b))
    if flip:
        return dot(ah, bh, 1, 1) + (dot(ah, bl, 1, 1) + dot(al, bh, 1, 1))
    return dot(jnp.concatenate([ah, ah, al], axis=1), jnp.concatenate([bh, bl, bh], axis=0))


def flip64(a):
    t = jnp.transpose(a)
    return jnp.concatenate([t[:64], t[64:]], axis=1)


def eye_pair():
    i = lax.broadcasted_iota(jnp.int32, (64, 128), 0)
    j = lax.broadcasted_iota(jnp.int32, (64, 128), 1)
    return jnp.where(i == j % 64, 1.0, 0.0).astype(F32)


def soft_combine(dst, other):
    m1, m2 = dst[64:65, :], other[64:65, :]
    m = jnp.maximum(m1, m2)
    a, b = jnp.exp(m1 - m), jnp.exp(m2 - m)
    dst[0:64, :] = dst[0:64, :] * a + other[0:64, :] * b
    dst[65:66, :] = dst[65:66, :] * a + other[65:66, :] * b
    dst[64:65, :] = m


def core_setup(qm, km):
    p2 = dot(qm, spread_diag(km), 1, 1) * (64 ** -0.5)
    e = jnp.exp(p2 - seg(jnp.max, p2, -jnp.inf))
    p2 = e / seg(jnp.sum, e, 0.0)
    factor = 1.0 / seg(jnp.max, colsum(p2), -jnp.inf)
    return p2, flip64(p2) * factor


def seg_sum(v):
    i = lax.broadcasted_iota(jnp.int32, (128, 128), 0)
    j = lax.broadcasted_iota(jnp.int32, (128, 128), 1)
    ones = jnp.where(i // 64 == j // 64, 1.0, 0.0).astype(BF)
    hi, lo = split(v)
    return dot(hi, ones) + dot(lo, ones)

def plain_add(dst, other):
    dst[...] = (dst[...].astype(F32) + other[...].astype(F32)).astype(dst.dtype)

class Gather:
    STAGES = 9
    def __init__(self, views, owns, last, sems, where):
        self.__dict__.update(locals())
        self.qa, self.qb, self.sz, self.s1, self.s2, self.sc, self.sl = sems
        s, z, c, p1, p2 = where
        t = 2 * z + c
        self.line = ((s, t + 2), (s, t - 2))
        self.d1, self.d2, self.dc = (p1, t), (p2, t), (s, 2 * z + 1 - c)
    def at(self, k, s_, z_, c_):
        return self.views[k](s_, z_, c_)
    def cp(self, k, s_, zz, send, got, dev, src=None):
        dst = self.at(k, s_, zz, self.where[2])
        return remote(dst if src is None else src, dst, send, self.qa.at[k, got], *dev)
    def to_z(self, k, zz, way, src=None): return self.cp(k, self.where[0], zz, self.sz.at[k, way], zz, self.line[way], src)
    def to_1(self, k, zz, src=None): return self.cp(k, self.where[0], zz, self.s1.at[k], 4 + zz, self.d1, src)
    def to_2(self, k, g, zz, src=None): return self.cp(k, self.where[3 if g else 0], zz, self.s2.at[k], 8, self.d2, src)
    def several(self, k, s_, zz, send, got): return self.cp(k, s_, zz, send, got, self.dc)
    def local(self, k):
        s, z, c, _, _ = self.where
        return pltpu.make_async_copy(self.owns(k), self.at(k, s, z, c), self.sl.at[k])
    def col(self, k, s_):
        b = self.at(k, s_, slice(None), self.where[2])
        return remote(b, b, self.sc.at[k], self.qb.at[k], *self.dc)
    def pair(self, d, f):
        z = self.where[1]
        if d == 0:
            f(z, 2); return
        @pl.when(z >= d)
        def _(): f(z - d, 0)
        @pl.when(z + d <= 3)
        def _(): f(z + d, 1)
    def plane_z(self, k, zz, way):
        return self.cp(k, slice(None), zz, self.sz.at[k, way], zz, self.line[way])
    def run_last(self, k, i):
        s, z, c, p1, p2 = self.where
        every = slice(None)
        if i == 0:
            self.local(k).start()
            self.to_2(k, 0, z, self.owns(k)).start(); self.to_1(k, z, self.owns(k)).start()
        elif i == 1:
            self.several(k, p1, z, self.s1.at[k], 4 + z).wait_recv()
            self.to_2(k, 1, z).start()
        elif i == 2:
            self.several(k, pl.ds(0, 2), z, self.s2.at[k], 8).wait_recv()
            self.local(k).wait()
            @pl.when(z < 3)
            def _(): self.plane_z(k, z, 0).start()
            @pl.when(z > 0)
            def _(): self.plane_z(k, z, 1).start()
        elif i < 6:
            def f(zz, side):
                self.several(k, every, zz, self.sz.at[k, 0], zz).wait_recv()
                if side == 0 and i < 5:
                    @pl.when(z < 3)
                    def _(): self.plane_z(k, zz, 0).start()
                if side == 1 and i < 5:
                    @pl.when(z > 0)
                    def _(): self.plane_z(k, zz, 1).start()
            self.pair(i - 2, f)
            if i == 5:
                b = self.at(k, every, every, c)
                remote(b, b, self.sc.at[k], self.qb.at[k], *self.dc).start()
    def run(self, k, i):
        if k in self.last: return self.run_last(k, i)
        s, z, c, p1, p2 = self.where
        if i < 4:
            def f(zz, side):
                src = None
                if side == 2:
                    src = self.owns(k)
                    self.local(k).start()
                else:
                    self.several(k, s, zz, self.s1.at[k], zz).wait_recv()
                if side != 1 and i < 3:
                    @pl.when(z < 3)
                    def _(): self.to_z(k, zz, 0, src).start()
                if side != 0 and i < 3:
                    @pl.when(z > 0)
                    def _(): self.to_z(k, zz, 1, src).start()
                self.to_2(k, 0, zz, src).start(); self.to_1(k, zz, src).start()
            self.pair(i, f)
            if i == 3:
                self.local(k).wait()
                self.col(k, s).start()
        elif i < 8:
            def f(zz, side):
                self.several(k, p1, zz, self.s1.at[k], 4 + zz).wait_recv()
                self.to_2(k, 1, zz).start()
            self.pair(i - 4, f)
            if i == 7: self.col(k, p1).start()
        else:
            self.several(k, pl.ds(0, 2), slice(None), self.s2.at[k], 8).wait_recv()
            for s_ in (p2, 3 - s): self.col(k, s_).start()
    def arrive(self, k):
        b = self.at(k, slice(None), slice(None), 1 - self.where[2])
        remote(b, b, self.sc.at[k], self.qb.at[k], *self.dc).wait_recv()
    def drain(self):
        s, z, c, p1, p2 = self.where
        every = slice(None)
        for k in range(len(self.views)):
            self.several(k, every, every, self.sc.at[k], 8).wait_send()
            last = k in self.last
            self.several(k, s, z if last else every, self.s1.at[k], 8).wait_send()
            self.several(k, pl.ds(0, 2), z if last else every, self.s2.at[k], 8).wait_send()
            line = every if last else s
            for q in range(3):
                @pl.when(z == q)
                def _(): self.several(k, line, pl.ds(0, q + 1), self.sz.at[k, 0], 8).wait_send()
                @pl.when(z == 3 - q)
                def _(): self.several(k, line, pl.ds(0, q + 1), self.sz.at[k, 1], 8).wait_send()

class Scatter:
    STAGES = 5
    def __init__(self, part, outs, zfirst, bufs, sems, where):
        self.__dict__.update(locals())
        self.rcb, self.r2, self.r1, self.rz = bufs
        self.s_c, self.q_c, self.s_2, self.q_2, self.s_1, self.q_1, self.s_z, self.q_z = sems
        s, z, c, p1, p2 = where
        t = 2 * z + c
        self.d1, self.d2, self.dc = (p1, t), (p2, t), (s, 2 * z + 1 - c)
    def own(self, k, *at): return self.part(k, self.where[2], *at)
    def cp_c(self, k): return remote(self.part(k, 1 - self.where[2]), self.rcb.at[k], self.s_c.at[k], self.q_c.at[k], *self.dc)
    def cp_2(self, k, g):
        b = self.where[4] if g == 0 else 3 - self.where[0]
        return remote(self.own(k, b), self.r2.at[k, g], self.s_2.at[k], self.q_2.at[k, g], *self.d2)
    def cp_1(self, k): return remote(self.own(k, self.where[3]), self.r1.at[k], self.s_1.at[k], self.q_1.at[k], *self.d1)
    def cp_z(self, k, d):
        s, z, c, p1, p2 = self.where
        zz = (z + d) % 4
        return remote(self.own(k, s, zz), self.rz.at[k, z], self.s_z.at[k], self.q_z.at[k], s, 2 * zz + c)
    def three(self, k):
        return remote(self.own(k, self.where[0], pl.ds(0, 3)), self.rz.at[k, pl.ds(0, 3)], self.s_z.at[k], self.q_z.at[k], *self.dc)
    def add4(self, k, i, v):
        a = self.own(k, i)
        a[...] = a[...] + v
    def first_z(self, k, d):
        s, z, c, p1, p2 = self.where
        dst = self.r1.at[k] if d == 3 else self.r2.at[k, d - 1]
        return remote(self.own(k, slice(None), (z + d) % 4), dst, self.s_z.at[k], self.q_z.at[k], s, 2 * ((z + d) % 4) + c)
    def first_2(self, k, g):
        b = self.where[4] if g == 0 else 3 - self.where[0]
        return remote(self.own(k, b, self.where[1]), self.rz.at[k, g], self.s_2.at[k], self.q_2.at[k, g], *self.d2)
    def first_1(self, k): return remote(self.own(k, self.where[3], self.where[1]), self.rz.at[k, 2], self.s_1.at[k], self.q_1.at[k], *self.d1)
    def twelve(self, k): return remote(self.own(k, pl.ds(0, 3)), self.rcb.at[k, pl.ds(0, 3)], self.s_z.at[k], self.q_z.at[k], *self.dc)
    def run_first(self, k, i):
        s, z, c, p1, p2 = self.where
        if i == 0:
            self.cp_c(k).start()
        elif i == 1:
            self.cp_c(k).wait_recv()
            for j in range(4): self.add4(k, j, self.rcb[k, j])
            for d in (2, 1, 3): self.first_z(k, d).start()
        elif i == 2:
            self.twelve(k).wait_recv()
            a = self.own(k, slice(None), z)
            tot = (a[...].astype(F32) + self.r2[k, 0].astype(F32)) + (self.r2[k, 1].astype(F32) + self.r1[k].astype(F32))
            a[...] = tot.astype(BF)
            for g in (1, 0): self.first_2(k, g).start()
        elif i == 3:
            for g, b in ((1, p1), (0, s)):
                self.first_2(k, g).wait_recv()
                a = self.own(k, b, z)
                a[...] = a[...] + self.rz[k, g]
                if g: self.first_1(k).start()
        else:
            self.first_1(k).wait_recv()
            self.outs(k)[...] = self.own(k, s, z)[...].astype(F32) + self.rz[k, 2].astype(F32)
    def run(self, k, i):
        if k in self.zfirst: return self.run_first(k, i)
        s, z, c, p1, p2 = self.where
        if i == 0:
            self.cp_c(k).start()
        elif i == 1:
            self.cp_c(k).wait_recv()
            for g, b in ((1, 3 - s), (0, p2)):
                self.add4(k, b, self.rcb[k, b])
                self.cp_2(k, g).start()
            for b in (p1, s): self.add4(k, b, self.rcb[k, b])
        elif i == 2:
            self.cp_2(k, 1).wait_recv()
            self.add4(k, p1, self.r2[k, 1])
            self.cp_1(k).start()
            self.cp_2(k, 0).wait_recv()
            self.add4(k, s, self.r2[k, 0])
        elif i == 3:
            self.cp_1(k).wait_recv()
            self.add4(k, s, self.r1[k])
            for d in (2, 1, 3): self.cp_z(k, d).start()
        else:
            self.three(k).wait_recv()
            tot = self.own(k, s, z)[...].astype(F32)
            for d in (1, 3, 2): tot = tot + self.rz[k, (z + d) % 4].astype(F32)
            self.outs(k)[...] = tot
    def drain(self, n):
        for k in range(n):
            self.cp_c(k).wait_send()
            if k in self.zfirst:
                self.twelve(k).wait_send(); self.first_1(k).wait_send()
                remote(self.own(k, 0, pl.ds(0, 2)), self.rz.at[k, pl.ds(0, 2)], self.s_2.at[k], self.q_2.at[k, 0], *self.d2).wait_send()
                continue
            remote(self.own(k, pl.ds(0, 2)), self.r2.at[k], self.s_2.at[k], self.q_2.at[k, 0], *self.d2).wait_send()
            self.cp_1(k).wait_send()
            self.three(k).wait_send()

CHUNKS = (("w", 1, 1), ("w", 0, 1), ("w", 2, 1), ("w", 3, 1), ("i", 0, 2), ("i", 1, 2), ("b", 0, 2), ("b", 1, 2))
LINE_LAST = (4,)
LINE_FIRST = ()
ORDER = (
    0, 9, 18, 27, 36, 1, 45, 10, 28, 2, 19, 13, 37, 54, 4, 177, 11, 31, 22, 5, 29, 14, 63, 178, 6, 23, 3, 32,
    20, 7, 21, 38, 179, 12, 24, 30, 15, 33, 46, 25, 55, 34, 58, 16, 39, 180, 47, 8, 26, 181, 17, 59, 81, 35, 56, 40,
    64, 182, 48, 84, 49, 83, 72, 82, 183, 57, 184, 60, 67, 41, 188, 61, 50, 187, 65, 150, 151, 152, 153, 42, 51, 73, 68, 76,
    52, 154, 66, 155, 189, 190, 62, 69, 70, 43, 185, 74, 75, 191, 53, 186, 77, 44, 78, 192, 193, 79, 71, 86, 85, 194, 87, 164,
    88, 80, 163, 165, 162, 89, 195, 196, 197, 105, 167, 100, 166, 168, 169, 106, 90, 101, 198, 199, 201, 91, 107, 173, 125, 203, 171, 115,
    170, 110, 126, 102, 108, 202, 116, 205, 206, 92, 95, 103, 156, 157, 158, 159, 127, 172, 207, 111, 93, 128, 209, 96, 210, 200, 130, 112,
    212, 211, 120, 131, 113, 117, 216, 97, 160, 161, 208, 129, 214, 215, 132, 135, 98, 118, 121, 204, 136, 217, 218, 219, 122, 222, 221, 133,
    174, 114, 145, 220, 140, 137, 109, 123, 146, 94, 119, 138, 175, 141, 213, 99, 147, 176, 148, 142, 139, 124, 223, 143, 149, 134, 224, 104,
    144,
)
UNROLL = True
UNROLL_T = 3

def body(order, lens, x_ref, cot_ref, wc_ref, wq_ref, wk_ref, wv_ref, wo_ref, win_ref, wback_ref, bin_ref, gains_ref, shifts_ref,
         res_o, gx_o, oq_o, ok_o, ov_o, oo_o, oi_o, ob_o, sums_o,
         own4, owni, ownb, ownv, vec, w4, wi, wb, lhs, xs, xa, xb, xm, nu, ra, rb, q_u, k_u, vpad, qm_u, km_u, p1_s, e3_s, ml_s, wz, sv, p2s, z6, nts, mden, cv, bias, wcp, wrp,
         ar, yt, gr, gp, gbs, rs1, acc, xh1, gb5, gi5, g4, dpad, e4, ra4, rb4, e6, ra6, rb6, sh5, core_g, sh7, dq1, memb, rcb, r2, r1b, rz, vr, va, vx, vy, vz, sums,
         qa, qb, sz, s1, s2, sc, sl, e0s, e0q, ua, ub, ug, uh, hs, s_c, q_c, s_2, q_2, s_1, q_1, s_z, q_z, va4, vb4, v6a, v6b, ug5, uh5, u7, u7h, hs2, vs, vq, osem, rsem):
    where = place()
    s, z, c, p1, p2 = where
    t = 2 * z + c
    nseq = vpad.shape[0]
    rows, width = x_ref.shape
    slots = rows // nseq
    pairs = width // 128
    n = nseq * pairs
    heads = 2 * pairs
    taps = wc_ref.shape[1]
    ff = wi.shape[1]
    nff = ff // width
    sub = wq_ref.shape[0]
    scale = 64 ** -0.5
    i32 = jnp.int32
    iota = lambda shape, d: lax.broadcasted_iota(i32, shape, d)
    four = [pltpu.make_async_copy(r, gp.at[pl.ds(sub, sub), pl.ds(i * width, width)], osem.at[i]) for i, r in enumerate((wq_ref, wk_ref, wv_ref, wo_ref))]
    four.append(pltpu.make_async_copy(win_ref, gp.at[pl.ds(0, sub)], osem.at[4]))
    four.append(pltpu.make_async_copy(wback_ref, gp.at[pl.ds(2 * sub, 4 * sub), pl.ds(0, width)], osem.at[5]))
    for cp in four: cp.start()
    greeted = greet(*where)
    for pad in (vpad, dpad):
        pad[:, 16 + slots:, :] = jnp.zeros((nseq, pad.shape[1] - 16 - slots, width), BF)
        pad[:, 0:16, :] = jnp.zeros((nseq, 16, width), BF)
    ownv[...] = jnp.zeros_like(ownv)
    ownv[0:2, 0:sub] = gains_ref[...]
    ownv[2:8, 0:sub] = shifts_ref[...]
    ownv[8:9, 0:4 * sub] = bin_ref[...]
    def edges(b, first, count):
        j = iota((count, 1), 0) + first
        return lax.shift_right_logical(j * lens[b], 6), lax.shift_right_logical((j + 1) * lens[b], 6)
    def counts(b, first, count):
        lo, hi = edges(b, first, count)
        return (hi - lo).astype(F32)
    def valid_of(b): return iota((slots, 1), 0) + t * slots < lens[b]
    def valid_all(): return jnp.concatenate([valid_of(b).astype(F32) for b in range(nseq)], axis=0)
    for b in range(nseq):
        lo, hi = edges(b, 0, 64)
        pos = iota((64, slots), 1) + t * slots
        memb[pl.ds(64 * b, 64), :] = jnp.where((pos >= lo) & (pos < hi), 1.0, 0.0).astype(BF)
    wcp[...] = jnp.zeros_like(wcp); wrp[...] = jnp.zeros_like(wrp)
    wcp[:, 0:taps] = wc_ref[...]
    w0 = wcp[:, 0:128]
    a1 = w0.astype(BF); rest = w0 - a1.astype(F32); a2 = rest.astype(BF); a3 = (rest - a2.astype(F32)).astype(BF)
    turn = jnp.where(iota((128, 128), 0) + iota((128, 128), 1) == taps - 1, 1.0, 0.0).astype(BF)
    wrp[:, 0:128] = (dot(a1, turn) + dot(a2, turn)) + dot(a3, turn)
    for cp in four: cp.wait()
    for i in range(4): own4[i] = gp[pl.ds(sub, sub), pl.ds(i * width, width)].astype(BF)
    owni[...] = gp[pl.ds(0, sub), :].astype(BF)
    ownb[...] = gp[pl.ds(2 * sub, 4 * sub), pl.ds(0, width)].astype(BF)
    pl.semaphore_wait(pltpu.get_barrier_semaphore(), greeted)
    chip = 2 * sub
    wv, iv, bv = w4.reshape(4, 4, 4, chip, width), wi.reshape(4, 4, chip, ff), wb.reshape(4, 4, 4 * chip, width)
    giv, gbv, gwv = gi5.reshape(4, 4, chip, ff), gb5.reshape(4, 4, 4 * chip, width), g4.reshape(4, 4, 4, chip, width)
    def span(c_, step, lo, cnt): return pl.ds(pl.multiple_of(c_ * step + lo, 8), cnt)
    views, srcs = [lambda s_, z_, c_: vec.at[s_, z_, c_]], [ownv]
    for kind, lo, cnt in CHUNKS:
        if kind == "w":
            views.append(lambda s_, z_, c_, lo=lo, cnt=cnt: wv.at[pl.ds(lo, cnt), s_, z_, span(c_, sub, 0, sub)])
            srcs.append(own4.at[pl.ds(lo, cnt)])
        elif kind == "i":
            m = ff // cnt
            views.append(lambda s_, z_, c_, lo=lo, m=m: iv.at[s_, z_, span(c_, sub, 0, sub), pl.ds(lo * m, m)])
            srcs.append(owni.at[:, pl.ds(lo * m, m)])
        else:
            m = 4 * sub // cnt
            views.append(lambda s_, z_, c_, lo=lo, m=m: bv.at[s_, z_, span(c_, 4 * sub, lo * m, m)])
            srcs.append(ownb.at[pl.ds(lo * m, m)])
    g = Gather(views, lambda k: srcs[k], LINE_LAST, (qa, qb, sz, s1, s2, sc, sl), where)
    e2 = UnitSum(nu, ra, rb, (ua.at[0], ua.at[1], ub.at[0], ub.at[1]), where, soft_combine)
    e3 = UnitShare(wz, (ug.at[0], uh, ug.at[1], ug.at[2]), where)
    halo = Halo(vpad, slots, hs.at[0], hs.at[1], where)
    dhalo = Halo(dpad, slots, hs2.at[0], hs2.at[1], where)
    sum4 = UnitSum(e4, ra4, rb4, (va4.at[0], va4.at[1], vb4.at[0], vb4.at[1]), where, plain_add)
    share5 = UnitShare(sh5, (ug5.at[0], uh5, ug5.at[1], ug5.at[2]), where)
    sum6 = UnitSum(e6, ra6, rb6, (v6a.at[0], v6a.at[1], v6b.at[0], v6b.at[1]), where, plain_add)
    share7 = UnitShare(sh7, (u7.at[0], u7h, u7.at[1], u7.at[2]), where)
    def part(k, c_, *at):
        at = (*at, *((slice(None),) * (2 - len(at))))
        if k < 4: return gbv.at[(*at, span(c_, 4 * sub, k * sub, sub))]
        if k < 4 + nff: return giv.at[(*at, span(c_, sub, 0, sub), pl.ds((k - 4) * width, width))]
        return gwv.at[(k - 4 - nff, *at, span(c_, sub, 0, sub))]
    def outs(k):
        if k < 4: return gp.at[pl.ds(k * sub, sub), pl.ds(0, width)]
        if k < 4 + nff: return gp.at[pl.ds(4 * sub, sub), pl.ds((k - 4) * width, width)]
        return gp.at[pl.ds(5 * sub, sub), pl.ds((k - 4 - nff) * width, width)]
    rs = Scatter(part, outs, LINE_FIRST, (rcb, r2, r1b, rz), (s_c, q_c, s_2, q_2, s_1, q_1, s_z, q_z), where)
    def xm_part():
        for b in range(nseq):
            xs[b] = dot(memb[pl.ds(64 * b, 64), :], x_ref[pl.ds(slots * b, slots), :])
        cp_xa().start(FIRST)
    def cp_xa(): return remote(xs.at[1 - c], xa, e0s.at[0], e0q.at[0], s, 2 * z + 1 - c)
    def cp_xb(d):
        zz = (z + d) % 4
        return remote(xs.at[c, pl.ds(pl.multiple_of(16 * zz, 16), 16)], xb.at[z], e0s.at[d], e0q.at[1 + z], s, 2 * zz + c)
    def cp_xm(d):
        return remote(xm.at[c, z], xm.at[c, z], e0s.at[3 + d], e0q.at[5 + z], s, 2 * ((z + d) % 4) + c)
    def cp_xc(zz):
        return remote(xm.at[c, zz], xm.at[c, zz], e0s.at[7 + zz], e0q.at[9 + zz], s, 2 * z + 1 - c)
    def xm_b():
        cp_xa().wait_recv()
        xs[c] = xs[c] + xa[...]
        for d in (2, 1, 3): cp_xb(d).start(FIRST)
    def xm_c():
        tot = xs[c, pl.ds(pl.multiple_of(16 * z, 16), 16), :]
        for d in (1, 3, 2):
            zz = (z + d) % 4
            remote(xb.at[zz], xb.at[zz], e0s.at[d], e0q.at[1 + zz], s, 2 * zz + c).wait_recv()
            tot = tot + xb[zz]
        xm[c, z] = tot / counts(c, 16 * z, 16)
        for d in (2, 1, 3): cp_xm(d).start(FIRST)
        cp_xc(z).start(FIRST)
    def xm_d():
        for d in (1, 3, 2):
            zz = (z + d) % 4
            remote(xm.at[c, zz], xm.at[c, zz], e0s.at[3 + d], e0q.at[5 + zz], s, 2 * zz + c).wait_recv()
            cp_xc(zz).start(FIRST)
    def xm_e():
        for zz in range(4):
            b = xm.at[1 - c, zz]
            remote(b, b, e0s.at[7 + zz], e0q.at[9 + zz], s, 2 * z + 1 - c).wait_recv()
        hi, lo = split(xm[...].reshape(64 * nseq, width))
        lhs[pl.ds(0, rows), :] = x_ref[...]
        lhs[pl.ds(rows, 64 * nseq), :] = hi
        lhs[pl.ds(rows + 64 * nseq, 64 * nseq), :] = lo
    def vectors():
        v = vec[...].reshape(32, 16, 128)
        def spread_rows(row, group, dst, at, count):
            for h in range(0, count, 256):
                k = iota((128, 256), 0); l = iota((128, 256), 1) + h
                w = dot(row, jnp.where((l % group == k) & (k < group), 1.0, 0.0).astype(BF)).reshape(32, 8, 256)
                mine = iota((32, 8, 256), 0) == (iota((32, 8, 256), 2) + h) // group
                dst(h, jnp.sum(jnp.where(mine, w, 0.0), axis=0))
        def to_cv(h, w): cv[:, pl.ds(h, 256)] = w
        def to_bias(h, w): bias[:, pl.ds(h, 256)] = w[0:1]
        spread_rows(v[:, 0:8, :].reshape(256, 128).astype(BF), sub, to_cv, 0, width)
        spread_rows(v[:, 8:16, :].reshape(256, 128).astype(BF), 4 * sub, to_bias, 0, ff)
    def projections():
        m_n = 64 * nseq
        valid = valid_all()
        for h in range(0, width, 256):
            cols = pl.ds(h, 256)
            v = ((dot(x_ref[...], w4[2, :, cols]) + cv[3:4, cols]) * valid).astype(BF)
            for b in range(nseq): vpad[b, pl.ds(16, slots), cols] = v[b * slots:(b + 1) * slots]
        halo.start()
        for i, (dst, marks) in ((1, (k_u, km_u)), (0, (q_u, qm_u))):
            for h in range(0, width, 256):
                cols = pl.ds(h, 256)
                r = dot(lhs[...], w4[i, :, cols])
                a = r[:rows]
                m = r[rows:rows + m_n] + r[rows + m_n:]
                if i == 0:
                    a = a + cv[2:3, cols]
                    m = m + cv[2:3, cols]
                a = a.astype(BF); m = m.astype(BF)
                for b in range(nseq):
                    for q in range(2):
                        u = b * pairs + h // 128 + q
                        dst[u] = a[b * slots:(b + 1) * slots, q * 128:(q + 1) * 128]
                        marks[u] = m[b * 64:(b + 1) * 64, q * 128:(q + 1) * 128]
    def cp_cot(): return pltpu.make_async_copy(cot_ref, lhs.at[pl.ds(rows, rows)], osem.at[0])
    def third():
        cp_cot().start()
        def unit(u, _):
            b, p = u // pairs, u % pairs
            ok = valid_of(b)
            sc3 = jnp.where(ok, dot(k_u[u], spread_diag(qm_u[u]), 1, 1) * scale, -1e30)
            m = jnp.max(sc3, axis=0, keepdims=True)
            e = jnp.where(ok, jnp.exp(sc3 - m), 0.0)
            e3_s[u] = e
            ml_s[u] = jnp.broadcast_to(m, (8, 128))
            v = vpad[b, pl.ds(16, slots), pl.ds(pl.multiple_of(p * 128, 128), 128)]
            nu[u // 3, u % 3, 0:64, :] = halves_diag(dot(v, e.astype(BF), 0, 0))
            nu[u // 3, u % 3, 64:72, :] = jnp.broadcast_to(m, (8, 128))
            nu[u // 3, u % 3, 65:66, :] = colsum(e)
            return 0
        lax.fori_loop(0, n, unit, 0, unroll=UNROLL)
        e2.start()
    def first(lo, hi):
        def unit(u, _):
            sc1 = dot(q_u[u], spread_diag(km_u[u]), 1, 1) * scale
            e = jnp.exp(sc1 - seg(jnp.max, sc1, -jnp.inf))
            pr = e / seg_sum(e)
            p1_s[u] = pr
            return 0
        lax.fori_loop(lo, hi, unit, 0, unroll=UNROLL)
    st = {}
    R2 = range(2)
    def slot(i): return 2 * c + i * (1 - c)
    def core_a():
        st["P"], st["Z"] = [], []
        for i in R2:
            pp, zz = core_setup(qm_u[3 * z + slot(i)], km_u[3 * z + slot(i)])
            p2s[i] = pp
            st["P"].append(pp); st["Z"].append(zz)
    def newton(it):
        eye = eye_pair()
        P, Z = st["P"], st["Z"]
        pr = [mm(P[i], Z[i]) for i in R2]
        t2 = [15.0 * eye - mm(pr[i], 7.0 * eye - pr[i]) for i in R2]
        t3 = [13.0 * eye - mm(pr[i], t2[i]) for i in R2]
        for i in R2:
            sv[i, it, 0] = Z[i]; sv[i, it, 1] = pr[i]; sv[i, it, 2] = t2[i]; sv[i, it, 3] = t3[i]
        st["Z"] = [0.25 * mm(Z[i], t3[i]) for i in R2]
    def core_z():
        for i in R2:
            k = slot(i)
            z6[i] = st["Z"][i]
            nt = nu[z, k, 0:64, :] / nu[z, k, 65:66, :]
            nts[i] = nt
            mden[i] = nu[z, k, 64:72, :]
            wz[z, k] = mm(st["Z"][i], nt, flip=True).astype(BF)
        e3.start()
    def attention():
        halo.end()
        def per(p, _):
            lanes = pl.ds(pl.multiple_of(p * 128, 128), 128)
            th = [split(skew(wcp[pl.ds(2 * p + e, 1), :], 256, slots)) for e in range(2)]
            low = lane_low((slots, 128))
            for b in range(nseq):
                u = b * pairs + p
                v = vpad[b, :, lanes]
                c0 = dot(th[0][0], v) + dot(th[0][1], v)
                c1 = dot(th[1][0], v) + dot(th[1][1], v)
                a = dot(p1_s[u].astype(BF), spread_diag(wz[u // 3, u % 3]))
                ar[pl.ds(b * slots, slots), lanes] = (a + jnp.where(low, c0, c1)).astype(BF)
            return 0
        lax.fori_loop(0, pairs, per, 0, unroll=UNROLL)
    def col_tiles(f):
        def tile(j, _):
            f(pl.ds(pl.multiple_of(j * 256, 256), 256)); return 0
        lax.fori_loop(0, width // 256, tile, 0, unroll=UNROLL)
    RB = 64
    def row_tiles(f):
        def tile(j, _):
            r0 = pl.multiple_of(j * RB, RB)
            f(pl.ds(r0, RB), r0); return 0
        lax.fori_loop(0, rows // RB, tile, 0)
    def valid_rows(r0):
        per = slots // RB
        b = r0 // slots
        return (iota((RB, 1), 0) + (r0 - b * slots + t * slots) < lens[b]).astype(F32)
    def out_proj():
        def proj(cols):
            acc[:, cols] = x_ref[:, cols].astype(F32) + dot(ar[...], w4[3, :, cols]) + cv[4:5, cols]
        col_tiles(proj)
        def norm(at, r0):
            xhat, rstd = norm_stats(acc[at, :])
            rs1[at, :] = rstd
            xh1[at, :] = xhat
            y = xhat * cv[0:1, :] + cv[5:6, :]
            yt[at, :] = y.astype(BF)
            acc[at, :] = y + cv[6:7, :]
        row_tiles(norm)
    def up(j):
        def tile(h, _):
            cols = pl.ds(pl.multiple_of(j * width + h * 256, 256), 256)
            u = dot(yt[...], wi[:, cols]) + bias[:, cols]
            phi = 0.5 * (1.0 + lax.erf(u * (0.5 ** 0.5)))
            gr[:, cols] = (u * phi).astype(BF)
            gp[:, cols] = phi + u * (jnp.exp(-0.5 * u * u) * 0.3989422804014327)
            return 0
        lax.fori_loop(0, width // 256, tile, 0, unroll=UNROLL)
    def down():
        def tile(cols): acc[:, cols] += dot(gr[...], wb[:, cols])
        col_tiles(tile)
    def cp_res(u):
        b, p = u // pairs, u % pairs
        return pltpu.make_async_copy(dq1.at[u], res_o.at[pl.ds(b * slots, slots), pl.ds(p * 128, 128)], rsem.at[0])
    def norm2():
        cp_cot().wait()
        vr[...] = jnp.zeros_like(vr)
        def norm(at, r0):
            xhat, rstd = norm_stats(acc[at, :])
            valid = valid_rows(r0)
            out = (xhat * cv[1:2, :] + cv[7:8, :]) * valid
            b = r0 // slots
            for p in range(pairs): dq1[b * pairs + p, pl.ds(pl.multiple_of(r0 - b * slots, RB), RB), :] = out[:, p * 128:(p + 1) * 128]
            dr = lhs[pl.ds(pl.multiple_of(rows + r0, RB), RB), :].astype(F32) * valid
            vr[1:2, :] += colsum(dr * xhat)
            vr[7:8, :] += colsum(dr)
            dh2 = norm_back(dr, cv[1:2, :], xhat, rstd)
            vr[6:7, :] += colsum(dh2)
            lhs[at, :] = dh2.astype(BF)
            acc[at, :] = dh2
        row_tiles(norm)
        for u in range(n): cp_res(u).start()
    def outer(dst, left, right):
        def tile(i, _):
            rows_ = pl.ds(pl.multiple_of(i * 256, 256), 256)
            lt = jnp.transpose(left[:, rows_])
            for h in range(0, width, 256): dst[rows_, pl.ds(h, 256)] = dot(lt, right[:, h:h + 256]).astype(BF)
            return 0
        lax.fori_loop(0, left.shape[1] // 256, tile, 0, unroll=UNROLL_T)
    def grad_back():
        outer(gb5, gr, lhs.at[pl.ds(0, rows)])
        for i in range(width // 256): yt[:, pl.ds(256 * i, 256)] = jnp.transpose(yt[:, pl.ds(256 * i, 256)])
    def bwd(j):
        def tile(h, _):
            cols = pl.ds(pl.multiple_of(j * width + h * 256, 256), 256)
            du = gp[:, cols] * dot(lhs[pl.ds(0, rows), :], wb[cols, :], 1, 1)
            gbs[:, cols] = colsum(du)
            dur = du.astype(BF)
            gr[:, cols] = dur
            return 0
        lax.fori_loop(0, width // 256, tile, 0, unroll=UNROLL)
    def grad_in(j):
        def tile(h, _):
            cols = pl.ds(pl.multiple_of(j * width + h * 256, 256), 256)
            for i in range(width // 256): gi5[pl.ds(256 * i, 256), cols] = dot(yt[:, pl.ds(256 * i, 256)], gr[:, cols]).astype(BF)
            return 0
        lax.fori_loop(0, width // 256, tile, 0, unroll=UNROLL)
    def dy():
        def tile(cols): acc[:, cols] += dot(gr[...], wi[cols, :], 1, 1)
        col_tiles(tile)
    def weight_grad(i, left, right): outer(g4.at[i], left, right)
    def norm1():
        def norm(at, r0):
            dy, xhat = acc[at, :], xh1[at, :]
            vr[0:1, :] += colsum(dy * xhat)
            vr[5:6, :] += colsum(dy)
            d = norm_back(dy, cv[0:1, :], xhat, rs1[at, :])
            vr[4:5, :] += colsum(d)
            acc[at, :] = d
            lhs[pl.ds(pl.multiple_of(rows + r0, RB), RB), :] = d.astype(BF)
        row_tiles(norm)
        def da_tile(cols):
            da = dot(lhs[pl.ds(rows, rows), :], w4[3, cols, :], 1, 1).astype(BF)
            for b in range(nseq): dpad[b, pl.ds(16, slots), cols] = da[b * slots:(b + 1) * slots]
        col_tiles(da_tile)
        dhalo.start()
    def units_a():
        pltpu.make_async_copy(dq1, dq1, rsem.at[0]).wait()
        def unit(u, _):
            b, p = u // pairs, u % pairs
            da = dpad[b, pl.ds(16, slots), pl.ds(p * 128, 128)]
            e4[u // 3, u % 3, 0:64, :] = halves_diag(dot(p1_s[u].astype(BF), da, 0, 0))
            return 0
        for u in range(n): unit(u, 0)
        sum4.start()
    def units_b():
        def unit(u, _):
            b, p = u // pairs, u % pairs
            da = dpad[b, pl.ds(16, slots), pl.ds(p * 128, 128)]
            pr = p1_s[u]
            dp1 = dot(da, spread_diag(wz[u // 3, u % 3]), 1, 1)
            ds1 = (pr * (dp1 - seg_sum(dp1 * pr)) * scale).astype(BF)
            e6[u // 3, u % 3, 64:128, :] = halves_diag(dot(ds1, q_u[u], 0, 0)).astype(BF)
            dq1[u] = dot(ds1, spread_diag(km_u[u]))
            return 0
        for u in range(n): unit(u, 0)
    def grad_conv():
        wcp[...] = jnp.zeros_like(wcp)
        def unit(u, _):
            b, p = u // pairs, u % pairs
            lanes = pl.ds(pl.multiple_of(p * 128, 128), 128)
            v = vpad[b, :, lanes]
            turn = jnp.where(iota((slots, slots), 0) + iota((slots, slots), 1) == slots - 1, 1.0, 0.0).astype(BF)
            da = dot(turn, dpad[b, pl.ds(16, slots), lanes]).astype(BF)
            low = lane_low(da.shape)
            zero = jnp.zeros_like(da)
            for e in range(2):
                m = dot(jnp.where(low, da, zero) if e == 0 else jnp.where(low, zero, da), v, 1, 1)
                m = pltpu.roll(m, m.shape[1] - slots + 1, 1, stride=1, stride_axis=0)
                wcp[pl.ds(2 * p + e, 1), :] += colsum(m)
            return 0
        lax.fori_loop(0, n, unit, 0, unroll=UNROLL)
        vr[12:24, 0:128] = wcp[:, 0:128]
    def cb_a():
        st["G"], st["DP"] = [], []
        for i in R2:
            k = slot(i)
            dwz = e4[z, k, 0:64, :]
            nt = nts[i]
            den = mden[i, 1:2, :]
            dnt = mm(flip64(dwz), z6[i])
            dden = -colsum(dnt * nt) / den
            tile = jnp.zeros((16, 128), F32)
            row = iota((16, 128), 0)
            for j, v in enumerate((mden[i, 0:1, :], dden)):
                for q in range(3):
                    h = v.astype(BF).astype(F32)
                    tile = jnp.where(row == 3 * j + q, h, tile)
                    v = v - h
            sh5[z, k, 0:64, :] = (dnt / den).astype(BF)
            sh5[z, k, 64:80, :] = tile.astype(BF)
            st["G"].append(mm(flip64(nt), dwz, flip=True))
            st["DP"].append(jnp.zeros((64, 128), F32))
        share5.start()
    def cb(it):
        eye = eye_pair()
        G, DP = st["G"], st["DP"]
        Z = [sv[i, it, 0] for i in R2]; Pr = [sv[i, it, 1] for i in R2]; T2 = [sv[i, it, 2] for i in R2]; T3 = [sv[i, it, 3] for i in R2]
        d3 = [0.25 * mm(G[i], Z[i]) for i in R2]
        d2 = [-mm(d3[i], Pr[i]) for i in R2]
        dz = [0.25 * mm(T3[i], G[i]) for i in R2]
        dp = [-mm(T2[i], d3[i]) for i in R2]
        d1 = [-mm(d2[i], Pr[i]) for i in R2]
        dp = [dp[i] - mm(7.0 * eye - Pr[i], d2[i]) - d1[i] for i in R2]
        st["G"] = [dz[i] + mm(dp[i], p2s[i]) for i in R2]
        st["DP"] = [DP[i] + mm(Z[i], dp[i]) for i in R2]
    def cb_z():
        for i in R2:
            u = 3 * z + slot(i)
            p, g0 = p2s[i], st["G"][i]
            col = colsum(p)
            top = seg(jnp.max, col, -jnp.inf)
            f = 1.0 / top
            df = seg(jnp.sum, colsum(g0 * p), 0.0)
            hit = (col == top).astype(F32)
            dcol = -f * f * df * hit / seg(jnp.sum, hit, 0.0)
            dp = flip64(st["DP"][i]) + f * g0 + dcol
            ds = p * (dp - seg(jnp.sum, dp * p, 0.0)) * scale
            hi, lo = split(ds)
            b = spread_diag(km_u[u])
            core_g[i, 0:64, :] = dot(hi, b) + dot(lo, b)
            hi, lo = split(flip64(ds))
            b = spread_diag(qm_u[u])
            core_g[i, 64:128, :] = dot(hi, b) + dot(lo, b)
    def third_b():
        def unit(u, _):
            b, p = u // pairs, u % pairs
            tile = sh5[u // 3, u % 3, 64:80, :].astype(F32)
            m = tile[0:1] + tile[1:2] + tile[2:3]
            dden = tile[3:4] + tile[4:5] + tile[5:6]
            e = e3_s[u] * jnp.exp(ml_s[u, 0:1, :] - m)
            dn = spread_diag(sh5[u // 3, u % 3, 0:64, :])
            v = vpad[b, pl.ds(16, slots), pl.ds(pl.multiple_of(p * 128, 128), 128)]
            de = dot(v, dn) + dden
            p1_s[u] = dot(e.astype(BF), dn, 1, 1)
            ds = (e * de * scale).astype(BF)
            e6[u // 3, u % 3, 0:64, :] = halves_diag(dot(ds, k_u[u], 0, 0)).astype(BF)
            e3_s[u] = dot(ds, spread_diag(qm_u[u]))
            return 0
        lax.fori_loop(0, n, unit, 0, unroll=UNROLL)
        sum6.start()
    def conv():
        dhalo.end()
        def per(p, _):
            lanes = pl.ds(pl.multiple_of(p * 128, 128), 128)
            th = [split(skew(wrp[pl.ds(2 * p + e, 1), :], 256, slots)) for e in range(2)]
            low = lane_low((slots, 128))
            tot = jnp.zeros((1, 128), F32)
            for b in range(nseq):
                u = b * pairs + p
                d = dpad[b, :, lanes]
                c0 = dot(th[0][0], d) + dot(th[0][1], d)
                c1 = dot(th[1][0], d) + dot(th[1][1], d)
                v = (p1_s[u] + jnp.where(low, c0, c1)) * valid_of(b).astype(F32)
                tot = tot + colsum(v)
                yt[pl.ds(b * slots, slots), lanes] = v.astype(BF)
            vr[3:4, lanes] = tot
            return 0
        lax.fori_loop(0, pairs, per, 0, unroll=UNROLL)
    def own_marks():
        cn = counts(z // 2, 0, 64)
        for i in R2:
            k = slot(i)
            sh7[z, k, 0:64, :] = ((core_g[i, 0:64, :] + e6[z, k, 0:64, :].astype(F32)) / cn).astype(BF)
            sh7[z, k, 64:128, :] = ((core_g[i, 64:128, :] + e6[z, k, 64:128, :].astype(F32)) / cn).astype(BF)
        share7.start()
    def queries():
        def unit(u, _):
            b, p = u // pairs, u % pairs
            lanes = pl.ds(pl.multiple_of(p * 128, 128), 128)
            r0 = pl.multiple_of(b * slots, slots)
            mb = memb[pl.ds(pl.multiple_of(64 * b, 64), 64), :]
            q = dot(mb, sh7[u // 3, u % 3, 0:64, :], 0, 0) + dq1[u]
            k = dot(mb, sh7[u // 3, u % 3, 64:128, :], 0, 0) + e3_s[u]
            lhs[pl.ds(r0, slots), lanes] = q.astype(BF)
            lhs[pl.ds(rows + r0, slots), lanes] = k.astype(BF)
            vr[2:3, lanes] += colsum(q)
            return 0
        lax.fori_loop(0, n, unit, 0, unroll=UNROLL)
    def gx1():
        def tile(cols): acc[:, cols] += dot(yt[...], w4[2, cols, :], 1, 1)
        col_tiles(tile)
    def cp_gx(): return pltpu.make_async_copy(acc, gx_o, osem.at[1])
    def gx2():
        def tile(cols):
            acc[:, cols] += dot(lhs[pl.ds(0, rows), :], w4[0, cols, :], 1, 1) + dot(lhs[pl.ds(rows, rows), :], w4[1, cols, :], 1, 1)
        col_tiles(tile)
        cp_gx().start()
    px = s + 1 - 2 * (s % 2)
    py = (s + 2) % 4
    def cp_v(i):
        dst, dev = ((va, (s, 2 * z + 1 - c)), (vx, (px, t)), (vy, (py, t)))[i]
        return remote(vr, dst, vs.at[i], vq.at[i], *dev)
    def cp_vz(d): return remote(vr, vz.at[z], vs.at[2 + d], vq.at[3 + z], s, 2 * ((z + d) % 4) + c)
    def vec_0():
        for i in range(nff): vr[8 + i:9 + i, :] = gbs[:, pl.ds(i * width, width)]
        cp_v(0).start(FIRST)
    def vec_step(i):
        cp_v(i).wait()
        vr[...] = vr[...] + (va, vx, vy)[i][...]
        if i < 2: cp_v(i + 1).start(FIRST)
        else:
            for d in (1, 2, 3): cp_vz(d).start(FIRST)
    def vec_z():
        for d in (1, 2, 3):
            zz = (z + d) % 4
            remote(vr, vz.at[zz], vs.at[2 + d], vq.at[3 + zz], s, 2 * zz + c).wait_recv()
        for d in (1, 2, 3): cp_vz(d).wait_send()
        vz[z] = vr[...]
        sums[...] = ((vz[0] + vz[1]) + vz[2]) + vz[3]
    half = n // 2
    P_ = functools.partial
    steps = [P_(g.run, k, i) for k in range(len(views)) for i in range(Gather.STAGES)] + [P_(g.arrive, k) for k in range(len(views))]
    nk = 8 + nff
    steps += [P_(rs.run, k, i) for k in range(nk) for i in range(Scatter.STAGES)]
    steps += [P_(newton, i) for i in range(ITERS)] + [P_(cb, ITERS - 1 - i) for i in range(ITERS)] + [P_(up, j) for j in range(nff)] + [P_(bwd, j) for j in range(nff)] + [P_(grad_in, j) for j in range(nff)]
    steps += [P_(vec_step, i) for i in range(3)]
    steps += [xm_part, xm_b, xm_c, xm_d, xm_e, vectors, projections, third, P_(first, 0, half), P_(first, half, n), core_a, e2.mid, e2.end, core_z, e3.mid, e3.end, attention, out_proj,
              down, norm2, grad_back, dy, norm1, P_(weight_grad, 0, ar, lhs.at[pl.ds(rows, rows)]), units_a, units_b, sum4.mid, grad_conv, sum4.end, cb_a, share5.mid, cb_z, share5.end, third_b,
              conv, sum6.mid, gx1, sum6.end, own_marks, P_(weight_grad, 1, x_ref, yt), share7.mid, share7.end, queries, P_(weight_grad, 2, x_ref, lhs.at[pl.ds(rows, rows)]),
              P_(weight_grad, 3, x_ref, lhs.at[pl.ds(0, rows)]), vec_0, gx2, vec_z]
    for i in order: steps[i]()
    o = [pltpu.make_async_copy(gp.at[pl.ds(a, m), pl.ds(b, w)], dst, osem.at[2 + i]) for i, (a, m, b, w, dst) in enumerate((
        (0, 4 * sub, 0, width, ob_o), (4 * sub, sub, 0, ff, oi_o), (5 * sub, sub, 0, width, oo_o), (5 * sub, sub, width, width, ov_o),
        (5 * sub, sub, 2 * width, width, ok_o), (5 * sub, sub, 3 * width, width, oq_o)))]
    o.append(pltpu.make_async_copy(sums, sums_o, osem.at[8]))
    for cp in o: cp.start()
    g.drain(); e2.drain(); e3.drain(); halo.drain()
    cp_xa().wait_send()
    for d in (1, 2, 3):
        cp_xb(d).wait_send(); cp_xm(d).wait_send()
    for zz in range(4): cp_xc(zz).wait_send()
    rs.drain(nk)
    sum4.drain(); share5.drain(); sum6.drain(); share7.drain(); dhalo.drain()
    cp_gx().wait()
    for cp in o: cp.wait()

def whole(lengths, x, cot, wc, shards, order=ORDER):
    S = jax.ShapeDtypeStruct
    rows, width = x.shape
    wq, wk, wv, wo, win, wback, bin_, gains, shifts = shards
    nseq = lengths.shape[0]
    slots = rows // nseq
    sub, ff = wq.shape[0], win.shape[1]
    n = nseq * width // 128
    nk = 8 + ff // width
    na = 1 + len(CHUNKS)
    V = lambda *sh: pltpu.VMEM(sh, F32)
    B = lambda *sh: pltpu.VMEM(sh, BF)
    D = lambda *sh: pltpu.SemaphoreType.DMA(sh)
    vm = pl.BlockSpec(memory_space=pltpu.VMEM); hb = pl.BlockSpec(memory_space=pl.ANY)
    return pl.pallas_call(
        functools.partial(body, tuple(order)),
        out_shape=(S((rows, width), F32),) * 2 + (S((sub, width), F32),) * 4 + (S((sub, ff), F32), S((4 * sub, width), F32), S((24, width), F32)),
        in_specs=[pl.BlockSpec(memory_space=pltpu.SMEM), vm, hb, vm] + [hb] * 6 + [vm] * 3,
        out_specs=(hb,) * 9,
        scratch_shapes=[B(4, sub, width), B(sub, ff), B(4 * sub, width), V(16, 128), V(4, 4, 2, 16, 128), B(4, width, width), B(width, ff), B(ff, width), B(rows + 128 * nseq, width),
                        V(2, 64, width), V(64, width), V(4, 16, width), V(2, 4, 16, width), V(4, 3, 72, 128), V(4, 2, 72, 128), V(4, 2, 72, 128),
                        B(n, slots, 128), B(n, slots, 128), B(nseq, 256, width), B(n, 64, 128), B(n, 64, 128), V(n, slots, 128), V(n, slots, 128), V(n, 8, 128),
                        B(4, 3, 64, 128), V(2, ITERS, 4, 64, 128), V(2, 64, 128), V(2, 64, 128), V(2, 64, 128), V(2, 8, 128), V(8, width), V(1, ff), V(wc.shape[0], 256), V(wc.shape[0], 256),
                        B(rows, width), B(rows, width), B(rows, ff), V(rows, ff), V(1, ff), V(rows, 1), V(rows, width), V(rows, width),
                        B(ff, width), B(width, ff), B(4, width, width), B(nseq, 256, width), V(4, 3, 64, 128), V(4, 2, 64, 128), V(4, 2, 64, 128), B(4, 3, 128, 128), B(4, 2, 128, 128), B(4, 2, 128, 128), B(4, 3, 80, 128),
                        V(2, 128, 128), B(4, 3, 128, 128), V(n, slots, 128), B(64 * nseq, slots),
                        B(nk, 4, 4, sub, width), B(nk, 2, 4, sub, width), B(nk, 4, sub, width), B(nk, 4, sub, width),
                        V(24, width), V(24, width), V(24, width), V(24, width), V(4, 24, width), V(24, width),
                        D(na, 9), D(na), D(na, 2), D(na), D(na), D(na), D(na), D(11), D(13), D(2), D(2, 2), D(3, 2), D(4, 2), D(2, 2),
                        D(nk), D(nk), D(nk), D(nk, 2), D(nk), D(nk), D(nk), D(nk), D(2), D(2, 2), D(2), D(2, 2), D(3, 2), D(4, 2), D(3, 2), D(4, 2), D(2, 2),
                        D(6), D(7), D(9), D(1)],
        compiler_params=pltpu.CompilerParams(collective_id=0, has_side_effects=True, vmem_limit_bytes=67043328),
        name="layer_whole",
    )(lengths, x, cot, wc, wq, wk, wv, wo, win, wback, bin_, gains, shifts)


def hand_out(taps, *refs):
    big, sums_ref = refs[:8], refs[8]
    outs, (conv_o, bias_o, gains_o, shifts_o) = refs[9:17], refs[17:21]
    bufs, sums, sin, sout = refs[21:29], refs[29], refs[30], refs[31]
    a = [pltpu.make_async_copy(r, b, sin.at[i]) for i, (r, b) in enumerate(zip((*big, sums_ref), (*bufs, sums)))]
    o = [pltpu.make_async_copy(b, r, sout.at[i]) for i, (r, b) in enumerate(zip(outs, bufs))]
    for cp in a: cp.start()
    me = lax.axis_index("seq") * 8 + lax.axis_index("tok")
    sub = gains_o.shape[1]
    width = sums.shape[1]
    a[8].wait()
    v = pltpu.roll(sums[0:8, :], (width - sub * me) % width, 1)
    gains_o[...] = v[0:2, 0:sub]
    shifts_o[...] = v[2:8, 0:sub]
    f4 = bias_o.shape[1]
    per = width // f4
    row = lax.broadcasted_iota(jnp.int32, (4, width), 0)
    b = jnp.sum(jnp.where(row == me // per, sums[8:12, :], 0.0), axis=0, keepdims=True)
    b = pltpu.roll(jnp.broadcast_to(b, (8, width)), (width - f4 * (me % per)) % width, 1)
    bias_o[...] = b[0:1, 0:f4]
    conv_o[...] = sums[12:24, 0:taps]
    for i in range(8):
        a[i].wait()
        o[i].start()
    for cp in o: cp.wait()

def finish(big, sums, taps):
    S = jax.ShapeDtypeStruct
    width = sums.shape[1]
    sub = width // 32
    vm = pl.BlockSpec(memory_space=pltpu.VMEM); hb = pl.BlockSpec(memory_space=pl.ANY)
    return pl.pallas_call(
        functools.partial(hand_out, taps),
        out_shape=tuple(S(b.shape, F32) for b in big) + (S((12, taps), F32), S((1, 4 * sub), F32), S((2, sub), F32), S((6, sub), F32)),
        in_specs=[hb] * 9,
        out_specs=(hb,) * 8 + (vm,) * 4,
        scratch_shapes=[pltpu.VMEM(b.shape, F32) for b in big] + [pltpu.VMEM(sums.shape, F32), pltpu.SemaphoreType.DMA((9,)), pltpu.SemaphoreType.DMA((8,))],
        name="hand_out",
    )(*big, sums)


def fast_shards(inputs, lengths, bounds, w_query, w_key, w_value, w_out, w_conv, w_in, w_back, b_in, gains, shifts, cotangent):
    shape = inputs.shape
    x = inputs.reshape(-1, shape[2])
    owned = (w_query, w_key, w_value, w_out, w_in, w_back, b_in.reshape(1, -1), gains, shifts)
    *big, sums = whole(lengths, x, cotangent.reshape(x.shape), w_conv, owned)
    res, gx, gq, gk, gv, go, gi, gb, conv, bias, gain, shift = finish(big, sums, w_conv.shape[1])
    return (res.reshape(shape), gx.reshape(shape), gq, gk, gv, go, conv, gi, gb, bias.reshape(-1), gain, shift)


def solution(mesh):
    placed = (
        P("seq", "tok", None),
        P("seq"),
        P("seq", None),
        P(("seq", "tok"), None),
        P(("seq", "tok"), None),
        P(("seq", "tok"), None),
        P(("seq", "tok"), None),
        P(),
        P(("seq", "tok"), None),
        P(("seq", "tok"), None),
        P(("seq", "tok")),
        P(None, ("seq", "tok")),
        P(None, ("seq", "tok")),
        P("seq", "tok", None),
    )
    return jax.shard_map(
        fast_shards if (mesh.shape["seq"], mesh.shape["tok"]) == (4, 8) else shards,
        mesh=mesh,
        in_specs=placed,
        out_specs=(
            P("seq", "tok", None),
            P("seq", "tok", None),
            P(("seq", "tok"), None),
            P(("seq", "tok"), None),
            P(("seq", "tok"), None),
            P(("seq", "tok"), None),
            P(),
            P(("seq", "tok"), None),
            P(("seq", "tok"), None),
            P(("seq", "tok")),
            P(None, ("seq", "tok")),
            P(None, ("seq", "tok")),
        ),
        check_vma=False,
    )
```
